32 devices in a mesh: fsdp: 8 (over y, x, core), context: 4 (over z).
Axes of the slice: x: 2, y: 2, z: 4, core: 2. Of those that a mesh axis runs over, the one named last changes fastest.
Arguments:
- hidden_in: bfloat16 [8, 1024, 1536], P('fsdp', 'context'), may hold values from -6 to 6
- cotangent: bfloat16 [8, 1024, 1536], P('fsdp', 'context'), may hold values from -6 to 6
- seq_lengths: int32 [8], P('fsdp'), may hold values from 1 to 1024, 6144 in all
- tile_place: int32 [8, 8], P('fsdp'), may hold values from 0 to 7, each once within a row
- norm_attn: bfloat16 [2, 1536], P(None, 'fsdp'), may hold values from 0.25 to 1.75
- w_qkv: bfloat16 [2, 1536, 2048], P(None, 'fsdp'), may hold values from -0.15625 to 0.15625
- b_qkv: bfloat16 [2, 2048], P(None, 'fsdp'), may hold values from -3 to 3
- w_out: bfloat16 [2, 1536, 1536], P(None, 'fsdp'), may hold values from -0.625 to 0.625
- norm_mlp: bfloat16 [2, 1536], P(None, 'fsdp'), may hold values from 0.25 to 1.75
- w_gate: bfloat16 [2, 1536, 8960], P(None, 'fsdp', 'context'), may hold values from -0.15625 to 0.15625
- w_up: bfloat16 [2, 1536, 8960], P(None, 'fsdp', 'context'), may hold values from -0.15625 to 0.15625
- w_down: bfloat16 [2, 8960, 1536], P(None, 'context', 'fsdp'), may hold values from -0.0625 to 0.0625
Outputs:
- layer_out: bfloat16 [8, 1024, 1536], P('fsdp', 'context')
- grad_in: float32 [8, 1024, 1536], P('fsdp', 'context')
- grad_norm_attn: float32 [2, 1536], P(None, 'fsdp')
- grad_w_qkv: float32 [2, 1536, 2048], P(None, 'fsdp')
- grad_b_qkv: float32 [2, 2048], P(None, 'fsdp')
- grad_w_out: float32 [2, 1536, 1536], P(None, 'fsdp')
- grad_norm_mlp: float32 [2, 1536], P(None, 'fsdp')
- grad_w_gate: float32 [2, 1536, 8960], P(None, 'fsdp', 'context')
- grad_w_up: float32 [2, 1536, 8960], P(None, 'fsdp', 'context')
- grad_w_down: float32 [2, 8960, 1536], P(None, 'context', 'fsdp')
The draws below stay inside these ranges and needn't reach their ends.
Inputs may be any that keep to these rules, and one draw needn't show every extreme that they name: `seq_lengths`: each index of fsdp holds one sequence of this many tokens, padded to 1024 rows; some sequence has exactly 1024. For each index of fsdp a permutation: rows 128 * j to 128 * j + 127 hold tile tile_place[j] of the sequence.
All inputs are finite; a program needn't handle non-finite values. No bound on the sum of `seq_lengths` on one device may be relied on, other than what follows from the above.
Results may differ from the reference program's by a relative error of at most 0.022.
Values may be sent and summed in bfloat16 or wider, within the bound.
A program may use at most 320 MiB of HBM per device.

```python
import math
import jax
import jax.numpy as jnp
import numpy as np
from jax import lax

D = 1536
QUERY_HEADS = 12
KEY_VALUE_HEADS = 2
HEAD_SIZE = 128
FF = 8960
LAYERS = 2
SEQUENCE_ROWS = 1024
TILE = 128
QKV = 2048
GROUP_TILES = 8
N_FSDP = 8


def shard_levels(stream_key, dims, pieces, least, high):
    loudness, own = 1.0, jax.random.fold_in(stream_key, 6)
    for dim, parts in pieces:
        draws = jnp.exp(jax.random.uniform(jax.random.fold_in(own, dim), (parts,), jnp.float32, least / len(pieces), high / len(pieces)))
        loudness = loudness * jnp.repeat(draws, dims[dim] // parts).reshape([-1 if axis == dim else 1 for axis in range(len(dims))])
    return loudness


def length_profile(number_of, total, most, skew):
    loads = [(1 << 20) // math.isqrt(rank ** skew) + 1 for rank in range(2, number_of + 1)]
    surplus, holding = total - most - (number_of - 1), [1] * (number_of - 1)
    while surplus > 0:
        movable = [i for i in range(number_of - 1) if holding[i] < most]
        mass, left = sum([loads[i] for i in movable]), surplus
        for i in movable:
            addition = min(most - holding[i], max(1, left * loads[i] // mass), surplus)
            holding[i] = holding[i] + addition
            surplus = surplus - addition
    return np.array([most] + holding)


def uneven(key, number_of, total, limit, skew):
    if number_of == 2:
        one = jax.random.randint(key, (), max(1, total - limit), min(limit, total - 1) + 1)
        return jnp.stack([one, total - one])
    sizes = jnp.asarray(length_profile(number_of, total, limit, skew), jnp.int32)
    couples = (number_of - 1) // 2
    giver, receiver = sizes[1:1 + 2 * couples:2], sizes[2:2 + 2 * couples:2]
    slack = jnp.minimum(giver - 1, limit - receiver)
    moved = jax.random.randint(jax.random.fold_in(key, 1), (couples,), 0, 1 << 20) % (slack + 1)
    sizes = sizes.at[1:1 + 2 * couples:2].set(giver - moved).at[2:2 + 2 * couples:2].set(receiver + moved)
    return sizes[jax.random.permutation(jax.random.fold_in(key, 2), number_of)]


def bell_draw(rng, extent, width, reach, split=(), kind=jnp.bfloat16):
    values = width * jax.random.normal(rng, extent, jnp.float32)
    if split:
        values = values * shard_levels(rng, extent, split, -0.22, 0.18)
    return jnp.clip(values, -reach, reach).astype(kind)


def setup_inputs(seed: int = 0) -> dict:
    key_of = jax.random.split(jax.random.key(seed), 13)
    return {
        "hidden_in": bell_draw(key_of[0], (N_FSDP, SEQUENCE_ROWS, D), 1.0, 6.0, ((0, 8), (1, 4))),
        "cotangent": bell_draw(key_of[1], (N_FSDP, SEQUENCE_ROWS, D), 1.0, 6.0, ((0, 8), (1, 4))),
        "seq_lengths": uneven(key_of[2], N_FSDP, N_FSDP * SEQUENCE_ROWS * 3 // 4, SEQUENCE_ROWS, 1).astype(jnp.int32),
        "tile_place": jax.vmap(lambda own: jax.random.permutation(own, GROUP_TILES))(jax.random.split(key_of[3], N_FSDP)).reshape((N_FSDP, GROUP_TILES)).astype(jnp.int32),
        "norm_attn": jnp.clip(1.0 + 0.15 * jax.random.normal(key_of[4], (LAYERS, D), jnp.float32), 0.25, 1.75).astype(jnp.bfloat16),
        "w_qkv": bell_draw(key_of[5], (LAYERS, D, QKV), D ** -0.5, 0.15625, ((1, 8),)),
        "b_qkv": bell_draw(key_of[6], (LAYERS, QKV), 0.5, 3.0, ((1, 8),)),
        "w_out": bell_draw(key_of[7], (LAYERS, QUERY_HEADS * HEAD_SIZE, D), (D // 16) ** -0.5, 0.625, ((1, 8),)),
        "norm_mlp": jnp.clip(1.0 + 0.15 * jax.random.normal(key_of[8], (LAYERS, D), jnp.float32), 0.25, 1.75).astype(jnp.bfloat16),
        "w_gate": bell_draw(key_of[9], (LAYERS, D, FF), D ** -0.5, 0.15625, ((1, 8), (2, 4))),
        "w_up": bell_draw(key_of[10], (LAYERS, D, FF), D ** -0.5, 0.15625, ((1, 8), (2, 4))),
        "w_down": bell_draw(key_of[11], (LAYERS, FF, D), FF ** -0.5, 0.0625, ((1, 4), (2, 8))),
    }


EPSILON = 1e-06
ROPE_BASE = 1000000.0

@jax.custom_vjp
def lowered_input(v):
    return lax.optimization_barrier(v.astype(jnp.bfloat16)).astype(jnp.float32)

@jax.custom_vjp
def low_back(v):
    return v

def low_keep(v):
    return (lowered_input(v), None)

def low_pass(kept, grad):
    return (grad,)

def back_keep(v):
    return (v, None)

def back_low(kept, grad):
    return (lowered_input(grad),)
lowered_input.defvjp(low_keep, low_pass)
low_back.defvjp(back_keep, back_low)

def highest(left, right):
    return jnp.dot(left, right, precision=lax.Precision.HIGHEST)

def normalize(stream, gain):
    return stream * lax.rsqrt(lax.optimization_barrier(jnp.mean(stream * stream, axis=-1, keepdims=True)) + EPSILON) * gain

def apply_rotation(heads, cosine_table, sine_values):
    half_width = heads.shape[-1] // 2
    first_half = heads[..., :half_width]
    second = heads[..., half_width:]
    return jnp.concatenate([first_half * cosine_table - second * sine_values, second * cosine_table + first_half * sine_values], axis=-1)

def frequencies():
    return jnp.power(ROPE_BASE, -(jnp.arange(HEAD_SIZE // 2, dtype=jnp.float32) * 2.0 / HEAD_SIZE))

def group_positions(length, tile_order):
    row_index = jnp.arange(SEQUENCE_ROWS, dtype=jnp.int32)
    tile_ids = tile_order[row_index // TILE]
    position = tile_ids * TILE + row_index % TILE
    return (position, position < length)

def attend(query_rows, gathered_keys, gathered_values, position, validity):
    inv_root = 1.0 / math.sqrt(HEAD_SIZE)
    scores = jnp.einsum('tgrd,kgd->grtk', query_rows, gathered_keys, precision=lax.Precision.HIGHEST) * inv_root
    allowed = (position[None, :] <= position[:, None]) & validity[None, :]
    scores = jnp.where(allowed, scores, -1e+30)
    softmax_weights = jax.nn.softmax(scores, axis=-1)
    return jnp.einsum('grtk,kgd->tgrd', softmax_weights, gathered_values, precision=lax.Precision.HIGHEST)

def attend_group(operands):
    return jax.checkpoint(attend)(operands[0], operands[1], operands[2], operands[3], operands[4])

def forward(stream, weight_set, position, validity, cosine_table, sine_values):
    gain_one, qkv_w, qkv_b, out_w, gain_two, gate_w, up_w, down_w = weight_set
    query_heads_width = QUERY_HEADS * HEAD_SIZE
    key_value_width = KEY_VALUE_HEADS * HEAD_SIZE
    for layer_index in range(LAYERS):
        flat = stream.reshape(N_FSDP * SEQUENCE_ROWS, D)
        normed = lowered_input(normalize(flat, gain_one[layer_index]))
        projected_output = low_back(highest(normed, qkv_w[layer_index]) + qkv_b[layer_index])
        projected_output = projected_output.reshape(N_FSDP, SEQUENCE_ROWS, query_heads_width + 2 * key_value_width)
        query_rows = lowered_input(apply_rotation(projected_output[..., :query_heads_width].reshape(N_FSDP, SEQUENCE_ROWS, QUERY_HEADS, HEAD_SIZE), cosine_table, sine_values))
        gathered_keys = lowered_input(apply_rotation(projected_output[..., query_heads_width:query_heads_width + key_value_width].reshape(N_FSDP, SEQUENCE_ROWS, KEY_VALUE_HEADS, HEAD_SIZE), cosine_table, sine_values))
        gathered_values = lowered_input(projected_output[..., query_heads_width + key_value_width:].reshape(N_FSDP, SEQUENCE_ROWS, KEY_VALUE_HEADS, HEAD_SIZE))
        query_rows = query_rows.reshape(N_FSDP, SEQUENCE_ROWS, KEY_VALUE_HEADS, QUERY_HEADS // KEY_VALUE_HEADS, HEAD_SIZE)
        attended_output = lax.map(attend_group, (query_rows, gathered_keys, gathered_values, position, validity))
        mixed = low_back(lowered_input(attended_output.reshape(N_FSDP * SEQUENCE_ROWS, query_heads_width)))
        middle = flat + low_back(highest(mixed, out_w[layer_index]))
        normed_two = lowered_input(normalize(middle, gain_two[layer_index]))
        gate_value = low_back(highest(normed_two, gate_w[layer_index]))
        up_value = low_back(highest(normed_two, up_w[layer_index]))
        hidden = lowered_input(jax.nn.silu(gate_value) * up_value)
        stream = (middle + low_back(highest(hidden, down_w[layer_index]))).reshape(N_FSDP, SEQUENCE_ROWS, D)
    return stream

def reference(hidden_in, cotangent, seq_lengths, tile_place, norm_attn, w_qkv, b_qkv, w_out, norm_mlp, w_gate, w_up, w_down):
    position, validity = jax.vmap(group_positions)(seq_lengths, tile_place)
    angles = position.astype(jnp.float32)[..., None] * frequencies()
    cosine_table = jnp.cos(angles)[:, :, None, :]
    sine_values = jnp.sin(angles)[:, :, None, :]
    stream = hidden_in.astype(jnp.float32)
    weight_set = (norm_attn.astype(jnp.float32), w_qkv.astype(jnp.float32), b_qkv.astype(jnp.float32), w_out.astype(jnp.float32), norm_mlp.astype(jnp.float32), w_gate.astype(jnp.float32), w_up.astype(jnp.float32), w_down.astype(jnp.float32))

    def run(stream_in, weights_in):
        return forward(stream_in, weights_in, position, validity, cosine_table, sine_values)
    layer_out, pullback = jax.vjp(run, stream, weight_set)
    seed_grad = cotangent.astype(jnp.float32) * validity[..., None].astype(jnp.float32)
    grad_in, weight_grads = pullback(seed_grad)
    return (layer_out.astype(jnp.bfloat16), grad_in, weight_grads[0], weight_grads[1], weight_grads[2], weight_grads[3], weight_grads[4], weight_grads[5], weight_grads[6], weight_grads[7])
```

```python
import functools
import math

import jax
import jax.numpy as jnp
from jax import lax
from jax.experimental import pallas as pl
from jax.experimental.pallas import tpu as pltpu
from jax.sharding import PartitionSpec as P

QUERY_HEADS = 12
KV_HEADS = 2
HEAD = 128
LAYERS = 2
TILE = 128
Q_WIDTH = QUERY_HEADS * HEAD
KV_WIDTH = KV_HEADS * HEAD
PER_GROUP = QUERY_HEADS // KV_HEADS
SCALE = 1.0 / math.sqrt(HEAD)
EPSILON = 1e-06
ROPE_BASE = 1000000.0
BF = jnp.bfloat16
F32 = jnp.float32
MESH = pl.DeviceIdType.MESH
VMEM_LIMIT = 66 * 1024 * 1024
ANY = pl.BlockSpec(memory_space=pl.ANY)
VM = pl.BlockSpec(memory_space=pltpu.VMEM)


def dot_nn(a, b):
    return lax.dot_general(a, b, (((1,), (0,)), ((), ())), preferred_element_type=F32)


def dot_nt(a, b):
    return lax.dot_general(a, b, (((1,), (1,)), ((), ())), preferred_element_type=F32)


def dot_tn(a, b):
    return lax.dot_general(a, b, (((0,), (0,)), ((), ())), preferred_element_type=F32)


def lane_tile(width, most):
    best = 128
    for k in range(1, most // 128 + 1):
        if width % (128 * k) == 0:
            best = 128 * k
    return best


class Line:
    def __init__(self, n):
        self.n = n
        self.z = lax.axis_index("context")
        self.right = lax.rem(self.z + 1, n)
        self.left = lax.rem(self.z + n - 1, n)
        self.has_right = self.z < n - 1
        self.has_left = self.z > 0

    def barrier(self):
        bar = pltpu.get_barrier_semaphore()

        @pl.when(self.has_right)
        def _():
            pl.semaphore_signal(bar, inc=1, device_id={"context": self.right}, device_id_type=MESH)

        @pl.when(self.has_left)
        def _():
            pl.semaphore_signal(bar, inc=1, device_id={"context": self.left}, device_id_type=MESH)

        both = self.has_right & self.has_left

        @pl.when(both)
        def _():
            pl.semaphore_wait(bar, 2)

        @pl.when(jnp.logical_not(both))
        def _():
            pl.semaphore_wait(bar, 1)

    def order(self, i):
        z, n = self.z, self.n
        short = jnp.minimum(z, n - 1 - z)
        j = i - 1
        paired = j < 2 * short
        k = jnp.where(paired, j // 2 + 1, j - short + 1)
        goes_left = jnp.where(paired, lax.rem(j, 2) == 0, z > n - 1 - z)
        return jnp.where(i == 0, z, jnp.where(goes_left, z - k, z + k))


def remote(src, dst, send, recv, target):
    return pltpu.make_async_remote_copy(
        src_ref=src, dst_ref=dst, send_sem=send, recv_sem=recv,
        device_id={"context": target}, device_id_type=MESH,
    )


class Gather:
    def __init__(self, line, slots, send_r, send_l, recv):
        self.line, self.slots = line, slots
        self.send_r, self.send_l, self.recv = send_r, send_l, recv

    def _right(self, b, src):
        return remote(src, self.slots.at[b], self.send_r.at[b], self.recv.at[b], self.line.right)

    def _left(self, b, src):
        return remote(src, self.slots.at[b], self.send_l.at[b], self.recv.at[b], self.line.left)

    def start(self, own):
        line = self.line

        @pl.when(line.has_right)
        def _():
            self._right(line.z, own).start()

        @pl.when(line.has_left)
        def _():
            self._left(line.z, own).start()

    def arrive(self, b):
        line = self.line
        self._right(b, self.slots.at[b]).wait_recv()

        @pl.when((b < line.z) & line.has_right)
        def _():
            self._right(b, self.slots.at[b]).start()

        @pl.when((b > line.z) & line.has_left)
        def _():
            self._left(b, self.slots.at[b]).start()

    def finish(self):
        line = self.line
        for b in range(line.n):
            @pl.when((b <= line.z) & line.has_right)
            def _():
                self._right(b, self.slots.at[b]).wait_send()

            @pl.when((b >= line.z) & line.has_left)
            def _():
                self._left(b, self.slots.at[b]).wait_send()


class Scatter:
    def __init__(self, line, pieces, part, from_left, from_right, send_r, send_l, recv_l, recv_r):
        self.line, self.pieces, self.part = line, pieces, part
        self.from_left, self.from_right = from_left, from_right
        self.send_r, self.send_l, self.recv_l, self.recv_r = send_r, send_l, recv_l, recv_r

    def _right(self, b, p):
        return remote(self.part.at[b, p], self.from_left.at[b, p], self.send_r.at[b, p],
                      self.recv_l.at[b, p], self.line.right)

    def _left(self, b, p):
        return remote(self.part.at[b, p], self.from_right.at[b, p], self.send_l.at[b, p],
                      self.recv_r.at[b, p], self.line.left)

    def computed(self, b, p):
        line = self.line

        @pl.when((line.z == 0) & (b > 0))
        def _():
            self._right(b, p).start()

        @pl.when((line.z == line.n - 1) & (b < line.n - 1))
        def _():
            self._left(b, p).start()

    def steps(self):
        return range(1, 2 * (self.line.n - 1) + 1)

    def step(self, t, add_own):
        line = self.line
        n, z = line.n, line.z
        b_left = t - z

        @pl.when(line.has_left & (b_left >= z) & (b_left < n))
        def _():
            for p in range(self.pieces):
                self._right(b_left, p).wait_recv()

                @pl.when(b_left == z)
                def _():
                    add_own(p, self.from_left[b_left, p].astype(F32))

                @pl.when(b_left != z)
                def _():
                    self.part[b_left, p] = (
                        self.part[b_left, p].astype(F32) + self.from_left[b_left, p].astype(F32)
                    ).astype(BF)
                    self._right(b_left, p).start()

        b_right = 2 * (n - 1) - t - z

        @pl.when(line.has_right & (b_right >= 0) & (b_right <= z))
        def _():
            for p in range(self.pieces):
                self._left(b_right, p).wait_recv()

                @pl.when(b_right == z)
                def _():
                    add_own(p, self.from_right[b_right, p].astype(F32))

                @pl.when(b_right != z)
                def _():
                    self.part[b_right, p] = (
                        self.part[b_right, p].astype(F32) + self.from_right[b_right, p].astype(F32)
                    ).astype(BF)
                    self._left(b_right, p).start()

    def finish(self):
        line = self.line
        for b in range(line.n):
            @pl.when((b > line.z) & line.has_right)
            def _():
                for p in range(self.pieces):
                    self._right(b, p).wait_send()

            @pl.when((b < line.z) & line.has_left)
            def _():
                for p in range(self.pieces):
                    self._left(b, p).wait_send()


def gather_sems(n):
    return [pltpu.SemaphoreType.DMA((n,))] * 3


def scatter_sems(n, pieces):
    return [pltpu.SemaphoreType.DMA((n, pieces))] * 4


def params(cid):
    return pltpu.CompilerParams(
        collective_id=cid, has_side_effects=True, vmem_limit_bytes=VMEM_LIMIT
    )


def ffn_forward_kernel(n, pieces, x_ref, w_ref, xall_ref, gate_ref, up_ref, y_ref,
                       w_v, xbuf, gbuf, ubuf, hbuf, part, from_l, from_r,
                       w_sem, x_sem, out_sem, *sems):
    line = Line(n)
    z = line.z
    owners, _, rows, width = w_ref.shape
    d_model = x_ref.shape[1]
    tile = lane_tile(width, 256)
    piece = d_model // pieces
    gather = Gather(line, xbuf, *sems[:3])
    scatter = Scatter(line, pieces, part, from_l, from_r, *sems[3:])

    def w_copy(k, f):
        return pltpu.make_async_copy(
            w_ref.at[f, k], w_v.at[k, pl.ds(f * rows, rows)], w_sem.at[k, f]
        )

    def out_copies(b):
        slot = lax.rem(b, 2)
        return (
            pltpu.make_async_copy(gbuf.at[slot], gate_ref.at[b], out_sem.at[0, slot]),
            pltpu.make_async_copy(ubuf.at[slot], up_ref.at[b], out_sem.at[1, slot]),
        )

    def x_out(b):
        return pltpu.make_async_copy(xbuf.at[b], xall_ref.at[b], x_sem.at[b])

    line.barrier()
    gather.start(x_ref)
    for k in range(3):
        for f in range(owners):
            w_copy(k, f).start()
    xbuf[z] = x_ref[...]
    for k in range(3):
        for f in range(owners):
            w_copy(k, f).wait()

    @pl.loop(0, n)
    def _(i):
        b = line.order(i)

        @pl.when(i > 0)
        def _():
            gather.arrive(b)

        x_out(b).start()
        slot = lax.rem(i, 2)
        g_copy = pltpu.make_async_copy(gbuf.at[slot], gate_ref.at[b], out_sem.at[0, slot])
        u_copy = pltpu.make_async_copy(ubuf.at[slot], up_ref.at[b], out_sem.at[1, slot])

        @pl.when(i > 1)
        def _():
            g_copy.wait()
            u_copy.wait()

        @pl.loop(0, width // tile)
        def _(j):
            cols = pl.ds(pl.multiple_of(j * tile, tile), tile)
            xb = xbuf[b]
            gate = dot_nn(xb, w_v[0, :, cols])
            up = dot_nn(xb, w_v[1, :, cols])
            gbuf[slot, :, cols] = gate.astype(BF)
            ubuf[slot, :, cols] = up.astype(BF)
            hbuf[:, cols] = (gate * jax.nn.sigmoid(gate) * up).astype(BF)

        g_copy.start()
        u_copy.start()
        for p in range(pieces):
            out = dot_nt(hbuf[...], w_v[2, pl.ds(p * piece, piece)])

            @pl.when(b == z)
            def _():
                y_ref[:, p * piece:(p + 1) * piece] = out

            @pl.when(b != z)
            def _():
                part[b, p] = out.astype(BF)

            scatter.computed(b, p)

    def add_own(p, value):
        cols = slice(p * piece, (p + 1) * piece)
        y_ref[:, cols] = y_ref[:, cols] + value

    for t in scatter.steps():
        scatter.step(t, add_own)
    for i in range(max(0, n - 2), n):
        slot = i % 2
        pltpu.make_async_copy(gbuf.at[slot], gate_ref.at[0], out_sem.at[0, slot]).wait()
        pltpu.make_async_copy(ubuf.at[slot], up_ref.at[0], out_sem.at[1, slot]).wait()
    for b in range(n):
        x_out(b).wait()
    gather.finish()
    scatter.finish()


def ffn_forward(x, w, n):
    rows, d_model = x.shape
    owners, _, shard, width = w.shape
    pieces = 3
    piece = d_model // pieces
    return pl.pallas_call(
        functools.partial(ffn_forward_kernel, n, pieces),
        out_shape=(
            jax.ShapeDtypeStruct((n, rows, d_model), BF),
            jax.ShapeDtypeStruct((n, rows, width), BF),
            jax.ShapeDtypeStruct((n, rows, width), BF),
            jax.ShapeDtypeStruct((rows, d_model), F32),
        ),
        in_specs=[VM, ANY],
        out_specs=[ANY, ANY, ANY, VM],
        scratch_shapes=[
            pltpu.VMEM((3, d_model, width), BF),
            pltpu.VMEM((n, rows, d_model), BF),
            pltpu.VMEM((2, rows, width), BF),
            pltpu.VMEM((2, rows, width), BF),
            pltpu.VMEM((rows, width), BF),
            pltpu.VMEM((n, pieces, rows, piece), BF),
            pltpu.VMEM((n, pieces, rows, piece), BF),
            pltpu.VMEM((n, pieces, rows, piece), BF),
            pltpu.SemaphoreType.DMA((3, owners)),
            pltpu.SemaphoreType.DMA((n,)),
            pltpu.SemaphoreType.DMA((2, 2)),
        ] + gather_sems(n) + scatter_sems(n, pieces),
        compiler_params=params(1),
        cost_estimate=pl.CostEstimate(
            flops=6 * n * rows * d_model * width, transcendentals=n * rows * width,
            bytes_accessed=60 << 20),
        name="ffn_forward",
    )(x, w)


def ffn_backward_kernel(n, pieces, groups, g_ref, w_ref, xall_ref, gate_ref, up_ref, dw_ref, dx_ref,
                        w_v, gbuf, xv, gate_v, up_v, hid_v, part, from_l, from_r, stage,
                        w_sem, in_sem, out_sem, *sems):
    line = Line(n)
    z = line.z
    owners, _, shard, width = w_ref.shape
    rows, d_model = g_ref.shape
    tile = lane_tile(width, 256)
    piece = d_model // pieces
    gather = Gather(line, gbuf, *sems[:3])
    scatter = Scatter(line, pieces, part, from_l, from_r, *sems[3:])

    def w_copy(k, f):
        return pltpu.make_async_copy(
            w_ref.at[f, k], w_v.at[k, pl.ds(f * shard, shard)], w_sem.at[k, f]
        )

    def loads(b):
        return (
            pltpu.make_async_copy(gate_ref.at[b], gate_v.at[b], in_sem.at[0, b]),
            pltpu.make_async_copy(up_ref.at[b], up_v.at[b], in_sem.at[1, b]),
        )

    def x_load(b):
        return pltpu.make_async_copy(xall_ref.at[b], xv.at[b], in_sem.at[2, b])

    line.barrier()
    gather.start(g_ref)
    for f in range(owners):
        w_copy(2, f).start()
    for c in loads(z):
        c.start()
    for k in range(2):
        for f in range(owners):
            w_copy(k, f).start()
    for b in range(n):
        @pl.when(b != z)
        def _():
            for c in loads(b):
                c.start()
    for b in range(n):
        x_load(b).start()
    gbuf[z] = g_ref[...]
    for k in (2, 0, 1):
        for f in range(owners):
            w_copy(k, f).wait()

    @pl.loop(0, n)
    def _(i):
        b = line.order(i)

        @pl.when(i > 0)
        def _():
            gather.arrive(b)

        for c in loads(b):
            c.wait()

        @pl.loop(0, width // tile)
        def _(j):
            cols = pl.ds(pl.multiple_of(j * tile, tile), tile)
            d_hidden = dot_nn(gbuf[b], w_v[2, :, cols])
            gate = gate_v[b, :, cols].astype(F32)
            up = up_v[b, :, cols].astype(F32)
            sig = jax.nn.sigmoid(gate)
            act = gate * sig
            hid_v[b, :, cols] = (act * up).astype(BF)
            gate_v[b, :, cols] = (d_hidden * up * (sig + act * (1.0 - sig))).astype(BF)
            up_v[b, :, cols] = (d_hidden * act).astype(BF)

        for p in range(pieces):
            sl = pl.ds(p * piece, piece)
            out = dot_nt(gate_v[b], w_v[0, sl]) + dot_nt(up_v[b], w_v[1, sl])

            @pl.when(b == z)
            def _():
                dx_ref[:, p * piece:(p + 1) * piece] = out

            @pl.when(b != z)
            def _():
                part[b, p] = out.astype(BF)

            scatter.computed(b, p)

    def add_own(p, value):
        cols = slice(p * piece, (p + 1) * piece)
        dx_ref[:, cols] = dx_ref[:, cols] + value

    for b in range(n):
        x_load(b).wait()

    group = d_model // groups
    per = group // shard

    def dw_copies(k, q, slot):
        return [
            pltpu.make_async_copy(
                stage.at[slot, pl.ds(s * shard, shard)], dw_ref.at[q * per + s, k],
                out_sem.at[slot, s])
            for s in range(per)
        ]

    def weight_unit(unit):
        k, q = unit // groups, unit % groups
        slot = unit % 2
        left = (xv, xv, gbuf)[k]
        right = (gate_v, up_v, hid_v)[k]
        if unit >= 2:
            for c in dw_copies((unit - 2) // groups, (unit - 2) % groups, slot):
                c.wait()
        lt = left[:, :, q * group:(q + 1) * group].reshape(n * rows, group)

        @pl.loop(0, width // tile)
        def _(j):
            cols = pl.ds(pl.multiple_of(j * tile, tile), tile)
            stage[slot, :, cols] = dot_tn(
                lt, right[:, :, cols].reshape(n * rows, tile)
            ).astype(BF)

        for c in dw_copies(k, q, slot):
            c.start()

    units = 3 * groups
    steps = list(scatter.steps())
    done = 0
    for index, t in enumerate(steps):
        scatter.step(t, add_own)
        until = units * (index + 1) // len(steps)
        while done < until:
            weight_unit(done)
            done += 1
    for unit in range(units - 2, units):
        for c in dw_copies(unit // groups, unit % groups, unit % 2):
            c.wait()
    gather.finish()
    scatter.finish()


def ffn_backward(g, w, xall, gate, up, n):
    rows, d_model = g.shape
    owners, _, shard, width = w.shape
    pieces, groups = 3, 4
    piece = d_model // pieces
    per = d_model // groups // shard
    return pl.pallas_call(
        functools.partial(ffn_backward_kernel, n, pieces, groups),
        out_shape=(
            jax.ShapeDtypeStruct((owners, 3, shard, width), BF),
            jax.ShapeDtypeStruct((rows, d_model), F32),
        ),
        in_specs=[VM, ANY, ANY, ANY, ANY],
        out_specs=[ANY, VM],
        scratch_shapes=[
            pltpu.VMEM((3, d_model, width), BF),
            pltpu.VMEM((n, rows, d_model), BF),
            pltpu.VMEM((n, rows, d_model), BF),
            pltpu.VMEM((n, rows, width), BF),
            pltpu.VMEM((n, rows, width), BF),
            pltpu.VMEM((n, rows, width), BF),
            pltpu.VMEM((n, pieces, rows, piece), BF),
            pltpu.VMEM((n, pieces, rows, piece), BF),
            pltpu.VMEM((n, pieces, rows, piece), BF),
            pltpu.VMEM((2, d_model // groups, width), BF),
            pltpu.SemaphoreType.DMA((3, owners)),
            pltpu.SemaphoreType.DMA((3, n)),
            pltpu.SemaphoreType.DMA((2, per)),
        ] + gather_sems(n) + scatter_sems(n, pieces),
        compiler_params=params(2),
        cost_estimate=pl.CostEstimate(
            flops=12 * n * rows * d_model * width, transcendentals=n * rows * width,
            bytes_accessed=100 << 20),
        name="ffn_backward",
    )(g, w, xall, gate, up)


def attention_forward_kernel(n, q_ref, kv_ref, pq_ref, pk_ref, mixed_ref, lse_ref, kvall_ref,
                             kvbuf, vt, *sems):
    line = Line(n)
    z = line.z
    rows = q_ref.shape[0]
    total = n * rows
    gather = Gather(line, kvbuf, *sems)
    line.barrier()
    gather.start(kv_ref)
    kvbuf[z] = kv_ref[...]
    for i in range(1, n):
        gather.arrive(line.order(i))
    kvall_ref[...] = kvbuf[...]
    allowed = pk_ref[...] <= pq_ref[...]
    for g in range(KV_HEADS):
        v = kvbuf[:, :, KV_WIDTH + g * HEAD:KV_WIDTH + (g + 1) * HEAD].reshape(total, HEAD)
        vt[g] = v.T
    for g in range(KV_HEADS):
        for r in range(PER_GROUP):
            h = g * PER_GROUP + r
            k = kvbuf[:, :, g * HEAD:(g + 1) * HEAD].reshape(total, HEAD)
            s = dot_nt(k, q_ref[:, h * HEAD:(h + 1) * HEAD]) * SCALE
            s = jnp.where(allowed, s, -1e30)
            top = jnp.max(s, axis=0, keepdims=True)
            e = jnp.exp(s - top)
            den = jnp.sum(e, axis=0, keepdims=True)
            o = dot_nn(vt[g], e.astype(BF)) / den
            mixed_ref[:, h * HEAD:(h + 1) * HEAD] = o.T.astype(BF)
            lse_ref[h:h + 1, :] = top + jnp.log(den)
    gather.finish()


def attention_forward(q, kv, pos_q, pos_k, n):
    rows = q.shape[0]
    return pl.pallas_call(
        functools.partial(attention_forward_kernel, n),
        out_shape=(
            jax.ShapeDtypeStruct((rows, Q_WIDTH), BF),
            jax.ShapeDtypeStruct((16, rows), F32),
            jax.ShapeDtypeStruct((n, rows, 2 * KV_WIDTH), BF),
        ),
        in_specs=[VM] * 4,
        out_specs=[VM] * 3,
        scratch_shapes=[
            pltpu.VMEM((n, rows, 2 * KV_WIDTH), BF),
            pltpu.VMEM((KV_HEADS, HEAD, n * rows), BF),
        ] + gather_sems(n),
        compiler_params=params(3),
        cost_estimate=pl.CostEstimate(
            flops=4 * n * rows * rows * Q_WIDTH, transcendentals=n * rows * rows * QUERY_HEADS,
            bytes_accessed=16 << 20),
        name="attention_forward",
    )(q, kv, pos_q, pos_k)


def attention_backward_kernel(n, q_ref, kvall_ref, lse_ref, dm_ref, pq_ref, pk_ref,
                              dq_ref, dkv_ref, kt, dk_acc, dv_acc, part, from_l, from_r, *sems):
    line = Line(n)
    z = line.z
    rows = q_ref.shape[0]
    total = n * rows
    pieces = KV_HEADS
    scatter = Scatter(line, pieces, part, from_l, from_r, *sems)
    line.barrier()
    allowed = pk_ref[...] <= pq_ref[...]
    for g in range(KV_HEADS):
        k = kvall_ref[:, :, g * HEAD:(g + 1) * HEAD].reshape(total, HEAD)
        kt[g] = k.T
    for g in range(KV_HEADS):
        for r in range(PER_GROUP):
            h = g * PER_GROUP + r
            cols = slice(h * HEAD, (h + 1) * HEAD)
            k = kvall_ref[:, :, g * HEAD:(g + 1) * HEAD].reshape(total, HEAD)
            v = kvall_ref[:, :, KV_WIDTH + g * HEAD:KV_WIDTH + (g + 1) * HEAD].reshape(total, HEAD)
            q = q_ref[:, cols]
            dm = dm_ref[:, cols]
            s = dot_nt(k, q) * SCALE
            pr = jnp.where(allowed, jnp.exp(s - lse_ref[h:h + 1, :]), 0.0)
            dp = dot_nt(v, dm)
            delta = jnp.sum(pr * dp, axis=0, keepdims=True)
            ds = (pr * (dp - delta) * SCALE).astype(BF)
            dv = dot_nn(pr.astype(BF), dm)
            dk = dot_nn(ds, q)
            if r == 0:
                dk_acc[...] = dk
                dv_acc[...] = dv
            else:
                dk_acc[...] += dk
                dv_acc[...] += dv
            dq_ref[:, cols] = dot_nn(kt[g], ds).T
        for b in range(n):
            sl = slice(b * rows, (b + 1) * rows)

            @pl.when(b == z)
            def _():
                dkv_ref[:, g * HEAD:(g + 1) * HEAD] = dk_acc[sl]
                dkv_ref[:, KV_WIDTH + g * HEAD:KV_WIDTH + (g + 1) * HEAD] = dv_acc[sl]

            @pl.when(b != z)
            def _():
                part[b, g, :, 0:HEAD] = dk_acc[sl].astype(BF)
                part[b, g, :, HEAD:2 * HEAD] = dv_acc[sl].astype(BF)

            scatter.computed(b, g)

    def add_own(p, value):
        a = slice(p * HEAD, (p + 1) * HEAD)
        c = slice(KV_WIDTH + p * HEAD, KV_WIDTH + (p + 1) * HEAD)
        dkv_ref[:, a] = dkv_ref[:, a] + value[:, :HEAD]
        dkv_ref[:, c] = dkv_ref[:, c] + value[:, HEAD:]

    for t in scatter.steps():
        scatter.step(t, add_own)
    scatter.finish()


def attention_backward(q, kvall, lse, dm, pos_q, pos_k, n):
    rows = q.shape[0]
    return pl.pallas_call(
        functools.partial(attention_backward_kernel, n),
        out_shape=(
            jax.ShapeDtypeStruct((rows, Q_WIDTH), F32),
            jax.ShapeDtypeStruct((rows, 2 * KV_WIDTH), F32),
        ),
        in_specs=[VM] * 6,
        out_specs=[VM] * 2,
        scratch_shapes=[
            pltpu.VMEM((KV_HEADS, HEAD, n * rows), BF),
            pltpu.VMEM((n * rows, HEAD), F32),
            pltpu.VMEM((n * rows, HEAD), F32),
        ] + [pltpu.VMEM((n, KV_HEADS, rows, 2 * HEAD), BF)] * 3 + scatter_sems(n, KV_HEADS),
        compiler_params=params(4),
        cost_estimate=pl.CostEstimate(
            flops=10 * n * rows * rows * Q_WIDTH, transcendentals=n * rows * rows * QUERY_HEADS,
            bytes_accessed=16 << 20),
        name="attention_backward",
    )(q, kvall, lse, dm, pos_q, pos_k)


def normalize(stream, gain):
    return stream * lax.rsqrt(jnp.mean(stream * stream, axis=-1, keepdims=True) + EPSILON) * gain


def normalize_back(grad, stream, gain):
    r = lax.rsqrt(jnp.mean(stream * stream, axis=-1, keepdims=True) + EPSILON)
    u = grad * gain
    back = r * (u - stream * (r * r) * jnp.mean(u * stream, axis=-1, keepdims=True))
    return back, jnp.sum(grad * stream * r, axis=0)


def rotate(heads, cosine, sine):
    half = HEAD // 2
    a, b = heads[..., :half], heads[..., half:]
    return jnp.concatenate([a * cosine - b * sine, b * cosine + a * sine], axis=-1)


def frequencies():
    return jnp.power(ROPE_BASE, -(jnp.arange(HEAD // 2, dtype=F32) * 2.0 / HEAD))


def shards(hidden_in, cotangent, seq_lengths, tile_place, norm_attn, w_qkv, b_qkv, w_out,
           norm_mlp, w_gate, w_up, w_down):
    n = lax.axis_size("context")
    owners = lax.axis_size("fsdp")
    rows, d_model = hidden_in.shape[1:]
    hidden_units = w_gate.shape[2]
    width = -(-hidden_units // 128) * 128
    pad = width - hidden_units
    total = n * rows

    row_index = jnp.arange(total, dtype=jnp.int32)
    tile_order = tile_place[0]
    selector = (
        row_index[:, None] // TILE == jnp.arange(tile_order.shape[0], dtype=jnp.int32)[None, :]
    ).astype(jnp.int32)
    position = jnp.sum(selector * tile_order[None, :], axis=1) * TILE + row_index % TILE
    valid = position < seq_lengths[0]
    offset = lax.axis_index("context") * rows
    my_position = lax.dynamic_slice_in_dim(position, offset, rows)
    my_valid = lax.dynamic_slice_in_dim(valid, offset, rows)
    pos_q = my_position[None, :]
    pos_k = jnp.where(valid, position, 1 << 30)[:, None]
    angles = my_position.astype(F32)[:, None] * frequencies()
    cosine, sine = jnp.cos(angles)[:, None, :], jnp.sin(angles)[:, None, :]

    small = jnp.concatenate(
        [norm_attn.reshape(-1), norm_mlp.reshape(-1), b_qkv.reshape(-1)])[None, None]
    small = lax.all_gather(small, "fsdp", axis=0, tiled=True)
    small = small[:, 0].astype(F32)
    shard = norm_attn.shape[1]
    bias_shard = b_qkv.shape[1]
    gains_attn, gains_mlp, biases = [], [], []
    for l in range(LAYERS):
        gains_attn.append(small[:, l * shard:(l + 1) * shard].reshape(-1))
        gains_mlp.append(small[:, (LAYERS + l) * shard:(LAYERS + l + 1) * shard].reshape(-1))
        start = 2 * LAYERS * shard + l * bias_shard
        biases.append(small[:, start:start + bias_shard].reshape(-1))

    def ffn_shard(l):
        return jnp.stack([
            jnp.pad(m, ((0, 0), (0, pad))) for m in (w_gate[l], w_up[l], w_down[l].T)])

    stream = hidden_in[0].astype(F32)
    kept = []
    for l in range(LAYERS):
        qkv_w = lax.all_gather(w_qkv[l], "fsdp", axis=0, tiled=True)
        out_w = lax.all_gather(w_out[l], "fsdp", axis=0, tiled=True)
        ffn_w = lax.all_gather(ffn_shard(l), "fsdp", axis=0, tiled=False)
        normed = normalize(stream, gains_attn[l]).astype(BF)
        projected = jnp.dot(normed, qkv_w, preferred_element_type=F32) + biases[l]
        qk = rotate(
            projected[:, :Q_WIDTH + KV_WIDTH].reshape(rows, QUERY_HEADS + KV_HEADS, HEAD),
            cosine, sine).astype(BF).reshape(rows, Q_WIDTH + KV_WIDTH)
        q = qk[:, :Q_WIDTH]
        kv = jnp.concatenate([qk[:, Q_WIDTH:], projected[:, Q_WIDTH + KV_WIDTH:].astype(BF)], axis=1)
        mixed, lse, kvall = attention_forward(q, kv, pos_q, pos_k, n)
        middle = stream + jnp.dot(mixed, out_w, preferred_element_type=F32)
        normed_two = normalize(middle, gains_mlp[l]).astype(BF)
        xall, gate, up, y = ffn_forward(normed_two, ffn_w, n)
        kept.append((stream, normed, q, kvall, lse, mixed, middle, xall, gate, up,
                     qkv_w, out_w, ffn_w))
        stream = middle + y
    layer_out = stream.astype(BF)[None]

    gradient = cotangent[0].astype(F32) * my_valid[:, None].astype(F32)
    small_grads = [None] * LAYERS
    big_grads = [None] * LAYERS
    for l in reversed(range(LAYERS)):
        (stream, normed, q, kvall, lse, mixed, middle, xall, gate, up,
         qkv_w, out_w, ffn_w) = kept[l]
        dw, dx = ffn_backward(gradient.astype(BF), ffn_w, xall, gate, up, n)
        dw = lax.psum_scatter(dw, "fsdp", scatter_dimension=0, tiled=False)
        back, gain_two = normalize_back(dx, middle, gains_mlp[l])
        d_middle = gradient + back
        d_low = d_middle.astype(BF)
        d_mixed = jnp.einsum("td,cd->tc", d_low, out_w, preferred_element_type=F32).astype(BF)
        out_grad = jnp.einsum("tc,td->cd", mixed, d_low, preferred_element_type=F32).astype(BF)
        out_grad = lax.psum_scatter(out_grad, "fsdp", scatter_dimension=0, tiled=True)
        out_grad = lax.psum(out_grad, "context")
        dq, dkv = attention_backward(q, kvall, lse, d_mixed, pos_q, pos_k, n)
        d_qk = rotate(
            jnp.concatenate([dq, dkv[:, :KV_WIDTH]], axis=1).reshape(
                rows, QUERY_HEADS + KV_HEADS, HEAD),
            cosine, -sine).reshape(rows, Q_WIDTH + KV_WIDTH)
        d_projected = jnp.concatenate([d_qk, dkv[:, KV_WIDTH:]], axis=1).astype(BF)
        bias_grad = jnp.sum(d_projected.astype(F32), axis=0)
        d_normed = jnp.einsum("tc,dc->td", d_projected, qkv_w, preferred_element_type=F32)
        qkv_grad = jnp.einsum(
            "td,tc->dc", normed, d_projected, preferred_element_type=F32).astype(BF)
        qkv_grad = lax.psum_scatter(qkv_grad, "fsdp", scatter_dimension=0, tiled=True)
        qkv_grad = lax.psum(qkv_grad, "context")
        back, gain_one = normalize_back(d_normed, stream, gains_attn[l])
        gradient = d_middle + back
        small_grads[l] = (gain_one, gain_two, bias_grad)
        big_grads[l] = (qkv_grad, out_grad, dw)

    rows_small = [
        m.reshape(owners, -1)
        for k in range(3) for m in (small_grads[l][k] for l in range(LAYERS))]
    small = jnp.concatenate(rows_small, axis=1).astype(BF)[:, None]
    small = lax.psum_scatter(small, "fsdp", scatter_dimension=0, tiled=True)
    small = lax.psum(small, "context")[0, 0].astype(F32)
    grad_norm_attn = small[:LAYERS * shard].reshape(LAYERS, shard)
    grad_norm_mlp = small[LAYERS * shard:2 * LAYERS * shard].reshape(LAYERS, shard)
    grad_b_qkv = small[2 * LAYERS * shard:].reshape(LAYERS, bias_shard)

    def stacked(pick):
        return jnp.stack([pick(big_grads[l]).astype(F32) for l in range(LAYERS)])

    return (
        layer_out,
        gradient[None],
        grad_norm_attn,
        stacked(lambda m: m[0]),
        grad_b_qkv,
        stacked(lambda m: m[1]),
        grad_norm_mlp,
        stacked(lambda m: m[2][0, :, :hidden_units]),
        stacked(lambda m: m[2][1, :, :hidden_units]),
        stacked(lambda m: m[2][2, :, :hidden_units].T),
    )


def solution(mesh):
    return jax.shard_map(
        shards,
        mesh=mesh,
        in_specs=(
            P("fsdp", "context", None),
            P("fsdp", "context", None),
            P("fsdp"),
            P("fsdp", None),
            P(None, "fsdp"),
            P(None, "fsdp", None),
            P(None, "fsdp"),
            P(None, "fsdp", None),
            P(None, "fsdp"),
            P(None, "fsdp", "context"),
            P(None, "fsdp", "context"),
            P(None, "context", "fsdp"),
        ),
        out_specs=(
            P("fsdp", "context", None),
            P("fsdp", "context", None),
            P(None, "fsdp"),
            P(None, "fsdp", None),
            P(None, "fsdp"),
            P(None, "fsdp", None),
            P(None, "fsdp"),
            P(None, "fsdp", "context"),
            P(None, "fsdp", "context"),
            P(None, "context", "fsdp"),
        ),
        check_vma=False,
    )
```

```python
import functools
import math

import jax
import jax.numpy as jnp
from jax import lax
from jax.experimental import pallas as pl
from jax.experimental.pallas import tpu as pltpu
from jax.sharding import PartitionSpec as P

QUERY_HEADS = 12
KV_HEADS = 2
HEAD = 128
LAYERS = 2
TILE = 128
Q_WIDTH = QUERY_HEADS * HEAD
KV_WIDTH = KV_HEADS * HEAD
PER_GROUP = QUERY_HEADS // KV_HEADS
SCALE = 1.0 / math.sqrt(HEAD)
EPSILON = 1e-06
ROPE_BASE = 1000000.0
BF = jnp.bfloat16
F32 = jnp.float32
MESH = pl.DeviceIdType.MESH
VMEM_LIMIT = 66 * 1024 * 1024
ANY = pl.BlockSpec(memory_space=pl.ANY)
VM = pl.BlockSpec(memory_space=pltpu.VMEM)


def dot_nn(a, b):
    return lax.dot_general(a, b, (((1,), (0,)), ((), ())), preferred_element_type=F32)


def dot_nt(a, b):
    return lax.dot_general(a, b, (((1,), (1,)), ((), ())), preferred_element_type=F32)


def dot_tn(a, b):
    return lax.dot_general(a, b, (((0,), (0,)), ((), ())), preferred_element_type=F32)


def lane_tile(width, most):
    best = 128
    for k in range(1, most // 128 + 1):
        if width % (128 * k) == 0:
            best = 128 * k
    return best


class Line:
    def __init__(self, n):
        self.n = n
        self.z = lax.axis_index("context")
        self.right = lax.rem(self.z + 1, n)
        self.left = lax.rem(self.z + n - 1, n)
        self.has_right = self.z < n - 1
        self.has_left = self.z > 0

    def barrier(self):
        bar = pltpu.get_barrier_semaphore()

        @pl.when(self.has_right)
        def _():
            pl.semaphore_signal(bar, inc=1, device_id={"context": self.right}, device_id_type=MESH)

        @pl.when(self.has_left)
        def _():
            pl.semaphore_signal(bar, inc=1, device_id={"context": self.left}, device_id_type=MESH)

        both = self.has_right & self.has_left

        @pl.when(both)
        def _():
            pl.semaphore_wait(bar, 2)

        @pl.when(jnp.logical_not(both))
        def _():
            pl.semaphore_wait(bar, 1)

    def order(self, i):
        z, n = self.z, self.n
        short = jnp.minimum(z, n - 1 - z)
        j = i - 1
        paired = j < 2 * short
        k = jnp.where(paired, j // 2 + 1, j - short + 1)
        goes_left = jnp.where(paired, lax.rem(j, 2) == 0, z > n - 1 - z)
        return jnp.where(i == 0, z, jnp.where(goes_left, z - k, z + k))


def remote(src, dst, send, recv, target):
    return pltpu.make_async_remote_copy(
        src_ref=src, dst_ref=dst, send_sem=send, recv_sem=recv,
        device_id={"context": target}, device_id_type=MESH,
    )


class Gather:
    def __init__(self, line, slots, send_r, send_l, recv):
        self.line, self.slots = line, slots
        self.send_r, self.send_l, self.recv = send_r, send_l, recv

    def _right(self, b, src):
        return remote(src, self.slots.at[b], self.send_r.at[b], self.recv.at[b], self.line.right)

    def _left(self, b, src):
        return remote(src, self.slots.at[b], self.send_l.at[b], self.recv.at[b], self.line.left)

    def start(self, own):
        line = self.line

        @pl.when(line.has_right)
        def _():
            self._right(line.z, own).start()

        @pl.when(line.has_left)
        def _():
            self._left(line.z, own).start()

    def arrive(self, b):
        line = self.line
        self._right(b, self.slots.at[b]).wait_recv()

        @pl.when((b < line.z) & line.has_right)
        def _():
            self._right(b, self.slots.at[b]).start()

        @pl.when((b > line.z) & line.has_left)
        def _():
            self._left(b, self.slots.at[b]).start()

    def finish(self):
        line = self.line
        for b in range(line.n):
            @pl.when((b <= line.z) & line.has_right)
            def _():
                self._right(b, self.slots.at[b]).wait_send()

            @pl.when((b >= line.z) & line.has_left)
            def _():
                self._left(b, self.slots.at[b]).wait_send()


class Scatter:
    def __init__(self, line, pieces, part, from_left, from_right, send_r, send_l, recv_l, recv_r):
        self.line, self.pieces, self.part = line, pieces, part
        self.from_left, self.from_right = from_left, from_right
        self.send_r, self.send_l, self.recv_l, self.recv_r = send_r, send_l, recv_l, recv_r

    def _right(self, b, p):
        return remote(self.part.at[b, p], self.from_left.at[b, p], self.send_r.at[b, p],
                      self.recv_l.at[b, p], self.line.right)

    def _left(self, b, p):
        return remote(self.part.at[b, p], self.from_right.at[b, p], self.send_l.at[b, p],
                      self.recv_r.at[b, p], self.line.left)

    def computed(self, b, p):
        line = self.line

        @pl.when((line.z == 0) & (b > 0))
        def _():
            self._right(b, p).start()

        @pl.when((line.z == line.n - 1) & (b < line.n - 1))
        def _():
            self._left(b, p).start()

    def steps(self):
        return range(1, 2 * (self.line.n - 1) + 1)

    def step(self, t, add_own):
        line = self.line
        n, z = line.n, line.z
        b_left = t - z

        @pl.when(line.has_left & (b_left >= z) & (b_left < n))
        def _():
            for p in range(self.pieces):
                self._right(b_left, p).wait_recv()

                @pl.when(b_left == z)
                def _():
                    add_own(p, self.from_left[b_left, p].astype(F32))

                @pl.when(b_left != z)
                def _():
                    self.part[b_left, p] = (
                        self.part[b_left, p].astype(F32) + self.from_left[b_left, p].astype(F32)
                    ).astype(BF)
                    self._right(b_left, p).start()

        b_right = 2 * (n - 1) - t - z

        @pl.when(line.has_right & (b_right >= 0) & (b_right <= z))
        def _():
            for p in range(self.pieces):
                self._left(b_right, p).wait_recv()

                @pl.when(b_right == z)
                def _():
                    add_own(p, self.from_right[b_right, p].astype(F32))

                @pl.when(b_right != z)
                def _():
                    self.part[b_right, p] = (
                        self.part[b_right, p].astype(F32) + self.from_right[b_right, p].astype(F32)
                    ).astype(BF)
                    self._left(b_right, p).start()

    def finish(self):
        line = self.line
        for b in range(line.n):
            @pl.when((b > line.z) & line.has_right)
            def _():
                for p in range(self.pieces):
                    self._right(b, p).wait_send()

            @pl.when((b < line.z) & line.has_left)
            def _():
                for p in range(self.pieces):
                    self._left(b, p).wait_send()


def gather_sems(n):
    return [pltpu.SemaphoreType.DMA((n,))] * 3


def scatter_sems(n, pieces):
    return [pltpu.SemaphoreType.DMA((n, pieces))] * 4


def params(cid):
    return pltpu.CompilerParams(
        collective_id=cid, has_side_effects=True, vmem_limit_bytes=VMEM_LIMIT
    )


def ffn_forward_kernel(n, pieces, x_ref, w_ref, xall_ref, gate_ref, up_ref, y_ref,
                       w_v, xbuf, gbuf, ubuf, hbuf, part, from_l, from_r,
                       w_sem, x_sem, out_sem, *sems):
    line = Line(n)
    z = line.z
    owners, _, rows, width = w_ref.shape
    d_model = x_ref.shape[1]
    tile = lane_tile(width, 256)
    piece = d_model // pieces
    gather = Gather(line, xbuf, *sems[:3])
    scatter = Scatter(line, pieces, part, from_l, from_r, *sems[3:])

    def w_copy(k, f):
        return pltpu.make_async_copy(
            w_ref.at[f, k], w_v.at[k, pl.ds(f * rows, rows)], w_sem.at[k, f]
        )

    def out_copies(b):
        slot = lax.rem(b, 2)
        return (
            pltpu.make_async_copy(gbuf.at[slot], gate_ref.at[b], out_sem.at[0, slot]),
            pltpu.make_async_copy(ubuf.at[slot], up_ref.at[b], out_sem.at[1, slot]),
        )

    def x_out(b):
        return pltpu.make_async_copy(xbuf.at[b], xall_ref.at[b], x_sem.at[b])

    line.barrier()
    gather.start(x_ref)
    for k in range(3):
        for f in range(owners):
            w_copy(k, f).start()
    xbuf[z] = x_ref[...]
    for k in range(3):
        for f in range(owners):
            w_copy(k, f).wait()

    @pl.loop(0, n)
    def _(i):
        b = line.order(i)

        @pl.when(i > 0)
        def _():
            gather.arrive(b)

        x_out(b).start()
        slot = lax.rem(i, 2)
        g_copy = pltpu.make_async_copy(gbuf.at[slot], gate_ref.at[b], out_sem.at[0, slot])
        u_copy = pltpu.make_async_copy(ubuf.at[slot], up_ref.at[b], out_sem.at[1, slot])

        @pl.when(i > 1)
        def _():
            g_copy.wait()
            u_copy.wait()

        @pl.loop(0, width // tile)
        def _(j):
            cols = pl.ds(pl.multiple_of(j * tile, tile), tile)
            xb = xbuf[b]
            gate = dot_nn(xb, w_v[0, :, cols])
            up = dot_nn(xb, w_v[1, :, cols])
            gbuf[slot, :, cols] = gate.astype(BF)
            ubuf[slot, :, cols] = up.astype(BF)
            hbuf[:, cols] = (gate * jax.nn.sigmoid(gate) * up).astype(BF)

        g_copy.start()
        u_copy.start()
        for p in range(pieces):
            out = dot_nt(hbuf[...], w_v[2, pl.ds(p * piece, piece)])

            @pl.when(b == z)
            def _():
                y_ref[:, p * piece:(p + 1) * piece] = out

            @pl.when(b != z)
            def _():
                part[b, p] = out.astype(BF)

            scatter.computed(b, p)

    def add_own(p, value):
        cols = slice(p * piece, (p + 1) * piece)
        y_ref[:, cols] = y_ref[:, cols] + value

    for t in scatter.steps():
        scatter.step(t, add_own)
    for i in range(max(0, n - 2), n):
        slot = i % 2
        pltpu.make_async_copy(gbuf.at[slot], gate_ref.at[0], out_sem.at[0, slot]).wait()
        pltpu.make_async_copy(ubuf.at[slot], up_ref.at[0], out_sem.at[1, slot]).wait()
    for b in range(n):
        x_out(b).wait()
    gather.finish()
    scatter.finish()


def ffn_forward(x, w, n):
    rows, d_model = x.shape
    owners, _, shard, width = w.shape
    pieces = 3
    piece = d_model // pieces
    return pl.pallas_call(
        functools.partial(ffn_forward_kernel, n, pieces),
        out_shape=(
            jax.ShapeDtypeStruct((n, rows, d_model), BF),
            jax.ShapeDtypeStruct((n, rows, width), BF),
            jax.ShapeDtypeStruct((n, rows, width), BF),
            jax.ShapeDtypeStruct((rows, d_model), F32),
        ),
        in_specs=[VM, ANY],
        out_specs=[ANY, ANY, ANY, VM],
        scratch_shapes=[
            pltpu.VMEM((3, d_model, width), BF),
            pltpu.VMEM((n, rows, d_model), BF),
            pltpu.VMEM((2, rows, width), BF),
            pltpu.VMEM((2, rows, width), BF),
            pltpu.VMEM((rows, width), BF),
            pltpu.VMEM((n, pieces, rows, piece), BF),
            pltpu.VMEM((n, pieces, rows, piece), BF),
            pltpu.VMEM((n, pieces, rows, piece), BF),
            pltpu.SemaphoreType.DMA((3, owners)),
            pltpu.SemaphoreType.DMA((n,)),
            pltpu.SemaphoreType.DMA((2, 2)),
        ] + gather_sems(n) + scatter_sems(n, pieces),
        compiler_params=params(1),
        cost_estimate=pl.CostEstimate(
            flops=6 * n * rows * d_model * width, transcendentals=n * rows * width,
            bytes_accessed=60 << 20),
        name="ffn_forward",
    )(x, w)


def ffn_backward_kernel(n, pieces, groups, g_ref, w_ref, xall_ref, gate_ref, up_ref, dw_ref, dx_ref,
                        w_v, gbuf, xv, gate_v, up_v, hid_v, part, from_l, from_r, stage,
                        w_sem, in_sem, out_sem, *sems):
    line = Line(n)
    z = line.z
    owners, _, shard, width = w_ref.shape
    rows, d_model = g_ref.shape
    tile = lane_tile(width, 256)
    piece = d_model // pieces
    gather = Gather(line, gbuf, *sems[:3])
    scatter = Scatter(line, pieces, part, from_l, from_r, *sems[3:])

    def w_copy(k, f):
        return pltpu.make_async_copy(
            w_ref.at[f, k], w_v.at[k, pl.ds(f * shard, shard)], w_sem.at[k, f]
        )

    def loads(b):
        return (
            pltpu.make_async_copy(gate_ref.at[b], gate_v.at[b], in_sem.at[0, b]),
            pltpu.make_async_copy(up_ref.at[b], up_v.at[b], in_sem.at[1, b]),
        )

    def x_load(b):
        return pltpu.make_async_copy(xall_ref.at[b], xv.at[b], in_sem.at[2, b])

    line.barrier()
    gather.start(g_ref)
    for f in range(owners):
        w_copy(2, f).start()
    for c in loads(z):
        c.start()
    for k in range(2):
        for f in range(owners):
            w_copy(k, f).start()
    for b in range(n):
        @pl.when(b != z)
        def _():
            for c in loads(b):
                c.start()
    for b in range(n):
        x_load(b).start()
    gbuf[z] = g_ref[...]
    for k in (2, 0, 1):
        for f in range(owners):
            w_copy(k, f).wait()

    @pl.loop(0, n)
    def _(i):
        b = line.order(i)

        @pl.when(i > 0)
        def _():
            gather.arrive(b)

        for c in loads(b):
            c.wait()

        @pl.loop(0, width // tile)
        def _(j):
            cols = pl.ds(pl.multiple_of(j * tile, tile), tile)
            d_hidden = dot_nn(gbuf[b], w_v[2, :, cols])
            gate = gate_v[b, :, cols].astype(F32)
            up = up_v[b, :, cols].astype(F32)
            sig = jax.nn.sigmoid(gate)
            act = gate * sig
            hid_v[b, :, cols] = (act * up).astype(BF)
            gate_v[b, :, cols] = (d_hidden * up * (sig + act * (1.0 - sig))).astype(BF)
            up_v[b, :, cols] = (d_hidden * act).astype(BF)

        for p in range(pieces):
            sl = pl.ds(p * piece, piece)
            out = dot_nt(gate_v[b], w_v[0, sl]) + dot_nt(up_v[b], w_v[1, sl])

            @pl.when(b == z)
            def _():
                dx_ref[:, p * piece:(p + 1) * piece] = out

            @pl.when(b != z)
            def _():
                part[b, p] = out.astype(BF)

            scatter.computed(b, p)

    def add_own(p, value):
        cols = slice(p * piece, (p + 1) * piece)
        dx_ref[:, cols] = dx_ref[:, cols] + value

    for b in range(n):
        x_load(b).wait()

    group = d_model // groups
    per = group // shard

    def dw_copies(k, q, slot):
        return [
            pltpu.make_async_copy(
                stage.at[slot, pl.ds(s * shard, shard)], dw_ref.at[q * per + s, k],
                out_sem.at[slot, s])
            for s in range(per)
        ]

    def weight_unit(unit):
        k, q = unit // groups, unit % groups
        slot = unit % 2
        left = (xv, xv, gbuf)[k]
        right = (gate_v, up_v, hid_v)[k]
        if unit >= 2:
            for c in dw_copies((unit - 2) // groups, (unit - 2) % groups, slot):
                c.wait()
        lt = left[:, :, q * group:(q + 1) * group].reshape(n * rows, group)

        @pl.loop(0, width // tile)
        def _(j):
            cols = pl.ds(pl.multiple_of(j * tile, tile), tile)
            stage[slot, :, cols] = dot_tn(
                lt, right[:, :, cols].reshape(n * rows, tile)
            ).astype(BF)

        for c in dw_copies(k, q, slot):
            c.start()

    units = 3 * groups
    steps = list(scatter.steps())
    done = 0
    for index, t in enumerate(steps):
        scatter.step(t, add_own)
        until = units * (index + 1) // len(steps)
        while done < until:
            weight_unit(done)
            done += 1
    for unit in range(units - 2, units):
        for c in dw_copies(unit // groups, unit % groups, unit % 2):
            c.wait()
    gather.finish()
    scatter.finish()


def ffn_backward(g, w, xall, gate, up, n):
    rows, d_model = g.shape
    owners, _, shard, width = w.shape
    pieces, groups = 3, 4
    piece = d_model // pieces
    per = d_model // groups // shard
    return pl.pallas_call(
        functools.partial(ffn_backward_kernel, n, pieces, groups),
        out_shape=(
            jax.ShapeDtypeStruct((owners, 3, shard, width), BF),
            jax.ShapeDtypeStruct((rows, d_model), F32),
        ),
        in_specs=[VM, ANY, ANY, ANY, ANY],
        out_specs=[ANY, VM],
        scratch_shapes=[
            pltpu.VMEM((3, d_model, width), BF),
            pltpu.VMEM((n, rows, d_model), BF),
            pltpu.VMEM((n, rows, d_model), BF),
            pltpu.VMEM((n, rows, width), BF),
            pltpu.VMEM((n, rows, width), BF),
            pltpu.VMEM((n, rows, width), BF),
            pltpu.VMEM((n, pieces, rows, piece), BF),
            pltpu.VMEM((n, pieces, rows, piece), BF),
            pltpu.VMEM((n, pieces, rows, piece), BF),
            pltpu.VMEM((2, d_model // groups, width), BF),
            pltpu.SemaphoreType.DMA((3, owners)),
            pltpu.SemaphoreType.DMA((3, n)),
            pltpu.SemaphoreType.DMA((2, per)),
        ] + gather_sems(n) + scatter_sems(n, pieces),
        compiler_params=params(2),
        cost_estimate=pl.CostEstimate(
            flops=12 * n * rows * d_model * width, transcendentals=n * rows * width,
            bytes_accessed=100 << 20),
        name="ffn_backward",
    )(g, w, xall, gate, up)


def attention_forward_kernel(n, q_ref, kv_ref, pq_ref, pk_ref, mixed_ref, lse_ref, kvall_ref,
                             kvbuf, vt, *sems):
    line = Line(n)
    z = line.z
    rows = q_ref.shape[0]
    total = n * rows
    gather = Gather(line, kvbuf, *sems)
    line.barrier()
    gather.start(kv_ref)
    kvbuf[z] = kv_ref[...]
    for i in range(1, n):
        gather.arrive(line.order(i))
    kvall_ref[...] = kvbuf[...]
    allowed = pk_ref[...] <= pq_ref[...]
    for g in range(KV_HEADS):
        v = kvbuf[:, :, KV_WIDTH + g * HEAD:KV_WIDTH + (g + 1) * HEAD].reshape(total, HEAD)
        vt[g] = v.T
    for g in range(KV_HEADS):
        for r in range(PER_GROUP):
            h = g * PER_GROUP + r
            k = kvbuf[:, :, g * HEAD:(g + 1) * HEAD].reshape(total, HEAD)
            s = dot_nt(k, q_ref[:, h * HEAD:(h + 1) * HEAD]) * SCALE
            s = jnp.where(allowed, s, -1e30)
            top = jnp.max(s, axis=0, keepdims=True)
            e = jnp.exp(s - top)
            den = jnp.sum(e, axis=0, keepdims=True)
            o = dot_nn(vt[g], e.astype(BF)) / den
            mixed_ref[:, h * HEAD:(h + 1) * HEAD] = o.T.astype(BF)
            lse_ref[h:h + 1, :] = top + jnp.log(den)
    gather.finish()


def attention_forward(q, kv, pos_q, pos_k, n):
    rows = q.shape[0]
    return pl.pallas_call(
        functools.partial(attention_forward_kernel, n),
        out_shape=(
            jax.ShapeDtypeStruct((rows, Q_WIDTH), BF),
            jax.ShapeDtypeStruct((16, rows), F32),
            jax.ShapeDtypeStruct((n, rows, 2 * KV_WIDTH), BF),
        ),
        in_specs=[VM] * 4,
        out_specs=[VM] * 3,
        scratch_shapes=[
            pltpu.VMEM((n, rows, 2 * KV_WIDTH), BF),
            pltpu.VMEM((KV_HEADS, HEAD, n * rows), BF),
        ] + gather_sems(n),
        compiler_params=params(3),
        cost_estimate=pl.CostEstimate(
            flops=4 * n * rows * rows * Q_WIDTH, transcendentals=n * rows * rows * QUERY_HEADS,
            bytes_accessed=16 << 20),
        name="attention_forward",
    )(q, kv, pos_q, pos_k)


def attention_backward_kernel(n, q_ref, kvall_ref, lse_ref, dm_ref, pq_ref, pk_ref,
                              dq_ref, dkv_ref, kt, dk_acc, dv_acc, part, from_l, from_r, *sems):
    line = Line(n)
    z = line.z
    rows = q_ref.shape[0]
    total = n * rows
    pieces = KV_HEADS
    scatter = Scatter(line, pieces, part, from_l, from_r, *sems)
    line.barrier()
    allowed = pk_ref[...] <= pq_ref[...]
    for g in range(KV_HEADS):
        k = kvall_ref[:, :, g * HEAD:(g + 1) * HEAD].reshape(total, HEAD)
        kt[g] = k.T
    for g in range(KV_HEADS):
        for r in range(PER_GROUP):
            h = g * PER_GROUP + r
            cols = slice(h * HEAD, (h + 1) * HEAD)
            k = kvall_ref[:, :, g * HEAD:(g + 1) * HEAD].reshape(total, HEAD)
            v = kvall_ref[:, :, KV_WIDTH + g * HEAD:KV_WIDTH + (g + 1) * HEAD].reshape(total, HEAD)
            q = q_ref[:, cols]
            dm = dm_ref[:, cols]
            s = dot_nt(k, q) * SCALE
            pr = jnp.where(allowed, jnp.exp(s - lse_ref[h:h + 1, :]), 0.0)
            dp = dot_nt(v, dm)
            delta = jnp.sum(pr * dp, axis=0, keepdims=True)
            ds = (pr * (dp - delta) * SCALE).astype(BF)
            dv = dot_nn(pr.astype(BF), dm)
            dk = dot_nn(ds, q)
            if r == 0:
                dk_acc[...] = dk
                dv_acc[...] = dv
            else:
                dk_acc[...] += dk
                dv_acc[...] += dv
            dq_ref[:, cols] = dot_nn(kt[g], ds).T
        for b in range(n):
            sl = slice(b * rows, (b + 1) * rows)

            @pl.when(b == z)
            def _():
                dkv_ref[:, g * HEAD:(g + 1) * HEAD] = dk_acc[sl]
                dkv_ref[:, KV_WIDTH + g * HEAD:KV_WIDTH + (g + 1) * HEAD] = dv_acc[sl]

            @pl.when(b != z)
            def _():
                part[b, g, :, 0:HEAD] = dk_acc[sl].astype(BF)
                part[b, g, :, HEAD:2 * HEAD] = dv_acc[sl].astype(BF)

            scatter.computed(b, g)

    def add_own(p, value):
        a = slice(p * HEAD, (p + 1) * HEAD)
        c = slice(KV_WIDTH + p * HEAD, KV_WIDTH + (p + 1) * HEAD)
        dkv_ref[:, a] = dkv_ref[:, a] + value[:, :HEAD]
        dkv_ref[:, c] = dkv_ref[:, c] + value[:, HEAD:]

    for t in scatter.steps():
        scatter.step(t, add_own)
    scatter.finish()


def attention_backward(q, kvall, lse, dm, pos_q, pos_k, n):
    rows = q.shape[0]
    return pl.pallas_call(
        functools.partial(attention_backward_kernel, n),
        out_shape=(
            jax.ShapeDtypeStruct((rows, Q_WIDTH), F32),
            jax.ShapeDtypeStruct((rows, 2 * KV_WIDTH), F32),
        ),
        in_specs=[VM] * 6,
        out_specs=[VM] * 2,
        scratch_shapes=[
            pltpu.VMEM((KV_HEADS, HEAD, n * rows), BF),
            pltpu.VMEM((n * rows, HEAD), F32),
            pltpu.VMEM((n * rows, HEAD), F32),
        ] + [pltpu.VMEM((n, KV_HEADS, rows, 2 * HEAD), BF)] * 3 + scatter_sems(n, KV_HEADS),
        compiler_params=params(4),
        cost_estimate=pl.CostEstimate(
            flops=10 * n * rows * rows * Q_WIDTH, transcendentals=n * rows * rows * QUERY_HEADS,
            bytes_accessed=16 << 20),
        name="attention_backward",
    )(q, kvall, lse, dm, pos_q, pos_k)


def bits_of(owners):
    return [1 << i for i in range(owners.bit_length() - 1)]


class Cube:
    def __init__(self, owners):
        self.owners = owners
        self.me = lax.axis_index("fsdp")
        self.bits = bits_of(owners)
        self.chip_bits = [b // 2 for b in self.bits[1:]]
        self.chips = owners // 2

    def flip(self, mask):
        index = self.me
        for b in self.bits:
            if mask & b:
                index = index + b - 2 * b * lax.rem(self.me // b, 2)
        return index

    def signal(self, bar):
        for b in self.bits:
            pl.semaphore_signal(bar, inc=1, device_id={"fsdp": self.flip(b)}, device_id_type=MESH)

    def order(self, half):
        return self.chip_bits[::-1] if half == 0 else self.chip_bits

    def plan(self):
        steps = {}
        for half in (0, 1):
            order, slot = self.order(half), 0
            for stage, bit in enumerate(order):
                rest = [0]
                for other in order[stage + 1:]:
                    rest = rest + [m | other for m in rest]
                steps[half, stage] = (bit, rest, slot)
                slot += len(rest)
        return steps


def joint_barrier(line, cube):
    bar = pltpu.get_barrier_semaphore()
    cube.signal(bar)
    peers = len(cube.bits)

    @pl.when(line.has_right)
    def _():
        pl.semaphore_signal(bar, inc=1, device_id={"context": line.right}, device_id_type=MESH)

    @pl.when(line.has_left)
    def _():
        pl.semaphore_signal(bar, inc=1, device_id={"context": line.left}, device_id_type=MESH)

    both = line.has_right & line.has_left

    @pl.when(both)
    def _():
        pl.semaphore_wait(bar, peers + 2)

    @pl.when(jnp.logical_not(both))
    def _():
        pl.semaphore_wait(bar, peers + 1)


class Fold:
    def __init__(self, cube, src, mine, first, later, load_sem, send1, recv1, send2, recv2):
        self.cube, self.src = cube, src
        self.mine, self.first, self.later = mine, first, later
        self.load_sem, self.send1, self.recv1 = load_sem, send1, recv1
        self.send2, self.recv2 = send2, recv2
        self.rows = mine.shape[1]
        self.half = self.rows // 2
        self.steps = cube.plan()
        self.stages = len(cube.chip_bits)

    def _load(self, d):
        return pltpu.make_async_copy(
            self.src(self.cube.flip(2 * d)), self.mine.at[d], self.load_sem.at[d])

    def _core(self, d):
        return pltpu.make_async_remote_copy(
            src_ref=self.src(self.cube.flip(2 * d | 1)), dst_ref=self.first.at[d],
            send_sem=self.send1.at[d], recv_sem=self.recv1.at[d],
            device_id={"fsdp": self.cube.flip(1)}, device_id_type=MESH)

    def _hop(self, half, stage, index):
        bit, rest, slot = self.steps[half, stage]
        rows = pl.ds(half * self.half, self.half)
        return pltpu.make_async_remote_copy(
            src_ref=self.mine.at[bit | rest[index], rows],
            dst_ref=self.later.at[half, slot + index],
            send_sem=self.send2.at[half, slot + index],
            recv_sem=self.recv2.at[half, slot + index],
            device_id={"fsdp": self.cube.flip(2 * bit)}, device_id_type=MESH)

    def _hops(self, stage):
        return [self._hop(half, stage, i)
                for half in (0, 1) for i in range(len(self.steps[half, stage][1]))]

    def _add(self, d, base, size, other):
        dtype = self.mine.dtype
        strip = 48 if size % 48 == 0 else size

        @pl.loop(0, size // strip)
        def _(i):
            into = pl.ds(pl.multiple_of(base + i * strip, 8), strip)
            rows = pl.ds(pl.multiple_of(i * strip, 8), strip)
            self.mine[d, into] = (
                self.mine[d, into].astype(F32) + other(rows).astype(F32)).astype(dtype)

    def start(self):
        for d in range(self.cube.chips):
            self._core(d).start()
        for d in range(self.cube.chips):
            self._load(d).start()

    def phase(self, k):
        if k == 0:
            for d in range(self.cube.chips):
                self._load(d).wait()
                self._core(d).wait_recv()
                self._add(d, 0, self.rows, lambda rows, d=d: self.first[d, rows])
        else:
            for half in (0, 1):
                _, rest, slot = self.steps[half, k - 1]
                for i, e in enumerate(rest):
                    self._hop(half, k - 1, i).wait_recv()
                    self._add(e, half * self.half, self.half,
                              lambda rows, h=half, j=slot + i: self.later[h, j, rows])
        if k < self.stages:
            for c in self._hops(k):
                c.start()

    def finish(self):
        for d in range(self.cube.chips):
            self._core(d).wait_send()
        for stage in range(self.stages):
            for c in self._hops(stage):
                c.wait_send()


def fold_scratch(owners, rows, width, dtype):
    chips = owners // 2
    return [
        pltpu.VMEM((chips, rows, width), dtype),
        pltpu.VMEM((chips, rows, width), dtype),
        pltpu.VMEM((2, chips - 1, rows // 2, width), dtype),
        pltpu.SemaphoreType.DMA((chips,)),
        pltpu.SemaphoreType.DMA((chips,)),
        pltpu.SemaphoreType.DMA((chips,)),
        pltpu.SemaphoreType.DMA((2, chips - 1)),
        pltpu.SemaphoreType.DMA((2, chips - 1)),
    ]


FOLD_REFS = 8


def reduce_kernel(n, owners, small_ref, out_ref, qkv_ref, dw_ref,
                  small_o, out_o, qkv_o, dw_o, *refs):
    line = Line(n)
    cube = Cube(owners)
    refs = list(refs)

    def take(count):
        taken = refs[:count]
        del refs[:count]
        return taken

    sources = [
        lambda q: small_ref.at[q],
        lambda q: out_ref.at[q],
        lambda q: qkv_ref.at[q],
        lambda q: dw_ref.at[q, 0],
        lambda q: dw_ref.at[q, 1],
        lambda q: dw_ref.at[q, 2],
    ]
    folds = [Fold(cube, src, *take(FOLD_REFS)) for src in sources]
    small_all, = take(1)
    gather_small = Gather(line, small_all, *take(3))
    shared = []
    for _ in range(2):
        part, from_l, from_r, total, own = take(5)
        shared.append((Scatter(line, 1, part, from_l, from_r, *take(4)), part,
                       Gather(line, total, *take(3)), total, own))
    write_sem, = take(1)

    joint_barrier(line, cube)
    for f in folds:
        f.start()
    last = folds[0].stages

    def after(index):
        fold = folds[index]
        if index == 0:
            small_all[line.z] = fold.mine[0]
            gather_small.start(small_all.at[line.z])
        elif index <= 2:
            scatter, part, _, _, own = shared[index - 1]
            rows = part.shape[2]
            for b in range(n):
                @pl.when(b == line.z)
                def _():
                    own[...] = fold.mine[0, b * rows:(b + 1) * rows].astype(F32)

                @pl.when(b != line.z)
                def _():
                    part[b, 0] = fold.mine[0, b * rows:(b + 1) * rows]

                scatter.computed(b, 0)
        else:
            pltpu.make_async_copy(fold.mine.at[0], dw_o.at[index - 3], write_sem.at[index - 3]).start()

    def along_line(index):
        scatter, part, gather, total, own = shared[index]

        def add_own(p, value):
            own[...] = own[...] + value

        for t in scatter.steps():
            scatter.step(t, add_own)
        total[line.z] = own[...].astype(BF)
        gather.start(total.at[line.z])

    def collect(index):
        _, _, gather, total, _ = shared[index]
        for i in range(1, n):
            gather.arrive(line.order(i))
        target = (out_o, qkv_o)[index]
        target[...] = total[...].reshape(target.shape)

    count = len(folds)
    for t in range(count + last):
        for k in range(last + 1):
            if 0 <= t - k < count:
                folds[t - k].phase(k)
                if k == last:
                    after(t - k)
        if t == last + 2:
            for i in range(1, n):
                gather_small.arrive(line.order(i))
            small_o[...] = jnp.sum(small_all[...], axis=0)
            along_line(0)
        if t == last + 3:
            along_line(1)
    collect(0)
    collect(1)
    for k in range(3):
        pltpu.make_async_copy(folds[3 + k].mine.at[0], dw_o.at[k], write_sem.at[k]).wait()
    for f in folds:
        f.finish()
    gather_small.finish()
    for scatter, _, gather, _, _ in shared:
        scatter.finish()
        gather.finish()


def reduce_all(small, out_g, qkv_g, dw, n):
    owners, shard, d_model = out_g.shape
    width = dw.shape[3]
    qkv_width = qkv_g.shape[2]
    scratch = fold_scratch(owners, small.shape[1], 128, F32)
    scratch += fold_scratch(owners, shard, d_model, BF)
    scratch += fold_scratch(owners, shard, qkv_width, BF)
    for _ in range(3):
        scratch += fold_scratch(owners, shard, width, BF)
    scratch += [pltpu.VMEM((n, small.shape[1], 128), F32)] + gather_sems(n)
    for w in (d_model, qkv_width):
        scratch += [pltpu.VMEM((n, 1, shard // n, w), BF)] * 3
        scratch += [pltpu.VMEM((n, shard // n, w), BF), pltpu.VMEM((shard // n, w), F32)]
        scratch += scatter_sems(n, 1) + gather_sems(n)
    scratch += [pltpu.SemaphoreType.DMA((3,))]
    return pl.pallas_call(
        functools.partial(reduce_kernel, n, owners),
        out_shape=(
            jax.ShapeDtypeStruct(small.shape[1:], F32),
            jax.ShapeDtypeStruct((shard, d_model), BF),
            jax.ShapeDtypeStruct((shard, qkv_width), BF),
            jax.ShapeDtypeStruct((3, shard, width), BF),
        ),
        in_specs=[ANY] * 4,
        out_specs=[VM, VM, VM, ANY],
        scratch_shapes=scratch,
        compiler_params=params(5),
        cost_estimate=pl.CostEstimate(
            flops=1 << 20, transcendentals=0, bytes_accessed=300 << 20),
        name="reduce_all",
    )(small, out_g, qkv_g, dw)


def normalize(stream, gain):
    return stream * lax.rsqrt(jnp.mean(stream * stream, axis=-1, keepdims=True) + EPSILON) * gain


def normalize_back(grad, stream, gain):
    r = lax.rsqrt(jnp.mean(stream * stream, axis=-1, keepdims=True) + EPSILON)
    u = grad * gain
    back = r * (u - stream * (r * r) * jnp.mean(u * stream, axis=-1, keepdims=True))
    return back, jnp.sum(grad * stream * r, axis=0)


def rotate(heads, cosine, sine):
    half = HEAD // 2
    a, b = heads[..., :half], heads[..., half:]
    return jnp.concatenate([a * cosine - b * sine, b * cosine + a * sine], axis=-1)


def frequencies():
    return jnp.power(ROPE_BASE, -(jnp.arange(HEAD // 2, dtype=F32) * 2.0 / HEAD))


def shards(hidden_in, cotangent, seq_lengths, tile_place, norm_attn, w_qkv, b_qkv, w_out,
           norm_mlp, w_gate, w_up, w_down):
    n = lax.axis_size("context")
    owners = lax.axis_size("fsdp")
    rows, d_model = hidden_in.shape[1:]
    hidden_units = w_gate.shape[2]
    width = -(-hidden_units // 128) * 128
    pad = width - hidden_units
    total = n * rows

    row_index = jnp.arange(total, dtype=jnp.int32)
    tile_order = tile_place[0]
    selector = (
        row_index[:, None] // TILE == jnp.arange(tile_order.shape[0], dtype=jnp.int32)[None, :]
    ).astype(jnp.int32)
    position = jnp.sum(selector * tile_order[None, :], axis=1) * TILE + row_index % TILE
    valid = position < seq_lengths[0]
    offset = lax.axis_index("context") * rows
    my_position = lax.dynamic_slice_in_dim(position, offset, rows)
    my_valid = lax.dynamic_slice_in_dim(valid, offset, rows)
    pos_q = my_position[None, :]
    pos_k = jnp.where(valid, position, 1 << 30)[:, None]
    angles = my_position.astype(F32)[:, None] * frequencies()
    cosine, sine = jnp.cos(angles)[:, None, :], jnp.sin(angles)[:, None, :]

    small = jnp.concatenate(
        [norm_attn.reshape(-1), norm_mlp.reshape(-1), b_qkv.reshape(-1)])[None, None]
    small = lax.all_gather(small, "fsdp", axis=0, tiled=True)
    small = small[:, 0].astype(F32)
    shard = norm_attn.shape[1]
    bias_shard = b_qkv.shape[1]
    gains_attn, gains_mlp, biases = [], [], []
    for l in range(LAYERS):
        gains_attn.append(small[:, l * shard:(l + 1) * shard].reshape(-1))
        gains_mlp.append(small[:, (LAYERS + l) * shard:(LAYERS + l + 1) * shard].reshape(-1))
        start = 2 * LAYERS * shard + l * bias_shard
        biases.append(small[:, start:start + bias_shard].reshape(-1))

    def ffn_shard(l):
        return jnp.stack([
            jnp.pad(m, ((0, 0), (0, pad))) for m in (w_gate[l], w_up[l], w_down[l].T)])

    stream = hidden_in[0].astype(F32)
    kept = []
    for l in range(LAYERS):
        qkv_w = lax.all_gather(w_qkv[l], "fsdp", axis=0, tiled=True)
        out_w = lax.all_gather(w_out[l], "fsdp", axis=0, tiled=True)
        ffn_w = lax.all_gather(ffn_shard(l), "fsdp", axis=0, tiled=False)
        normed = normalize(stream, gains_attn[l]).astype(BF)
        projected = jnp.dot(normed, qkv_w, preferred_element_type=F32) + biases[l]
        qk = rotate(
            projected[:, :Q_WIDTH + KV_WIDTH].reshape(rows, QUERY_HEADS + KV_HEADS, HEAD),
            cosine, sine).astype(BF).reshape(rows, Q_WIDTH + KV_WIDTH)
        q = qk[:, :Q_WIDTH]
        kv = jnp.concatenate([qk[:, Q_WIDTH:], projected[:, Q_WIDTH + KV_WIDTH:].astype(BF)], axis=1)
        mixed, lse, kvall = attention_forward(q, kv, pos_q, pos_k, n)
        middle = stream + jnp.dot(mixed, out_w, preferred_element_type=F32)
        normed_two = normalize(middle, gains_mlp[l]).astype(BF)
        xall, gate, up, y = ffn_forward(normed_two, ffn_w, n)
        kept.append((stream, normed, q, kvall, lse, mixed, middle, xall, gate, up,
                     qkv_w, out_w, ffn_w))
        stream = middle + y
    layer_out = stream.astype(BF)[None]

    gradient = cotangent[0].astype(F32) * my_valid[:, None].astype(F32)
    small_grads = [None] * LAYERS
    big_grads = [None] * LAYERS
    for l in reversed(range(LAYERS)):
        (stream, normed, q, kvall, lse, mixed, middle, xall, gate, up,
         qkv_w, out_w, ffn_w) = kept[l]
        dw, dx = ffn_backward(gradient.astype(BF), ffn_w, xall, gate, up, n)
        if l < LAYERS - 1:
            out_sum, qkv_sum, dw_sum = big_grads[l + 1]
            dx, dw_sum = lax.optimization_barrier((dx, dw_sum))
        back, gain_two = normalize_back(dx, middle, gains_mlp[l])
        d_middle = gradient + back
        d_low = d_middle.astype(BF)
        d_mixed = jnp.einsum("td,cd->tc", d_low, out_w, preferred_element_type=F32).astype(BF)
        out_grad = jnp.einsum("tc,td->cd", mixed, d_low, preferred_element_type=F32).astype(BF)
        dq, dkv = attention_backward(q, kvall, lse, d_mixed, pos_q, pos_k, n)
        if l < LAYERS - 1:
            dq, out_sum, qkv_sum = lax.optimization_barrier((dq, out_sum, qkv_sum))
            big_grads[l + 1] = (
                lax.psum(out_sum, "context"), lax.psum(qkv_sum, "context"), dw_sum)
        d_qk = rotate(
            jnp.concatenate([dq, dkv[:, :KV_WIDTH]], axis=1).reshape(
                rows, QUERY_HEADS + KV_HEADS, HEAD),
            cosine, -sine).reshape(rows, Q_WIDTH + KV_WIDTH)
        d_projected = jnp.concatenate([d_qk, dkv[:, KV_WIDTH:]], axis=1).astype(BF)
        bias_grad = jnp.sum(d_projected.astype(F32), axis=0)
        d_normed = jnp.einsum("tc,dc->td", d_projected, qkv_w, preferred_element_type=F32)
        qkv_grad = jnp.einsum(
            "td,tc->dc", normed, d_projected, preferred_element_type=F32).astype(BF)
        back, gain_one = normalize_back(d_normed, stream, gains_attn[l])
        gradient = d_middle + back
        small_grads[l] = (gain_one, gain_two, bias_grad)
        if l > 0:
            big_grads[l] = (
                lax.psum_scatter(out_grad, "fsdp", scatter_dimension=0, tiled=True),
                lax.psum_scatter(qkv_grad, "fsdp", scatter_dimension=0, tiled=True),
                lax.psum_scatter(dw, "fsdp", scatter_dimension=0, tiled=False))
        else:
            pieces = [
                m.reshape(owners, -1)
                for k in range(3) for m in (small_grads[i][k] for i in range(LAYERS))]
            small = jnp.concatenate(pieces, axis=1)
            used = small.shape[1]
            small_rows = -(-used // (16 * 128)) * 16
            small = jnp.pad(small, ((0, 0), (0, small_rows * 128 - used)))
            small, out_sum, qkv_sum, dw_sum = reduce_all(
                small.reshape(owners, small_rows, 128),
                out_grad.reshape(owners, shard, d_model),
                qkv_grad.reshape(owners, shard, qkv_grad.shape[1]), dw, n)
            small = small.reshape(-1)
            big_grads[l] = (out_sum, qkv_sum, dw_sum)

    grad_norm_attn = small[:LAYERS * shard].reshape(LAYERS, shard)
    grad_norm_mlp = small[LAYERS * shard:2 * LAYERS * shard].reshape(LAYERS, shard)
    start = 2 * LAYERS * shard
    grad_b_qkv = small[start:start + LAYERS * bias_shard].reshape(LAYERS, bias_shard)

    def stacked(pick):
        return jnp.stack([pick(big_grads[l]).astype(F32) for l in range(LAYERS)])

    return (
        layer_out,
        gradient[None],
        grad_norm_attn,
        stacked(lambda m: m[1]),
        grad_b_qkv,
        stacked(lambda m: m[0]),
        grad_norm_mlp,
        stacked(lambda m: m[2][0, :, :hidden_units]),
        stacked(lambda m: m[2][1, :, :hidden_units]),
        stacked(lambda m: m[2][2, :, :hidden_units].T),
    )


def solution(mesh):
    return jax.shard_map(
        shards,
        mesh=mesh,
        in_specs=(
            P("fsdp", "context", None),
            P("fsdp", "context", None),
            P("fsdp"),
            P("fsdp", None),
            P(None, "fsdp"),
            P(None, "fsdp", None),
            P(None, "fsdp"),
            P(None, "fsdp", None),
            P(None, "fsdp"),
            P(None, "fsdp", "context"),
            P(None, "fsdp", "context"),
            P(None, "context", "fsdp"),
        ),
        out_specs=(
            P("fsdp", "context", None),
            P("fsdp", "context", None),
            P(None, "fsdp"),
            P(None, "fsdp", None),
            P(None, "fsdp"),
            P(None, "fsdp", None),
            P(None, "fsdp"),
            P(None, "fsdp", "context"),
            P(None, "fsdp", "context"),
            P(None, "context", "fsdp"),
        ),
        check_vma=False,
    )
```

```python
import functools
import math

import jax
import jax.numpy as jnp
from jax import lax
from jax.experimental import pallas as pl
from jax.experimental.pallas import tpu as pltpu
from jax.sharding import PartitionSpec as P

QUERY_HEADS = 12
KV_HEADS = 2
HEAD = 128
LAYERS = 2
TILE = 128
Q_WIDTH = QUERY_HEADS * HEAD
KV_WIDTH = KV_HEADS * HEAD
PER_GROUP = QUERY_HEADS // KV_HEADS
SCALE = 1.0 / math.sqrt(HEAD)
EPSILON = 1e-06
ROPE_BASE = 1000000.0
BF = jnp.bfloat16
F32 = jnp.float32
MESH = pl.DeviceIdType.MESH
VMEM_LIMIT = 66 * 1024 * 1024
ANY = pl.BlockSpec(memory_space=pl.ANY)
VM = pl.BlockSpec(memory_space=pltpu.VMEM)


def dot_nn(a, b):
    return lax.dot_general(a, b, (((1,), (0,)), ((), ())), preferred_element_type=F32)


def dot_nt(a, b):
    return lax.dot_general(a, b, (((1,), (1,)), ((), ())), preferred_element_type=F32)


def dot_tn(a, b):
    return lax.dot_general(a, b, (((0,), (0,)), ((), ())), preferred_element_type=F32)


def lane_tile(width, most):
    best = 128
    for k in range(1, most // 128 + 1):
        if width % (128 * k) == 0:
            best = 128 * k
    return best


class Line:
    def __init__(self, n):
        self.n = n
        self.z = lax.axis_index("context")
        self.right = lax.rem(self.z + 1, n)
        self.left = lax.rem(self.z + n - 1, n)
        self.has_right = self.z < n - 1
        self.has_left = self.z > 0

    def barrier(self):
        bar = pltpu.get_barrier_semaphore()

        @pl.when(self.has_right)
        def _():
            pl.semaphore_signal(bar, inc=1, device_id={"context": self.right}, device_id_type=MESH)

        @pl.when(self.has_left)
        def _():
            pl.semaphore_signal(bar, inc=1, device_id={"context": self.left}, device_id_type=MESH)

        both = self.has_right & self.has_left

        @pl.when(both)
        def _():
            pl.semaphore_wait(bar, 2)

        @pl.when(jnp.logical_not(both))
        def _():
            pl.semaphore_wait(bar, 1)

    def order(self, i):
        z, n = self.z, self.n
        short = jnp.minimum(z, n - 1 - z)
        j = i - 1
        paired = j < 2 * short
        k = jnp.where(paired, j // 2 + 1, j - short + 1)
        goes_left = jnp.where(paired, lax.rem(j, 2) == 0, z > n - 1 - z)
        return jnp.where(i == 0, z, jnp.where(goes_left, z - k, z + k))


def remote(src, dst, send, recv, target):
    return pltpu.make_async_remote_copy(
        src_ref=src, dst_ref=dst, send_sem=send, recv_sem=recv,
        device_id={"context": target}, device_id_type=MESH,
    )


class Gather:
    def __init__(self, line, slots, send_r, send_l, recv):
        self.line, self.slots = line, slots
        self.send_r, self.send_l, self.recv = send_r, send_l, recv

    def _right(self, b, src):
        return remote(src, self.slots.at[b], self.send_r.at[b], self.recv.at[b], self.line.right)

    def _left(self, b, src):
        return remote(src, self.slots.at[b], self.send_l.at[b], self.recv.at[b], self.line.left)

    def start(self, own):
        line = self.line

        @pl.when(line.has_right)
        def _():
            self._right(line.z, own).start()

        @pl.when(line.has_left)
        def _():
            self._left(line.z, own).start()

    def arrive(self, b):
        line = self.line
        self._right(b, self.slots.at[b]).wait_recv()

        @pl.when((b < line.z) & line.has_right)
        def _():
            self._right(b, self.slots.at[b]).start()

        @pl.when((b > line.z) & line.has_left)
        def _():
            self._left(b, self.slots.at[b]).start()

    def finish(self):
        line = self.line
        for b in range(line.n):
            @pl.when((b <= line.z) & line.has_right)
            def _():
                self._right(b, self.slots.at[b]).wait_send()

            @pl.when((b >= line.z) & line.has_left)
            def _():
                self._left(b, self.slots.at[b]).wait_send()


class Scatter:
    def __init__(self, line, pieces, part, from_left, from_right, send_r, send_l, recv_l, recv_r):
        self.line, self.pieces, self.part = line, pieces, part
        self.from_left, self.from_right = from_left, from_right
        self.send_r, self.send_l, self.recv_l, self.recv_r = send_r, send_l, recv_l, recv_r

    def _right(self, b, p):
        return remote(self.part.at[b, p], self.from_left.at[b, p], self.send_r.at[b, p],
                      self.recv_l.at[b, p], self.line.right)

    def _left(self, b, p):
        return remote(self.part.at[b, p], self.from_right.at[b, p], self.send_l.at[b, p],
                      self.recv_r.at[b, p], self.line.left)

    def computed(self, b, p):
        line = self.line

        @pl.when((line.z == 0) & (b > 0))
        def _():
            self._right(b, p).start()

        @pl.when((line.z == line.n - 1) & (b < line.n - 1))
        def _():
            self._left(b, p).start()

    def steps(self):
        return range(1, 2 * (self.line.n - 1) + 1)

    def step(self, t, add_own):
        line = self.line
        n, z = line.n, line.z
        b_left = t - z

        @pl.when(line.has_left & (b_left >= z) & (b_left < n))
        def _():
            for p in range(self.pieces):
                self._right(b_left, p).wait_recv()

                @pl.when(b_left == z)
                def _():
                    add_own(p, self.from_left[b_left, p].astype(F32))

                @pl.when(b_left != z)
                def _():
                    self.part[b_left, p] = (
                        self.part[b_left, p].astype(F32) + self.from_left[b_left, p].astype(F32)
                    ).astype(BF)
                    self._right(b_left, p).start()

        b_right = 2 * (n - 1) - t - z

        @pl.when(line.has_right & (b_right >= 0) & (b_right <= z))
        def _():
            for p in range(self.pieces):
                self._left(b_right, p).wait_recv()

                @pl.when(b_right == z)
                def _():
                    add_own(p, self.from_right[b_right, p].astype(F32))

                @pl.when(b_right != z)
                def _():
                    self.part[b_right, p] = (
                        self.part[b_right, p].astype(F32) + self.from_right[b_right, p].astype(F32)
                    ).astype(BF)
                    self._left(b_right, p).start()

    def finish(self):
        line = self.line
        for b in range(line.n):
            @pl.when((b > line.z) & line.has_right)
            def _():
                for p in range(self.pieces):
                    self._right(b, p).wait_send()

            @pl.when((b < line.z) & line.has_left)
            def _():
                for p in range(self.pieces):
                    self._left(b, p).wait_send()


def gather_sems(n):
    return [pltpu.SemaphoreType.DMA((n,))] * 3


def scatter_sems(n, pieces):
    return [pltpu.SemaphoreType.DMA((n, pieces))] * 4


def params(cid):
    return pltpu.CompilerParams(
        collective_id=cid, has_side_effects=True, vmem_limit_bytes=VMEM_LIMIT
    )


def bits_of(owners):
    return [1 << i for i in range(owners.bit_length() - 1)]


class Cube:
    def __init__(self, owners):
        self.owners = owners
        self.me = lax.axis_index("fsdp")
        self.bits = bits_of(owners)
        self.chip_bits = [b // 2 for b in self.bits[1:]]
        self.chips = owners // 2

    def flip(self, mask):
        index = self.me
        for b in self.bits:
            if mask & b:
                index = index + b - 2 * b * lax.rem(self.me // b, 2)
        return index

    def signal(self, bar):
        for b in self.bits:
            pl.semaphore_signal(bar, inc=1, device_id={"fsdp": self.flip(b)}, device_id_type=MESH)

    def order(self, half):
        return self.chip_bits[::-1] if half == 0 else self.chip_bits

    def plan(self):
        steps = {}
        for half in (0, 1):
            order, slot = self.order(half), 0
            for stage, bit in enumerate(order):
                rest = [0]
                for other in order[stage + 1:]:
                    rest = rest + [m | other for m in rest]
                steps[half, stage] = (bit, rest, slot)
                slot += len(rest)
        return steps


def joint_barrier(line, cube):
    bar = pltpu.get_barrier_semaphore()
    cube.signal(bar)
    peers = len(cube.bits)

    @pl.when(line.has_right)
    def _():
        pl.semaphore_signal(bar, inc=1, device_id={"context": line.right}, device_id_type=MESH)

    @pl.when(line.has_left)
    def _():
        pl.semaphore_signal(bar, inc=1, device_id={"context": line.left}, device_id_type=MESH)

    both = line.has_right & line.has_left

    @pl.when(both)
    def _():
        pl.semaphore_wait(bar, peers + 2)

    @pl.when(jnp.logical_not(both))
    def _():
        pl.semaphore_wait(bar, peers + 1)


class Spread:
    def __init__(self, cube, own, full, own_sem, send, recv, core_send, core_recv):
        self.cube, self.own, self.full = cube, own, full
        self.own_sem, self.send, self.recv = own_sem, send, recv
        self.core_send, self.core_recv = core_send, core_recv
        self.half = own.shape[0] // 2
        self.stages = len(cube.chip_bits)

    def _rows(self, half):
        return pl.ds(half * self.half, self.half)

    def _block(self, half, mask):
        return self.full.at[self.cube.flip(mask), self._rows(half)]

    def _source(self, half, mask):
        return self._block(half, 2 * mask) if mask else self.own.at[self._rows(half)]

    def _masks(self, half, stage):
        masks = [0]
        for bit in self.cube.order(half)[:stage]:
            masks = masks + [m | bit for m in masks]
        return masks

    def _hop(self, half, stage, mask):
        bit = self.cube.order(half)[stage]
        return pltpu.make_async_remote_copy(
            src_ref=self._source(half, mask), dst_ref=self._block(half, 2 * mask),
            send_sem=self.send.at[half, mask | bit], recv_sem=self.recv.at[half, mask | bit],
            device_id={"fsdp": self.cube.flip(2 * bit)}, device_id_type=MESH)

    def _arrival(self, half, mask):
        block = self._block(half, 2 * mask)
        return pltpu.make_async_remote_copy(
            src_ref=block, dst_ref=block,
            send_sem=self.send.at[half, mask], recv_sem=self.recv.at[half, mask],
            device_id={"fsdp": self.cube.flip(1)}, device_id_type=MESH)

    def _core(self, half, mask):
        return pltpu.make_async_remote_copy(
            src_ref=self._source(half, mask), dst_ref=self._block(half, 2 * mask),
            send_sem=self.core_send.at[half, mask], recv_sem=self.core_recv.at[half, mask],
            device_id={"fsdp": self.cube.flip(1)}, device_id_type=MESH)

    def _core_arrival(self, half, mask):
        block = self._block(half, 2 * mask | 1)
        return pltpu.make_async_remote_copy(
            src_ref=block, dst_ref=block,
            send_sem=self.core_send.at[half, mask], recv_sem=self.core_recv.at[half, mask],
            device_id={"fsdp": self.cube.flip(1)}, device_id_type=MESH)

    def _own_copy(self):
        return pltpu.make_async_copy(self.own, self.full.at[self.cube.me], self.own_sem)

    def start(self):
        for stage in range(self.stages):
            for half in (0, 1):
                self._hop(half, stage, 0).start()
        for half in (0, 1):
            self._core(half, 0).start()
        self._own_copy().start()

    def phase(self, k):
        for half in (0, 1):
            bit = self.cube.order(half)[k - 1]
            for m in self._masks(half, k - 1):
                self._arrival(half, m | bit).wait_recv()
                for stage in range(k, self.stages):
                    self._hop(half, stage, m | bit).start()
                self._core(half, m | bit).start()

    def finish(self):
        self._own_copy().wait()
        for half in (0, 1):
            for m in range(self.cube.chips):
                self._core_arrival(half, m).wait_recv()
                self._core(half, m).wait_send()
            for stage in range(self.stages):
                for m in self._masks(half, stage):
                    self._hop(half, stage, m).wait_send()


SPREAD_SEMS = 5


def spread_sems(owners):
    chips = owners // 2
    return [pltpu.SemaphoreType.DMA] + [pltpu.SemaphoreType.DMA((2, chips))] * 4


def spread_shapes(owners, shards):
    return tuple(jax.ShapeDtypeStruct((owners,) + m.shape, m.dtype) for m in shards)


def spread_kernel(owners, count, *refs):
    cube = Cube(owners)
    spreads = [
        Spread(cube, refs[i], refs[count + i],
               *refs[2 * count + SPREAD_SEMS * i:2 * count + SPREAD_SEMS * (i + 1)])
        for i in range(count)]
    bar = pltpu.get_barrier_semaphore()
    cube.signal(bar)
    pl.semaphore_wait(bar, len(cube.bits))
    for s in spreads:
        s.start()
    for k in range(1, len(cube.chip_bits) + 1):
        for s in spreads:
            s.phase(k)
    for s in spreads:
        s.finish()


def spread_all(owners, *shards):
    count = len(shards)
    return pl.pallas_call(
        functools.partial(spread_kernel, owners, count),
        out_shape=spread_shapes(owners, shards),
        in_specs=[VM] * count,
        out_specs=[ANY] * count,
        scratch_shapes=spread_sems(owners) * count,
        compiler_params=params(6),
        cost_estimate=pl.CostEstimate(
            flops=1 << 20, transcendentals=0, bytes_accessed=150 << 20),
        name="spread_all",
    )(*shards)


def ffn_forward_kernel(n, pieces, count, *refs):
    x_ref, w_ref = refs[:2]
    next_own = refs[2:2 + count]
    xall_ref, gate_ref, up_ref, y_ref = refs[2 + count:6 + count]
    next_full = refs[6 + count:6 + 2 * count]
    (w_v, xbuf, gbuf, ubuf, hbuf, part, from_l, from_r,
     w_sem, x_sem, out_sem, *sems) = refs[6 + 2 * count:]
    line = Line(n)
    z = line.z
    owners, _, rows, width = w_ref.shape
    d_model = x_ref.shape[1]
    tile = lane_tile(width, 256)
    piece = d_model // pieces
    gather = Gather(line, xbuf, *sems[:3])
    scatter = Scatter(line, pieces, part, from_l, from_r, *sems[3:7])
    spreads = []
    stages = 0
    if count:
        cube = Cube(owners)
        stages = len(cube.chip_bits)
        for i in range(count):
            at = 7 + SPREAD_SEMS * i
            spreads.append(Spread(cube, next_own[i], next_full[i], *sems[at:at + SPREAD_SEMS]))

    def w_copy(k, f):
        return pltpu.make_async_copy(
            w_ref.at[f, k], w_v.at[k, pl.ds(f * rows, rows)], w_sem.at[k, f]
        )

    def x_out(b):
        return pltpu.make_async_copy(xbuf.at[b], xall_ref.at[b], x_sem.at[b])

    if count:
        joint_barrier(line, cube)
    else:
        line.barrier()
    gather.start(x_ref)
    for s in spreads:
        s.start()
    for k in range(3):
        for f in range(owners):
            w_copy(k, f).start()
    xbuf[z] = x_ref[...]
    for k in range(3):
        for f in range(owners):
            w_copy(k, f).wait()

    @pl.loop(0, n)
    def _(i):
        b = line.order(i)

        @pl.when(i > 0)
        def _():
            gather.arrive(b)

        x_out(b).start()
        slot = lax.rem(i, 2)
        g_copy = pltpu.make_async_copy(gbuf.at[slot], gate_ref.at[b], out_sem.at[0, slot])
        u_copy = pltpu.make_async_copy(ubuf.at[slot], up_ref.at[b], out_sem.at[1, slot])

        @pl.when(i > 1)
        def _():
            g_copy.wait()
            u_copy.wait()

        @pl.loop(0, width // tile)
        def _(j):
            cols = pl.ds(pl.multiple_of(j * tile, tile), tile)
            xb = xbuf[b]
            gate = dot_nn(xb, w_v[0, :, cols])
            up = dot_nn(xb, w_v[1, :, cols])
            gbuf[slot, :, cols] = gate.astype(BF)
            ubuf[slot, :, cols] = up.astype(BF)
            hbuf[:, cols] = (gate * jax.nn.sigmoid(gate) * up).astype(BF)

        g_copy.start()
        u_copy.start()
        for p in range(pieces):
            out = dot_nt(hbuf[...], w_v[2, pl.ds(p * piece, piece)])

            @pl.when(b == z)
            def _():
                y_ref[:, p * piece:(p + 1) * piece] = out

            @pl.when(b != z)
            def _():
                part[b, p] = out.astype(BF)

            scatter.computed(b, p)

        if spreads:
            @pl.when(i == n // 2)
            def _():
                for s in spreads:
                    s.phase(1)

    def add_own(p, value):
        cols = slice(p * piece, (p + 1) * piece)
        y_ref[:, cols] = y_ref[:, cols] + value

    passed = 2
    for t in scatter.steps():
        scatter.step(t, add_own)
        if t >= 4 and t % 2 == 0 and passed <= stages:
            for s in spreads:
                s.phase(passed)
            passed += 1
    for k in range(passed, stages + 1):
        for s in spreads:
            s.phase(k)
    for i in range(max(0, n - 2), n):
        slot = i % 2
        pltpu.make_async_copy(gbuf.at[slot], gate_ref.at[0], out_sem.at[0, slot]).wait()
        pltpu.make_async_copy(ubuf.at[slot], up_ref.at[0], out_sem.at[1, slot]).wait()
    for b in range(n):
        x_out(b).wait()
    gather.finish()
    scatter.finish()
    for s in spreads:
        s.finish()


def ffn_forward(x, w, n, following=()):
    rows, d_model = x.shape
    owners, _, shard, width = w.shape
    pieces = 3
    piece = d_model // pieces
    count = len(following)
    return pl.pallas_call(
        functools.partial(ffn_forward_kernel, n, pieces, count),
        out_shape=(
            jax.ShapeDtypeStruct((n, rows, d_model), BF),
            jax.ShapeDtypeStruct((n, rows, width), BF),
            jax.ShapeDtypeStruct((n, rows, width), BF),
            jax.ShapeDtypeStruct((rows, d_model), F32),
        ) + spread_shapes(owners, following),
        in_specs=[VM, ANY] + [VM] * count,
        out_specs=[ANY, ANY, ANY, VM] + [ANY] * count,
        scratch_shapes=[
            pltpu.VMEM((3, d_model, width), BF),
            pltpu.VMEM((n, rows, d_model), BF),
            pltpu.VMEM((2, rows, width), BF),
            pltpu.VMEM((2, rows, width), BF),
            pltpu.VMEM((rows, width), BF),
            pltpu.VMEM((n, pieces, rows, piece), BF),
            pltpu.VMEM((n, pieces, rows, piece), BF),
            pltpu.VMEM((n, pieces, rows, piece), BF),
            pltpu.SemaphoreType.DMA((3, owners)),
            pltpu.SemaphoreType.DMA((n,)),
            pltpu.SemaphoreType.DMA((2, 2)),
        ] + gather_sems(n) + scatter_sems(n, pieces) + spread_sems(owners) * count,
        compiler_params=params(7 if count else 1),
        cost_estimate=pl.CostEstimate(
            flops=6 * n * rows * d_model * width, transcendentals=n * rows * width,
            bytes_accessed=60 << 20),
        name="ffn_forward",
    )(x, w, *following)


def ffn_backward_kernel(n, pieces, groups, g_ref, w_ref, xall_ref, gate_ref, up_ref, dw_ref, dx_ref,
                        w_v, gbuf, xv, gate_v, up_v, hid_v, part, from_l, from_r, stage,
                        w_sem, in_sem, out_sem, *sems):
    line = Line(n)
    z = line.z
    owners, _, shard, width = w_ref.shape
    rows, d_model = g_ref.shape
    tile = lane_tile(width, 256)
    piece = d_model // pieces
    gather = Gather(line, gbuf, *sems[:3])
    scatter = Scatter(line, pieces, part, from_l, from_r, *sems[3:])

    def w_copy(k, f):
        return pltpu.make_async_copy(
            w_ref.at[f, k], w_v.at[k, pl.ds(f * shard, shard)], w_sem.at[k, f]
        )

    def loads(b):
        return (
            pltpu.make_async_copy(gate_ref.at[b], gate_v.at[b], in_sem.at[0, b]),
            pltpu.make_async_copy(up_ref.at[b], up_v.at[b], in_sem.at[1, b]),
        )

    def x_load(b):
        return pltpu.make_async_copy(xall_ref.at[b], xv.at[b], in_sem.at[2, b])

    line.barrier()
    gather.start(g_ref)
    for f in range(owners):
        w_copy(2, f).start()
    for c in loads(z):
        c.start()
    for k in range(2):
        for f in range(owners):
            w_copy(k, f).start()
    for b in range(n):
        @pl.when(b != z)
        def _():
            for c in loads(b):
                c.start()
    for b in range(n):
        x_load(b).start()
    gbuf[z] = g_ref[...]
    for k in (2, 0, 1):
        for f in range(owners):
            w_copy(k, f).wait()

    @pl.loop(0, n)
    def _(i):
        b = line.order(i)

        @pl.when(i > 0)
        def _():
            gather.arrive(b)

        for c in loads(b):
            c.wait()

        @pl.loop(0, width // tile)
        def _(j):
            cols = pl.ds(pl.multiple_of(j * tile, tile), tile)
            d_hidden = dot_nn(gbuf[b], w_v[2, :, cols])
            gate = gate_v[b, :, cols].astype(F32)
            up = up_v[b, :, cols].astype(F32)
            sig = jax.nn.sigmoid(gate)
            act = gate * sig
            hid_v[b, :, cols] = (act * up).astype(BF)
            gate_v[b, :, cols] = (d_hidden * up * (sig + act * (1.0 - sig))).astype(BF)
            up_v[b, :, cols] = (d_hidden * act).astype(BF)

        for p in range(pieces):
            sl = pl.ds(p * piece, piece)
            out = dot_nt(gate_v[b], w_v[0, sl]) + dot_nt(up_v[b], w_v[1, sl])

            @pl.when(b == z)
            def _():
                dx_ref[:, p * piece:(p + 1) * piece] = out

            @pl.when(b != z)
            def _():
                part[b, p] = out.astype(BF)

            scatter.computed(b, p)

    def add_own(p, value):
        cols = slice(p * piece, (p + 1) * piece)
        dx_ref[:, cols] = dx_ref[:, cols] + value

    for b in range(n):
        x_load(b).wait()

    group = d_model // groups
    per = group // shard

    def dw_copies(k, q, slot):
        return [
            pltpu.make_async_copy(
                stage.at[slot, pl.ds(s * shard, shard)], dw_ref.at[q * per + s, k],
                out_sem.at[slot, s])
            for s in range(per)
        ]

    def weight_unit(unit):
        k, q = unit // groups, unit % groups
        slot = unit % 2
        left = (xv, xv, gbuf)[k]
        right = (gate_v, up_v, hid_v)[k]
        if unit >= 2:
            for c in dw_copies((unit - 2) // groups, (unit - 2) % groups, slot):
                c.wait()
        lt = left[:, :, q * group:(q + 1) * group].reshape(n * rows, group)

        @pl.loop(0, width // tile)
        def _(j):
            cols = pl.ds(pl.multiple_of(j * tile, tile), tile)
            stage[slot, :, cols] = dot_tn(
                lt, right[:, :, cols].reshape(n * rows, tile)
            ).astype(BF)

        for c in dw_copies(k, q, slot):
            c.start()

    units = 3 * groups
    steps = list(scatter.steps())
    done = 0
    for index, t in enumerate(steps):
        scatter.step(t, add_own)
        until = units * (index + 1) // len(steps)
        while done < until:
            weight_unit(done)
            done += 1
    for unit in range(units - 2, units):
        for c in dw_copies(unit // groups, unit % groups, unit % 2):
            c.wait()
    gather.finish()
    scatter.finish()


def ffn_backward(g, w, xall, gate, up, n):
    rows, d_model = g.shape
    owners, _, shard, width = w.shape
    pieces, groups = 3, 4
    piece = d_model // pieces
    per = d_model // groups // shard
    return pl.pallas_call(
        functools.partial(ffn_backward_kernel, n, pieces, groups),
        out_shape=(
            jax.ShapeDtypeStruct((owners, 3, shard, width), BF),
            jax.ShapeDtypeStruct((rows, d_model), F32),
        ),
        in_specs=[VM, ANY, ANY, ANY, ANY],
        out_specs=[ANY, VM],
        scratch_shapes=[
            pltpu.VMEM((3, d_model, width), BF),
            pltpu.VMEM((n, rows, d_model), BF),
            pltpu.VMEM((n, rows, d_model), BF),
            pltpu.VMEM((n, rows, width), BF),
            pltpu.VMEM((n, rows, width), BF),
            pltpu.VMEM((n, rows, width), BF),
            pltpu.VMEM((n, pieces, rows, piece), BF),
            pltpu.VMEM((n, pieces, rows, piece), BF),
            pltpu.VMEM((n, pieces, rows, piece), BF),
            pltpu.VMEM((2, d_model // groups, width), BF),
            pltpu.SemaphoreType.DMA((3, owners)),
            pltpu.SemaphoreType.DMA((3, n)),
            pltpu.SemaphoreType.DMA((2, per)),
        ] + gather_sems(n) + scatter_sems(n, pieces),
        compiler_params=params(2),
        cost_estimate=pl.CostEstimate(
            flops=12 * n * rows * d_model * width, transcendentals=n * rows * width,
            bytes_accessed=100 << 20),
        name="ffn_backward",
    )(g, w, xall, gate, up)


def attention_forward_kernel(n, q_ref, kv_ref, pq_ref, pk_ref, mixed_ref, lse_ref, kvall_ref,
                             kvbuf, vt, *sems):
    line = Line(n)
    z = line.z
    rows = q_ref.shape[0]
    total = n * rows
    gather = Gather(line, kvbuf, *sems)
    line.barrier()
    gather.start(kv_ref)
    kvbuf[z] = kv_ref[...]
    for i in range(1, n):
        gather.arrive(line.order(i))
    kvall_ref[...] = kvbuf[...]
    allowed = pk_ref[...] <= pq_ref[...]
    for g in range(KV_HEADS):
        v = kvbuf[:, :, KV_WIDTH + g * HEAD:KV_WIDTH + (g + 1) * HEAD].reshape(total, HEAD)
        vt[g] = v.T
    for g in range(KV_HEADS):
        for r in range(PER_GROUP):
            h = g * PER_GROUP + r
            k = kvbuf[:, :, g * HEAD:(g + 1) * HEAD].reshape(total, HEAD)
            s = dot_nt(k, q_ref[:, h * HEAD:(h + 1) * HEAD]) * SCALE
            s = jnp.where(allowed, s, -1e30)
            top = jnp.max(s, axis=0, keepdims=True)
            e = jnp.exp(s - top)
            den = jnp.sum(e, axis=0, keepdims=True)
            o = dot_nn(vt[g], e.astype(BF)) / den
            mixed_ref[:, h * HEAD:(h + 1) * HEAD] = o.T.astype(BF)
            lse_ref[h:h + 1, :] = top + jnp.log(den)
    gather.finish()


def attention_forward(q, kv, pos_q, pos_k, n):
    rows = q.shape[0]
    return pl.pallas_call(
        functools.partial(attention_forward_kernel, n),
        out_shape=(
            jax.ShapeDtypeStruct((rows, Q_WIDTH), BF),
            jax.ShapeDtypeStruct((16, rows), F32),
            jax.ShapeDtypeStruct((n, rows, 2 * KV_WIDTH), BF),
        ),
        in_specs=[VM] * 4,
        out_specs=[VM] * 3,
        scratch_shapes=[
            pltpu.VMEM((n, rows, 2 * KV_WIDTH), BF),
            pltpu.VMEM((KV_HEADS, HEAD, n * rows), BF),
        ] + gather_sems(n),
        compiler_params=params(3),
        cost_estimate=pl.CostEstimate(
            flops=4 * n * rows * rows * Q_WIDTH, transcendentals=n * rows * rows * QUERY_HEADS,
            bytes_accessed=16 << 20),
        name="attention_forward",
    )(q, kv, pos_q, pos_k)


def attention_backward_kernel(n, q_ref, kvall_ref, lse_ref, dm_ref, pq_ref, pk_ref,
                              dq_ref, dkv_ref, kt, dk_acc, dv_acc, part, from_l, from_r, *sems):
    line = Line(n)
    z = line.z
    rows = q_ref.shape[0]
    total = n * rows
    pieces = KV_HEADS
    scatter = Scatter(line, pieces, part, from_l, from_r, *sems)
    line.barrier()
    allowed = pk_ref[...] <= pq_ref[...]
    for g in range(KV_HEADS):
        k = kvall_ref[:, :, g * HEAD:(g + 1) * HEAD].reshape(total, HEAD)
        kt[g] = k.T
    for g in range(KV_HEADS):
        for r in range(PER_GROUP):
            h = g * PER_GROUP + r
            cols = slice(h * HEAD, (h + 1) * HEAD)
            k = kvall_ref[:, :, g * HEAD:(g + 1) * HEAD].reshape(total, HEAD)
            v = kvall_ref[:, :, KV_WIDTH + g * HEAD:KV_WIDTH + (g + 1) * HEAD].reshape(total, HEAD)
            q = q_ref[:, cols]
            dm = dm_ref[:, cols]
            s = dot_nt(k, q) * SCALE
            pr = jnp.where(allowed, jnp.exp(s - lse_ref[h:h + 1, :]), 0.0)
            dp = dot_nt(v, dm)
            delta = jnp.sum(pr * dp, axis=0, keepdims=True)
            ds = (pr * (dp - delta) * SCALE).astype(BF)
            dv = dot_nn(pr.astype(BF), dm)
            dk = dot_nn(ds, q)
            if r == 0:
                dk_acc[...] = dk
                dv_acc[...] = dv
            else:
                dk_acc[...] += dk
                dv_acc[...] += dv
            dq_ref[:, cols] = dot_nn(kt[g], ds).T
        for b in range(n):
            sl = slice(b * rows, (b + 1) * rows)

            @pl.when(b == z)
            def _():
                dkv_ref[:, g * HEAD:(g + 1) * HEAD] = dk_acc[sl]
                dkv_ref[:, KV_WIDTH + g * HEAD:KV_WIDTH + (g + 1) * HEAD] = dv_acc[sl]

            @pl.when(b != z)
            def _():
                part[b, g, :, 0:HEAD] = dk_acc[sl].astype(BF)
                part[b, g, :, HEAD:2 * HEAD] = dv_acc[sl].astype(BF)

            scatter.computed(b, g)

    def add_own(p, value):
        a = slice(p * HEAD, (p + 1) * HEAD)
        c = slice(KV_WIDTH + p * HEAD, KV_WIDTH + (p + 1) * HEAD)
        dkv_ref[:, a] = dkv_ref[:, a] + value[:, :HEAD]
        dkv_ref[:, c] = dkv_ref[:, c] + value[:, HEAD:]

    for t in scatter.steps():
        scatter.step(t, add_own)
    scatter.finish()


def attention_backward(q, kvall, lse, dm, pos_q, pos_k, n):
    rows = q.shape[0]
    return pl.pallas_call(
        functools.partial(attention_backward_kernel, n),
        out_shape=(
            jax.ShapeDtypeStruct((rows, Q_WIDTH), F32),
            jax.ShapeDtypeStruct((rows, 2 * KV_WIDTH), F32),
        ),
        in_specs=[VM] * 6,
        out_specs=[VM] * 2,
        scratch_shapes=[
            pltpu.VMEM((KV_HEADS, HEAD, n * rows), BF),
            pltpu.VMEM((n * rows, HEAD), F32),
            pltpu.VMEM((n * rows, HEAD), F32),
        ] + [pltpu.VMEM((n, KV_HEADS, rows, 2 * HEAD), BF)] * 3 + scatter_sems(n, KV_HEADS),
        compiler_params=params(4),
        cost_estimate=pl.CostEstimate(
            flops=10 * n * rows * rows * Q_WIDTH, transcendentals=n * rows * rows * QUERY_HEADS,
            bytes_accessed=16 << 20),
        name="attention_backward",
    )(q, kvall, lse, dm, pos_q, pos_k)


class Fold:
    def __init__(self, cube, src, mine, first, later, load_sem, send1, recv1, send2, recv2):
        self.cube, self.src = cube, src
        self.mine, self.first, self.later = mine, first, later
        self.load_sem, self.send1, self.recv1 = load_sem, send1, recv1
        self.send2, self.recv2 = send2, recv2
        self.rows = mine.shape[1]
        self.half = self.rows // 2
        self.steps = cube.plan()
        self.stages = len(cube.chip_bits)

    def _load(self, d):
        return pltpu.make_async_copy(
            self.src(self.cube.flip(2 * d)), self.mine.at[d], self.load_sem.at[d])

    def _core(self, d):
        return pltpu.make_async_remote_copy(
            src_ref=self.src(self.cube.flip(2 * d | 1)), dst_ref=self.first.at[d],
            send_sem=self.send1.at[d], recv_sem=self.recv1.at[d],
            device_id={"fsdp": self.cube.flip(1)}, device_id_type=MESH)

    def _hop(self, half, stage, index):
        bit, rest, slot = self.steps[half, stage]
        rows = pl.ds(half * self.half, self.half)
        return pltpu.make_async_remote_copy(
            src_ref=self.mine.at[bit | rest[index], rows],
            dst_ref=self.later.at[half, slot + index],
            send_sem=self.send2.at[half, slot + index],
            recv_sem=self.recv2.at[half, slot + index],
            device_id={"fsdp": self.cube.flip(2 * bit)}, device_id_type=MESH)

    def _hops(self, stage):
        return [self._hop(half, stage, i)
                for half in (0, 1) for i in range(len(self.steps[half, stage][1]))]

    def _add(self, d, base, size, other):
        dtype = self.mine.dtype
        strip = 48 if size % 48 == 0 else size

        @pl.loop(0, size // strip)
        def _(i):
            into = pl.ds(pl.multiple_of(base + i * strip, 8), strip)
            rows = pl.ds(pl.multiple_of(i * strip, 8), strip)
            self.mine[d, into] = (
                self.mine[d, into].astype(F32) + other(rows).astype(F32)).astype(dtype)

    def start(self):
        for d in range(self.cube.chips):
            self._core(d).start()
        for d in range(self.cube.chips):
            self._load(d).start()

    def phase(self, k):
        if k == 0:
            for d in range(self.cube.chips):
                self._load(d).wait()
                self._core(d).wait_recv()
                self._add(d, 0, self.rows, lambda rows, d=d: self.first[d, rows])
        else:
            for half in (0, 1):
                _, rest, slot = self.steps[half, k - 1]
                for i, e in enumerate(rest):
                    self._hop(half, k - 1, i).wait_recv()
                    self._add(e, half * self.half, self.half,
                              lambda rows, h=half, j=slot + i: self.later[h, j, rows])
        if k < self.stages:
            for c in self._hops(k):
                c.start()

    def finish(self):
        for d in range(self.cube.chips):
            self._core(d).wait_send()
        for stage in range(self.stages):
            for c in self._hops(stage):
                c.wait_send()


def fold_scratch(owners, rows, width, dtype):
    chips = owners // 2
    return [
        pltpu.VMEM((chips, rows, width), dtype),
        pltpu.VMEM((chips, rows, width), dtype),
        pltpu.VMEM((2, chips - 1, rows // 2, width), dtype),
        pltpu.SemaphoreType.DMA((chips,)),
        pltpu.SemaphoreType.DMA((chips,)),
        pltpu.SemaphoreType.DMA((chips,)),
        pltpu.SemaphoreType.DMA((2, chips - 1)),
        pltpu.SemaphoreType.DMA((2, chips - 1)),
    ]


FOLD_REFS = 8


def reduce_kernel(n, owners, small_ref, out_ref, qkv_ref, dw_ref, early_out, early_qkv,
                  small_o, out_o, qkv_o, dw_o, early_out_o, early_qkv_o, *refs):
    line = Line(n)
    cube = Cube(owners)
    refs = list(refs)

    def take(count):
        taken = refs[:count]
        del refs[:count]
        return taken

    sources = [
        lambda q: small_ref.at[q],
        lambda q: out_ref.at[q],
        lambda q: qkv_ref.at[q],
        lambda q: dw_ref.at[q, 0],
        lambda q: dw_ref.at[q, 1],
        lambda q: dw_ref.at[q, 2],
    ]
    folds = [Fold(cube, src, *take(FOLD_REFS)) for src in sources]
    small_all, = take(1)
    gather_small = Gather(line, small_all, *take(3))
    shared = []
    for _ in range(4):
        part, from_l, from_r, total, own = take(5)
        shared.append((Scatter(line, 1, part, from_l, from_r, *take(4)), part,
                       Gather(line, total, *take(3)), total, own))
    write_sem, = take(1)
    targets = (out_o, qkv_o, early_out_o, early_qkv_o)

    def share(index, value):
        scatter, part, _, _, own = shared[index]
        rows = part.shape[2]
        for b in range(n):
            @pl.when(b == line.z)
            def _():
                own[...] = value(slice(b * rows, (b + 1) * rows)).astype(F32)

            @pl.when(b != line.z)
            def _():
                part[b, 0] = value(slice(b * rows, (b + 1) * rows))

            scatter.computed(b, 0)

    def scatter_step(indices, t):
        for index in indices:
            scatter, _, _, _, own = shared[index]

            def add_own(p, value):
                own[...] = own[...] + value

            scatter.step(t, add_own)

    def gather_start(indices):
        for index in indices:
            _, _, gather, total, own = shared[index]
            total[line.z] = own[...].astype(BF)
            gather.start(total.at[line.z])

    def gather_step(indices, i):
        for index in indices:
            shared[index][2].arrive(line.order(i))

    def collect(indices):
        for index in indices:
            targets[index][...] = shared[index][3][...].reshape(targets[index].shape)

    def line_jobs(indices):
        jobs = [functools.partial(scatter_step, indices, t)
                for t in range(1, 2 * (n - 1) + 1)]
        jobs.append(functools.partial(gather_start, indices))
        jobs += [functools.partial(gather_step, indices, i) for i in range(1, n)]
        jobs.append(functools.partial(collect, indices))
        return jobs

    def small_job():
        for i in range(1, n):
            gather_small.arrive(line.order(i))
        small_o[...] = jnp.sum(small_all[...], axis=0)

    joint_barrier(line, cube)
    for f in folds:
        f.start()
    share(2, lambda rows: early_out[rows])
    share(3, lambda rows: early_qkv[rows])
    last = folds[0].stages
    jobs = line_jobs((2, 3))

    def after(index):
        fold = folds[index]
        if index == 0:
            small_all[line.z] = fold.mine[0]
            gather_small.start(small_all.at[line.z])
            jobs.append(small_job)
        elif index <= 2:
            share(index - 1, lambda rows: fold.mine[0, rows])
            if index == 2:
                jobs.extend(line_jobs((0, 1)))
        else:
            pltpu.make_async_copy(fold.mine.at[0], dw_o.at[index - 3], write_sem.at[index - 3]).start()

    count = len(folds)
    for t in range(count + last):
        for k in range(last + 1):
            if 0 <= t - k < count:
                folds[t - k].phase(k)
                if k == last:
                    after(t - k)
                for _ in range(2):
                    if jobs and t >= 1:
                        jobs.pop(0)()
    for job in jobs:
        job()
    for k in range(3):
        pltpu.make_async_copy(folds[3 + k].mine.at[0], dw_o.at[k], write_sem.at[k]).wait()
    for f in folds:
        f.finish()
    gather_small.finish()
    for scatter, _, gather, _, _ in shared:
        scatter.finish()
        gather.finish()


def reduce_all(small, out_g, qkv_g, dw, early_out, early_qkv, n):
    owners, shard, d_model = out_g.shape
    width = dw.shape[3]
    qkv_width = qkv_g.shape[2]
    scratch = fold_scratch(owners, small.shape[1], 128, F32)
    scratch += fold_scratch(owners, shard, d_model, BF)
    scratch += fold_scratch(owners, shard, qkv_width, BF)
    for _ in range(3):
        scratch += fold_scratch(owners, shard, width, BF)
    scratch += [pltpu.VMEM((n, small.shape[1], 128), F32)] + gather_sems(n)
    for w in (d_model, qkv_width, d_model, qkv_width):
        scratch += [pltpu.VMEM((n, 1, shard // n, w), BF)] * 3
        scratch += [pltpu.VMEM((n, shard // n, w), BF), pltpu.VMEM((shard // n, w), F32)]
        scratch += scatter_sems(n, 1) + gather_sems(n)
    scratch += [pltpu.SemaphoreType.DMA((3,))]
    return pl.pallas_call(
        functools.partial(reduce_kernel, n, owners),
        out_shape=(
            jax.ShapeDtypeStruct(small.shape[1:], F32),
            jax.ShapeDtypeStruct((shard, d_model), BF),
            jax.ShapeDtypeStruct((shard, qkv_width), BF),
            jax.ShapeDtypeStruct((3, shard, width), BF),
            jax.ShapeDtypeStruct((shard, d_model), BF),
            jax.ShapeDtypeStruct((shard, qkv_width), BF),
        ),
        in_specs=[ANY] * 4 + [VM] * 2,
        out_specs=[VM, VM, VM, ANY, VM, VM],
        scratch_shapes=scratch,
        compiler_params=params(5),
        cost_estimate=pl.CostEstimate(
            flops=1 << 20, transcendentals=0, bytes_accessed=300 << 20),
        name="reduce_all",
    )(small, out_g, qkv_g, dw, early_out, early_qkv)


def normalize(stream, gain):
    return stream * lax.rsqrt(jnp.mean(stream * stream, axis=-1, keepdims=True) + EPSILON) * gain


def normalize_back(grad, stream, gain):
    r = lax.rsqrt(jnp.mean(stream * stream, axis=-1, keepdims=True) + EPSILON)
    u = grad * gain
    back = r * (u - stream * (r * r) * jnp.mean(u * stream, axis=-1, keepdims=True))
    return back, jnp.sum(grad * stream * r, axis=0)


def rotate(heads, cosine, sine):
    half = HEAD // 2
    a, b = heads[..., :half], heads[..., half:]
    return jnp.concatenate([a * cosine - b * sine, b * cosine + a * sine], axis=-1)


def frequencies():
    return jnp.power(ROPE_BASE, -(jnp.arange(HEAD // 2, dtype=F32) * 2.0 / HEAD))


def shards(hidden_in, cotangent, seq_lengths, tile_place, norm_attn, w_qkv, b_qkv, w_out,
           norm_mlp, w_gate, w_up, w_down):
    n = lax.axis_size("context")
    owners = lax.axis_size("fsdp")
    rows, d_model = hidden_in.shape[1:]
    hidden_units = w_gate.shape[2]
    width = -(-hidden_units // 128) * 128
    pad = width - hidden_units
    total = n * rows

    row_index = jnp.arange(total, dtype=jnp.int32)
    tile_order = tile_place[0]
    selector = (
        row_index[:, None] // TILE == jnp.arange(tile_order.shape[0], dtype=jnp.int32)[None, :]
    ).astype(jnp.int32)
    position = jnp.sum(selector * tile_order[None, :], axis=1) * TILE + row_index % TILE
    valid = position < seq_lengths[0]
    offset = lax.axis_index("context") * rows
    my_position = lax.dynamic_slice_in_dim(position, offset, rows)
    my_valid = lax.dynamic_slice_in_dim(valid, offset, rows)
    pos_q = my_position[None, :]
    pos_k = jnp.where(valid, position, 1 << 30)[:, None]
    angles = my_position.astype(F32)[:, None] * frequencies()
    cosine, sine = jnp.cos(angles)[:, None, :], jnp.sin(angles)[:, None, :]

    shard = norm_attn.shape[1]
    bias_shard = b_qkv.shape[1]

    def ffn_shard(l):
        return jnp.stack([
            jnp.pad(m, ((0, 0), (0, pad))) for m in (w_gate[l], w_up[l], w_down[l].T)])

    def packed(parts, lead):
        flat = jnp.concatenate(parts, axis=-1)
        used = flat.shape[-1]
        lines = -(-used // (16 * 128)) * 16
        flat = jnp.pad(flat, ((0, 0),) * (flat.ndim - 1) + ((0, lines * 128 - used),))
        return flat.reshape(lead + (lines, 128))

    small = packed(
        [m.reshape(-1).astype(F32) for m in (norm_attn, norm_mlp, b_qkv)], ())
    first_ffn = ffn_shard(0)
    first_ffn, small = lax.optimization_barrier((first_ffn, small))
    ffn_weights = [lax.all_gather(first_ffn, "fsdp", axis=0, tiled=False)]
    small, qkv_w, out_w = spread_all(owners, small, w_qkv[0], w_out[0])
    qkv_weights = [qkv_w.reshape(d_model, -1)]
    out_weights = [out_w.reshape(Q_WIDTH, d_model)]
    small = small.reshape(owners, -1)
    gains_attn, gains_mlp, biases = [], [], []
    for l in range(LAYERS):
        gains_attn.append(small[:, l * shard:(l + 1) * shard].reshape(-1))
        gains_mlp.append(small[:, (LAYERS + l) * shard:(LAYERS + l + 1) * shard].reshape(-1))
        start = 2 * LAYERS * shard + l * bias_shard
        biases.append(small[:, start:start + bias_shard].reshape(-1))

    stream = hidden_in[0].astype(F32)
    kept = []
    for l in range(LAYERS):
        qkv_w, out_w, ffn_w = qkv_weights[l], out_weights[l], ffn_weights[l]
        if l + 1 < LAYERS:
            ffn_weights.append(lax.all_gather(ffn_shard(l + 1), "fsdp", axis=0, tiled=False))
        normed = normalize(stream, gains_attn[l]).astype(BF)
        projected = jnp.dot(normed, qkv_w, preferred_element_type=F32) + biases[l]
        qk = rotate(
            projected[:, :Q_WIDTH + KV_WIDTH].reshape(rows, QUERY_HEADS + KV_HEADS, HEAD),
            cosine, sine).astype(BF).reshape(rows, Q_WIDTH + KV_WIDTH)
        q = qk[:, :Q_WIDTH]
        kv = jnp.concatenate([qk[:, Q_WIDTH:], projected[:, Q_WIDTH + KV_WIDTH:].astype(BF)], axis=1)
        mixed, lse, kvall = attention_forward(q, kv, pos_q, pos_k, n)
        middle = stream + jnp.dot(mixed, out_w, preferred_element_type=F32)
        normed_two = normalize(middle, gains_mlp[l]).astype(BF)
        if l + 1 < LAYERS:
            xall, gate, up, y, next_qkv, next_out = ffn_forward(
                normed_two, ffn_w, n, (w_qkv[l + 1], w_out[l + 1]))
            qkv_weights.append(next_qkv.reshape(d_model, -1))
            out_weights.append(next_out.reshape(Q_WIDTH, d_model))
        else:
            xall, gate, up, y = ffn_forward(normed_two, ffn_w, n)
        kept.append((stream, normed, q, kvall, lse, mixed, middle, xall, gate, up,
                     qkv_w, out_w, ffn_w))
        stream = middle + y
    layer_out = stream.astype(BF)[None]

    gradient = cotangent[0].astype(F32) * my_valid[:, None].astype(F32)
    small_grads = [None] * LAYERS
    big_grads = [None] * LAYERS
    for l in reversed(range(LAYERS)):
        (stream, normed, q, kvall, lse, mixed, middle, xall, gate, up,
         qkv_w, out_w, ffn_w) = kept[l]
        dw, dx = ffn_backward(gradient.astype(BF), ffn_w, xall, gate, up, n)
        if l < LAYERS - 1:
            out_sum, qkv_sum, dw_sum = big_grads[l + 1]
            dx, dw_sum = lax.optimization_barrier((dx, dw_sum))
        back, gain_two = normalize_back(dx, middle, gains_mlp[l])
        d_middle = gradient + back
        d_low = d_middle.astype(BF)
        d_mixed = jnp.einsum("td,cd->tc", d_low, out_w, preferred_element_type=F32).astype(BF)
        out_grad = jnp.einsum("tc,td->cd", mixed, d_low, preferred_element_type=F32).astype(BF)
        dq, dkv = attention_backward(q, kvall, lse, d_mixed, pos_q, pos_k, n)
        if l < LAYERS - 1:
            dq, out_sum, qkv_sum = lax.optimization_barrier((dq, out_sum, qkv_sum))
            big_grads[l + 1] = (out_sum, qkv_sum, dw_sum)
        d_qk = rotate(
            jnp.concatenate([dq, dkv[:, :KV_WIDTH]], axis=1).reshape(
                rows, QUERY_HEADS + KV_HEADS, HEAD),
            cosine, -sine).reshape(rows, Q_WIDTH + KV_WIDTH)
        d_projected = jnp.concatenate([d_qk, dkv[:, KV_WIDTH:]], axis=1).astype(BF)
        bias_grad = jnp.sum(d_projected.astype(F32), axis=0)
        d_normed = jnp.einsum("tc,dc->td", d_projected, qkv_w, preferred_element_type=F32)
        qkv_grad = jnp.einsum(
            "td,tc->dc", normed, d_projected, preferred_element_type=F32).astype(BF)
        back, gain_one = normalize_back(d_normed, stream, gains_attn[l])
        gradient = d_middle + back
        small_grads[l] = (gain_one, gain_two, bias_grad)
        if l > 0:
            big_grads[l] = (
                lax.psum_scatter(out_grad, "fsdp", scatter_dimension=0, tiled=True),
                lax.psum_scatter(qkv_grad, "fsdp", scatter_dimension=0, tiled=True),
                lax.psum_scatter(dw, "fsdp", scatter_dimension=0, tiled=False))
        else:
            small = packed([
                m.reshape(owners, -1)
                for k in range(3) for m in (small_grads[i][k] for i in range(LAYERS))], (owners,))
            out_early, qkv_early, dw_sum = big_grads[l + 1]
            small, out_sum, qkv_sum, dw_last, out_early, qkv_early = reduce_all(
                small, out_grad.reshape(owners, shard, d_model),
                qkv_grad.reshape(owners, shard, qkv_grad.shape[1]), dw, out_early, qkv_early, n)
            big_grads[l + 1] = (out_early, qkv_early, dw_sum)
            small = small.reshape(-1)
            big_grads[l] = (out_sum, qkv_sum, dw_last)

    grad_norm_attn = small[:LAYERS * shard].reshape(LAYERS, shard)
    grad_norm_mlp = small[LAYERS * shard:2 * LAYERS * shard].reshape(LAYERS, shard)
    start = 2 * LAYERS * shard
    grad_b_qkv = small[start:start + LAYERS * bias_shard].reshape(LAYERS, bias_shard)

    def stacked(pick):
        return jnp.stack([pick(big_grads[l]).astype(F32) for l in range(LAYERS)])

    return (
        layer_out,
        gradient[None],
        grad_norm_attn,
        stacked(lambda m: m[1]),
        grad_b_qkv,
        stacked(lambda m: m[0]),
        grad_norm_mlp,
        stacked(lambda m: m[2][0, :, :hidden_units]),
        stacked(lambda m: m[2][1, :, :hidden_units]),
        stacked(lambda m: m[2][2, :, :hidden_units].T),
    )


def solution(mesh):
    return jax.shard_map(
        shards,
        mesh=mesh,
        in_specs=(
            P("fsdp", "context", None),
            P("fsdp", "context", None),
            P("fsdp"),
            P("fsdp", None),
            P(None, "fsdp"),
            P(None, "fsdp", None),
            P(None, "fsdp"),
            P(None, "fsdp", None),
            P(None, "fsdp"),
            P(None, "fsdp", "context"),
            P(None, "fsdp", "context"),
            P(None, "context", "fsdp"),
        ),
        out_specs=(
            P("fsdp", "context", None),
            P("fsdp", "context", None),
            P(None, "fsdp"),
            P(None, "fsdp", None),
            P(None, "fsdp"),
            P(None, "fsdp", None),
            P(None, "fsdp"),
            P(None, "fsdp", "context"),
            P(None, "fsdp", "context"),
            P(None, "context", "fsdp"),
        ),
        check_vma=False,
    )
```

```python
import functools
import math

import jax
import jax.numpy as jnp
from jax import lax
from jax.experimental import pallas as pl
from jax.experimental.pallas import tpu as pltpu
from jax.sharding import PartitionSpec as P

QUERY_HEADS = 12
KV_HEADS = 2
HEAD = 128
LAYERS = 2
TILE = 128
Q_WIDTH = QUERY_HEADS * HEAD
KV_WIDTH = KV_HEADS * HEAD
PER_GROUP = QUERY_HEADS // KV_HEADS
SCALE = 1.0 / math.sqrt(HEAD)
EPSILON = 1e-06
ROPE_BASE = 1000000.0
BF = jnp.bfloat16
F32 = jnp.float32
MESH = pl.DeviceIdType.MESH
VMEM_LIMIT = 66 * 1024 * 1024
ANY = pl.BlockSpec(memory_space=pl.ANY)
VM = pl.BlockSpec(memory_space=pltpu.VMEM)


def dot_nn(a, b):
    return lax.dot_general(a, b, (((1,), (0,)), ((), ())), preferred_element_type=F32)


def dot_nt(a, b):
    return lax.dot_general(a, b, (((1,), (1,)), ((), ())), preferred_element_type=F32)


def dot_tn(a, b):
    return lax.dot_general(a, b, (((0,), (0,)), ((), ())), preferred_element_type=F32)


def lane_tile(width, most):
    best = 128
    for k in range(1, most // 128 + 1):
        if width % (128 * k) == 0:
            best = 128 * k
    return best


class Line:
    def __init__(self, n):
        self.n = n
        self.z = lax.axis_index("context")
        self.right = lax.rem(self.z + 1, n)
        self.left = lax.rem(self.z + n - 1, n)
        self.has_right = self.z < n - 1
        self.has_left = self.z > 0

    def barrier(self):
        bar = pltpu.get_barrier_semaphore()

        @pl.when(self.has_right)
        def _():
            pl.semaphore_signal(bar, inc=1, device_id={"context": self.right}, device_id_type=MESH)

        @pl.when(self.has_left)
        def _():
            pl.semaphore_signal(bar, inc=1, device_id={"context": self.left}, device_id_type=MESH)

        both = self.has_right & self.has_left

        @pl.when(both)
        def _():
            pl.semaphore_wait(bar, 2)

        @pl.when(jnp.logical_not(both))
        def _():
            pl.semaphore_wait(bar, 1)

    def order(self, i):
        z, n = self.z, self.n
        short = jnp.minimum(z, n - 1 - z)
        j = i - 1
        paired = j < 2 * short
        k = jnp.where(paired, j // 2 + 1, j - short + 1)
        goes_left = jnp.where(paired, lax.rem(j, 2) == 0, z > n - 1 - z)
        return jnp.where(i == 0, z, jnp.where(goes_left, z - k, z + k))


def remote(src, dst, send, recv, target):
    return pltpu.make_async_remote_copy(
        src_ref=src, dst_ref=dst, send_sem=send, recv_sem=recv,
        device_id={"context": target}, device_id_type=MESH,
    )


class Gather:
    def __init__(self, line, slots, send_r, send_l, recv):
        self.line, self.slots = line, slots
        self.send_r, self.send_l, self.recv = send_r, send_l, recv

    def _right(self, b, src):
        return remote(src, self.slots.at[b], self.send_r.at[b], self.recv.at[b], self.line.right)

    def _left(self, b, src):
        return remote(src, self.slots.at[b], self.send_l.at[b], self.recv.at[b], self.line.left)

    def start(self, own):
        line = self.line

        @pl.when(line.has_right)
        def _():
            self._right(line.z, own).start()

        @pl.when(line.has_left)
        def _():
            self._left(line.z, own).start()

    def arrive(self, b):
        line = self.line
        self._right(b, self.slots.at[b]).wait_recv()

        @pl.when((b < line.z) & line.has_right)
        def _():
            self._right(b, self.slots.at[b]).start()

        @pl.when((b > line.z) & line.has_left)
        def _():
            self._left(b, self.slots.at[b]).start()

    def finish(self):
        line = self.line
        for b in range(line.n):
            @pl.when((b <= line.z) & line.has_right)
            def _():
                self._right(b, self.slots.at[b]).wait_send()

            @pl.when((b >= line.z) & line.has_left)
            def _():
                self._left(b, self.slots.at[b]).wait_send()


class Scatter:
    def __init__(self, line, pieces, part, from_left, from_right, send_r, send_l, recv_l, recv_r):
        self.line, self.pieces, self.part = line, pieces, part
        self.from_left, self.from_right = from_left, from_right
        self.send_r, self.send_l, self.recv_l, self.recv_r = send_r, send_l, recv_l, recv_r

    def _right(self, b, p):
        return remote(self.part.at[b, p], self.from_left.at[b, p], self.send_r.at[b, p],
                      self.recv_l.at[b, p], self.line.right)

    def _left(self, b, p):
        return remote(self.part.at[b, p], self.from_right.at[b, p], self.send_l.at[b, p],
                      self.recv_r.at[b, p], self.line.left)

    def computed(self, b, p):
        line = self.line

        @pl.when((line.z == 0) & (b > 0))
        def _():
            self._right(b, p).start()

        @pl.when((line.z == line.n - 1) & (b < line.n - 1))
        def _():
            self._left(b, p).start()

    def steps(self):
        return range(1, 2 * (self.line.n - 1) + 1)

    def step(self, t, add_own):
        line = self.line
        n, z = line.n, line.z
        b_left = t - z

        @pl.when(line.has_left & (b_left >= z) & (b_left < n))
        def _():
            for p in range(self.pieces):
                self._right(b_left, p).wait_recv()

                @pl.when(b_left == z)
                def _():
                    add_own(p, self.from_left[b_left, p].astype(F32))

                @pl.when(b_left != z)
                def _():
                    self.part[b_left, p] = (
                        self.part[b_left, p].astype(F32) + self.from_left[b_left, p].astype(F32)
                    ).astype(BF)
                    self._right(b_left, p).start()

        b_right = 2 * (n - 1) - t - z

        @pl.when(line.has_right & (b_right >= 0) & (b_right <= z))
        def _():
            for p in range(self.pieces):
                self._left(b_right, p).wait_recv()

                @pl.when(b_right == z)
                def _():
                    add_own(p, self.from_right[b_right, p].astype(F32))

                @pl.when(b_right != z)
                def _():
                    self.part[b_right, p] = (
                        self.part[b_right, p].astype(F32) + self.from_right[b_right, p].astype(F32)
                    ).astype(BF)
                    self._left(b_right, p).start()

    def finish(self):
        line = self.line
        for b in range(line.n):
            @pl.when((b > line.z) & line.has_right)
            def _():
                for p in range(self.pieces):
                    self._right(b, p).wait_send()

            @pl.when((b < line.z) & line.has_left)
            def _():
                for p in range(self.pieces):
                    self._left(b, p).wait_send()


def gather_sems(n):
    return [pltpu.SemaphoreType.DMA((n,))] * 3


def scatter_sems(n, pieces):
    return [pltpu.SemaphoreType.DMA((n, pieces))] * 4


def params(cid):
    return pltpu.CompilerParams(
        collective_id=cid, has_side_effects=True, vmem_limit_bytes=VMEM_LIMIT
    )


def bits_of(owners):
    return [1 << i for i in range(owners.bit_length() - 1)]


class Cube:
    def __init__(self, owners):
        self.owners = owners
        self.me = lax.axis_index("fsdp")
        self.bits = bits_of(owners)
        self.chip_bits = [b // 2 for b in self.bits[1:]]
        self.chips = owners // 2

    def flip(self, mask):
        index = self.me
        for b in self.bits:
            if mask & b:
                index = index + b - 2 * b * lax.rem(self.me // b, 2)
        return index

    def signal(self, bar):
        for b in self.bits:
            pl.semaphore_signal(bar, inc=1, device_id={"fsdp": self.flip(b)}, device_id_type=MESH)

    def order(self, half):
        return self.chip_bits[::-1] if half == 0 else self.chip_bits

    def plan(self):
        steps = {}
        for half in (0, 1):
            order, slot = self.order(half), 0
            for stage, bit in enumerate(order):
                rest = [0]
                for other in order[stage + 1:]:
                    rest = rest + [m | other for m in rest]
                steps[half, stage] = (bit, rest, slot)
                slot += len(rest)
        return steps


def joint_barrier(line, cube):
    bar = pltpu.get_barrier_semaphore()
    cube.signal(bar)
    peers = len(cube.bits)

    @pl.when(line.has_right)
    def _():
        pl.semaphore_signal(bar, inc=1, device_id={"context": line.right}, device_id_type=MESH)

    @pl.when(line.has_left)
    def _():
        pl.semaphore_signal(bar, inc=1, device_id={"context": line.left}, device_id_type=MESH)

    both = line.has_right & line.has_left

    @pl.when(both)
    def _():
        pl.semaphore_wait(bar, peers + 2)

    @pl.when(jnp.logical_not(both))
    def _():
        pl.semaphore_wait(bar, peers + 1)


class Spread:
    def __init__(self, cube, own, full, own_sem, send, recv, core_send, core_recv):
        self.cube, self.own, self.full = cube, own, full
        self.own_sem, self.send, self.recv = own_sem, send, recv
        self.core_send, self.core_recv = core_send, core_recv
        self.half = own.shape[0] // 2
        self.stages = len(cube.chip_bits)

    def _rows(self, half):
        return pl.ds(half * self.half, self.half)

    def _block(self, half, mask):
        return self.full.at[self.cube.flip(mask), self._rows(half)]

    def _source(self, half, mask):
        return self._block(half, 2 * mask) if mask else self.own.at[self._rows(half)]

    def _masks(self, half, stage):
        masks = [0]
        for bit in self.cube.order(half)[:stage]:
            masks = masks + [m | bit for m in masks]
        return masks

    def _hop(self, half, stage, mask):
        bit = self.cube.order(half)[stage]
        return pltpu.make_async_remote_copy(
            src_ref=self._source(half, mask), dst_ref=self._block(half, 2 * mask),
            send_sem=self.send.at[half, mask | bit], recv_sem=self.recv.at[half, mask | bit],
            device_id={"fsdp": self.cube.flip(2 * bit)}, device_id_type=MESH)

    def _arrival(self, half, mask):
        block = self._block(half, 2 * mask)
        return pltpu.make_async_remote_copy(
            src_ref=block, dst_ref=block,
            send_sem=self.send.at[half, mask], recv_sem=self.recv.at[half, mask],
            device_id={"fsdp": self.cube.flip(1)}, device_id_type=MESH)

    def _core(self, half, mask):
        return pltpu.make_async_remote_copy(
            src_ref=self._source(half, mask), dst_ref=self._block(half, 2 * mask),
            send_sem=self.core_send.at[half, mask], recv_sem=self.core_recv.at[half, mask],
            device_id={"fsdp": self.cube.flip(1)}, device_id_type=MESH)

    def _core_arrival(self, half, mask):
        block = self._block(half, 2 * mask | 1)
        return pltpu.make_async_remote_copy(
            src_ref=block, dst_ref=block,
            send_sem=self.core_send.at[half, mask], recv_sem=self.core_recv.at[half, mask],
            device_id={"fsdp": self.cube.flip(1)}, device_id_type=MESH)

    def _own_copy(self):
        return pltpu.make_async_copy(self.own, self.full.at[self.cube.me], self.own_sem)

    def start(self):
        for stage in range(self.stages):
            for half in (0, 1):
                self._hop(half, stage, 0).start()
        for half in (0, 1):
            self._core(half, 0).start()
        self._own_copy().start()

    def phase(self, k):
        for half in (0, 1):
            bit = self.cube.order(half)[k - 1]
            for m in self._masks(half, k - 1):
                self._arrival(half, m | bit).wait_recv()
                for stage in range(k, self.stages):
                    self._hop(half, stage, m | bit).start()
                self._core(half, m | bit).start()

    def finish(self):
        self._own_copy().wait()
        for half in (0, 1):
            for m in range(self.cube.chips):
                self._core_arrival(half, m).wait_recv()
                self._core(half, m).wait_send()
            for stage in range(self.stages):
                for m in self._masks(half, stage):
                    self._hop(half, stage, m).wait_send()


SPREAD_SEMS = 5


def spread_sems(owners):
    chips = owners // 2
    return [pltpu.SemaphoreType.DMA] + [pltpu.SemaphoreType.DMA((2, chips))] * 4


def spread_shapes(owners, shards):
    return tuple(jax.ShapeDtypeStruct((owners,) + m.shape, m.dtype) for m in shards)


def spread_kernel(owners, count, *refs):
    cube = Cube(owners)
    spreads = [
        Spread(cube, refs[i], refs[count + i],
               *refs[2 * count + SPREAD_SEMS * i:2 * count + SPREAD_SEMS * (i + 1)])
        for i in range(count)]
    bar = pltpu.get_barrier_semaphore()
    cube.signal(bar)
    pl.semaphore_wait(bar, len(cube.bits))
    for s in spreads:
        s.start()
    for k in range(1, len(cube.chip_bits) + 1):
        for s in spreads:
            s.phase(k)
    for s in spreads:
        s.finish()


def spread_all(owners, *shards):
    count = len(shards)
    return pl.pallas_call(
        functools.partial(spread_kernel, owners, count),
        out_shape=spread_shapes(owners, shards),
        in_specs=[VM] * count,
        out_specs=[ANY] * count,
        scratch_shapes=spread_sems(owners) * count,
        compiler_params=params(6),
        cost_estimate=pl.CostEstimate(
            flops=1 << 20, transcendentals=0, bytes_accessed=150 << 20),
        name="spread_all",
    )(*shards)


def ffn_forward_kernel(n, pieces, count, *refs):
    x_ref, w_ref = refs[:2]
    next_own = refs[2:2 + count]
    xall_ref, gate_ref, up_ref, y_ref = refs[2 + count:6 + count]
    next_full = refs[6 + count:6 + 2 * count]
    (w_v, xbuf, gbuf, ubuf, hbuf, part, from_l, from_r,
     w_sem, x_sem, out_sem, *sems) = refs[6 + 2 * count:]
    line = Line(n)
    z = line.z
    owners, _, rows, width = w_ref.shape
    d_model = x_ref.shape[1]
    tile = lane_tile(width, 256)
    piece = d_model // pieces
    gather = Gather(line, xbuf, *sems[:3])
    scatter = Scatter(line, pieces, part, from_l, from_r, *sems[3:7])
    spreads = []
    stages = 0
    if count:
        cube = Cube(owners)
        stages = len(cube.chip_bits)
        for i in range(count):
            at = 7 + SPREAD_SEMS * i
            spreads.append(Spread(cube, next_own[i], next_full[i], *sems[at:at + SPREAD_SEMS]))

    def w_copy(k, f):
        return pltpu.make_async_copy(
            w_ref.at[f, k], w_v.at[k, pl.ds(f * rows, rows)], w_sem.at[k, f]
        )

    def x_out(b):
        return pltpu.make_async_copy(xbuf.at[b], xall_ref.at[b], x_sem.at[b])

    if count:
        joint_barrier(line, cube)
    else:
        line.barrier()
    gather.start(x_ref)
    for s in spreads:
        s.start()
    for k in range(3):
        for f in range(owners):
            w_copy(k, f).start()
    xbuf[z] = x_ref[...]
    for k in range(3):
        for f in range(owners):
            w_copy(k, f).wait()

    @pl.loop(0, n)
    def _(i):
        b = line.order(i)

        @pl.when(i > 0)
        def _():
            gather.arrive(b)

        x_out(b).start()
        slot = lax.rem(i, 2)
        g_copy = pltpu.make_async_copy(gbuf.at[slot], gate_ref.at[b], out_sem.at[0, slot])
        u_copy = pltpu.make_async_copy(ubuf.at[slot], up_ref.at[b], out_sem.at[1, slot])

        @pl.when(i > 1)
        def _():
            g_copy.wait()
            u_copy.wait()

        @pl.loop(0, width // tile)
        def _(j):
            cols = pl.ds(pl.multiple_of(j * tile, tile), tile)
            xb = xbuf[b]
            gate = dot_nn(xb, w_v[0, :, cols])
            up = dot_nn(xb, w_v[1, :, cols])
            gbuf[slot, :, cols] = gate.astype(BF)
            ubuf[slot, :, cols] = up.astype(BF)
            hbuf[:, cols] = (gate * jax.nn.sigmoid(gate) * up).astype(BF)

        g_copy.start()
        u_copy.start()
        for p in range(pieces):
            out = dot_nt(hbuf[...], w_v[2, pl.ds(p * piece, piece)])

            @pl.when(b == z)
            def _():
                y_ref[:, p * piece:(p + 1) * piece] = out

            @pl.when(b != z)
            def _():
                part[b, p] = out.astype(BF)

            scatter.computed(b, p)

        if spreads:
            @pl.when(i == n // 2)
            def _():
                for s in spreads:
                    s.phase(1)

    def add_own(p, value):
        cols = slice(p * piece, (p + 1) * piece)
        y_ref[:, cols] = y_ref[:, cols] + value

    passed = 2
    for t in scatter.steps():
        scatter.step(t, add_own)
        if t >= 4 and t % 2 == 0 and passed <= stages:
            for s in spreads:
                s.phase(passed)
            passed += 1
    for k in range(passed, stages + 1):
        for s in spreads:
            s.phase(k)
    for i in range(max(0, n - 2), n):
        slot = i % 2
        pltpu.make_async_copy(gbuf.at[slot], gate_ref.at[0], out_sem.at[0, slot]).wait()
        pltpu.make_async_copy(ubuf.at[slot], up_ref.at[0], out_sem.at[1, slot]).wait()
    for b in range(n):
        x_out(b).wait()
    gather.finish()
    scatter.finish()
    for s in spreads:
        s.finish()


def ffn_forward(x, w, n, following=()):
    rows, d_model = x.shape
    owners, _, shard, width = w.shape
    pieces = 3
    piece = d_model // pieces
    count = len(following)
    return pl.pallas_call(
        functools.partial(ffn_forward_kernel, n, pieces, count),
        out_shape=(
            jax.ShapeDtypeStruct((n, rows, d_model), BF),
            jax.ShapeDtypeStruct((n, rows, width), BF),
            jax.ShapeDtypeStruct((n, rows, width), BF),
            jax.ShapeDtypeStruct((rows, d_model), F32),
        ) + spread_shapes(owners, following),
        in_specs=[VM, ANY] + [VM] * count,
        out_specs=[ANY, ANY, ANY, VM] + [ANY] * count,
        scratch_shapes=[
            pltpu.VMEM((3, d_model, width), BF),
            pltpu.VMEM((n, rows, d_model), BF),
            pltpu.VMEM((2, rows, width), BF),
            pltpu.VMEM((2, rows, width), BF),
            pltpu.VMEM((rows, width), BF),
            pltpu.VMEM((n, pieces, rows, piece), BF),
            pltpu.VMEM((n, pieces, rows, piece), BF),
            pltpu.VMEM((n, pieces, rows, piece), BF),
            pltpu.SemaphoreType.DMA((3, owners)),
            pltpu.SemaphoreType.DMA((n,)),
            pltpu.SemaphoreType.DMA((2, 2)),
        ] + gather_sems(n) + scatter_sems(n, pieces) + spread_sems(owners) * count,
        compiler_params=params(7 if count else 1),
        cost_estimate=pl.CostEstimate(
            flops=6 * n * rows * d_model * width, transcendentals=n * rows * width,
            bytes_accessed=60 << 20),
        name="ffn_forward",
    )(x, w, *following)


def ffn_backward_kernel(n, pieces, groups, g_ref, w_ref, xall_ref, gate_ref, up_ref,
                        dw_ref, dwd_ref, dx_ref,
                        w_v, gbuf, xv, gate_v, up_v, hid_v, part, from_l, from_r, stage,
                        w_sem, in_sem, out_sem, *sems):
    line = Line(n)
    z = line.z
    owners, _, shard, width = w_ref.shape
    rows, d_model = g_ref.shape
    tile = lane_tile(width, 256)
    piece = d_model // pieces
    gather = Gather(line, gbuf, *sems[:3])
    scatter = Scatter(line, pieces, part, from_l, from_r, *sems[3:])

    def w_copy(k, f):
        return pltpu.make_async_copy(
            w_ref.at[f, k], w_v.at[k, pl.ds(f * shard, shard)], w_sem.at[k, f]
        )

    def loads(b):
        return (
            pltpu.make_async_copy(gate_ref.at[b], gate_v.at[b], in_sem.at[0, b]),
            pltpu.make_async_copy(up_ref.at[b], up_v.at[b], in_sem.at[1, b]),
        )

    def x_load(b):
        return pltpu.make_async_copy(xall_ref.at[b], xv.at[b], in_sem.at[2, b])

    line.barrier()
    gather.start(g_ref)
    for f in range(owners):
        w_copy(2, f).start()
    for c in loads(z):
        c.start()
    for k in range(2):
        for f in range(owners):
            w_copy(k, f).start()
    for b in range(n):
        @pl.when(b != z)
        def _():
            for c in loads(b):
                c.start()
    for b in range(n):
        x_load(b).start()
    gbuf[z] = g_ref[...]
    for k in (2, 0, 1):
        for f in range(owners):
            w_copy(k, f).wait()

    @pl.loop(0, n)
    def _(i):
        b = line.order(i)

        @pl.when(i > 0)
        def _():
            gather.arrive(b)

        for c in loads(b):
            c.wait()

        @pl.loop(0, width // tile)
        def _(j):
            cols = pl.ds(pl.multiple_of(j * tile, tile), tile)
            d_hidden = dot_nn(gbuf[b], w_v[2, :, cols])
            gate = gate_v[b, :, cols].astype(F32)
            up = up_v[b, :, cols].astype(F32)
            sig = jax.nn.sigmoid(gate)
            act = gate * sig
            hid_v[b, :, cols] = (act * up).astype(BF)
            gate_v[b, :, cols] = (d_hidden * up * (sig + act * (1.0 - sig))).astype(BF)
            up_v[b, :, cols] = (d_hidden * act).astype(BF)

        for p in range(pieces):
            sl = pl.ds(p * piece, piece)
            out = dot_nt(gate_v[b], w_v[0, sl]) + dot_nt(up_v[b], w_v[1, sl])

            @pl.when(b == z)
            def _():
                dx_ref[:, p * piece:(p + 1) * piece] = out

            @pl.when(b != z)
            def _():
                part[b, p] = out.astype(BF)

            scatter.computed(b, p)

    def add_own(p, value):
        cols = slice(p * piece, (p + 1) * piece)
        dx_ref[:, cols] = dx_ref[:, cols] + value

    for b in range(n):
        x_load(b).wait()

    group = d_model // groups
    per = group // shard

    def dw_copies(k, q, slot):
        def target(owner):
            return dw_ref.at[owner, k] if k < 2 else dwd_ref.at[owner]

        return [
            pltpu.make_async_copy(
                stage.at[slot, pl.ds(s * shard, shard)], target(q * per + s), out_sem.at[slot, s])
            for s in range(per)
        ]

    def weight_unit(unit):
        k, q = unit // groups, unit % groups
        slot = unit % 2
        left = (xv, xv, gbuf)[k]
        right = (gate_v, up_v, hid_v)[k]
        if unit >= 2:
            for c in dw_copies((unit - 2) // groups, (unit - 2) % groups, slot):
                c.wait()
        lt = left[:, :, q * group:(q + 1) * group].reshape(n * rows, group)

        @pl.loop(0, width // tile)
        def _(j):
            cols = pl.ds(pl.multiple_of(j * tile, tile), tile)
            stage[slot, :, cols] = dot_tn(
                lt, right[:, :, cols].reshape(n * rows, tile)
            ).astype(BF)

        for c in dw_copies(k, q, slot):
            c.start()

    units = 3 * groups
    steps = list(scatter.steps())
    done = 0
    for index, t in enumerate(steps):
        scatter.step(t, add_own)
        until = units * (index + 1) // len(steps)
        while done < until:
            weight_unit(done)
            done += 1
    for unit in range(units - 2, units):
        for c in dw_copies(unit // groups, unit % groups, unit % 2):
            c.wait()
    gather.finish()
    scatter.finish()


def ffn_backward(g, w, xall, gate, up, n):
    rows, d_model = g.shape
    owners, _, shard, width = w.shape
    pieces, groups = 3, 4
    piece = d_model // pieces
    per = d_model // groups // shard
    return pl.pallas_call(
        functools.partial(ffn_backward_kernel, n, pieces, groups),
        out_shape=(
            jax.ShapeDtypeStruct((owners, 2, shard, width), BF),
            jax.ShapeDtypeStruct((owners, shard, width), BF),
            jax.ShapeDtypeStruct((rows, d_model), F32),
        ),
        in_specs=[VM, ANY, ANY, ANY, ANY],
        out_specs=[ANY, ANY, VM],
        scratch_shapes=[
            pltpu.VMEM((3, d_model, width), BF),
            pltpu.VMEM((n, rows, d_model), BF),
            pltpu.VMEM((n, rows, d_model), BF),
            pltpu.VMEM((n, rows, width), BF),
            pltpu.VMEM((n, rows, width), BF),
            pltpu.VMEM((n, rows, width), BF),
            pltpu.VMEM((n, pieces, rows, piece), BF),
            pltpu.VMEM((n, pieces, rows, piece), BF),
            pltpu.VMEM((n, pieces, rows, piece), BF),
            pltpu.VMEM((2, d_model // groups, width), BF),
            pltpu.SemaphoreType.DMA((3, owners)),
            pltpu.SemaphoreType.DMA((3, n)),
            pltpu.SemaphoreType.DMA((2, per)),
        ] + gather_sems(n) + scatter_sems(n, pieces),
        compiler_params=params(2),
        cost_estimate=pl.CostEstimate(
            flops=12 * n * rows * d_model * width, transcendentals=n * rows * width,
            bytes_accessed=100 << 20),
        name="ffn_backward",
    )(g, w, xall, gate, up)


class Fold:
    def __init__(self, cube, src, mine, first, later, load_sem, send1, recv1, send2, recv2):
        self.cube, self.src = cube, src
        self.mine, self.first, self.later = mine, first, later
        self.load_sem, self.send1, self.recv1 = load_sem, send1, recv1
        self.send2, self.recv2 = send2, recv2
        self.rows = mine.shape[1]
        self.half = self.rows // 2
        self.steps = cube.plan()
        self.stages = len(cube.chip_bits)

    def _load(self, d):
        return pltpu.make_async_copy(
            self.src(self.cube.flip(2 * d)), self.mine.at[d], self.load_sem.at[d])

    def _core(self, d):
        return pltpu.make_async_remote_copy(
            src_ref=self.src(self.cube.flip(2 * d | 1)), dst_ref=self.first.at[d],
            send_sem=self.send1.at[d], recv_sem=self.recv1.at[d],
            device_id={"fsdp": self.cube.flip(1)}, device_id_type=MESH)

    def _hop(self, half, stage, index):
        bit, rest, slot = self.steps[half, stage]
        rows = pl.ds(half * self.half, self.half)
        return pltpu.make_async_remote_copy(
            src_ref=self.mine.at[bit | rest[index], rows],
            dst_ref=self.later.at[half, slot + index],
            send_sem=self.send2.at[half, slot + index],
            recv_sem=self.recv2.at[half, slot + index],
            device_id={"fsdp": self.cube.flip(2 * bit)}, device_id_type=MESH)

    def _hops(self, stage):
        return [self._hop(half, stage, i)
                for half in (0, 1) for i in range(len(self.steps[half, stage][1]))]

    def _add(self, d, base, size, other):
        dtype = self.mine.dtype
        strip = 48 if size % 48 == 0 else size

        @pl.loop(0, size // strip)
        def _(i):
            into = pl.ds(pl.multiple_of(base + i * strip, 8), strip)
            rows = pl.ds(pl.multiple_of(i * strip, 8), strip)
            self.mine[d, into] = (
                self.mine[d, into].astype(F32) + other(rows).astype(F32)).astype(dtype)

    def start(self):
        for d in range(self.cube.chips):
            self._core(d).start()
        for d in range(self.cube.chips):
            self._load(d).start()

    def phase(self, k):
        if k == 0:
            for d in range(self.cube.chips):
                self._load(d).wait()
                self._core(d).wait_recv()
                self._add(d, 0, self.rows, lambda rows, d=d: self.first[d, rows])
        else:
            for half in (0, 1):
                _, rest, slot = self.steps[half, k - 1]
                for i, e in enumerate(rest):
                    self._hop(half, k - 1, i).wait_recv()
                    self._add(e, half * self.half, self.half,
                              lambda rows, h=half, j=slot + i: self.later[h, j, rows])
        if k < self.stages:
            for c in self._hops(k):
                c.start()

    def finish(self):
        for d in range(self.cube.chips):
            self._core(d).wait_send()
        for stage in range(self.stages):
            for c in self._hops(stage):
                c.wait_send()


def fold_scratch(owners, rows, width, dtype):
    chips = owners // 2
    return [
        pltpu.VMEM((chips, rows, width), dtype),
        pltpu.VMEM((chips, rows, width), dtype),
        pltpu.VMEM((2, chips - 1, rows // 2, width), dtype),
        pltpu.SemaphoreType.DMA((chips,)),
        pltpu.SemaphoreType.DMA((chips,)),
        pltpu.SemaphoreType.DMA((chips,)),
        pltpu.SemaphoreType.DMA((2, chips - 1)),
        pltpu.SemaphoreType.DMA((2, chips - 1)),
    ]


FOLD_REFS = 8


def attention_forward_kernel(n, q_ref, kv_ref, pq_ref, pk_ref, mixed_ref, lse_ref, kvall_ref,
                             kvbuf, vt, *sems):
    line = Line(n)
    z = line.z
    rows = q_ref.shape[0]
    total = n * rows
    gather = Gather(line, kvbuf, *sems)
    line.barrier()
    gather.start(kv_ref)
    kvbuf[z] = kv_ref[...]
    for i in range(1, n):
        gather.arrive(line.order(i))
    kvall_ref[...] = kvbuf[...]
    allowed = pk_ref[...] <= pq_ref[...]
    for g in range(KV_HEADS):
        v = kvbuf[:, :, KV_WIDTH + g * HEAD:KV_WIDTH + (g + 1) * HEAD].reshape(total, HEAD)
        vt[g] = v.T
    for g in range(KV_HEADS):
        for r in range(PER_GROUP):
            h = g * PER_GROUP + r
            k = kvbuf[:, :, g * HEAD:(g + 1) * HEAD].reshape(total, HEAD)
            s = dot_nt(k, q_ref[:, h * HEAD:(h + 1) * HEAD]) * SCALE
            s = jnp.where(allowed, s, -1e30)
            top = jnp.max(s, axis=0, keepdims=True)
            e = jnp.exp(s - top)
            den = jnp.sum(e, axis=0, keepdims=True)
            o = dot_nn(vt[g], e.astype(BF)) / den
            mixed_ref[:, h * HEAD:(h + 1) * HEAD] = o.T.astype(BF)
            lse_ref[h:h + 1, :] = top + jnp.log(den)
    gather.finish()


def attention_forward(q, kv, pos_q, pos_k, n):
    rows = q.shape[0]
    return pl.pallas_call(
        functools.partial(attention_forward_kernel, n),
        out_shape=(
            jax.ShapeDtypeStruct((rows, Q_WIDTH), BF),
            jax.ShapeDtypeStruct((16, rows), F32),
            jax.ShapeDtypeStruct((n, rows, 2 * KV_WIDTH), BF),
        ),
        in_specs=[VM] * 4,
        out_specs=[VM] * 3,
        scratch_shapes=[
            pltpu.VMEM((n, rows, 2 * KV_WIDTH), BF),
            pltpu.VMEM((KV_HEADS, HEAD, n * rows), BF),
        ] + gather_sems(n),
        compiler_params=params(3),
        cost_estimate=pl.CostEstimate(
            flops=4 * n * rows * rows * Q_WIDTH, transcendentals=n * rows * rows * QUERY_HEADS,
            bytes_accessed=16 << 20),
        name="attention_forward",
    )(q, kv, pos_q, pos_k)


def attention_backward_kernel(n, owners, q_ref, kvall_ref, lse_ref, dm_ref, pq_ref, pk_ref,
                              grad_ref, dq_ref, dkv_ref, sum_ref,
                              kt, dk_acc, dv_acc, part, from_l, from_r, *refs):
    fold_refs, sems = refs[:FOLD_REFS], refs[FOLD_REFS:]
    line = Line(n)
    cube = Cube(owners)
    fold = Fold(cube, lambda q: grad_ref.at[q], *fold_refs)
    z = line.z
    rows = q_ref.shape[0]
    total = n * rows
    pieces = KV_HEADS
    scatter = Scatter(line, pieces, part, from_l, from_r, *sems)
    joint_barrier(line, cube)
    fold.start()
    allowed = pk_ref[...] <= pq_ref[...]
    for g in range(KV_HEADS):
        k = kvall_ref[:, :, g * HEAD:(g + 1) * HEAD].reshape(total, HEAD)
        kt[g] = k.T
    for g in range(KV_HEADS):
        for r in range(PER_GROUP):
            h = g * PER_GROUP + r
            cols = slice(h * HEAD, (h + 1) * HEAD)
            k = kvall_ref[:, :, g * HEAD:(g + 1) * HEAD].reshape(total, HEAD)
            v = kvall_ref[:, :, KV_WIDTH + g * HEAD:KV_WIDTH + (g + 1) * HEAD].reshape(total, HEAD)
            q = q_ref[:, cols]
            dm = dm_ref[:, cols]
            s = dot_nt(k, q) * SCALE
            pr = jnp.where(allowed, jnp.exp(s - lse_ref[h:h + 1, :]), 0.0)
            dp = dot_nt(v, dm)
            delta = jnp.sum(pr * dp, axis=0, keepdims=True)
            ds = (pr * (dp - delta) * SCALE).astype(BF)
            dv = dot_nn(pr.astype(BF), dm)
            dk = dot_nn(ds, q)
            if r == 0:
                dk_acc[...] = dk
                dv_acc[...] = dv
            else:
                dk_acc[...] += dk
                dv_acc[...] += dv
            dq_ref[:, cols] = dot_nn(kt[g], ds).T
            if h == 1:
                fold.phase(0)
            if h == 8:
                fold.phase(1)
        for b in range(n):
            sl = slice(b * rows, (b + 1) * rows)

            @pl.when(b == z)
            def _():
                dkv_ref[:, g * HEAD:(g + 1) * HEAD] = dk_acc[sl]
                dkv_ref[:, KV_WIDTH + g * HEAD:KV_WIDTH + (g + 1) * HEAD] = dv_acc[sl]

            @pl.when(b != z)
            def _():
                part[b, g, :, 0:HEAD] = dk_acc[sl].astype(BF)
                part[b, g, :, HEAD:2 * HEAD] = dv_acc[sl].astype(BF)

            scatter.computed(b, g)

    def add_own(p, value):
        a = slice(p * HEAD, (p + 1) * HEAD)
        c = slice(KV_WIDTH + p * HEAD, KV_WIDTH + (p + 1) * HEAD)
        dkv_ref[:, a] = dkv_ref[:, a] + value[:, :HEAD]
        dkv_ref[:, c] = dkv_ref[:, c] + value[:, HEAD:]

    for t in scatter.steps():
        scatter.step(t, add_own)
    for k in range(2, fold.stages + 1):
        fold.phase(k)
    sum_ref[...] = fold.mine[0]
    scatter.finish()
    fold.finish()


def attention_backward(q, kvall, lse, dm, pos_q, pos_k, grad, n):
    rows = q.shape[0]
    owners, shard, d_model = grad.shape
    return pl.pallas_call(
        functools.partial(attention_backward_kernel, n, owners),
        out_shape=(
            jax.ShapeDtypeStruct((rows, Q_WIDTH), F32),
            jax.ShapeDtypeStruct((rows, 2 * KV_WIDTH), F32),
            jax.ShapeDtypeStruct((shard, d_model), BF),
        ),
        in_specs=[VM] * 6 + [ANY],
        out_specs=[VM] * 3,
        scratch_shapes=[
            pltpu.VMEM((KV_HEADS, HEAD, n * rows), BF),
            pltpu.VMEM((n * rows, HEAD), F32),
            pltpu.VMEM((n * rows, HEAD), F32),
        ] + [pltpu.VMEM((n, KV_HEADS, rows, 2 * HEAD), BF)] * 3
        + fold_scratch(owners, shard, d_model, BF) + scatter_sems(n, KV_HEADS),
        compiler_params=params(4),
        cost_estimate=pl.CostEstimate(
            flops=10 * n * rows * rows * Q_WIDTH, transcendentals=n * rows * rows * QUERY_HEADS,
            bytes_accessed=16 << 20),
        name="attention_backward",
    )(q, kvall, lse, dm, pos_q, pos_k, grad)


def reduce_kernel(n, owners, count, small_ref, qkv_ref, dw_ref, *refs):
    early = refs[:count]
    small_o, qkv_o, dw_o = refs[count:count + 3]
    targets = (qkv_o,) + refs[count + 3:2 * count + 3]
    refs = refs[2 * count + 3:]
    line = Line(n)
    cube = Cube(owners)
    refs = list(refs)

    def take(count):
        taken = refs[:count]
        del refs[:count]
        return taken

    sources = [
        lambda q: small_ref.at[q],
        lambda q: qkv_ref.at[q],
        lambda q: dw_ref.at[q],
    ]
    folds = [Fold(cube, src, *take(FOLD_REFS)) for src in sources]
    small_all, = take(1)
    gather_small = Gather(line, small_all, *take(3))
    shared = []
    for _ in targets:
        part, from_l, from_r, total, own = take(5)
        shared.append((Scatter(line, 1, part, from_l, from_r, *take(4)), part,
                       Gather(line, total, *take(3)), total, own))
    write_sem, = take(1)

    def share(index, value):
        scatter, part, _, _, own = shared[index]
        rows = part.shape[2]
        for b in range(n):
            @pl.when(b == line.z)
            def _():
                own[...] = value(slice(b * rows, (b + 1) * rows)).astype(F32)

            @pl.when(b != line.z)
            def _():
                part[b, 0] = value(slice(b * rows, (b + 1) * rows))

            scatter.computed(b, 0)

    def scatter_step(indices, t):
        for index in indices:
            scatter, _, _, _, own = shared[index]

            def add_own(p, value):
                own[...] = own[...] + value

            scatter.step(t, add_own)

    def gather_start(indices):
        for index in indices:
            _, _, gather, total, own = shared[index]
            total[line.z] = own[...].astype(BF)
            gather.start(total.at[line.z])

    def gather_step(indices, i):
        for index in indices:
            shared[index][2].arrive(line.order(i))

    def collect(indices):
        for index in indices:
            targets[index][...] = shared[index][3][...].reshape(targets[index].shape)

    def line_jobs(indices):
        jobs = [functools.partial(scatter_step, indices, t)
                for t in range(1, 2 * (n - 1) + 1)]
        jobs.append(functools.partial(gather_start, indices))
        jobs += [functools.partial(gather_step, indices, i) for i in range(1, n)]
        jobs.append(functools.partial(collect, indices))
        return jobs

    def small_job():
        for i in range(1, n):
            gather_small.arrive(line.order(i))
        small_o[...] = jnp.sum(small_all[...], axis=0)

    joint_barrier(line, cube)
    for f in folds:
        f.start()
    for i, ref in enumerate(early):
        share(1 + i, lambda rows, ref=ref: ref[rows])
    last = folds[0].stages
    jobs = line_jobs(range(1, 1 + count))

    def after(index):
        fold = folds[index]
        if index == 0:
            small_all[line.z] = fold.mine[0]
            gather_small.start(small_all.at[line.z])
            jobs.append(small_job)
        elif index == 1:
            share(0, lambda rows: fold.mine[0, rows])
            jobs.extend(line_jobs((0,)))
        else:
            pltpu.make_async_copy(fold.mine.at[0], dw_o, write_sem).start()

    for t in range(len(folds) + last):
        for k in range(last + 1):
            if 0 <= t - k < len(folds):
                folds[t - k].phase(k)
                if k == last:
                    after(t - k)
                for _ in range(3):
                    if jobs and t >= 1:
                        jobs.pop(0)()
    for job in jobs:
        job()
    pltpu.make_async_copy(folds[2].mine.at[0], dw_o, write_sem).wait()
    for f in folds:
        f.finish()
    gather_small.finish()
    for scatter, _, gather, _, _ in shared:
        scatter.finish()
        gather.finish()


def reduce_all(small, qkv_g, dw, early, n):
    owners, shard, qkv_width = qkv_g.shape
    width = dw.shape[2]
    scratch = fold_scratch(owners, small.shape[1], 128, F32)
    scratch += fold_scratch(owners, shard, qkv_width, BF)
    scratch += fold_scratch(owners, shard, width, BF)
    scratch += [pltpu.VMEM((n, small.shape[1], 128), F32)] + gather_sems(n)
    for w in [qkv_width] + [m.shape[1] for m in early]:
        scratch += [pltpu.VMEM((n, 1, shard // n, w), BF)] * 3
        scratch += [pltpu.VMEM((n, shard // n, w), BF), pltpu.VMEM((shard // n, w), F32)]
        scratch += scatter_sems(n, 1) + gather_sems(n)
    scratch += [pltpu.SemaphoreType.DMA]
    return pl.pallas_call(
        functools.partial(reduce_kernel, n, owners, len(early)),
        out_shape=(
            jax.ShapeDtypeStruct(small.shape[1:], F32),
            jax.ShapeDtypeStruct((shard, qkv_width), BF),
            jax.ShapeDtypeStruct((shard, width), BF),
        ) + tuple(jax.ShapeDtypeStruct(m.shape, BF) for m in early),
        in_specs=[ANY] * 3 + [VM] * len(early),
        out_specs=[VM, VM, ANY] + [VM] * len(early),
        scratch_shapes=scratch,
        compiler_params=params(5),
        cost_estimate=pl.CostEstimate(
            flops=1 << 20, transcendentals=0, bytes_accessed=300 << 20),
        name="reduce_all",
    )(small, qkv_g, dw, *early)


def normalize(stream, gain):
    return stream * lax.rsqrt(jnp.mean(stream * stream, axis=-1, keepdims=True) + EPSILON) * gain


def normalize_back(grad, stream, gain):
    r = lax.rsqrt(jnp.mean(stream * stream, axis=-1, keepdims=True) + EPSILON)
    u = grad * gain
    back = r * (u - stream * (r * r) * jnp.mean(u * stream, axis=-1, keepdims=True))
    return back, jnp.sum(grad * stream * r, axis=0)


def rotate(heads, cosine, sine):
    half = HEAD // 2
    a, b = heads[..., :half], heads[..., half:]
    return jnp.concatenate([a * cosine - b * sine, b * cosine + a * sine], axis=-1)


def frequencies():
    return jnp.power(ROPE_BASE, -(jnp.arange(HEAD // 2, dtype=F32) * 2.0 / HEAD))


def shards(hidden_in, cotangent, seq_lengths, tile_place, norm_attn, w_qkv, b_qkv, w_out,
           norm_mlp, w_gate, w_up, w_down):
    n = lax.axis_size("context")
    owners = lax.axis_size("fsdp")
    rows, d_model = hidden_in.shape[1:]
    hidden_units = w_gate.shape[2]
    width = -(-hidden_units // 128) * 128
    pad = width - hidden_units
    total = n * rows

    row_index = jnp.arange(total, dtype=jnp.int32)
    tile_order = tile_place[0]
    selector = (
        row_index[:, None] // TILE == jnp.arange(tile_order.shape[0], dtype=jnp.int32)[None, :]
    ).astype(jnp.int32)
    position = jnp.sum(selector * tile_order[None, :], axis=1) * TILE + row_index % TILE
    valid = position < seq_lengths[0]
    offset = lax.axis_index("context") * rows
    my_position = lax.dynamic_slice_in_dim(position, offset, rows)
    my_valid = lax.dynamic_slice_in_dim(valid, offset, rows)
    pos_q = my_position[None, :]
    pos_k = jnp.where(valid, position, 1 << 30)[:, None]
    angles = my_position.astype(F32)[:, None] * frequencies()
    cosine, sine = jnp.cos(angles)[:, None, :], jnp.sin(angles)[:, None, :]

    shard = norm_attn.shape[1]
    bias_shard = b_qkv.shape[1]

    def ffn_shard(l):
        return jnp.stack([
            jnp.pad(m, ((0, 0), (0, pad))) for m in (w_gate[l], w_up[l], w_down[l].T)])

    def packed(parts, lead):
        flat = jnp.concatenate(parts, axis=-1)
        used = flat.shape[-1]
        lines = -(-used // (16 * 128)) * 16
        flat = jnp.pad(flat, ((0, 0),) * (flat.ndim - 1) + ((0, lines * 128 - used),))
        return flat.reshape(lead + (lines, 128))

    small = packed(
        [m.reshape(-1).astype(F32) for m in (norm_attn, norm_mlp, b_qkv)], ())
    first_ffn = ffn_shard(0)
    first_ffn, small = lax.optimization_barrier((first_ffn, small))
    ffn_weights = [lax.all_gather(first_ffn, "fsdp", axis=0, tiled=False)]
    small, qkv_w, out_w = spread_all(owners, small, w_qkv[0], w_out[0])
    qkv_weights = [qkv_w.reshape(d_model, -1)]
    out_weights = [out_w.reshape(Q_WIDTH, d_model)]
    small = small.reshape(owners, -1)
    gains_attn, gains_mlp, biases = [], [], []
    for l in range(LAYERS):
        gains_attn.append(small[:, l * shard:(l + 1) * shard].reshape(-1))
        gains_mlp.append(small[:, (LAYERS + l) * shard:(LAYERS + l + 1) * shard].reshape(-1))
        start = 2 * LAYERS * shard + l * bias_shard
        biases.append(small[:, start:start + bias_shard].reshape(-1))

    stream = hidden_in[0].astype(F32)
    kept = []
    for l in range(LAYERS):
        qkv_w, out_w, ffn_w = qkv_weights[l], out_weights[l], ffn_weights[l]
        if l + 1 < LAYERS:
            ffn_weights.append(lax.all_gather(ffn_shard(l + 1), "fsdp", axis=0, tiled=False))
        normed = normalize(stream, gains_attn[l]).astype(BF)
        projected = jnp.dot(normed, qkv_w, preferred_element_type=F32) + biases[l]
        qk = rotate(
            projected[:, :Q_WIDTH + KV_WIDTH].reshape(rows, QUERY_HEADS + KV_HEADS, HEAD),
            cosine, sine).astype(BF).reshape(rows, Q_WIDTH + KV_WIDTH)
        q = qk[:, :Q_WIDTH]
        kv = jnp.concatenate([qk[:, Q_WIDTH:], projected[:, Q_WIDTH + KV_WIDTH:].astype(BF)], axis=1)
        mixed, lse, kvall = attention_forward(q, kv, pos_q, pos_k, n)
        middle = stream + jnp.dot(mixed, out_w, preferred_element_type=F32)
        normed_two = normalize(middle, gains_mlp[l]).astype(BF)
        if l + 1 < LAYERS:
            xall, gate, up, y, next_qkv, next_out = ffn_forward(
                normed_two, ffn_w, n, (w_qkv[l + 1], w_out[l + 1]))
            qkv_weights.append(next_qkv.reshape(d_model, -1))
            out_weights.append(next_out.reshape(Q_WIDTH, d_model))
        else:
            xall, gate, up, y = ffn_forward(normed_two, ffn_w, n)
        kept.append((stream, normed, q, kvall, lse, mixed, middle, xall, gate, up,
                     qkv_w, out_w, ffn_w))
        stream = middle + y
    layer_out = stream.astype(BF)[None]

    gradient = cotangent[0].astype(F32) * my_valid[:, None].astype(F32)
    small_grads = [None] * LAYERS
    out_sums, qkv_sums, ffn_sums, down_sums = ([None] * LAYERS for _ in range(4))
    for l in reversed(range(LAYERS)):
        (stream, normed, q, kvall, lse, mixed, middle, xall, gate, up,
         qkv_w, out_w, ffn_w) = kept[l]
        dw, dw_down, dx = ffn_backward(gradient.astype(BF), ffn_w, xall, gate, up, n)
        if l < LAYERS - 1:
            dx, ffn_sums[l + 1], down_sums[l + 1] = lax.optimization_barrier(
                (dx, ffn_sums[l + 1], down_sums[l + 1]))
        ffn_sums[l] = lax.psum_scatter(dw, "fsdp", scatter_dimension=0, tiled=False)
        if l > 0:
            down_sums[l] = lax.psum_scatter(dw_down, "fsdp", scatter_dimension=0, tiled=False)
        back, gain_two = normalize_back(dx, middle, gains_mlp[l])
        d_middle = gradient + back
        d_low = d_middle.astype(BF)
        d_mixed = jnp.einsum("td,cd->tc", d_low, out_w, preferred_element_type=F32).astype(BF)
        out_grad = jnp.einsum("tc,td->cd", mixed, d_low, preferred_element_type=F32).astype(BF)
        dq, dkv, out_sums[l] = attention_backward(
            q, kvall, lse, d_mixed, pos_q, pos_k, out_grad.reshape(owners, shard, d_model), n)
        if l < LAYERS - 1:
            dq, qkv_sums[l + 1] = lax.optimization_barrier((dq, qkv_sums[l + 1]))
        d_qk = rotate(
            jnp.concatenate([dq, dkv[:, :KV_WIDTH]], axis=1).reshape(
                rows, QUERY_HEADS + KV_HEADS, HEAD),
            cosine, -sine).reshape(rows, Q_WIDTH + KV_WIDTH)
        d_projected = jnp.concatenate([d_qk, dkv[:, KV_WIDTH:]], axis=1).astype(BF)
        bias_grad = jnp.sum(d_projected.astype(F32), axis=0)
        d_normed = jnp.einsum("tc,dc->td", d_projected, qkv_w, preferred_element_type=F32)
        qkv_grad = jnp.einsum(
            "td,tc->dc", normed, d_projected, preferred_element_type=F32).astype(BF)
        back, gain_one = normalize_back(d_normed, stream, gains_attn[l])
        gradient = d_middle + back
        small_grads[l] = (gain_one, gain_two, bias_grad)
        if l > 0:
            qkv_sums[l] = lax.psum_scatter(qkv_grad, "fsdp", scatter_dimension=0, tiled=True)
    small = packed([
        m.reshape(owners, -1)
        for k in range(3) for m in (small_grads[i][k] for i in range(LAYERS))], (owners,))
    small, qkv_sums[0], down_sums[0], *early = reduce_all(
        small, qkv_grad.reshape(owners, shard, qkv_grad.shape[1]), dw_down,
        out_sums + qkv_sums[1:], n)
    out_sums, qkv_sums = early[:LAYERS], qkv_sums[:1] + early[LAYERS:]
    small = small.reshape(-1)

    grad_norm_attn = small[:LAYERS * shard].reshape(LAYERS, shard)
    grad_norm_mlp = small[LAYERS * shard:2 * LAYERS * shard].reshape(LAYERS, shard)
    start = 2 * LAYERS * shard
    grad_b_qkv = small[start:start + LAYERS * bias_shard].reshape(LAYERS, bias_shard)

    def stacked(sums, pick=lambda m: m):
        return jnp.stack([pick(m).astype(F32) for m in sums])

    return (
        layer_out,
        gradient[None],
        grad_norm_attn,
        stacked(qkv_sums),
        grad_b_qkv,
        stacked(out_sums),
        grad_norm_mlp,
        stacked(ffn_sums, lambda m: m[0, :, :hidden_units]),
        stacked(ffn_sums, lambda m: m[1, :, :hidden_units]),
        stacked(down_sums, lambda m: m[:, :hidden_units].T),
    )


def solution(mesh):
    return jax.shard_map(
        shards,
        mesh=mesh,
        in_specs=(
            P("fsdp", "context", None),
            P("fsdp", "context", None),
            P("fsdp"),
            P("fsdp", None),
            P(None, "fsdp"),
            P(None, "fsdp", None),
            P(None, "fsdp"),
            P(None, "fsdp", None),
            P(None, "fsdp"),
            P(None, "fsdp", "context"),
            P(None, "fsdp", "context"),
            P(None, "context", "fsdp"),
        ),
        out_specs=(
            P("fsdp", "context", None),
            P("fsdp", "context", None),
            P(None, "fsdp"),
            P(None, "fsdp", None),
            P(None, "fsdp"),
            P(None, "fsdp", None),
            P(None, "fsdp"),
            P(None, "fsdp", "context"),
            P(None, "fsdp", "context"),
            P(None, "context", "fsdp"),
        ),
        check_vma=False,
    )
```

```python
import functools
import math

import jax
import jax.numpy as jnp
from jax import lax
from jax.experimental import pallas as pl
from jax.experimental.pallas import tpu as pltpu
from jax.sharding import PartitionSpec as P

QUERY_HEADS = 12
KV_HEADS = 2
HEAD = 128
LAYERS = 2
TILE = 128
Q_WIDTH = QUERY_HEADS * HEAD
KV_WIDTH = KV_HEADS * HEAD
PER_GROUP = QUERY_HEADS // KV_HEADS
SCALE = 1.0 / math.sqrt(HEAD)
EPSILON = 1e-06
ROPE_BASE = 1000000.0
BF = jnp.bfloat16
F32 = jnp.float32
MESH = pl.DeviceIdType.MESH
VMEM_LIMIT = 66 * 1024 * 1024
ANY = pl.BlockSpec(memory_space=pl.ANY)
VM = pl.BlockSpec(memory_space=pltpu.VMEM)


def dot_nn(a, b):
    return lax.dot_general(a, b, (((1,), (0,)), ((), ())), preferred_element_type=F32)


def dot_nt(a, b):
    return lax.dot_general(a, b, (((1,), (1,)), ((), ())), preferred_element_type=F32)


def dot_tn(a, b):
    return lax.dot_general(a, b, (((0,), (0,)), ((), ())), preferred_element_type=F32)


def lane_tile(width, most):
    best = 128
    for k in range(1, most // 128 + 1):
        if width % (128 * k) == 0:
            best = 128 * k
    return best


class Line:
    def __init__(self, n):
        self.n = n
        self.z = lax.axis_index("context")
        self.right = lax.rem(self.z + 1, n)
        self.left = lax.rem(self.z + n - 1, n)
        self.has_right = self.z < n - 1
        self.has_left = self.z > 0

    def barrier(self):
        bar = pltpu.get_barrier_semaphore()

        @pl.when(self.has_right)
        def _():
            pl.semaphore_signal(bar, inc=1, device_id={"context": self.right}, device_id_type=MESH)

        @pl.when(self.has_left)
        def _():
            pl.semaphore_signal(bar, inc=1, device_id={"context": self.left}, device_id_type=MESH)

        both = self.has_right & self.has_left

        @pl.when(both)
        def _():
            pl.semaphore_wait(bar, 2)

        @pl.when(jnp.logical_not(both))
        def _():
            pl.semaphore_wait(bar, 1)

    def order(self, i):
        z, n = self.z, self.n
        short = jnp.minimum(z, n - 1 - z)
        j = i - 1
        paired = j < 2 * short
        k = jnp.where(paired, j // 2 + 1, j - short + 1)
        goes_left = jnp.where(paired, lax.rem(j, 2) == 0, z > n - 1 - z)
        return jnp.where(i == 0, z, jnp.where(goes_left, z - k, z + k))


def remote(src, dst, send, recv, target):
    return pltpu.make_async_remote_copy(
        src_ref=src, dst_ref=dst, send_sem=send, recv_sem=recv,
        device_id={"context": target}, device_id_type=MESH,
    )


class Gather:
    def __init__(self, line, slots, send_r, send_l, recv):
        self.line, self.slots = line, slots
        self.send_r, self.send_l, self.recv = send_r, send_l, recv

    def _right(self, b, src):
        return remote(src, self.slots.at[b], self.send_r.at[b], self.recv.at[b], self.line.right)

    def _left(self, b, src):
        return remote(src, self.slots.at[b], self.send_l.at[b], self.recv.at[b], self.line.left)

    def start(self, own):
        line = self.line

        @pl.when(line.has_right)
        def _():
            self._right(line.z, own).start()

        @pl.when(line.has_left)
        def _():
            self._left(line.z, own).start()

    def arrive(self, b):
        line = self.line
        self._right(b, self.slots.at[b]).wait_recv()

        @pl.when((b < line.z) & line.has_right)
        def _():
            self._right(b, self.slots.at[b]).start()

        @pl.when((b > line.z) & line.has_left)
        def _():
            self._left(b, self.slots.at[b]).start()

    def finish(self):
        line = self.line
        for b in range(line.n):
            @pl.when((b <= line.z) & line.has_right)
            def _():
                self._right(b, self.slots.at[b]).wait_send()

            @pl.when((b >= line.z) & line.has_left)
            def _():
                self._left(b, self.slots.at[b]).wait_send()


class Scatter:
    def __init__(self, line, pieces, part, from_left, from_right, send_r, send_l, recv_l, recv_r):
        self.line, self.pieces, self.part = line, pieces, part
        self.from_left, self.from_right = from_left, from_right
        self.send_r, self.send_l, self.recv_l, self.recv_r = send_r, send_l, recv_l, recv_r

    def _right(self, b, p):
        return remote(self.part.at[b, p], self.from_left.at[b, p], self.send_r.at[b, p],
                      self.recv_l.at[b, p], self.line.right)

    def _left(self, b, p):
        return remote(self.part.at[b, p], self.from_right.at[b, p], self.send_l.at[b, p],
                      self.recv_r.at[b, p], self.line.left)

    def computed(self, b, p):
        line = self.line

        @pl.when((line.z == 0) & (b > 0))
        def _():
            self._right(b, p).start()

        @pl.when((line.z == line.n - 1) & (b < line.n - 1))
        def _():
            self._left(b, p).start()

    def steps(self):
        return range(1, 2 * (self.line.n - 1) + 1)

    def step(self, t, add_own):
        line = self.line
        n, z = line.n, line.z
        b_left = t - z

        @pl.when(line.has_left & (b_left >= z) & (b_left < n))
        def _():
            for p in range(self.pieces):
                self._right(b_left, p).wait_recv()

                @pl.when(b_left == z)
                def _():
                    add_own(p, self.from_left[b_left, p].astype(F32))

                @pl.when(b_left != z)
                def _():
                    self.part[b_left, p] = (
                        self.part[b_left, p].astype(F32) + self.from_left[b_left, p].astype(F32)
                    ).astype(BF)
                    self._right(b_left, p).start()

        b_right = 2 * (n - 1) - t - z

        @pl.when(line.has_right & (b_right >= 0) & (b_right <= z))
        def _():
            for p in range(self.pieces):
                self._left(b_right, p).wait_recv()

                @pl.when(b_right == z)
                def _():
                    add_own(p, self.from_right[b_right, p].astype(F32))

                @pl.when(b_right != z)
                def _():
                    self.part[b_right, p] = (
                        self.part[b_right, p].astype(F32) + self.from_right[b_right, p].astype(F32)
                    ).astype(BF)
                    self._left(b_right, p).start()

    def finish(self):
        line = self.line
        for b in range(line.n):
            @pl.when((b > line.z) & line.has_right)
            def _():
                for p in range(self.pieces):
                    self._right(b, p).wait_send()

            @pl.when((b < line.z) & line.has_left)
            def _():
                for p in range(self.pieces):
                    self._left(b, p).wait_send()


def gather_sems(n):
    return [pltpu.SemaphoreType.DMA((n,))] * 3


def scatter_sems(n, pieces):
    return [pltpu.SemaphoreType.DMA((n, pieces))] * 4


def params(cid):
    return pltpu.CompilerParams(
        collective_id=cid, has_side_effects=True, vmem_limit_bytes=VMEM_LIMIT
    )


def bits_of(owners):
    return [1 << i for i in range(owners.bit_length() - 1)]


class Cube:
    def __init__(self, owners):
        self.owners = owners
        self.me = lax.axis_index("fsdp")
        self.bits = bits_of(owners)
        self.chip_bits = [b // 2 for b in self.bits[1:]]
        self.chips = owners // 2

    def flip(self, mask):
        index = self.me
        for b in self.bits:
            if mask & b:
                index = index + b - 2 * b * lax.rem(self.me // b, 2)
        return index

    def signal(self, bar):
        for b in self.bits:
            pl.semaphore_signal(bar, inc=1, device_id={"fsdp": self.flip(b)}, device_id_type=MESH)

    def order(self, half):
        return self.chip_bits[::-1] if half == 0 else self.chip_bits

    def plan(self):
        steps = {}
        for half in (0, 1):
            order, slot = self.order(half), 0
            for stage, bit in enumerate(order):
                rest = [0]
                for other in order[stage + 1:]:
                    rest = rest + [m | other for m in rest]
                steps[half, stage] = (bit, rest, slot)
                slot += len(rest)
        return steps


def joint_barrier(line, cube):
    bar = pltpu.get_barrier_semaphore()
    cube.signal(bar)
    peers = len(cube.bits)

    @pl.when(line.has_right)
    def _():
        pl.semaphore_signal(bar, inc=1, device_id={"context": line.right}, device_id_type=MESH)

    @pl.when(line.has_left)
    def _():
        pl.semaphore_signal(bar, inc=1, device_id={"context": line.left}, device_id_type=MESH)

    both = line.has_right & line.has_left

    @pl.when(both)
    def _():
        pl.semaphore_wait(bar, peers + 2)

    @pl.when(jnp.logical_not(both))
    def _():
        pl.semaphore_wait(bar, peers + 1)


class Spread:
    def __init__(self, cube, own, full, own_sem, send, recv, core_send, core_recv):
        self.cube, self.own, self.full = cube, own, full
        self.own_sem, self.send, self.recv = own_sem, send, recv
        self.core_send, self.core_recv = core_send, core_recv
        self.half = own.shape[0] // 2
        self.stages = len(cube.chip_bits)

    def _rows(self, half):
        return pl.ds(half * self.half, self.half)

    def _block(self, half, mask):
        return self.full.at[self.cube.flip(mask), self._rows(half)]

    def _source(self, half, mask):
        return self._block(half, 2 * mask) if mask else self.own.at[self._rows(half)]

    def _masks(self, half, stage):
        masks = [0]
        for bit in self.cube.order(half)[:stage]:
            masks = masks + [m | bit for m in masks]
        return masks

    def _hop(self, half, stage, mask):
        bit = self.cube.order(half)[stage]
        return pltpu.make_async_remote_copy(
            src_ref=self._source(half, mask), dst_ref=self._block(half, 2 * mask),
            send_sem=self.send.at[half, mask | bit], recv_sem=self.recv.at[half, mask | bit],
            device_id={"fsdp": self.cube.flip(2 * bit)}, device_id_type=MESH)

    def _arrival(self, half, mask):
        block = self._block(half, 2 * mask)
        return pltpu.make_async_remote_copy(
            src_ref=block, dst_ref=block,
            send_sem=self.send.at[half, mask], recv_sem=self.recv.at[half, mask],
            device_id={"fsdp": self.cube.flip(1)}, device_id_type=MESH)

    def _core(self, half, mask):
        return pltpu.make_async_remote_copy(
            src_ref=self._source(half, mask), dst_ref=self._block(half, 2 * mask),
            send_sem=self.core_send.at[half, mask], recv_sem=self.core_recv.at[half, mask],
            device_id={"fsdp": self.cube.flip(1)}, device_id_type=MESH)

    def _core_arrival(self, half, mask):
        block = self._block(half, 2 * mask | 1)
        return pltpu.make_async_remote_copy(
            src_ref=block, dst_ref=block,
            send_sem=self.core_send.at[half, mask], recv_sem=self.core_recv.at[half, mask],
            device_id={"fsdp": self.cube.flip(1)}, device_id_type=MESH)

    def _own_copy(self):
        return pltpu.make_async_copy(self.own, self.full.at[self.cube.me], self.own_sem)

    def start(self):
        for stage in range(self.stages):
            for half in (0, 1):
                self._hop(half, stage, 0).start()
        for half in (0, 1):
            self._core(half, 0).start()
        self._own_copy().start()

    def phase(self, k):
        for half in (0, 1):
            bit = self.cube.order(half)[k - 1]
            for m in self._masks(half, k - 1):
                self._arrival(half, m | bit).wait_recv()
                for stage in range(k, self.stages):
                    self._hop(half, stage, m | bit).start()
                self._core(half, m | bit).start()

    def finish(self):
        self._own_copy().wait()
        for half in (0, 1):
            for m in range(self.cube.chips):
                self._core_arrival(half, m).wait_recv()
                self._core(half, m).wait_send()
            for stage in range(self.stages):
                for m in self._masks(half, stage):
                    self._hop(half, stage, m).wait_send()


SPREAD_SEMS = 5


def spread_sems(owners):
    chips = owners // 2
    return [pltpu.SemaphoreType.DMA] + [pltpu.SemaphoreType.DMA((2, chips))] * 4


def spread_shapes(owners, shards):
    return tuple(jax.ShapeDtypeStruct((owners,) + m.shape, m.dtype) for m in shards)


def spread_kernel(owners, count, *refs):
    cube = Cube(owners)
    spreads = [
        Spread(cube, refs[i], refs[count + i],
               *refs[2 * count + SPREAD_SEMS * i:2 * count + SPREAD_SEMS * (i + 1)])
        for i in range(count)]
    bar = pltpu.get_barrier_semaphore()
    cube.signal(bar)
    pl.semaphore_wait(bar, len(cube.bits))
    for s in spreads:
        s.start()
    for k in range(1, len(cube.chip_bits) + 1):
        for s in spreads:
            s.phase(k)
    for s in spreads:
        s.finish()


def spread_all(owners, *shards):
    count = len(shards)
    return pl.pallas_call(
        functools.partial(spread_kernel, owners, count),
        out_shape=spread_shapes(owners, shards),
        in_specs=[VM] * count,
        out_specs=[ANY] * count,
        scratch_shapes=spread_sems(owners) * count,
        compiler_params=params(6),
        cost_estimate=pl.CostEstimate(
            flops=1 << 20, transcendentals=0, bytes_accessed=150 << 20),
        name="spread_all",
    )(*shards)


class Fold:
    def __init__(self, cube, src, mine, first, later, load_sem, send1, recv1, send2, recv2):
        self.cube, self.src = cube, src
        self.mine, self.first, self.later = mine, first, later
        self.load_sem, self.send1, self.recv1 = load_sem, send1, recv1
        self.send2, self.recv2 = send2, recv2
        self.rows = mine.shape[1]
        self.half = self.rows // 2
        self.steps = cube.plan()
        self.stages = len(cube.chip_bits)

    def _load(self, d):
        return pltpu.make_async_copy(
            self.src(self.cube.flip(2 * d)), self.mine.at[d], self.load_sem.at[d])

    def _core(self, d):
        return pltpu.make_async_remote_copy(
            src_ref=self.src(self.cube.flip(2 * d | 1)), dst_ref=self.first.at[d],
            send_sem=self.send1.at[d], recv_sem=self.recv1.at[d],
            device_id={"fsdp": self.cube.flip(1)}, device_id_type=MESH)

    def _hop(self, half, stage, index):
        bit, rest, slot = self.steps[half, stage]
        rows = pl.ds(half * self.half, self.half)
        return pltpu.make_async_remote_copy(
            src_ref=self.mine.at[bit | rest[index], rows],
            dst_ref=self.later.at[half, slot + index],
            send_sem=self.send2.at[half, slot + index],
            recv_sem=self.recv2.at[half, slot + index],
            device_id={"fsdp": self.cube.flip(2 * bit)}, device_id_type=MESH)

    def _hops(self, stage):
        return [self._hop(half, stage, i)
                for half in (0, 1) for i in range(len(self.steps[half, stage][1]))]

    def _add(self, d, base, size, other):
        dtype = self.mine.dtype
        strip = 48 if size % 48 == 0 else size

        @pl.loop(0, size // strip)
        def _(i):
            into = pl.ds(pl.multiple_of(base + i * strip, 8), strip)
            rows = pl.ds(pl.multiple_of(i * strip, 8), strip)
            self.mine[d, into] = (
                self.mine[d, into].astype(F32) + other(rows).astype(F32)).astype(dtype)

    def start(self):
        for d in range(self.cube.chips):
            self._core(d).start()
        for d in range(self.cube.chips):
            self._load(d).start()

    def phase(self, k):
        if k == 0:
            for d in range(self.cube.chips):
                self._load(d).wait()
                self._core(d).wait_recv()
                self._add(d, 0, self.rows, lambda rows, d=d: self.first[d, rows])
        else:
            for half in (0, 1):
                _, rest, slot = self.steps[half, k - 1]
                for i, e in enumerate(rest):
                    self._hop(half, k - 1, i).wait_recv()
                    self._add(e, half * self.half, self.half,
                              lambda rows, h=half, j=slot + i: self.later[h, j, rows])
        if k < self.stages:
            for c in self._hops(k):
                c.start()

    def finish(self):
        for d in range(self.cube.chips):
            self._core(d).wait_send()
        for stage in range(self.stages):
            for c in self._hops(stage):
                c.wait_send()


def fold_scratch(owners, rows, width, dtype):
    chips = owners // 2
    return [
        pltpu.VMEM((chips, rows, width), dtype),
        pltpu.VMEM((chips, rows, width), dtype),
        pltpu.VMEM((2, chips - 1, rows // 2, width), dtype),
        pltpu.SemaphoreType.DMA((chips,)),
        pltpu.SemaphoreType.DMA((chips,)),
        pltpu.SemaphoreType.DMA((chips,)),
        pltpu.SemaphoreType.DMA((2, chips - 1)),
        pltpu.SemaphoreType.DMA((2, chips - 1)),
    ]


FOLD_REFS = 8


def ffn_forward_kernel(n, pieces, count, *refs):
    x_ref, w_ref = refs[:2]
    next_own = refs[2:2 + count]
    xall_ref, gate_ref, up_ref, y_ref = refs[2 + count:6 + count]
    next_full = refs[6 + count:6 + 2 * count]
    (w_v, xbuf, gbuf, ubuf, hbuf, part, from_l, from_r,
     w_sem, x_sem, out_sem, *sems) = refs[6 + 2 * count:]
    line = Line(n)
    z = line.z
    owners, _, rows, width = w_ref.shape
    d_model = x_ref.shape[1]
    tile = lane_tile(width, 256)
    piece = d_model // pieces
    gather = Gather(line, xbuf, *sems[:3])
    scatter = Scatter(line, pieces, part, from_l, from_r, *sems[3:7])
    spreads = []
    stages = 0
    if count:
        cube = Cube(owners)
        stages = len(cube.chip_bits)
        for i in range(count):
            at = 7 + SPREAD_SEMS * i
            spreads.append(Spread(cube, next_own[i], next_full[i], *sems[at:at + SPREAD_SEMS]))

    def w_copy(k, f):
        return pltpu.make_async_copy(
            w_ref.at[f, k], w_v.at[k, pl.ds(f * rows, rows)], w_sem.at[k, f]
        )

    def x_out(b):
        return pltpu.make_async_copy(xbuf.at[b], xall_ref.at[b], x_sem.at[b])

    if count:
        joint_barrier(line, cube)
    else:
        line.barrier()
    gather.start(x_ref)
    for s in spreads:
        s.start()
    for k in range(3):
        for f in range(owners):
            w_copy(k, f).start()
    xbuf[z] = x_ref[...]
    for k in range(3):
        for f in range(owners):
            w_copy(k, f).wait()

    @pl.loop(0, n)
    def _(i):
        b = line.order(i)

        @pl.when(i > 0)
        def _():
            gather.arrive(b)

        x_out(b).start()
        slot = lax.rem(i, 2)
        g_copy = pltpu.make_async_copy(gbuf.at[slot], gate_ref.at[b], out_sem.at[0, slot])
        u_copy = pltpu.make_async_copy(ubuf.at[slot], up_ref.at[b], out_sem.at[1, slot])

        @pl.when(i > 1)
        def _():
            g_copy.wait()
            u_copy.wait()

        @pl.loop(0, width // tile)
        def _(j):
            cols = pl.ds(pl.multiple_of(j * tile, tile), tile)
            xb = xbuf[b]
            gate = dot_nn(xb, w_v[0, :, cols])
            up = dot_nn(xb, w_v[1, :, cols])
            gbuf[slot, :, cols] = gate.astype(BF)
            ubuf[slot, :, cols] = up.astype(BF)
            hbuf[:, cols] = (gate * jax.nn.sigmoid(gate) * up).astype(BF)

        g_copy.start()
        u_copy.start()
        for p in range(pieces):
            out = dot_nt(hbuf[...], w_v[2, pl.ds(p * piece, piece)])

            @pl.when(b == z)
            def _():
                y_ref[:, p * piece:(p + 1) * piece] = out

            @pl.when(b != z)
            def _():
                part[b, p] = out.astype(BF)

            scatter.computed(b, p)

        if spreads:
            @pl.when(i == n // 2)
            def _():
                for s in spreads:
                    s.phase(1)

    def add_own(p, value):
        cols = slice(p * piece, (p + 1) * piece)
        y_ref[:, cols] = y_ref[:, cols] + value

    passed = 2
    for t in scatter.steps():
        scatter.step(t, add_own)
        if t >= 4 and t % 2 == 0 and passed <= stages:
            for s in spreads:
                s.phase(passed)
            passed += 1
    for k in range(passed, stages + 1):
        for s in spreads:
            s.phase(k)
    for i in range(max(0, n - 2), n):
        slot = i % 2
        pltpu.make_async_copy(gbuf.at[slot], gate_ref.at[0], out_sem.at[0, slot]).wait()
        pltpu.make_async_copy(ubuf.at[slot], up_ref.at[0], out_sem.at[1, slot]).wait()
    for b in range(n):
        x_out(b).wait()
    gather.finish()
    scatter.finish()
    for s in spreads:
        s.finish()


def ffn_forward(x, w, n, following=()):
    rows, d_model = x.shape
    owners, _, shard, width = w.shape
    pieces = 3
    piece = d_model // pieces
    count = len(following)
    return pl.pallas_call(
        functools.partial(ffn_forward_kernel, n, pieces, count),
        out_shape=(
            jax.ShapeDtypeStruct((n, rows, d_model), BF),
            jax.ShapeDtypeStruct((n, rows, width), BF),
            jax.ShapeDtypeStruct((n, rows, width), BF),
            jax.ShapeDtypeStruct((rows, d_model), F32),
        ) + spread_shapes(owners, following),
        in_specs=[VM, ANY] + [VM] * count,
        out_specs=[ANY, ANY, ANY, VM] + [ANY] * count,
        scratch_shapes=[
            pltpu.VMEM((3, d_model, width), BF),
            pltpu.VMEM((n, rows, d_model), BF),
            pltpu.VMEM((2, rows, width), BF),
            pltpu.VMEM((2, rows, width), BF),
            pltpu.VMEM((rows, width), BF),
            pltpu.VMEM((n, pieces, rows, piece), BF),
            pltpu.VMEM((n, pieces, rows, piece), BF),
            pltpu.VMEM((n, pieces, rows, piece), BF),
            pltpu.SemaphoreType.DMA((3, owners)),
            pltpu.SemaphoreType.DMA((n,)),
            pltpu.SemaphoreType.DMA((2, 2)),
        ] + gather_sems(n) + scatter_sems(n, pieces) + spread_sems(owners) * count,
        compiler_params=params(7 if count else 1),
        cost_estimate=pl.CostEstimate(
            flops=6 * n * rows * d_model * width, transcendentals=n * rows * width,
            bytes_accessed=60 << 20),
        name="ffn_forward",
    )(x, w, *following)


def ffn_backward_kernel(n, pieces, groups, count, *refs):
    g_ref, w_ref, xall_ref, gate_ref, up_ref = refs[:5]
    later_grads = refs[5:5 + count]
    dw_ref, dwd_ref, dx_ref = refs[5 + count:8 + count]
    later_sums = refs[8 + count:8 + 2 * count]
    (w_v, gbuf, xv, gate_v, up_v, hid_v, part, from_l, from_r, stage,
     w_sem, in_sem, out_sem, *sems) = refs[8 + 2 * count:]
    line = Line(n)
    z = line.z
    owners, _, shard, width = w_ref.shape
    rows, d_model = g_ref.shape
    tile = lane_tile(width, 256)
    piece = d_model // pieces
    gather = Gather(line, gbuf, *sems[:3])
    scatter = Scatter(line, pieces, part, from_l, from_r, *sems[3:7])
    folds = []
    stages = 0
    if count:
        cube = Cube(owners)
        stages = len(cube.chip_bits)
        for i in range(count):
            at = 7 + FOLD_REFS * i
            folds.append(Fold(cube, lambda q, ref=later_grads[i]: ref.at[q],
                              *sems[at:at + FOLD_REFS]))

    def fold_phase(k):
        for fold in folds:
            fold.phase(k)

    def w_copy(k, f):
        return pltpu.make_async_copy(
            w_ref.at[f, k], w_v.at[k, pl.ds(f * shard, shard)], w_sem.at[k, f]
        )

    def loads(b):
        return (
            pltpu.make_async_copy(gate_ref.at[b], gate_v.at[b], in_sem.at[0, b]),
            pltpu.make_async_copy(up_ref.at[b], up_v.at[b], in_sem.at[1, b]),
        )

    def x_load(b):
        return pltpu.make_async_copy(xall_ref.at[b], xv.at[b], in_sem.at[2, b])

    if count:
        joint_barrier(line, cube)
    else:
        line.barrier()
    gather.start(g_ref)
    for f in range(owners):
        w_copy(2, f).start()
    for c in loads(z):
        c.start()
    for k in range(2):
        for f in range(owners):
            w_copy(k, f).start()
    for b in range(n):
        @pl.when(b != z)
        def _():
            for c in loads(b):
                c.start()
    for b in range(n):
        x_load(b).start()
    for fold in folds:
        fold.start()
    gbuf[z] = g_ref[...]
    for k in (2, 0, 1):
        for f in range(owners):
            w_copy(k, f).wait()

    @pl.loop(0, n)
    def _(i):
        b = line.order(i)

        @pl.when(i > 0)
        def _():
            gather.arrive(b)

        for c in loads(b):
            c.wait()

        @pl.loop(0, width // tile)
        def _(j):
            cols = pl.ds(pl.multiple_of(j * tile, tile), tile)
            d_hidden = dot_nn(gbuf[b], w_v[2, :, cols])
            gate = gate_v[b, :, cols].astype(F32)
            up = up_v[b, :, cols].astype(F32)
            sig = jax.nn.sigmoid(gate)
            act = gate * sig
            hid_v[b, :, cols] = (act * up).astype(BF)
            gate_v[b, :, cols] = (d_hidden * up * (sig + act * (1.0 - sig))).astype(BF)
            up_v[b, :, cols] = (d_hidden * act).astype(BF)

        for p in range(pieces):
            sl = pl.ds(p * piece, piece)
            out = dot_nt(gate_v[b], w_v[0, sl]) + dot_nt(up_v[b], w_v[1, sl])

            @pl.when(b == z)
            def _():
                dx_ref[:, p * piece:(p + 1) * piece] = out

            @pl.when(b != z)
            def _():
                part[b, p] = out.astype(BF)

            scatter.computed(b, p)

        if folds:
            @pl.when(i == 1)
            def _():
                fold_phase(0)

            @pl.when(i == n - 1)
            def _():
                fold_phase(1)

    def add_own(p, value):
        cols = slice(p * piece, (p + 1) * piece)
        dx_ref[:, cols] = dx_ref[:, cols] + value

    for b in range(n):
        x_load(b).wait()

    group = d_model // groups
    per = group // shard

    def dw_copies(k, q, slot):
        def target(owner):
            return dw_ref.at[owner, k] if k < 2 else dwd_ref.at[owner]

        return [
            pltpu.make_async_copy(
                stage.at[slot, pl.ds(s * shard, shard)], target(q * per + s), out_sem.at[slot, s])
            for s in range(per)
        ]

    def weight_unit(unit):
        k, q = unit // groups, unit % groups
        slot = unit % 2
        left = (xv, xv, gbuf)[k]
        right = (gate_v, up_v, hid_v)[k]
        if unit >= 2:
            for c in dw_copies((unit - 2) // groups, (unit - 2) % groups, slot):
                c.wait()
        lt = left[:, :, q * group:(q + 1) * group].reshape(n * rows, group)

        @pl.loop(0, width // tile)
        def _(j):
            cols = pl.ds(pl.multiple_of(j * tile, tile), tile)
            stage[slot, :, cols] = dot_tn(
                lt, right[:, :, cols].reshape(n * rows, tile)
            ).astype(BF)

        for c in dw_copies(k, q, slot):
            c.start()

    units = 3 * groups
    steps = list(scatter.steps())
    done = 0
    passed = 2
    for index, t in enumerate(steps):
        scatter.step(t, add_own)
        until = units * (index + 1) // len(steps)
        while done < until:
            weight_unit(done)
            done += 1
        if t >= 4 and t % 2 == 0 and passed <= stages:
            fold_phase(passed)
            passed += 1
    for k in range(passed, stages + 1):
        fold_phase(k)
    for fold, ref in zip(folds, later_sums):
        ref[...] = fold.mine[0]
    for unit in range(units - 2, units):
        for c in dw_copies(unit // groups, unit % groups, unit % 2):
            c.wait()
    gather.finish()
    scatter.finish()
    for fold in folds:
        fold.finish()


def ffn_backward(g, w, xall, gate, up, n, later=()):
    rows, d_model = g.shape
    owners, _, shard, width = w.shape
    pieces, groups = 3, 4
    piece = d_model // pieces
    per = d_model // groups // shard
    count = len(later)
    fold_refs = []
    for m in later:
        fold_refs += fold_scratch(owners, m.shape[1], m.shape[2], BF)
    return pl.pallas_call(
        functools.partial(ffn_backward_kernel, n, pieces, groups, count),
        out_shape=(
            jax.ShapeDtypeStruct((owners, 2, shard, width), BF),
            jax.ShapeDtypeStruct((owners, shard, width), BF),
            jax.ShapeDtypeStruct((rows, d_model), F32),
        ) + tuple(jax.ShapeDtypeStruct(m.shape[1:], BF) for m in later),
        in_specs=[VM, ANY, ANY, ANY, ANY] + [ANY] * count,
        out_specs=[ANY, ANY, VM] + [VM] * count,
        scratch_shapes=[
            pltpu.VMEM((3, d_model, width), BF),
            pltpu.VMEM((n, rows, d_model), BF),
            pltpu.VMEM((n, rows, d_model), BF),
            pltpu.VMEM((n, rows, width), BF),
            pltpu.VMEM((n, rows, width), BF),
            pltpu.VMEM((n, rows, width), BF),
            pltpu.VMEM((n, pieces, rows, piece), BF),
            pltpu.VMEM((n, pieces, rows, piece), BF),
            pltpu.VMEM((n, pieces, rows, piece), BF),
            pltpu.VMEM((2, d_model // groups, width), BF),
            pltpu.SemaphoreType.DMA((3, owners)),
            pltpu.SemaphoreType.DMA((3, n)),
            pltpu.SemaphoreType.DMA((2, per)),
        ] + gather_sems(n) + scatter_sems(n, pieces) + fold_refs,
        compiler_params=params(8 if count else 2),
        cost_estimate=pl.CostEstimate(
            flops=12 * n * rows * d_model * width, transcendentals=n * rows * width,
            bytes_accessed=100 << 20),
        name="ffn_backward",
    )(g, w, xall, gate, up, *later)


def attention_forward_kernel(n, owners, q_ref, kv_ref, pq_ref, pk_ref, w_ref,
                             mixed_ref, lse_ref, kvall_ref, full_ref, kvbuf, vt, *sems):
    line = Line(n)
    cube = Cube(owners)
    spread = Spread(cube, w_ref, full_ref, *sems[3:])
    z = line.z
    rows = q_ref.shape[0]
    total = n * rows
    gather = Gather(line, kvbuf, *sems[:3])
    joint_barrier(line, cube)
    gather.start(kv_ref)
    spread.start()
    kvbuf[z] = kv_ref[...]
    for i in range(1, n):
        gather.arrive(line.order(i))
    kvall_ref[...] = kvbuf[...]
    allowed = pk_ref[...] <= pq_ref[...]
    for g in range(KV_HEADS):
        v = kvbuf[:, :, KV_WIDTH + g * HEAD:KV_WIDTH + (g + 1) * HEAD].reshape(total, HEAD)
        vt[g] = v.T
    for g in range(KV_HEADS):
        for r in range(PER_GROUP):
            h = g * PER_GROUP + r
            k = kvbuf[:, :, g * HEAD:(g + 1) * HEAD].reshape(total, HEAD)
            s = dot_nt(k, q_ref[:, h * HEAD:(h + 1) * HEAD]) * SCALE
            s = jnp.where(allowed, s, -1e30)
            top = jnp.max(s, axis=0, keepdims=True)
            e = jnp.exp(s - top)
            den = jnp.sum(e, axis=0, keepdims=True)
            o = dot_nn(vt[g], e.astype(BF)) / den
            mixed_ref[:, h * HEAD:(h + 1) * HEAD] = o.T.astype(BF)
            lse_ref[h:h + 1, :] = top + jnp.log(den)
            if h == 5:
                spread.phase(1)
    for k in range(2, spread.stages + 1):
        spread.phase(k)
    spread.finish()
    gather.finish()


def attention_forward(q, kv, pos_q, pos_k, w_out, n, owners):
    rows = q.shape[0]
    return pl.pallas_call(
        functools.partial(attention_forward_kernel, n, owners),
        out_shape=(
            jax.ShapeDtypeStruct((rows, Q_WIDTH), BF),
            jax.ShapeDtypeStruct((16, rows), F32),
            jax.ShapeDtypeStruct((n, rows, 2 * KV_WIDTH), BF),
        ) + spread_shapes(owners, (w_out,)),
        in_specs=[VM] * 5,
        out_specs=[VM] * 3 + [ANY],
        scratch_shapes=[
            pltpu.VMEM((n, rows, 2 * KV_WIDTH), BF),
            pltpu.VMEM((KV_HEADS, HEAD, n * rows), BF),
        ] + gather_sems(n) + spread_sems(owners),
        compiler_params=params(3),
        cost_estimate=pl.CostEstimate(
            flops=4 * n * rows * rows * Q_WIDTH, transcendentals=n * rows * rows * QUERY_HEADS,
            bytes_accessed=16 << 20),
        name="attention_forward",
    )(q, kv, pos_q, pos_k, w_out)


def attention_backward_kernel(n, q_ref, kvall_ref, lse_ref, dm_ref, pq_ref, pk_ref,
                              dq_ref, dkv_ref, kt, dk_acc, dv_acc, part, from_l, from_r, *sems):
    line = Line(n)
    z = line.z
    rows = q_ref.shape[0]
    total = n * rows
    pieces = KV_HEADS
    scatter = Scatter(line, pieces, part, from_l, from_r, *sems)
    line.barrier()
    allowed = pk_ref[...] <= pq_ref[...]
    for g in range(KV_HEADS):
        k = kvall_ref[:, :, g * HEAD:(g + 1) * HEAD].reshape(total, HEAD)
        kt[g] = k.T
    for g in range(KV_HEADS):
        for r in range(PER_GROUP):
            h = g * PER_GROUP + r
            cols = slice(h * HEAD, (h + 1) * HEAD)
            k = kvall_ref[:, :, g * HEAD:(g + 1) * HEAD].reshape(total, HEAD)
            v = kvall_ref[:, :, KV_WIDTH + g * HEAD:KV_WIDTH + (g + 1) * HEAD].reshape(total, HEAD)
            q = q_ref[:, cols]
            dm = dm_ref[:, cols]
            s = dot_nt(k, q) * SCALE
            pr = jnp.where(allowed, jnp.exp(s - lse_ref[h:h + 1, :]), 0.0)
            dp = dot_nt(v, dm)
            delta = jnp.sum(pr * dp, axis=0, keepdims=True)
            ds = (pr * (dp - delta) * SCALE).astype(BF)
            dv = dot_nn(pr.astype(BF), dm)
            dk = dot_nn(ds, q)
            if r == 0:
                dk_acc[...] = dk
                dv_acc[...] = dv
            else:
                dk_acc[...] += dk
                dv_acc[...] += dv
            dq_ref[:, cols] = dot_nn(kt[g], ds).T
        for b in range(n):
            sl = slice(b * rows, (b + 1) * rows)

            @pl.when(b == z)
            def _():
                dkv_ref[:, g * HEAD:(g + 1) * HEAD] = dk_acc[sl]
                dkv_ref[:, KV_WIDTH + g * HEAD:KV_WIDTH + (g + 1) * HEAD] = dv_acc[sl]

            @pl.when(b != z)
            def _():
                part[b, g, :, 0:HEAD] = dk_acc[sl].astype(BF)
                part[b, g, :, HEAD:2 * HEAD] = dv_acc[sl].astype(BF)

            scatter.computed(b, g)

    def add_own(p, value):
        a = slice(p * HEAD, (p + 1) * HEAD)
        c = slice(KV_WIDTH + p * HEAD, KV_WIDTH + (p + 1) * HEAD)
        dkv_ref[:, a] = dkv_ref[:, a] + value[:, :HEAD]
        dkv_ref[:, c] = dkv_ref[:, c] + value[:, HEAD:]

    for t in scatter.steps():
        scatter.step(t, add_own)
    scatter.finish()


def attention_backward(q, kvall, lse, dm, pos_q, pos_k, n):
    rows = q.shape[0]
    return pl.pallas_call(
        functools.partial(attention_backward_kernel, n),
        out_shape=(
            jax.ShapeDtypeStruct((rows, Q_WIDTH), F32),
            jax.ShapeDtypeStruct((rows, 2 * KV_WIDTH), F32),
        ),
        in_specs=[VM] * 6,
        out_specs=[VM] * 2,
        scratch_shapes=[
            pltpu.VMEM((KV_HEADS, HEAD, n * rows), BF),
            pltpu.VMEM((n * rows, HEAD), F32),
            pltpu.VMEM((n * rows, HEAD), F32),
        ] + [pltpu.VMEM((n, KV_HEADS, rows, 2 * HEAD), BF)] * 3 + scatter_sems(n, KV_HEADS),
        compiler_params=params(4),
        cost_estimate=pl.CostEstimate(
            flops=10 * n * rows * rows * Q_WIDTH, transcendentals=n * rows * rows * QUERY_HEADS,
            bytes_accessed=16 << 20),
        name="attention_backward",
    )(q, kvall, lse, dm, pos_q, pos_k)


def reduce_kernel(n, owners, count, small_ref, out_ref, qkv_ref, dw_ref, *refs):
    early = refs[:count]
    small_o, out_o, qkv_o, dw_o = refs[count:count + 4]
    targets = (out_o, qkv_o) + refs[count + 4:2 * count + 4]
    refs = refs[2 * count + 4:]
    line = Line(n)
    cube = Cube(owners)
    refs = list(refs)

    def take(count):
        taken = refs[:count]
        del refs[:count]
        return taken

    sources = [
        lambda q: small_ref.at[q],
        lambda q: out_ref.at[q],
        lambda q: qkv_ref.at[q],
        lambda q: dw_ref.at[q],
    ]
    folds = [Fold(cube, src, *take(FOLD_REFS)) for src in sources]
    small_all, = take(1)
    gather_small = Gather(line, small_all, *take(3))
    shared = []
    for _ in targets:
        part, from_l, from_r, total, own = take(5)
        shared.append((Scatter(line, 1, part, from_l, from_r, *take(4)), part,
                       Gather(line, total, *take(3)), total, own))
    write_sem, = take(1)

    def share(index, value):
        scatter, part, _, _, own = shared[index]
        rows = part.shape[2]
        for b in range(n):
            @pl.when(b == line.z)
            def _():
                own[...] = value(slice(b * rows, (b + 1) * rows)).astype(F32)

            @pl.when(b != line.z)
            def _():
                part[b, 0] = value(slice(b * rows, (b + 1) * rows))

            scatter.computed(b, 0)

    def scatter_step(indices, t):
        for index in indices:
            scatter, _, _, _, own = shared[index]

            def add_own(p, value):
                own[...] = own[...] + value

            scatter.step(t, add_own)

    def gather_start(indices):
        for index in indices:
            _, _, gather, total, own = shared[index]
            total[line.z] = own[...].astype(BF)
            gather.start(total.at[line.z])

    def gather_step(indices, i):
        for index in indices:
            shared[index][2].arrive(line.order(i))

    def collect(indices):
        for index in indices:
            targets[index][...] = shared[index][3][...].reshape(targets[index].shape)

    def line_jobs(indices):
        jobs = [functools.partial(scatter_step, indices, t)
                for t in range(1, 2 * (n - 1) + 1)]
        jobs.append(functools.partial(gather_start, indices))
        jobs += [functools.partial(gather_step, indices, i) for i in range(1, n)]
        jobs.append(functools.partial(collect, indices))
        return jobs

    def small_job():
        for i in range(1, n):
            gather_small.arrive(line.order(i))
        small_o[...] = jnp.sum(small_all[...], axis=0)

    joint_barrier(line, cube)
    for f in folds:
        f.start()
    for i, ref in enumerate(early):
        share(2 + i, lambda rows, ref=ref: ref[rows])
    last = folds[0].stages
    jobs = line_jobs(range(2, 2 + count))

    def after(index):
        fold = folds[index]
        if index == 0:
            small_all[line.z] = fold.mine[0]
            gather_small.start(small_all.at[line.z])
            jobs.append(small_job)
        elif index <= 2:
            share(index - 1, lambda rows: fold.mine[0, rows])
            jobs.extend(line_jobs((index - 1,)))
        else:
            pltpu.make_async_copy(fold.mine.at[0], dw_o, write_sem).start()

    for t in range(len(folds) + last):
        for k in range(last + 1):
            if 0 <= t - k < len(folds):
                folds[t - k].phase(k)
                if k == last:
                    after(t - k)
                for _ in range(2):
                    if jobs and t >= 1:
                        jobs.pop(0)()
    for job in jobs:
        job()
    pltpu.make_async_copy(folds[3].mine.at[0], dw_o, write_sem).wait()
    for f in folds:
        f.finish()
    gather_small.finish()
    for scatter, _, gather, _, _ in shared:
        scatter.finish()
        gather.finish()


def reduce_all(small, out_g, qkv_g, dw, early, n):
    owners, shard, qkv_width = qkv_g.shape
    d_model = out_g.shape[2]
    width = dw.shape[2]
    scratch = fold_scratch(owners, small.shape[1], 128, F32)
    scratch += fold_scratch(owners, shard, d_model, BF)
    scratch += fold_scratch(owners, shard, qkv_width, BF)
    scratch += fold_scratch(owners, shard, width, BF)
    scratch += [pltpu.VMEM((n, small.shape[1], 128), F32)] + gather_sems(n)
    for w in [d_model, qkv_width] + [m.shape[1] for m in early]:
        scratch += [pltpu.VMEM((n, 1, shard // n, w), BF)] * 3
        scratch += [pltpu.VMEM((n, shard // n, w), BF), pltpu.VMEM((shard // n, w), F32)]
        scratch += scatter_sems(n, 1) + gather_sems(n)
    scratch += [pltpu.SemaphoreType.DMA]
    return pl.pallas_call(
        functools.partial(reduce_kernel, n, owners, len(early)),
        out_shape=(
            jax.ShapeDtypeStruct(small.shape[1:], F32),
            jax.ShapeDtypeStruct((shard, d_model), BF),
            jax.ShapeDtypeStruct((shard, qkv_width), BF),
            jax.ShapeDtypeStruct((shard, width), BF),
        ) + tuple(jax.ShapeDtypeStruct(m.shape, BF) for m in early),
        in_specs=[ANY] * 4 + [VM] * len(early),
        out_specs=[VM, VM, VM, ANY] + [VM] * len(early),
        scratch_shapes=scratch,
        compiler_params=params(5),
        cost_estimate=pl.CostEstimate(
            flops=1 << 20, transcendentals=0, bytes_accessed=300 << 20),
        name="reduce_all",
    )(small, out_g, qkv_g, dw, *early)


def normalize(stream, gain):
    return stream * lax.rsqrt(jnp.mean(stream * stream, axis=-1, keepdims=True) + EPSILON) * gain


def normalize_back(grad, stream, gain):
    r = lax.rsqrt(jnp.mean(stream * stream, axis=-1, keepdims=True) + EPSILON)
    u = grad * gain
    back = r * (u - stream * (r * r) * jnp.mean(u * stream, axis=-1, keepdims=True))
    return back, jnp.sum(grad * stream * r, axis=0)


def rotate(heads, cosine, sine):
    half = HEAD // 2
    a, b = heads[..., :half], heads[..., half:]
    return jnp.concatenate([a * cosine - b * sine, b * cosine + a * sine], axis=-1)


def frequencies():
    return jnp.power(ROPE_BASE, -(jnp.arange(HEAD // 2, dtype=F32) * 2.0 / HEAD))


def shards(hidden_in, cotangent, seq_lengths, tile_place, norm_attn, w_qkv, b_qkv, w_out,
           norm_mlp, w_gate, w_up, w_down):
    n = lax.axis_size("context")
    owners = lax.axis_size("fsdp")
    rows, d_model = hidden_in.shape[1:]
    hidden_units = w_gate.shape[2]
    width = -(-hidden_units // 128) * 128
    pad = width - hidden_units
    total = n * rows

    row_index = jnp.arange(total, dtype=jnp.int32)
    tile_order = tile_place[0]
    selector = (
        row_index[:, None] // TILE == jnp.arange(tile_order.shape[0], dtype=jnp.int32)[None, :]
    ).astype(jnp.int32)
    position = jnp.sum(selector * tile_order[None, :], axis=1) * TILE + row_index % TILE
    valid = position < seq_lengths[0]
    offset = lax.axis_index("context") * rows
    my_position = lax.dynamic_slice_in_dim(position, offset, rows)
    my_valid = lax.dynamic_slice_in_dim(valid, offset, rows)
    pos_q = my_position[None, :]
    pos_k = jnp.where(valid, position, 1 << 30)[:, None]
    angles = my_position.astype(F32)[:, None] * frequencies()
    cosine, sine = jnp.cos(angles)[:, None, :], jnp.sin(angles)[:, None, :]

    shard = norm_attn.shape[1]
    bias_shard = b_qkv.shape[1]

    def ffn_shard(l):
        return jnp.stack([
            jnp.pad(m, ((0, 0), (0, pad))) for m in (w_gate[l], w_up[l], w_down[l].T)])

    def packed(parts, lead):
        flat = jnp.concatenate(parts, axis=-1)
        used = flat.shape[-1]
        lines = -(-used // (16 * 128)) * 16
        flat = jnp.pad(flat, ((0, 0),) * (flat.ndim - 1) + ((0, lines * 128 - used),))
        return flat.reshape(lead + (lines, 128))

    small = packed(
        [m.reshape(-1).astype(F32) for m in (norm_attn, norm_mlp, b_qkv)], ())
    first_ffn = ffn_shard(0)
    first_ffn, small = lax.optimization_barrier((first_ffn, small))
    ffn_weights = [lax.all_gather(first_ffn, "fsdp", axis=0, tiled=False)]
    small, qkv_w = spread_all(owners, small, w_qkv[0])
    qkv_weights = [qkv_w.reshape(d_model, -1)]
    small = small.reshape(owners, -1)
    gains_attn, gains_mlp, biases = [], [], []
    for l in range(LAYERS):
        gains_attn.append(small[:, l * shard:(l + 1) * shard].reshape(-1))
        gains_mlp.append(small[:, (LAYERS + l) * shard:(LAYERS + l + 1) * shard].reshape(-1))
        start = 2 * LAYERS * shard + l * bias_shard
        biases.append(small[:, start:start + bias_shard].reshape(-1))

    stream = hidden_in[0].astype(F32)
    kept = []
    for l in range(LAYERS):
        qkv_w, ffn_w = qkv_weights[l], ffn_weights[l]
        if l + 1 < LAYERS:
            ffn_weights.append(lax.all_gather(ffn_shard(l + 1), "fsdp", axis=0, tiled=False))
        normed = normalize(stream, gains_attn[l]).astype(BF)
        projected = jnp.dot(normed, qkv_w, preferred_element_type=F32) + biases[l]
        qk = rotate(
            projected[:, :Q_WIDTH + KV_WIDTH].reshape(rows, QUERY_HEADS + KV_HEADS, HEAD),
            cosine, sine).astype(BF).reshape(rows, Q_WIDTH + KV_WIDTH)
        q = qk[:, :Q_WIDTH]
        kv = jnp.concatenate([qk[:, Q_WIDTH:], projected[:, Q_WIDTH + KV_WIDTH:].astype(BF)], axis=1)
        mixed, lse, kvall, out_w = attention_forward(q, kv, pos_q, pos_k, w_out[l], n, owners)
        out_w = out_w.reshape(Q_WIDTH, d_model)
        middle = stream + jnp.dot(mixed, out_w, preferred_element_type=F32)
        normed_two = normalize(middle, gains_mlp[l]).astype(BF)
        if l + 1 < LAYERS:
            xall, gate, up, y, next_qkv = ffn_forward(normed_two, ffn_w, n, (w_qkv[l + 1],))
            qkv_weights.append(next_qkv.reshape(d_model, -1))
        else:
            xall, gate, up, y = ffn_forward(normed_two, ffn_w, n)
        kept.append((stream, normed, q, kvall, lse, mixed, middle, xall, gate, up,
                     qkv_w, out_w, ffn_w))
        stream = middle + y
    layer_out = stream.astype(BF)[None]

    gradient = cotangent[0].astype(F32) * my_valid[:, None].astype(F32)
    small_grads = [None] * LAYERS
    out_sums, qkv_sums, ffn_sums, down_sums = ([None] * LAYERS for _ in range(4))
    for l in reversed(range(LAYERS)):
        (stream, normed, q, kvall, lse, mixed, middle, xall, gate, up,
         qkv_w, out_w, ffn_w) = kept[l]
        later = (out_grad.reshape(owners, shard, d_model),) if l < LAYERS - 1 else ()
        dw, dw_down, dx, *later_sums = ffn_backward(
            gradient.astype(BF), ffn_w, xall, gate, up, n, later)
        if l < LAYERS - 1:
            out_sums[l + 1], = later_sums
            dx, ffn_sums[l + 1], down_sums[l + 1] = lax.optimization_barrier(
                (dx, ffn_sums[l + 1], down_sums[l + 1]))
        ffn_sums[l] = lax.psum_scatter(dw, "fsdp", scatter_dimension=0, tiled=False)
        if l > 0:
            down_sums[l] = lax.psum_scatter(dw_down, "fsdp", scatter_dimension=0, tiled=False)
        back, gain_two = normalize_back(dx, middle, gains_mlp[l])
        d_middle = gradient + back
        d_low = d_middle.astype(BF)
        d_mixed = jnp.einsum("td,cd->tc", d_low, out_w, preferred_element_type=F32).astype(BF)
        out_grad = jnp.einsum("tc,td->cd", mixed, d_low, preferred_element_type=F32).astype(BF)
        dq, dkv = attention_backward(q, kvall, lse, d_mixed, pos_q, pos_k, n)
        if l < LAYERS - 1:
            dq, qkv_sums[l + 1] = lax.optimization_barrier((dq, qkv_sums[l + 1]))
        d_qk = rotate(
            jnp.concatenate([dq, dkv[:, :KV_WIDTH]], axis=1).reshape(
                rows, QUERY_HEADS + KV_HEADS, HEAD),
            cosine, -sine).reshape(rows, Q_WIDTH + KV_WIDTH)
        d_projected = jnp.concatenate([d_qk, dkv[:, KV_WIDTH:]], axis=1).astype(BF)
        bias_grad = jnp.sum(d_projected.astype(F32), axis=0)
        d_normed = jnp.einsum("tc,dc->td", d_projected, qkv_w, preferred_element_type=F32)
        qkv_grad = jnp.einsum(
            "td,tc->dc", normed, d_projected, preferred_element_type=F32).astype(BF)
        back, gain_one = normalize_back(d_normed, stream, gains_attn[l])
        gradient = d_middle + back
        small_grads[l] = (gain_one, gain_two, bias_grad)
        if l > 0:
            qkv_sums[l] = lax.psum_scatter(qkv_grad, "fsdp", scatter_dimension=0, tiled=True)
    small = packed([
        m.reshape(owners, -1)
        for k in range(3) for m in (small_grads[i][k] for i in range(LAYERS))], (owners,))
    small, out_sums[0], qkv_sums[0], down_sums[0], *early = reduce_all(
        small, out_grad.reshape(owners, shard, d_model),
        qkv_grad.reshape(owners, shard, qkv_grad.shape[1]), dw_down,
        out_sums[1:] + qkv_sums[1:], n)
    out_sums[1:], qkv_sums[1:] = early[:LAYERS - 1], early[LAYERS - 1:]
    small = small.reshape(-1)

    grad_norm_attn = small[:LAYERS * shard].reshape(LAYERS, shard)
    grad_norm_mlp = small[LAYERS * shard:2 * LAYERS * shard].reshape(LAYERS, shard)
    start = 2 * LAYERS * shard
    grad_b_qkv = small[start:start + LAYERS * bias_shard].reshape(LAYERS, bias_shard)

    def stacked(sums, pick=lambda m: m):
        return jnp.stack([pick(m).astype(F32) for m in sums])

    return (
        layer_out,
        gradient[None],
        grad_norm_attn,
        stacked(qkv_sums),
        grad_b_qkv,
        stacked(out_sums),
        grad_norm_mlp,
        stacked(ffn_sums, lambda m: m[0, :, :hidden_units]),
        stacked(ffn_sums, lambda m: m[1, :, :hidden_units]),
        stacked(down_sums, lambda m: m[:, :hidden_units].T),
    )


def solution(mesh):
    return jax.shard_map(
        shards,
        mesh=mesh,
        in_specs=(
            P("fsdp", "context", None),
            P("fsdp", "context", None),
            P("fsdp"),
            P("fsdp", None),
            P(None, "fsdp"),
            P(None, "fsdp", None),
            P(None, "fsdp"),
            P(None, "fsdp", None),
            P(None, "fsdp"),
            P(None, "fsdp", "context"),
            P(None, "fsdp", "context"),
            P(None, "context", "fsdp"),
        ),
        out_specs=(
            P("fsdp", "context", None),
            P("fsdp", "context", None),
            P(None, "fsdp"),
            P(None, "fsdp", None),
            P(None, "fsdp"),
            P(None, "fsdp", None),
            P(None, "fsdp"),
            P(None, "fsdp", "context"),
            P(None, "fsdp", "context"),
            P(None, "context", "fsdp"),
        ),
        check_vma=False,
    )
```

```python
import functools
import math

import jax
import jax.numpy as jnp
from jax import lax
from jax.experimental import pallas as pl
from jax.experimental.pallas import tpu as pltpu
from jax.sharding import PartitionSpec as P

QUERY_HEADS = 12
KV_HEADS = 2
HEAD = 128
LAYERS = 2
TILE = 128
Q_WIDTH = QUERY_HEADS * HEAD
KV_WIDTH = KV_HEADS * HEAD
PER_GROUP = QUERY_HEADS // KV_HEADS
SCALE = 1.0 / math.sqrt(HEAD)
EPSILON = 1e-06
ROPE_BASE = 1000000.0
BF = jnp.bfloat16
F32 = jnp.float32
MESH = pl.DeviceIdType.MESH
VMEM_LIMIT = 66 * 1024 * 1024
ANY = pl.BlockSpec(memory_space=pl.ANY)
VM = pl.BlockSpec(memory_space=pltpu.VMEM)


def dot_nn(a, b):
    return lax.dot_general(a, b, (((1,), (0,)), ((), ())), preferred_element_type=F32)


def dot_nt(a, b):
    return lax.dot_general(a, b, (((1,), (1,)), ((), ())), preferred_element_type=F32)


def dot_tn(a, b):
    return lax.dot_general(a, b, (((0,), (0,)), ((), ())), preferred_element_type=F32)


def lane_tile(width, most):
    best = 128
    for k in range(1, most // 128 + 1):
        if width % (128 * k) == 0:
            best = 128 * k
    return best


class Line:
    def __init__(self, n):
        self.n = n
        self.z = lax.axis_index("context")
        self.right = lax.rem(self.z + 1, n)
        self.left = lax.rem(self.z + n - 1, n)
        self.has_right = self.z < n - 1
        self.has_left = self.z > 0

    def barrier(self):
        bar = pltpu.get_barrier_semaphore()

        @pl.when(self.has_right)
        def _():
            pl.semaphore_signal(bar, inc=1, device_id={"context": self.right}, device_id_type=MESH)

        @pl.when(self.has_left)
        def _():
            pl.semaphore_signal(bar, inc=1, device_id={"context": self.left}, device_id_type=MESH)

        both = self.has_right & self.has_left

        @pl.when(both)
        def _():
            pl.semaphore_wait(bar, 2)

        @pl.when(jnp.logical_not(both))
        def _():
            pl.semaphore_wait(bar, 1)

    def order(self, i):
        z, n = self.z, self.n
        short = jnp.minimum(z, n - 1 - z)
        j = i - 1
        paired = j < 2 * short
        k = jnp.where(paired, j // 2 + 1, j - short + 1)
        goes_left = jnp.where(paired, lax.rem(j, 2) == 0, z > n - 1 - z)
        return jnp.where(i == 0, z, jnp.where(goes_left, z - k, z + k))


def remote(src, dst, send, recv, target):
    return pltpu.make_async_remote_copy(
        src_ref=src, dst_ref=dst, send_sem=send, recv_sem=recv,
        device_id={"context": target}, device_id_type=MESH,
    )


class Gather:
    def __init__(self, line, slots, send_r, send_l, recv):
        self.line, self.slots = line, slots
        self.send_r, self.send_l, self.recv = send_r, send_l, recv

    def _right(self, b, src):
        return remote(src, self.slots.at[b], self.send_r.at[b], self.recv.at[b], self.line.right)

    def _left(self, b, src):
        return remote(src, self.slots.at[b], self.send_l.at[b], self.recv.at[b], self.line.left)

    def start(self, own):
        line = self.line

        @pl.when(line.has_right)
        def _():
            self._right(line.z, own).start()

        @pl.when(line.has_left)
        def _():
            self._left(line.z, own).start()

    def arrive(self, b):
        line = self.line
        self._right(b, self.slots.at[b]).wait_recv()

        @pl.when((b < line.z) & line.has_right)
        def _():
            self._right(b, self.slots.at[b]).start()

        @pl.when((b > line.z) & line.has_left)
        def _():
            self._left(b, self.slots.at[b]).start()

    def finish(self):
        line = self.line
        for b in range(line.n):
            @pl.when((b <= line.z) & line.has_right)
            def _():
                self._right(b, self.slots.at[b]).wait_send()

            @pl.when((b >= line.z) & line.has_left)
            def _():
                self._left(b, self.slots.at[b]).wait_send()


class Scatter:
    def __init__(self, line, pieces, part, from_left, from_right, send_r, send_l, recv_l, recv_r):
        self.line, self.pieces, self.part = line, pieces, part
        self.from_left, self.from_right = from_left, from_right
        self.send_r, self.send_l, self.recv_l, self.recv_r = send_r, send_l, recv_l, recv_r

    def _right(self, b, p):
        return remote(self.part.at[b, p], self.from_left.at[b, p], self.send_r.at[b, p],
                      self.recv_l.at[b, p], self.line.right)

    def _left(self, b, p):
        return remote(self.part.at[b, p], self.from_right.at[b, p], self.send_l.at[b, p],
                      self.recv_r.at[b, p], self.line.left)

    def computed(self, b, p):
        line = self.line

        @pl.when((line.z == 0) & (b > 0))
        def _():
            self._right(b, p).start()

        @pl.when((line.z == line.n - 1) & (b < line.n - 1))
        def _():
            self._left(b, p).start()

    def steps(self):
        return range(1, 2 * (self.line.n - 1) + 1)

    def step(self, t, add_own):
        line = self.line
        n, z = line.n, line.z
        b_left = t - z

        @pl.when(line.has_left & (b_left >= z) & (b_left < n))
        def _():
            for p in range(self.pieces):
                self._right(b_left, p).wait_recv()

                @pl.when(b_left == z)
                def _():
                    add_own(p, self.from_left[b_left, p].astype(F32))

                @pl.when(b_left != z)
                def _():
                    self.part[b_left, p] = (
                        self.part[b_left, p].astype(F32) + self.from_left[b_left, p].astype(F32)
                    ).astype(BF)
                    self._right(b_left, p).start()

        b_right = 2 * (n - 1) - t - z

        @pl.when(line.has_right & (b_right >= 0) & (b_right <= z))
        def _():
            for p in range(self.pieces):
                self._left(b_right, p).wait_recv()

                @pl.when(b_right == z)
                def _():
                    add_own(p, self.from_right[b_right, p].astype(F32))

                @pl.when(b_right != z)
                def _():
                    self.part[b_right, p] = (
                        self.part[b_right, p].astype(F32) + self.from_right[b_right, p].astype(F32)
                    ).astype(BF)
                    self._left(b_right, p).start()

    def finish(self):
        line = self.line
        for b in range(line.n):
            @pl.when((b > line.z) & line.has_right)
            def _():
                for p in range(self.pieces):
                    self._right(b, p).wait_send()

            @pl.when((b < line.z) & line.has_left)
            def _():
                for p in range(self.pieces):
                    self._left(b, p).wait_send()


def gather_sems(n):
    return [pltpu.SemaphoreType.DMA((n,))] * 3


def scatter_sems(n, pieces):
    return [pltpu.SemaphoreType.DMA((n, pieces))] * 4


def params(cid):
    return pltpu.CompilerParams(
        collective_id=cid, has_side_effects=True, vmem_limit_bytes=VMEM_LIMIT
    )


def bits_of(owners):
    return [1 << i for i in range(owners.bit_length() - 1)]


class Cube:
    def __init__(self, owners):
        self.owners = owners
        self.me = lax.axis_index("fsdp")
        self.bits = bits_of(owners)
        self.chip_bits = [b // 2 for b in self.bits[1:]]
        self.chips = owners // 2

    def flip(self, mask):
        index = self.me
        for b in self.bits:
            if mask & b:
                index = index + b - 2 * b * lax.rem(self.me // b, 2)
        return index

    def signal(self, bar):
        for b in self.bits:
            pl.semaphore_signal(bar, inc=1, device_id={"fsdp": self.flip(b)}, device_id_type=MESH)

    def order(self, half):
        return self.chip_bits[::-1] if half == 0 else self.chip_bits

    def plan(self):
        steps = {}
        for half in (0, 1):
            order, slot = self.order(half), 0
            for stage, bit in enumerate(order):
                rest = [0]
                for other in order[stage + 1:]:
                    rest = rest + [m | other for m in rest]
                steps[half, stage] = (bit, rest, slot)
                slot += len(rest)
        return steps


def joint_barrier(line, cube):
    bar = pltpu.get_barrier_semaphore()
    cube.signal(bar)
    peers = len(cube.bits)

    @pl.when(line.has_right)
    def _():
        pl.semaphore_signal(bar, inc=1, device_id={"context": line.right}, device_id_type=MESH)

    @pl.when(line.has_left)
    def _():
        pl.semaphore_signal(bar, inc=1, device_id={"context": line.left}, device_id_type=MESH)

    both = line.has_right & line.has_left

    @pl.when(both)
    def _():
        pl.semaphore_wait(bar, peers + 2)

    @pl.when(jnp.logical_not(both))
    def _():
        pl.semaphore_wait(bar, peers + 1)


class Spread:
    def __init__(self, cube, own, full, own_sem, send, recv, core_send, core_recv):
        self.cube, self.own, self.full = cube, own, full
        self.own_sem, self.send, self.recv = own_sem, send, recv
        self.core_send, self.core_recv = core_send, core_recv
        self.half = own.shape[0] // 2
        self.stages = len(cube.chip_bits)

    def _rows(self, half):
        return pl.ds(half * self.half, self.half)

    def _block(self, half, mask):
        return self.full.at[self.cube.flip(mask), self._rows(half)]

    def _source(self, half, mask):
        return self._block(half, 2 * mask) if mask else self.own.at[self._rows(half)]

    def _masks(self, half, stage):
        masks = [0]
        for bit in self.cube.order(half)[:stage]:
            masks = masks + [m | bit for m in masks]
        return masks

    def _hop(self, half, stage, mask):
        bit = self.cube.order(half)[stage]
        return pltpu.make_async_remote_copy(
            src_ref=self._source(half, mask), dst_ref=self._block(half, 2 * mask),
            send_sem=self.send.at[half, mask | bit], recv_sem=self.recv.at[half, mask | bit],
            device_id={"fsdp": self.cube.flip(2 * bit)}, device_id_type=MESH)

    def _arrival(self, half, mask):
        block = self._block(half, 2 * mask)
        return pltpu.make_async_remote_copy(
            src_ref=block, dst_ref=block,
            send_sem=self.send.at[half, mask], recv_sem=self.recv.at[half, mask],
            device_id={"fsdp": self.cube.flip(1)}, device_id_type=MESH)

    def _core(self, half, mask):
        return pltpu.make_async_remote_copy(
            src_ref=self._source(half, mask), dst_ref=self._block(half, 2 * mask),
            send_sem=self.core_send.at[half, mask], recv_sem=self.core_recv.at[half, mask],
            device_id={"fsdp": self.cube.flip(1)}, device_id_type=MESH)

    def _core_arrival(self, half, mask):
        block = self._block(half, 2 * mask | 1)
        return pltpu.make_async_remote_copy(
            src_ref=block, dst_ref=block,
            send_sem=self.core_send.at[half, mask], recv_sem=self.core_recv.at[half, mask],
            device_id={"fsdp": self.cube.flip(1)}, device_id_type=MESH)

    def _own_copy(self):
        return pltpu.make_async_copy(self.own, self.full.at[self.cube.me], self.own_sem)

    def start(self):
        for stage in range(self.stages):
            for half in (0, 1):
                self._hop(half, stage, 0).start()
        for half in (0, 1):
            self._core(half, 0).start()
        self._own_copy().start()

    def phase(self, k):
        for half in (0, 1):
            bit = self.cube.order(half)[k - 1]
            for m in self._masks(half, k - 1):
                self._arrival(half, m | bit).wait_recv()
                for stage in range(k, self.stages):
                    self._hop(half, stage, m | bit).start()
                self._core(half, m | bit).start()

    def finish(self):
        self._own_copy().wait()
        for half in (0, 1):
            for m in range(self.cube.chips):
                self._core_arrival(half, m).wait_recv()
                self._core(half, m).wait_send()
            for stage in range(self.stages):
                for m in self._masks(half, stage):
                    self._hop(half, stage, m).wait_send()


SPREAD_SEMS = 5


def spread_sems(owners):
    chips = owners // 2
    return [pltpu.SemaphoreType.DMA] + [pltpu.SemaphoreType.DMA((2, chips))] * 4


def spread_shapes(owners, shards):
    return tuple(jax.ShapeDtypeStruct((owners,) + m.shape, m.dtype) for m in shards)


def spread_kernel(owners, count, *refs):
    cube = Cube(owners)
    spreads = [
        Spread(cube, refs[i], refs[count + i],
               *refs[2 * count + SPREAD_SEMS * i:2 * count + SPREAD_SEMS * (i + 1)])
        for i in range(count)]
    bar = pltpu.get_barrier_semaphore()
    cube.signal(bar)
    pl.semaphore_wait(bar, len(cube.bits))
    for s in spreads:
        s.start()
    for k in range(1, len(cube.chip_bits) + 1):
        for s in spreads:
            s.phase(k)
    for s in spreads:
        s.finish()


def spread_all(owners, *shards):
    count = len(shards)
    return pl.pallas_call(
        functools.partial(spread_kernel, owners, count),
        out_shape=spread_shapes(owners, shards),
        in_specs=[VM] * count,
        out_specs=[ANY] * count,
        scratch_shapes=spread_sems(owners) * count,
        compiler_params=params(6),
        cost_estimate=pl.CostEstimate(
            flops=1 << 20, transcendentals=0, bytes_accessed=150 << 20),
        name="spread_all",
    )(*shards)


def ffn_forward_kernel(n, pieces, count, *refs):
    x_ref, w_ref = refs[:2]
    next_own = refs[2:2 + count]
    xall_ref, gate_ref, up_ref, y_ref = refs[2 + count:6 + count]
    next_full = refs[6 + count:6 + 2 * count]
    (w_v, xbuf, gbuf, ubuf, hbuf, part, from_l, from_r,
     w_sem, x_sem, out_sem, *sems) = refs[6 + 2 * count:]
    line = Line(n)
    z = line.z
    owners, _, rows, width = w_ref.shape
    d_model = x_ref.shape[1]
    tile = lane_tile(width, 256)
    piece = d_model // pieces
    gather = Gather(line, xbuf, *sems[:3])
    scatter = Scatter(line, pieces, part, from_l, from_r, *sems[3:7])
    spreads = []
    stages = 0
    if count:
        cube = Cube(owners)
        stages = len(cube.chip_bits)
        for i in range(count):
            at = 7 + SPREAD_SEMS * i
            spreads.append(Spread(cube, next_own[i], next_full[i], *sems[at:at + SPREAD_SEMS]))

    def w_copy(k, f):
        return pltpu.make_async_copy(
            w_ref.at[f, k], w_v.at[k, pl.ds(f * rows, rows)], w_sem.at[k, f]
        )

    def x_out(b):
        return pltpu.make_async_copy(xbuf.at[b], xall_ref.at[b], x_sem.at[b])

    if count:
        joint_barrier(line, cube)
    else:
        line.barrier()
    gather.start(x_ref)
    for s in spreads:
        s.start()
    for k in range(3):
        for f in range(owners):
            w_copy(k, f).start()
    xbuf[z] = x_ref[...]
    for k in range(3):
        for f in range(owners):
            w_copy(k, f).wait()

    @pl.loop(0, n)
    def _(i):
        b = line.order(i)

        @pl.when(i > 0)
        def _():
            gather.arrive(b)

        x_out(b).start()
        slot = lax.rem(i, 2)
        g_copy = pltpu.make_async_copy(gbuf.at[slot], gate_ref.at[b], out_sem.at[0, slot])
        u_copy = pltpu.make_async_copy(ubuf.at[slot], up_ref.at[b], out_sem.at[1, slot])

        @pl.when(i > 1)
        def _():
            g_copy.wait()
            u_copy.wait()

        @pl.loop(0, width // tile)
        def _(j):
            cols = pl.ds(pl.multiple_of(j * tile, tile), tile)
            xb = xbuf[b]
            gate = dot_nn(xb, w_v[0, :, cols])
            up = dot_nn(xb, w_v[1, :, cols])
            gbuf[slot, :, cols] = gate.astype(BF)
            ubuf[slot, :, cols] = up.astype(BF)
            hbuf[:, cols] = (gate * jax.nn.sigmoid(gate) * up).astype(BF)

        g_copy.start()
        u_copy.start()
        for p in range(pieces):
            out = dot_nt(hbuf[...], w_v[2, pl.ds(p * piece, piece)])

            @pl.when(b == z)
            def _():
                y_ref[:, p * piece:(p + 1) * piece] = out

            @pl.when(b != z)
            def _():
                part[b, p] = out.astype(BF)

            scatter.computed(b, p)

        if spreads:
            @pl.when(i == n // 2)
            def _():
                for s in spreads:
                    s.phase(1)

    def add_own(p, value):
        cols = slice(p * piece, (p + 1) * piece)
        y_ref[:, cols] = y_ref[:, cols] + value

    passed = 2
    for t in scatter.steps():
        scatter.step(t, add_own)
        if t >= 4 and t % 2 == 0 and passed <= stages:
            for s in spreads:
                s.phase(passed)
            passed += 1
    for k in range(passed, stages + 1):
        for s in spreads:
            s.phase(k)
    for i in range(max(0, n - 2), n):
        slot = i % 2
        pltpu.make_async_copy(gbuf.at[slot], gate_ref.at[0], out_sem.at[0, slot]).wait()
        pltpu.make_async_copy(ubuf.at[slot], up_ref.at[0], out_sem.at[1, slot]).wait()
    for b in range(n):
        x_out(b).wait()
    gather.finish()
    scatter.finish()
    for s in spreads:
        s.finish()


def ffn_forward(x, w, n, following=()):
    rows, d_model = x.shape
    owners, _, shard, width = w.shape
    pieces = 6
    piece = d_model // pieces
    count = len(following)
    return pl.pallas_call(
        functools.partial(ffn_forward_kernel, n, pieces, count),
        out_shape=(
            jax.ShapeDtypeStruct((n, rows, d_model), BF),
            jax.ShapeDtypeStruct((n, rows, width), BF),
            jax.ShapeDtypeStruct((n, rows, width), BF),
            jax.ShapeDtypeStruct((rows, d_model), F32),
        ) + spread_shapes(owners, following),
        in_specs=[VM, ANY] + [VM] * count,
        out_specs=[ANY, ANY, ANY, VM] + [ANY] * count,
        scratch_shapes=[
            pltpu.VMEM((3, d_model, width), BF),
            pltpu.VMEM((n, rows, d_model), BF),
            pltpu.VMEM((2, rows, width), BF),
            pltpu.VMEM((2, rows, width), BF),
            pltpu.VMEM((rows, width), BF),
            pltpu.VMEM((n, pieces, rows, piece), BF),
            pltpu.VMEM((n, pieces, rows, piece), BF),
            pltpu.VMEM((n, pieces, rows, piece), BF),
            pltpu.SemaphoreType.DMA((3, owners)),
            pltpu.SemaphoreType.DMA((n,)),
            pltpu.SemaphoreType.DMA((2, 2)),
        ] + gather_sems(n) + scatter_sems(n, pieces) + spread_sems(owners) * count,
        compiler_params=params(7 if count else 1),
        cost_estimate=pl.CostEstimate(
            flops=6 * n * rows * d_model * width, transcendentals=n * rows * width,
            bytes_accessed=60 << 20),
        name="ffn_forward",
    )(x, w, *following)


def ffn_backward_kernel(n, pieces, groups, g_ref, w_ref, xall_ref, gate_ref, up_ref, dw_ref, dx_ref,
                        w_v, gbuf, xv, gate_v, up_v, hid_v, part, from_l, from_r, stage,
                        w_sem, in_sem, out_sem, *sems):
    line = Line(n)
    z = line.z
    owners, _, shard, width = w_ref.shape
    rows, d_model = g_ref.shape
    tile = lane_tile(width, 256)
    piece = d_model // pieces
    gather = Gather(line, gbuf, *sems[:3])
    scatter = Scatter(line, pieces, part, from_l, from_r, *sems[3:])

    def w_copy(k, f):
        return pltpu.make_async_copy(
            w_ref.at[f, k], w_v.at[k, pl.ds(f * shard, shard)], w_sem.at[k, f]
        )

    def loads(b):
        return (
            pltpu.make_async_copy(gate_ref.at[b], gate_v.at[b], in_sem.at[0, b]),
            pltpu.make_async_copy(up_ref.at[b], up_v.at[b], in_sem.at[1, b]),
        )

    def x_load(b):
        return pltpu.make_async_copy(xall_ref.at[b], xv.at[b], in_sem.at[2, b])

    line.barrier()
    gather.start(g_ref)
    for f in range(owners):
        w_copy(2, f).start()
    for c in loads(z):
        c.start()
    for k in range(2):
        for f in range(owners):
            w_copy(k, f).start()
    for b in range(n):
        @pl.when(b != z)
        def _():
            for c in loads(b):
                c.start()
    for b in range(n):
        x_load(b).start()
    gbuf[z] = g_ref[...]
    for k in (2, 0, 1):
        for f in range(owners):
            w_copy(k, f).wait()

    @pl.loop(0, n)
    def _(i):
        b = line.order(i)

        @pl.when(i > 0)
        def _():
            gather.arrive(b)

        for c in loads(b):
            c.wait()

        @pl.loop(0, width // tile)
        def _(j):
            cols = pl.ds(pl.multiple_of(j * tile, tile), tile)
            d_hidden = dot_nn(gbuf[b], w_v[2, :, cols])
            gate = gate_v[b, :, cols].astype(F32)
            up = up_v[b, :, cols].astype(F32)
            sig = jax.nn.sigmoid(gate)
            act = gate * sig
            hid_v[b, :, cols] = (act * up).astype(BF)
            gate_v[b, :, cols] = (d_hidden * up * (sig + act * (1.0 - sig))).astype(BF)
            up_v[b, :, cols] = (d_hidden * act).astype(BF)

        for p in range(pieces):
            sl = pl.ds(p * piece, piece)
            out = dot_nt(gate_v[b], w_v[0, sl]) + dot_nt(up_v[b], w_v[1, sl])

            @pl.when(b == z)
            def _():
                dx_ref[:, p * piece:(p + 1) * piece] = out

            @pl.when(b != z)
            def _():
                part[b, p] = out.astype(BF)

            scatter.computed(b, p)

    def add_own(p, value):
        cols = slice(p * piece, (p + 1) * piece)
        dx_ref[:, cols] = dx_ref[:, cols] + value

    for b in range(n):
        x_load(b).wait()

    group = d_model // groups
    per = group // shard

    def dw_copies(k, q, slot):
        return [
            pltpu.make_async_copy(
                stage.at[slot, pl.ds(s * shard, shard)], dw_ref.at[q * per + s, k],
                out_sem.at[slot, s])
            for s in range(per)
        ]

    def weight_unit(unit):
        k, q = unit // groups, unit % groups
        slot = unit % 2
        left = (xv, xv, gbuf)[k]
        right = (gate_v, up_v, hid_v)[k]
        if unit >= 2:
            for c in dw_copies((unit - 2) // groups, (unit - 2) % groups, slot):
                c.wait()
        lt = left[:, :, q * group:(q + 1) * group].reshape(n * rows, group)

        @pl.loop(0, width // tile)
        def _(j):
            cols = pl.ds(pl.multiple_of(j * tile, tile), tile)
            stage[slot, :, cols] = dot_tn(
                lt, right[:, :, cols].reshape(n * rows, tile)
            ).astype(BF)

        for c in dw_copies(k, q, slot):
            c.start()

    units = 3 * groups
    steps = list(scatter.steps())
    done = 0
    for index, t in enumerate(steps):
        scatter.step(t, add_own)
        until = units * (index + 1) // len(steps)
        while done < until:
            weight_unit(done)
            done += 1
    for unit in range(units - 2, units):
        for c in dw_copies(unit // groups, unit % groups, unit % 2):
            c.wait()
    gather.finish()
    scatter.finish()


def ffn_backward(g, w, xall, gate, up, n):
    rows, d_model = g.shape
    owners, _, shard, width = w.shape
    pieces, groups = 6, 4
    piece = d_model // pieces
    per = d_model // groups // shard
    return pl.pallas_call(
        functools.partial(ffn_backward_kernel, n, pieces, groups),
        out_shape=(
            jax.ShapeDtypeStruct((owners, 3, shard, width), BF),
            jax.ShapeDtypeStruct((rows, d_model), F32),
        ),
        in_specs=[VM, ANY, ANY, ANY, ANY],
        out_specs=[ANY, VM],
        scratch_shapes=[
            pltpu.VMEM((3, d_model, width), BF),
            pltpu.VMEM((n, rows, d_model), BF),
            pltpu.VMEM((n, rows, d_model), BF),
            pltpu.VMEM((n, rows, width), BF),
            pltpu.VMEM((n, rows, width), BF),
            pltpu.VMEM((n, rows, width), BF),
            pltpu.VMEM((n, pieces, rows, piece), BF),
            pltpu.VMEM((n, pieces, rows, piece), BF),
            pltpu.VMEM((n, pieces, rows, piece), BF),
            pltpu.VMEM((2, d_model // groups, width), BF),
            pltpu.SemaphoreType.DMA((3, owners)),
            pltpu.SemaphoreType.DMA((3, n)),
            pltpu.SemaphoreType.DMA((2, per)),
        ] + gather_sems(n) + scatter_sems(n, pieces),
        compiler_params=params(2),
        cost_estimate=pl.CostEstimate(
            flops=12 * n * rows * d_model * width, transcendentals=n * rows * width,
            bytes_accessed=100 << 20),
        name="ffn_backward",
    )(g, w, xall, gate, up)


def half_turn(x):
    return pltpu.roll(x, HEAD // 2, 1)


def attention_forward_kernel(n, owners, count, proj_ref, cos_ref, sin_ref, pq_ref, pk_ref, *refs):
    own = refs[:count]
    mixed_ref, lse_ref, kvall_ref, q_ref = refs[count:count + 4]
    full = refs[count + 4:2 * count + 4]
    kvbuf, vt, *sems = refs[2 * count + 4:]
    line = Line(n)
    z = line.z
    rows = q_ref.shape[0]
    total = n * rows
    gather = Gather(line, kvbuf, *sems[:3])

    def rotated(h):
        x = proj_ref[:, h * HEAD:(h + 1) * HEAD]
        return (x * cos_ref[...] + half_turn(x) * sin_ref[...]).astype(BF)

    for g in range(KV_HEADS):
        kvbuf[z, :, g * HEAD:(g + 1) * HEAD] = rotated(QUERY_HEADS + g)
    kvbuf[z, :, KV_WIDTH:] = proj_ref[:, Q_WIDTH + KV_WIDTH:].astype(BF)
    spreads = []
    stages = 0
    if count:
        cube = Cube(owners)
        stages = len(cube.chip_bits)
        for i in range(count):
            at = 3 + SPREAD_SEMS * i
            spreads.append(Spread(cube, own[i], full[i], *sems[at:at + SPREAD_SEMS]))
        joint_barrier(line, cube)
    else:
        line.barrier()
    gather.start(kvbuf.at[z])
    for s in spreads:
        s.start()
    for h in range(QUERY_HEADS):
        q_ref[:, h * HEAD:(h + 1) * HEAD] = rotated(h)
    for i in range(1, n):
        gather.arrive(line.order(i))
    kvall_ref[...] = kvbuf[...]
    allowed = pk_ref[...] <= pq_ref[...]
    for g in range(KV_HEADS):
        v = kvbuf[:, :, KV_WIDTH + g * HEAD:KV_WIDTH + (g + 1) * HEAD].reshape(total, HEAD)
        vt[g] = v.T
    for g in range(KV_HEADS):
        for r in range(PER_GROUP):
            h = g * PER_GROUP + r
            k = kvbuf[:, :, g * HEAD:(g + 1) * HEAD].reshape(total, HEAD)
            s = dot_nt(k, q_ref[:, h * HEAD:(h + 1) * HEAD]) * SCALE
            s = jnp.where(allowed, s, -1e30)
            top = jnp.max(s, axis=0, keepdims=True)
            e = jnp.exp(s - top)
            den = jnp.sum(e, axis=0, keepdims=True)
            o = dot_nn(vt[g], e.astype(BF)) / den
            mixed_ref[:, h * HEAD:(h + 1) * HEAD] = o.T.astype(BF)
            lse_ref[h:h + 1, :] = top + jnp.log(den)
            if h == 5 and stages:
                for sp in spreads:
                    sp.phase(1)
    for k in range(2, stages + 1):
        for sp in spreads:
            sp.phase(k)
    gather.finish()
    for sp in spreads:
        sp.finish()


def attention_forward(projected, cosine, sine, pos_q, pos_k, n, owners, following=()):
    rows = projected.shape[0]
    count = len(following)
    return pl.pallas_call(
        functools.partial(attention_forward_kernel, n, owners, count),
        out_shape=(
            jax.ShapeDtypeStruct((rows, Q_WIDTH), BF),
            jax.ShapeDtypeStruct((16, rows), F32),
            jax.ShapeDtypeStruct((n, rows, 2 * KV_WIDTH), BF),
            jax.ShapeDtypeStruct((rows, Q_WIDTH), BF),
        ) + spread_shapes(owners, following),
        in_specs=[VM] * (5 + count),
        out_specs=[VM] * 4 + [ANY] * count,
        scratch_shapes=[
            pltpu.VMEM((n, rows, 2 * KV_WIDTH), BF),
            pltpu.VMEM((KV_HEADS, HEAD, n * rows), BF),
        ] + gather_sems(n) + spread_sems(owners) * count,
        compiler_params=params(9 if count else 3),
        cost_estimate=pl.CostEstimate(
            flops=4 * n * rows * rows * Q_WIDTH, transcendentals=n * rows * rows * QUERY_HEADS,
            bytes_accessed=16 << 20),
        name="attention_forward",
    )(projected, cosine, sine, pos_q, pos_k, *following)


def attention_backward_kernel(n, q_ref, kvall_ref, lse_ref, dm_ref, cos_ref, sin_ref, pq_ref,
                              pk_ref, dproj_ref, dkv_ref, kt, dk_acc, dv_acc, part,
                              from_l, from_r, *sems):
    line = Line(n)
    z = line.z
    rows = q_ref.shape[0]
    total = n * rows
    pieces = KV_HEADS
    scatter = Scatter(line, pieces, part, from_l, from_r, *sems)
    line.barrier()

    def rotated_back(x):
        return (x * cos_ref[...] - half_turn(x) * sin_ref[...]).astype(BF)

    allowed = pk_ref[...] <= pq_ref[...]
    for g in range(KV_HEADS):
        k = kvall_ref[:, :, g * HEAD:(g + 1) * HEAD].reshape(total, HEAD)
        kt[g] = k.T
    for g in range(KV_HEADS):
        for r in range(PER_GROUP):
            h = g * PER_GROUP + r
            cols = slice(h * HEAD, (h + 1) * HEAD)
            k = kvall_ref[:, :, g * HEAD:(g + 1) * HEAD].reshape(total, HEAD)
            v = kvall_ref[:, :, KV_WIDTH + g * HEAD:KV_WIDTH + (g + 1) * HEAD].reshape(total, HEAD)
            q = q_ref[:, cols]
            dm = dm_ref[:, cols]
            s = dot_nt(k, q) * SCALE
            pr = jnp.where(allowed, jnp.exp(s - lse_ref[h:h + 1, :]), 0.0)
            dp = dot_nt(v, dm)
            delta = jnp.sum(pr * dp, axis=0, keepdims=True)
            ds = (pr * (dp - delta) * SCALE).astype(BF)
            dv = dot_nn(pr.astype(BF), dm)
            dk = dot_nn(ds, q)
            if r == 0:
                dk_acc[...] = dk
                dv_acc[...] = dv
            else:
                dk_acc[...] += dk
                dv_acc[...] += dv
            dproj_ref[:, cols] = rotated_back(dot_nn(kt[g], ds).T)
        for b in range(n):
            sl = slice(b * rows, (b + 1) * rows)

            @pl.when(b == z)
            def _():
                dkv_ref[:, g * HEAD:(g + 1) * HEAD] = dk_acc[sl]
                dkv_ref[:, KV_WIDTH + g * HEAD:KV_WIDTH + (g + 1) * HEAD] = dv_acc[sl]

            @pl.when(b != z)
            def _():
                part[b, g, :, 0:HEAD] = dk_acc[sl].astype(BF)
                part[b, g, :, HEAD:2 * HEAD] = dv_acc[sl].astype(BF)

            scatter.computed(b, g)

    def add_own(p, value):
        a = slice(p * HEAD, (p + 1) * HEAD)
        c = slice(KV_WIDTH + p * HEAD, KV_WIDTH + (p + 1) * HEAD)
        dkv_ref[:, a] = dkv_ref[:, a] + value[:, :HEAD]
        dkv_ref[:, c] = dkv_ref[:, c] + value[:, HEAD:]

    for t in scatter.steps():
        scatter.step(t, add_own)
    for g in range(KV_HEADS):
        cols = slice(Q_WIDTH + g * HEAD, Q_WIDTH + (g + 1) * HEAD)
        dproj_ref[:, cols] = rotated_back(dkv_ref[:, g * HEAD:(g + 1) * HEAD])
    dproj_ref[:, Q_WIDTH + KV_WIDTH:] = dkv_ref[:, KV_WIDTH:].astype(BF)
    scatter.finish()


def attention_backward(q, kvall, lse, dm, cosine, sine, pos_q, pos_k, n):
    rows = q.shape[0]
    return pl.pallas_call(
        functools.partial(attention_backward_kernel, n),
        out_shape=jax.ShapeDtypeStruct((rows, Q_WIDTH + 2 * KV_WIDTH), BF),
        in_specs=[VM] * 8,
        out_specs=VM,
        scratch_shapes=[
            pltpu.VMEM((rows, 2 * KV_WIDTH), F32),
            pltpu.VMEM((KV_HEADS, HEAD, n * rows), BF),
            pltpu.VMEM((n * rows, HEAD), F32),
            pltpu.VMEM((n * rows, HEAD), F32),
        ] + [pltpu.VMEM((n, KV_HEADS, rows, 2 * HEAD), BF)] * 3 + scatter_sems(n, KV_HEADS),
        compiler_params=params(4),
        cost_estimate=pl.CostEstimate(
            flops=10 * n * rows * rows * Q_WIDTH, transcendentals=n * rows * rows * QUERY_HEADS,
            bytes_accessed=16 << 20),
        name="attention_backward",
    )(q, kvall, lse, dm, cosine, sine, pos_q, pos_k)


class Fold:
    def __init__(self, cube, src, mine, first, later, load_sem, send1, recv1, send2, recv2):
        self.cube, self.src = cube, src
        self.mine, self.first, self.later = mine, first, later
        self.load_sem, self.send1, self.recv1 = load_sem, send1, recv1
        self.send2, self.recv2 = send2, recv2
        self.rows = mine.shape[1]
        self.half = self.rows // 2
        self.steps = cube.plan()
        self.stages = len(cube.chip_bits)

    def _load(self, d):
        return pltpu.make_async_copy(
            self.src(self.cube.flip(2 * d)), self.mine.at[d], self.load_sem.at[d])

    def _core(self, d):
        return pltpu.make_async_remote_copy(
            src_ref=self.src(self.cube.flip(2 * d | 1)), dst_ref=self.first.at[d],
            send_sem=self.send1.at[d], recv_sem=self.recv1.at[d],
            device_id={"fsdp": self.cube.flip(1)}, device_id_type=MESH)

    def _hop(self, half, stage, index):
        bit, rest, slot = self.steps[half, stage]
        rows = pl.ds(half * self.half, self.half)
        return pltpu.make_async_remote_copy(
            src_ref=self.mine.at[bit | rest[index], rows],
            dst_ref=self.later.at[half, slot + index],
            send_sem=self.send2.at[half, slot + index],
            recv_sem=self.recv2.at[half, slot + index],
            device_id={"fsdp": self.cube.flip(2 * bit)}, device_id_type=MESH)

    def _hops(self, stage):
        return [self._hop(half, stage, i)
                for half in (0, 1) for i in range(len(self.steps[half, stage][1]))]

    def _add(self, d, base, size, other):
        dtype = self.mine.dtype
        strip = 48 if size % 48 == 0 else size

        @pl.loop(0, size // strip)
        def _(i):
            into = pl.ds(pl.multiple_of(base + i * strip, 8), strip)
            rows = pl.ds(pl.multiple_of(i * strip, 8), strip)
            self.mine[d, into] = (
                self.mine[d, into].astype(F32) + other(rows).astype(F32)).astype(dtype)

    def start(self):
        for d in range(self.cube.chips):
            self._core(d).start()
        for d in range(self.cube.chips):
            self._load(d).start()

    def phase(self, k):
        if k == 0:
            for d in range(self.cube.chips):
                self._load(d).wait()
                self._core(d).wait_recv()
                self._add(d, 0, self.rows, lambda rows, d=d: self.first[d, rows])
        else:
            for half in (0, 1):
                _, rest, slot = self.steps[half, k - 1]
                for i, e in enumerate(rest):
                    self._hop(half, k - 1, i).wait_recv()
                    self._add(e, half * self.half, self.half,
                              lambda rows, h=half, j=slot + i: self.later[h, j, rows])
        if k < self.stages:
            for c in self._hops(k):
                c.start()

    def finish(self):
        for d in range(self.cube.chips):
            self._core(d).wait_send()
        for stage in range(self.stages):
            for c in self._hops(stage):
                c.wait_send()


def fold_scratch(owners, rows, width, dtype):
    chips = owners // 2
    return [
        pltpu.VMEM((chips, rows, width), dtype),
        pltpu.VMEM((chips, rows, width), dtype),
        pltpu.VMEM((2, chips - 1, rows // 2, width), dtype),
        pltpu.SemaphoreType.DMA((chips,)),
        pltpu.SemaphoreType.DMA((chips,)),
        pltpu.SemaphoreType.DMA((chips,)),
        pltpu.SemaphoreType.DMA((2, chips - 1)),
        pltpu.SemaphoreType.DMA((2, chips - 1)),
    ]


FOLD_REFS = 8


def reduce_kernel(n, owners, small_ref, out_ref, qkv_ref, dw_ref, early_out, early_qkv,
                  small_o, out_o, qkv_o, dw_o, early_out_o, early_qkv_o, *refs):
    line = Line(n)
    cube = Cube(owners)
    refs = list(refs)

    def take(count):
        taken = refs[:count]
        del refs[:count]
        return taken

    sources = [
        lambda q: small_ref.at[q],
        lambda q: out_ref.at[q],
        lambda q: qkv_ref.at[q],
        lambda q: dw_ref.at[q, 0],
        lambda q: dw_ref.at[q, 1],
        lambda q: dw_ref.at[q, 2],
    ]
    folds = [Fold(cube, src, *take(FOLD_REFS)) for src in sources]
    small_all, = take(1)
    gather_small = Gather(line, small_all, *take(3))
    shared = []
    for _ in range(4):
        part, from_l, from_r, total, own = take(5)
        shared.append((Scatter(line, 1, part, from_l, from_r, *take(4)), part,
                       Gather(line, total, *take(3)), total, own))
    write_sem, = take(1)
    targets = (out_o, qkv_o, early_out_o, early_qkv_o)

    def share(index, value):
        scatter, part, _, _, own = shared[index]
        rows = part.shape[2]
        for b in range(n):
            @pl.when(b == line.z)
            def _():
                own[...] = value(slice(b * rows, (b + 1) * rows)).astype(F32)

            @pl.when(b != line.z)
            def _():
                part[b, 0] = value(slice(b * rows, (b + 1) * rows))

            scatter.computed(b, 0)

    def scatter_step(indices, t):
        for index in indices:
            scatter, _, _, _, own = shared[index]

            def add_own(p, value):
                own[...] = own[...] + value

            scatter.step(t, add_own)

    def gather_start(indices):
        for index in indices:
            _, _, gather, total, own = shared[index]
            total[line.z] = own[...].astype(BF)
            gather.start(total.at[line.z])

    def gather_step(indices, i):
        for index in indices:
            shared[index][2].arrive(line.order(i))

    def collect(indices):
        for index in indices:
            targets[index][...] = shared[index][3][...].reshape(targets[index].shape)

    def line_jobs(indices):
        jobs = [functools.partial(scatter_step, indices, t)
                for t in range(1, 2 * (n - 1) + 1)]
        jobs.append(functools.partial(gather_start, indices))
        jobs += [functools.partial(gather_step, indices, i) for i in range(1, n)]
        jobs.append(functools.partial(collect, indices))
        return jobs

    def small_job():
        for i in range(1, n):
            gather_small.arrive(line.order(i))
        small_o[...] = jnp.sum(small_all[...], axis=0)

    joint_barrier(line, cube)
    for f in folds:
        f.start()
    share(2, lambda rows: early_out[rows])
    share(3, lambda rows: early_qkv[rows])
    last = folds[0].stages
    jobs = line_jobs((2, 3))

    def after(index):
        fold = folds[index]
        if index == 0:
            small_all[line.z] = fold.mine[0]
            gather_small.start(small_all.at[line.z])
            jobs.append(small_job)
        elif index <= 2:
            share(index - 1, lambda rows: fold.mine[0, rows])
            if index == 2:
                jobs.extend(line_jobs((0, 1)))
        else:
            pltpu.make_async_copy(fold.mine.at[0], dw_o.at[index - 3], write_sem.at[index - 3]).start()

    count = len(folds)
    for t in range(count + last):
        for k in range(last + 1):
            if 0 <= t - k < count:
                folds[t - k].phase(k)
                if k == last:
                    after(t - k)
                for _ in range(2):
                    if jobs and t >= 1:
                        jobs.pop(0)()
    for job in jobs:
        job()
    for k in range(3):
        pltpu.make_async_copy(folds[3 + k].mine.at[0], dw_o.at[k], write_sem.at[k]).wait()
    for f in folds:
        f.finish()
    gather_small.finish()
    for scatter, _, gather, _, _ in shared:
        scatter.finish()
        gather.finish()


def reduce_all(small, out_g, qkv_g, dw, early_out, early_qkv, n):
    owners, shard, d_model = out_g.shape
    width = dw.shape[3]
    qkv_width = qkv_g.shape[2]
    scratch = fold_scratch(owners, small.shape[1], 128, F32)
    scratch += fold_scratch(owners, shard, d_model, BF)
    scratch += fold_scratch(owners, shard, qkv_width, BF)
    for _ in range(3):
        scratch += fold_scratch(owners, shard, width, BF)
    scratch += [pltpu.VMEM((n, small.shape[1], 128), F32)] + gather_sems(n)
    for w in (d_model, qkv_width, d_model, qkv_width):
        scratch += [pltpu.VMEM((n, 1, shard // n, w), BF)] * 3
        scratch += [pltpu.VMEM((n, shard // n, w), BF), pltpu.VMEM((shard // n, w), F32)]
        scratch += scatter_sems(n, 1) + gather_sems(n)
    scratch += [pltpu.SemaphoreType.DMA((3,))]
    return pl.pallas_call(
        functools.partial(reduce_kernel, n, owners),
        out_shape=(
            jax.ShapeDtypeStruct(small.shape[1:], F32),
            jax.ShapeDtypeStruct((shard, d_model), BF),
            jax.ShapeDtypeStruct((shard, qkv_width), BF),
            jax.ShapeDtypeStruct((3, shard, width), BF),
            jax.ShapeDtypeStruct((shard, d_model), BF),
            jax.ShapeDtypeStruct((shard, qkv_width), BF),
        ),
        in_specs=[ANY] * 4 + [VM] * 2,
        out_specs=[VM, VM, VM, ANY, VM, VM],
        scratch_shapes=scratch,
        compiler_params=params(5),
        cost_estimate=pl.CostEstimate(
            flops=1 << 20, transcendentals=0, bytes_accessed=300 << 20),
        name="reduce_all",
    )(small, out_g, qkv_g, dw, early_out, early_qkv)


def normalize(stream, gain):
    return stream * lax.rsqrt(jnp.mean(stream * stream, axis=-1, keepdims=True) + EPSILON) * gain


def normalize_back(grad, stream, gain):
    r = lax.rsqrt(jnp.mean(stream * stream, axis=-1, keepdims=True) + EPSILON)
    u = grad * gain
    back = r * (u - stream * (r * r) * jnp.mean(u * stream, axis=-1, keepdims=True))
    return back, jnp.sum(grad * stream * r, axis=0)


def frequencies():
    return jnp.power(ROPE_BASE, -(jnp.arange(HEAD // 2, dtype=F32) * 2.0 / HEAD))


def shards(hidden_in, cotangent, seq_lengths, tile_place, norm_attn, w_qkv, b_qkv, w_out,
           norm_mlp, w_gate, w_up, w_down):
    n = lax.axis_size("context")
    owners = lax.axis_size("fsdp")
    rows, d_model = hidden_in.shape[1:]
    hidden_units = w_gate.shape[2]
    width = -(-hidden_units // 128) * 128
    pad = width - hidden_units
    total = n * rows

    row_index = jnp.arange(total, dtype=jnp.int32)
    tile_order = tile_place[0]
    selector = (
        row_index[:, None] // TILE == jnp.arange(tile_order.shape[0], dtype=jnp.int32)[None, :]
    ).astype(jnp.int32)
    position = jnp.sum(selector * tile_order[None, :], axis=1) * TILE + row_index % TILE
    valid = position < seq_lengths[0]
    offset = lax.axis_index("context") * rows
    my_position = lax.dynamic_slice_in_dim(position, offset, rows)
    my_valid = lax.dynamic_slice_in_dim(valid, offset, rows)
    pos_q = my_position[None, :]
    pos_k = jnp.where(valid, position, 1 << 30)[:, None]
    angles = my_position.astype(F32)[:, None] * frequencies()
    cosine, sine = jnp.cos(angles), jnp.sin(angles)
    cosine = jnp.concatenate([cosine, cosine], axis=1)
    sine = jnp.concatenate([-sine, sine], axis=1)

    shard = norm_attn.shape[1]
    bias_shard = b_qkv.shape[1]

    def ffn_shard(l):
        return jnp.stack([
            jnp.pad(m, ((0, 0), (0, pad))) for m in (w_gate[l], w_up[l], w_down[l].T)])

    def packed(parts, lead):
        flat = jnp.concatenate(parts, axis=-1)
        used = flat.shape[-1]
        lines = -(-used // (16 * 128)) * 16
        flat = jnp.pad(flat, ((0, 0),) * (flat.ndim - 1) + ((0, lines * 128 - used),))
        return flat.reshape(lead + (lines, 128))

    small = packed(
        [m.reshape(-1).astype(F32) for m in (norm_attn, norm_mlp, b_qkv)], ())
    first_ffn = ffn_shard(0)
    first_ffn, small = lax.optimization_barrier((first_ffn, small))
    ffn_weights = [lax.all_gather(first_ffn, "fsdp", axis=0, tiled=False)]
    small, qkv_w = spread_all(owners, small, w_qkv[0])
    qkv_weights = [qkv_w.reshape(d_model, -1)]
    out_weights = []
    small = small.reshape(owners, -1)
    gains_attn, gains_mlp, biases = [], [], []
    for l in range(LAYERS):
        gains_attn.append(small[:, l * shard:(l + 1) * shard].reshape(-1))
        gains_mlp.append(small[:, (LAYERS + l) * shard:(LAYERS + l + 1) * shard].reshape(-1))
        start = 2 * LAYERS * shard + l * bias_shard
        biases.append(small[:, start:start + bias_shard].reshape(-1))

    stream = hidden_in[0].astype(F32)
    kept = []
    for l in range(LAYERS):
        qkv_w, ffn_w = qkv_weights[l], ffn_weights[l]
        if l + 1 < LAYERS:
            ffn_weights.append(lax.all_gather(ffn_shard(l + 1), "fsdp", axis=0, tiled=False))
        normed = normalize(stream, gains_attn[l]).astype(BF)
        projected = jnp.dot(normed, qkv_w, preferred_element_type=F32) + biases[l]
        following = (w_out[l],) if l == 0 else ()
        mixed, lse, kvall, q, *out_w = attention_forward(
            projected, cosine, sine, pos_q, pos_k, n, owners, following)
        out_weights += [m.reshape(Q_WIDTH, d_model) for m in out_w]
        out_w = out_weights[l]
        middle = stream + jnp.dot(mixed, out_w, preferred_element_type=F32)
        normed_two = normalize(middle, gains_mlp[l]).astype(BF)
        if l + 1 < LAYERS:
            xall, gate, up, y, next_qkv, next_out = ffn_forward(
                normed_two, ffn_w, n, (w_qkv[l + 1], w_out[l + 1]))
            qkv_weights.append(next_qkv.reshape(d_model, -1))
            out_weights.append(next_out.reshape(Q_WIDTH, d_model))
        else:
            xall, gate, up, y = ffn_forward(normed_two, ffn_w, n)
        kept.append((stream, normed, q, kvall, lse, mixed, middle, xall, gate, up,
                     qkv_w, out_w, ffn_w))
        stream = middle + y
    layer_out = stream.astype(BF)[None]

    gradient = cotangent[0].astype(F32) * my_valid[:, None].astype(F32)
    small_grads = [None] * LAYERS
    big_grads = [None] * LAYERS
    for l in reversed(range(LAYERS)):
        (stream, normed, q, kvall, lse, mixed, middle, xall, gate, up,
         qkv_w, out_w, ffn_w) = kept[l]
        dw, dx = ffn_backward(gradient.astype(BF), ffn_w, xall, gate, up, n)
        if l < LAYERS - 1:
            out_sum, qkv_sum, dw_sum = big_grads[l + 1]
            dx, dw_sum = lax.optimization_barrier((dx, dw_sum))
        back, gain_two = normalize_back(dx, middle, gains_mlp[l])
        d_middle = gradient + back
        d_low = d_middle.astype(BF)
        d_mixed = jnp.einsum("td,cd->tc", d_low, out_w, preferred_element_type=F32).astype(BF)
        out_grad = jnp.einsum("tc,td->cd", mixed, d_low, preferred_element_type=F32).astype(BF)
        d_projected = attention_backward(
            q, kvall, lse, d_mixed, cosine, sine, pos_q, pos_k, n)
        if l < LAYERS - 1:
            d_projected, out_sum = lax.optimization_barrier((d_projected, out_sum))
            big_grads[l + 1] = (out_sum, qkv_sum, dw_sum)
        bias_grad = jnp.sum(d_projected.astype(F32), axis=0)
        d_normed = jnp.einsum("tc,dc->td", d_projected, qkv_w, preferred_element_type=F32)
        qkv_grad = jnp.einsum(
            "td,tc->dc", normed, d_projected, preferred_element_type=F32).astype(BF)
        back, gain_one = normalize_back(d_normed, stream, gains_attn[l])
        gradient = d_middle + back
        small_grads[l] = (gain_one, gain_two, bias_grad)
        if l > 0:
            big_grads[l] = (
                lax.psum_scatter(out_grad, "fsdp", scatter_dimension=0, tiled=True),
                lax.psum_scatter(qkv_grad, "fsdp", scatter_dimension=0, tiled=True),
                lax.psum_scatter(dw, "fsdp", scatter_dimension=0, tiled=False))
        else:
            small = packed([
                m.reshape(owners, -1)
                for k in range(3) for m in (small_grads[i][k] for i in range(LAYERS))], (owners,))
            out_early, qkv_early, dw_sum = big_grads[l + 1]
            small, out_sum, qkv_sum, dw_last, out_early, qkv_early = reduce_all(
                small, out_grad.reshape(owners, shard, d_model),
                qkv_grad.reshape(owners, shard, qkv_grad.shape[1]), dw, out_early, qkv_early, n)
            big_grads[l + 1] = (out_early, qkv_early, dw_sum)
            small = small.reshape(-1)
            big_grads[l] = (out_sum, qkv_sum, dw_last)

    grad_norm_attn = small[:LAYERS * shard].reshape(LAYERS, shard)
    grad_norm_mlp = small[LAYERS * shard:2 * LAYERS * shard].reshape(LAYERS, shard)
    start = 2 * LAYERS * shard
    grad_b_qkv = small[start:start + LAYERS * bias_shard].reshape(LAYERS, bias_shard)

    def stacked(pick):
        return jnp.stack([pick(big_grads[l]).astype(F32) for l in range(LAYERS)])

    return (
        layer_out,
        gradient[None],
        grad_norm_attn,
        stacked(lambda m: m[1]),
        grad_b_qkv,
        stacked(lambda m: m[0]),
        grad_norm_mlp,
        stacked(lambda m: m[2][0, :, :hidden_units]),
        stacked(lambda m: m[2][1, :, :hidden_units]),
        stacked(lambda m: m[2][2, :, :hidden_units].T),
    )


def solution(mesh):
    return jax.shard_map(
        shards,
        mesh=mesh,
        in_specs=(
            P("fsdp", "context", None),
            P("fsdp", "context", None),
            P("fsdp"),
            P("fsdp", None),
            P(None, "fsdp"),
            P(None, "fsdp", None),
            P(None, "fsdp"),
            P(None, "fsdp", None),
            P(None, "fsdp"),
            P(None, "fsdp", "context"),
            P(None, "fsdp", "context"),
            P(None, "context", "fsdp"),
        ),
        out_specs=(
            P("fsdp", "context", None),
            P("fsdp", "context", None),
            P(None, "fsdp"),
            P(None, "fsdp", None),
            P(None, "fsdp"),
            P(None, "fsdp", None),
            P(None, "fsdp"),
            P(None, "fsdp", "context"),
            P(None, "fsdp", "context"),
            P(None, "context", "fsdp"),
        ),
        check_vma=False,
    )
```

```python
import functools
import math

import jax
import jax.numpy as jnp
from jax import lax
from jax.experimental import pallas as pl
from jax.experimental.pallas import tpu as pltpu
from jax.sharding import PartitionSpec as P

QUERY_HEADS = 12
KV_HEADS = 2
HEAD = 128
LAYERS = 2
TILE = 128
Q_WIDTH = QUERY_HEADS * HEAD
KV_WIDTH = KV_HEADS * HEAD
PER_GROUP = QUERY_HEADS // KV_HEADS
SCALE = 1.0 / math.sqrt(HEAD)
EPSILON = 1e-06
ROPE_BASE = 1000000.0
BF = jnp.bfloat16
F32 = jnp.float32
MESH = pl.DeviceIdType.MESH
VMEM_LIMIT = 66 * 1024 * 1024
ANY = pl.BlockSpec(memory_space=pl.ANY)
VM = pl.BlockSpec(memory_space=pltpu.VMEM)


def dot_nn(a, b):
    return lax.dot_general(a, b, (((1,), (0,)), ((), ())), preferred_element_type=F32)


def dot_nt(a, b):
    return lax.dot_general(a, b, (((1,), (1,)), ((), ())), preferred_element_type=F32)


def dot_tn(a, b):
    return lax.dot_general(a, b, (((0,), (0,)), ((), ())), preferred_element_type=F32)


def lane_tile(width, most):
    best = 128
    for k in range(1, most // 128 + 1):
        if width % (128 * k) == 0:
            best = 128 * k
    return best


class Line:
    def __init__(self, n):
        self.n = n
        self.z = lax.axis_index("context")
        self.right = lax.rem(self.z + 1, n)
        self.left = lax.rem(self.z + n - 1, n)
        self.has_right = self.z < n - 1
        self.has_left = self.z > 0

    def barrier(self):
        bar = pltpu.get_barrier_semaphore()

        @pl.when(self.has_right)
        def _():
            pl.semaphore_signal(bar, inc=1, device_id={"context": self.right}, device_id_type=MESH)

        @pl.when(self.has_left)
        def _():
            pl.semaphore_signal(bar, inc=1, device_id={"context": self.left}, device_id_type=MESH)

        both = self.has_right & self.has_left

        @pl.when(both)
        def _():
            pl.semaphore_wait(bar, 2)

        @pl.when(jnp.logical_not(both))
        def _():
            pl.semaphore_wait(bar, 1)

    def order(self, i):
        z, n = self.z, self.n
        short = jnp.minimum(z, n - 1 - z)
        j = i - 1
        paired = j < 2 * short
        k = jnp.where(paired, j // 2 + 1, j - short + 1)
        goes_left = jnp.where(paired, lax.rem(j, 2) == 0, z > n - 1 - z)
        return jnp.where(i == 0, z, jnp.where(goes_left, z - k, z + k))


def remote(src, dst, send, recv, target):
    return pltpu.make_async_remote_copy(
        src_ref=src, dst_ref=dst, send_sem=send, recv_sem=recv,
        device_id={"context": target}, device_id_type=MESH,
    )


class Gather:
    def __init__(self, line, slots, send_r, send_l, recv):
        self.line, self.slots = line, slots
        self.send_r, self.send_l, self.recv = send_r, send_l, recv

    def _right(self, b, src):
        return remote(src, self.slots.at[b], self.send_r.at[b], self.recv.at[b], self.line.right)

    def _left(self, b, src):
        return remote(src, self.slots.at[b], self.send_l.at[b], self.recv.at[b], self.line.left)

    def start(self, own):
        line = self.line

        @pl.when(line.has_right)
        def _():
            self._right(line.z, own).start()

        @pl.when(line.has_left)
        def _():
            self._left(line.z, own).start()

    def arrive(self, b):
        line = self.line
        self._right(b, self.slots.at[b]).wait_recv()

        @pl.when((b < line.z) & line.has_right)
        def _():
            self._right(b, self.slots.at[b]).start()

        @pl.when((b > line.z) & line.has_left)
        def _():
            self._left(b, self.slots.at[b]).start()

    def finish(self):
        line = self.line
        for b in range(line.n):
            @pl.when((b <= line.z) & line.has_right)
            def _():
                self._right(b, self.slots.at[b]).wait_send()

            @pl.when((b >= line.z) & line.has_left)
            def _():
                self._left(b, self.slots.at[b]).wait_send()


class Scatter:
    def __init__(self, line, pieces, part, from_left, from_right, send_r, send_l, recv_l, recv_r):
        self.line, self.pieces, self.part = line, pieces, part
        self.from_left, self.from_right = from_left, from_right
        self.send_r, self.send_l, self.recv_l, self.recv_r = send_r, send_l, recv_l, recv_r

    def _right(self, b, p):
        return remote(self.part.at[b, p], self.from_left.at[b, p], self.send_r.at[b, p],
                      self.recv_l.at[b, p], self.line.right)

    def _left(self, b, p):
        return remote(self.part.at[b, p], self.from_right.at[b, p], self.send_l.at[b, p],
                      self.recv_r.at[b, p], self.line.left)

    def computed(self, b, p):
        line = self.line

        @pl.when((line.z == 0) & (b > 0))
        def _():
            self._right(b, p).start()

        @pl.when((line.z == line.n - 1) & (b < line.n - 1))
        def _():
            self._left(b, p).start()

    def steps(self):
        return range(1, 2 * (self.line.n - 1) + 1)

    def step(self, t, add_own):
        line = self.line
        n, z = line.n, line.z
        b_left = t - z

        @pl.when(line.has_left & (b_left >= z) & (b_left < n))
        def _():
            for p in range(self.pieces):
                self._right(b_left, p).wait_recv()

                @pl.when(b_left == z)
                def _():
                    add_own(p, self.from_left[b_left, p].astype(F32))

                @pl.when(b_left != z)
                def _():
                    self.part[b_left, p] = (
                        self.part[b_left, p].astype(F32) + self.from_left[b_left, p].astype(F32)
                    ).astype(BF)
                    self._right(b_left, p).start()

        b_right = 2 * (n - 1) - t - z

        @pl.when(line.has_right & (b_right >= 0) & (b_right <= z))
        def _():
            for p in range(self.pieces):
                self._left(b_right, p).wait_recv()

                @pl.when(b_right == z)
                def _():
                    add_own(p, self.from_right[b_right, p].astype(F32))

                @pl.when(b_right != z)
                def _():
                    self.part[b_right, p] = (
                        self.part[b_right, p].astype(F32) + self.from_right[b_right, p].astype(F32)
                    ).astype(BF)
                    self._left(b_right, p).start()

    def finish(self):
        line = self.line
        for b in range(line.n):
            @pl.when((b > line.z) & line.has_right)
            def _():
                for p in range(self.pieces):
                    self._right(b, p).wait_send()

            @pl.when((b < line.z) & line.has_left)
            def _():
                for p in range(self.pieces):
                    self._left(b, p).wait_send()


def gather_sems(n):
    return [pltpu.SemaphoreType.DMA((n,))] * 3


def scatter_sems(n, pieces):
    return [pltpu.SemaphoreType.DMA((n, pieces))] * 4


def params(cid):
    return pltpu.CompilerParams(
        collective_id=cid, has_side_effects=True, vmem_limit_bytes=VMEM_LIMIT
    )


def bits_of(owners):
    return [1 << i for i in range(owners.bit_length() - 1)]


class Cube:
    def __init__(self, owners):
        self.owners = owners
        self.me = lax.axis_index("fsdp")
        self.bits = bits_of(owners)
        self.chip_bits = [b // 2 for b in self.bits[1:]]
        self.chips = owners // 2

    def flip(self, mask):
        index = self.me
        for b in self.bits:
            if mask & b:
                index = index + b - 2 * b * lax.rem(self.me // b, 2)
        return index

    def signal(self, bar):
        for b in self.bits:
            pl.semaphore_signal(bar, inc=1, device_id={"fsdp": self.flip(b)}, device_id_type=MESH)

    def order(self, half):
        return self.chip_bits[::-1] if half == 0 else self.chip_bits

    def plan(self):
        steps = {}
        for half in (0, 1):
            order, slot = self.order(half), 0
            for stage, bit in enumerate(order):
                rest = [0]
                for other in order[stage + 1:]:
                    rest = rest + [m | other for m in rest]
                steps[half, stage] = (bit, rest, slot)
                slot += len(rest)
        return steps


def joint_barrier(line, cube):
    bar = pltpu.get_barrier_semaphore()
    cube.signal(bar)
    peers = len(cube.bits)

    @pl.when(line.has_right)
    def _():
        pl.semaphore_signal(bar, inc=1, device_id={"context": line.right}, device_id_type=MESH)

    @pl.when(line.has_left)
    def _():
        pl.semaphore_signal(bar, inc=1, device_id={"context": line.left}, device_id_type=MESH)

    both = line.has_right & line.has_left

    @pl.when(both)
    def _():
        pl.semaphore_wait(bar, peers + 2)

    @pl.when(jnp.logical_not(both))
    def _():
        pl.semaphore_wait(bar, peers + 1)


class Spread:
    def __init__(self, cube, own, full, own_sem, send, recv, core_send, core_recv):
        self.cube, self.own, self.full = cube, own, full
        self.own_sem, self.send, self.recv = own_sem, send, recv
        self.core_send, self.core_recv = core_send, core_recv
        self.half = own.shape[0] // 2
        self.stages = len(cube.chip_bits)

    def _rows(self, half):
        return pl.ds(half * self.half, self.half)

    def _block(self, half, mask):
        return self.full.at[self.cube.flip(mask), self._rows(half)]

    def _source(self, half, mask):
        return self._block(half, 2 * mask) if mask else self.own.at[self._rows(half)]

    def _masks(self, half, stage):
        masks = [0]
        for bit in self.cube.order(half)[:stage]:
            masks = masks + [m | bit for m in masks]
        return masks

    def _hop(self, half, stage, mask):
        bit = self.cube.order(half)[stage]
        return pltpu.make_async_remote_copy(
            src_ref=self._source(half, mask), dst_ref=self._block(half, 2 * mask),
            send_sem=self.send.at[half, mask | bit], recv_sem=self.recv.at[half, mask | bit],
            device_id={"fsdp": self.cube.flip(2 * bit)}, device_id_type=MESH)

    def _arrival(self, half, mask):
        block = self._block(half, 2 * mask)
        return pltpu.make_async_remote_copy(
            src_ref=block, dst_ref=block,
            send_sem=self.send.at[half, mask], recv_sem=self.recv.at[half, mask],
            device_id={"fsdp": self.cube.flip(1)}, device_id_type=MESH)

    def _core(self, half, mask):
        return pltpu.make_async_remote_copy(
            src_ref=self._source(half, mask), dst_ref=self._block(half, 2 * mask),
            send_sem=self.core_send.at[half, mask], recv_sem=self.core_recv.at[half, mask],
            device_id={"fsdp": self.cube.flip(1)}, device_id_type=MESH)

    def _core_arrival(self, half, mask):
        block = self._block(half, 2 * mask | 1)
        return pltpu.make_async_remote_copy(
            src_ref=block, dst_ref=block,
            send_sem=self.core_send.at[half, mask], recv_sem=self.core_recv.at[half, mask],
            device_id={"fsdp": self.cube.flip(1)}, device_id_type=MESH)

    def _own_copy(self):
        return pltpu.make_async_copy(self.own, self.full.at[self.cube.me], self.own_sem)

    def start(self):
        for stage in range(self.stages):
            for half in (0, 1):
                self._hop(half, stage, 0).start()
        for half in (0, 1):
            self._core(half, 0).start()
        self._own_copy().start()

    def phase(self, k):
        for half in (0, 1):
            bit = self.cube.order(half)[k - 1]
            for m in self._masks(half, k - 1):
                self._arrival(half, m | bit).wait_recv()
                for stage in range(k, self.stages):
                    self._hop(half, stage, m | bit).start()
                self._core(half, m | bit).start()

    def finish(self):
        self._own_copy().wait()
        for half in (0, 1):
            for m in range(self.cube.chips):
                self._core_arrival(half, m).wait_recv()
                self._core(half, m).wait_send()
            for stage in range(self.stages):
                for m in self._masks(half, stage):
                    self._hop(half, stage, m).wait_send()


SPREAD_SEMS = 5


def spread_sems(owners):
    chips = owners // 2
    return [pltpu.SemaphoreType.DMA] + [pltpu.SemaphoreType.DMA((2, chips))] * 4


def spread_shapes(owners, shards):
    return tuple(jax.ShapeDtypeStruct((owners,) + m.shape, m.dtype) for m in shards)


def spread_kernel(owners, count, *refs):
    cube = Cube(owners)
    spreads = [
        Spread(cube, refs[i], refs[count + i],
               *refs[2 * count + SPREAD_SEMS * i:2 * count + SPREAD_SEMS * (i + 1)])
        for i in range(count)]
    bar = pltpu.get_barrier_semaphore()
    cube.signal(bar)
    pl.semaphore_wait(bar, len(cube.bits))
    for s in spreads:
        s.start()
    for k in range(1, len(cube.chip_bits) + 1):
        for s in spreads:
            s.phase(k)
    for s in spreads:
        s.finish()


def spread_all(owners, *shards):
    count = len(shards)
    return pl.pallas_call(
        functools.partial(spread_kernel, owners, count),
        out_shape=spread_shapes(owners, shards),
        in_specs=[VM] * count,
        out_specs=[ANY] * count,
        scratch_shapes=spread_sems(owners) * count,
        compiler_params=params(6),
        cost_estimate=pl.CostEstimate(
            flops=1 << 20, transcendentals=0, bytes_accessed=150 << 20),
        name="spread_all",
    )(*shards)


def ffn_forward_kernel(n, pieces, count, *refs):
    x_ref, w_ref = refs[:2]
    next_own = refs[2:2 + count]
    xall_ref, gate_ref, up_ref, y_ref = refs[2 + count:6 + count]
    next_full = refs[6 + count:6 + 2 * count]
    (w_v, xbuf, gbuf, ubuf, hbuf, part, from_l, from_r,
     w_sem, x_sem, out_sem, *sems) = refs[6 + 2 * count:]
    line = Line(n)
    z = line.z
    owners, _, rows, width = w_ref.shape
    d_model = x_ref.shape[1]
    tile = lane_tile(width, 256)
    piece = d_model // pieces
    gather = Gather(line, xbuf, *sems[:3])
    scatter = Scatter(line, pieces, part, from_l, from_r, *sems[3:7])
    spreads = []
    stages = 0
    if count:
        cube = Cube(owners)
        stages = len(cube.chip_bits)
        for i in range(count):
            at = 7 + SPREAD_SEMS * i
            spreads.append(Spread(cube, next_own[i], next_full[i], *sems[at:at + SPREAD_SEMS]))

    def w_copy(k, f):
        return pltpu.make_async_copy(
            w_ref.at[f, k], w_v.at[k, pl.ds(f * rows, rows)], w_sem.at[k, f]
        )

    def x_out(b):
        return pltpu.make_async_copy(xbuf.at[b], xall_ref.at[b], x_sem.at[b])

    if count:
        joint_barrier(line, cube)
    else:
        line.barrier()
    gather.start(x_ref)
    for s in spreads:
        s.start()
    for k in range(3):
        for f in range(owners):
            w_copy(k, f).start()
    xbuf[z] = x_ref[...]
    for k in range(3):
        for f in range(owners):
            w_copy(k, f).wait()

    @pl.loop(0, n)
    def _(i):
        b = line.order(i)

        @pl.when(i > 0)
        def _():
            gather.arrive(b)

        x_out(b).start()
        slot = lax.rem(i, 2)
        g_copy = pltpu.make_async_copy(gbuf.at[slot], gate_ref.at[b], out_sem.at[0, slot])
        u_copy = pltpu.make_async_copy(ubuf.at[slot], up_ref.at[b], out_sem.at[1, slot])

        @pl.when(i > 1)
        def _():
            g_copy.wait()
            u_copy.wait()

        @pl.loop(0, width // tile)
        def _(j):
            cols = pl.ds(pl.multiple_of(j * tile, tile), tile)
            xb = xbuf[b]
            gate = dot_nn(xb, w_v[0, :, cols])
            up = dot_nn(xb, w_v[1, :, cols])
            gbuf[slot, :, cols] = gate.astype(BF)
            ubuf[slot, :, cols] = up.astype(BF)
            hbuf[:, cols] = (gate * jax.nn.sigmoid(gate) * up).astype(BF)

        g_copy.start()
        u_copy.start()
        for p in range(pieces):
            out = dot_nt(hbuf[...], w_v[2, pl.ds(p * piece, piece)])

            @pl.when(b == z)
            def _():
                y_ref[:, p * piece:(p + 1) * piece] = out

            @pl.when(b != z)
            def _():
                part[b, p] = out.astype(BF)

            scatter.computed(b, p)

        if spreads:
            @pl.when(i == n // 2)
            def _():
                for s in spreads:
                    s.phase(1)

    def add_own(p, value):
        cols = slice(p * piece, (p + 1) * piece)
        y_ref[:, cols] = y_ref[:, cols] + value

    for t in scatter.steps():
        scatter.step(t, add_own)
    for k in range(2, stages + 1):
        for s in spreads:
            s.phase(k)
    for i in range(max(0, n - 2), n):
        slot = i % 2
        pltpu.make_async_copy(gbuf.at[slot], gate_ref.at[0], out_sem.at[0, slot]).wait()
        pltpu.make_async_copy(ubuf.at[slot], up_ref.at[0], out_sem.at[1, slot]).wait()
    for b in range(n):
        x_out(b).wait()
    gather.finish()
    scatter.finish()
    for s in spreads:
        s.finish()


def ffn_forward(x, w, n, following=()):
    rows, d_model = x.shape
    owners, _, shard, width = w.shape
    pieces = 3
    piece = d_model // pieces
    count = len(following)
    return pl.pallas_call(
        functools.partial(ffn_forward_kernel, n, pieces, count),
        out_shape=(
            jax.ShapeDtypeStruct((n, rows, d_model), BF),
            jax.ShapeDtypeStruct((n, rows, width), BF),
            jax.ShapeDtypeStruct((n, rows, width), BF),
            jax.ShapeDtypeStruct((rows, d_model), F32),
        ) + spread_shapes(owners, following),
        in_specs=[VM, ANY] + [VM] * count,
        out_specs=[ANY, ANY, ANY, VM] + [ANY] * count,
        scratch_shapes=[
            pltpu.VMEM((3, d_model, width), BF),
            pltpu.VMEM((n, rows, d_model), BF),
            pltpu.VMEM((2, rows, width), BF),
            pltpu.VMEM((2, rows, width), BF),
            pltpu.VMEM((rows, width), BF),
            pltpu.VMEM((n, pieces, rows, piece), BF),
            pltpu.VMEM((n, pieces, rows, piece), BF),
            pltpu.VMEM((n, pieces, rows, piece), BF),
            pltpu.SemaphoreType.DMA((3, owners)),
            pltpu.SemaphoreType.DMA((n,)),
            pltpu.SemaphoreType.DMA((2, 2)),
        ] + gather_sems(n) + scatter_sems(n, pieces) + spread_sems(owners) * count,
        compiler_params=params(7 if count else 1),
        cost_estimate=pl.CostEstimate(
            flops=6 * n * rows * d_model * width, transcendentals=n * rows * width,
            bytes_accessed=60 << 20),
        name="ffn_forward",
    )(x, w, *following)


def ffn_backward_kernel(n, pieces, groups, g_ref, w_ref, xall_ref, gate_ref, up_ref, dw_ref, dx_ref,
                        w_v, gbuf, xv, gate_v, up_v, hid_v, part, from_l, from_r, stage,
                        w_sem, in_sem, out_sem, *sems):
    line = Line(n)
    z = line.z
    owners, _, shard, width = w_ref.shape
    rows, d_model = g_ref.shape
    tile = lane_tile(width, 256)
    piece = d_model // pieces
    gather = Gather(line, gbuf, *sems[:3])
    scatter = Scatter(line, pieces, part, from_l, from_r, *sems[3:])

    def w_copy(k, f):
        return pltpu.make_async_copy(
            w_ref.at[f, k], w_v.at[k, pl.ds(f * shard, shard)], w_sem.at[k, f]
        )

    def loads(b):
        return (
            pltpu.make_async_copy(gate_ref.at[b], gate_v.at[b], in_sem.at[0, b]),
            pltpu.make_async_copy(up_ref.at[b], up_v.at[b], in_sem.at[1, b]),
        )

    def x_load(b):
        return pltpu.make_async_copy(xall_ref.at[b], xv.at[b], in_sem.at[2, b])

    line.barrier()
    gather.start(g_ref)
    for f in range(owners):
        w_copy(2, f).start()
    for c in loads(z):
        c.start()
    for k in range(2):
        for f in range(owners):
            w_copy(k, f).start()
    for b in range(n):
        @pl.when(b != z)
        def _():
            for c in loads(b):
                c.start()
    for b in range(n):
        x_load(b).start()
    gbuf[z] = g_ref[...]
    for k in (2, 0, 1):
        for f in range(owners):
            w_copy(k, f).wait()

    @pl.loop(0, n)
    def _(i):
        b = line.order(i)

        @pl.when(i > 0)
        def _():
            gather.arrive(b)

        for c in loads(b):
            c.wait()

        @pl.loop(0, width // tile)
        def _(j):
            cols = pl.ds(pl.multiple_of(j * tile, tile), tile)
            d_hidden = dot_nn(gbuf[b], w_v[2, :, cols])
            gate = gate_v[b, :, cols].astype(F32)
            up = up_v[b, :, cols].astype(F32)
            sig = jax.nn.sigmoid(gate)
            act = gate * sig
            hid_v[b, :, cols] = (act * up).astype(BF)
            gate_v[b, :, cols] = (d_hidden * up * (sig + act * (1.0 - sig))).astype(BF)
            up_v[b, :, cols] = (d_hidden * act).astype(BF)

        for p in range(pieces):
            sl = pl.ds(p * piece, piece)
            out = dot_nt(gate_v[b], w_v[0, sl]) + dot_nt(up_v[b], w_v[1, sl])

            @pl.when(b == z)
            def _():
                dx_ref[:, p * piece:(p + 1) * piece] = out

            @pl.when(b != z)
            def _():
                part[b, p] = out.astype(BF)

            scatter.computed(b, p)

    def add_own(p, value):
        cols = slice(p * piece, (p + 1) * piece)
        dx_ref[:, cols] = dx_ref[:, cols] + value

    for b in range(n):
        x_load(b).wait()

    group = d_model // groups
    per = group // shard

    def dw_copies(k, q, slot):
        return [
            pltpu.make_async_copy(
                stage.at[slot, pl.ds(s * shard, shard)], dw_ref.at[q * per + s, k],
                out_sem.at[slot, s])
            for s in range(per)
        ]

    def weight_unit(unit):
        k, q = unit // groups, unit % groups
        slot = unit % 2
        left = (xv, xv, gbuf)[k]
        right = (gate_v, up_v, hid_v)[k]
        if unit >= 2:
            for c in dw_copies((unit - 2) // groups, (unit - 2) % groups, slot):
                c.wait()
        lt = left[:, :, q * group:(q + 1) * group].reshape(n * rows, group)

        @pl.loop(0, width // tile)
        def _(j):
            cols = pl.ds(pl.multiple_of(j * tile, tile), tile)
            stage[slot, :, cols] = dot_tn(
                lt, right[:, :, cols].reshape(n * rows, tile)
            ).astype(BF)

        for c in dw_copies(k, q, slot):
            c.start()

    units = 3 * groups
    steps = list(scatter.steps())
    done = 0
    for index, t in enumerate(steps):
        scatter.step(t, add_own)
        until = units * (index + 1) // len(steps)
        while done < until:
            weight_unit(done)
            done += 1
    for unit in range(units - 2, units):
        for c in dw_copies(unit // groups, unit % groups, unit % 2):
            c.wait()
    gather.finish()
    scatter.finish()


def ffn_backward(g, w, xall, gate, up, n):
    rows, d_model = g.shape
    owners, _, shard, width = w.shape
    pieces, groups = 3, 4
    piece = d_model // pieces
    per = d_model // groups // shard
    return pl.pallas_call(
        functools.partial(ffn_backward_kernel, n, pieces, groups),
        out_shape=(
            jax.ShapeDtypeStruct((owners, 3, shard, width), BF),
            jax.ShapeDtypeStruct((rows, d_model), F32),
        ),
        in_specs=[VM, ANY, ANY, ANY, ANY],
        out_specs=[ANY, VM],
        scratch_shapes=[
            pltpu.VMEM((3, d_model, width), BF),
            pltpu.VMEM((n, rows, d_model), BF),
            pltpu.VMEM((n, rows, d_model), BF),
            pltpu.VMEM((n, rows, width), BF),
            pltpu.VMEM((n, rows, width), BF),
            pltpu.VMEM((n, rows, width), BF),
            pltpu.VMEM((n, pieces, rows, piece), BF),
            pltpu.VMEM((n, pieces, rows, piece), BF),
            pltpu.VMEM((n, pieces, rows, piece), BF),
            pltpu.VMEM((2, d_model // groups, width), BF),
            pltpu.SemaphoreType.DMA((3, owners)),
            pltpu.SemaphoreType.DMA((3, n)),
            pltpu.SemaphoreType.DMA((2, per)),
        ] + gather_sems(n) + scatter_sems(n, pieces),
        compiler_params=params(2),
        cost_estimate=pl.CostEstimate(
            flops=12 * n * rows * d_model * width, transcendentals=n * rows * width,
            bytes_accessed=100 << 20),
        name="ffn_backward",
    )(g, w, xall, gate, up)


def half_turn(x):
    return pltpu.roll(x, HEAD // 2, 1)


def attention_forward_kernel(n, owners, count, proj_ref, cos_ref, sin_ref, pq_ref, pk_ref, *refs):
    own = refs[:count]
    mixed_ref, lse_ref, kvall_ref, q_ref = refs[count:count + 4]
    full = refs[count + 4:2 * count + 4]
    kvbuf, vt, *sems = refs[2 * count + 4:]
    line = Line(n)
    z = line.z
    rows = q_ref.shape[0]
    total = n * rows
    gather = Gather(line, kvbuf, *sems[:3])

    def rotated(h):
        x = proj_ref[:, h * HEAD:(h + 1) * HEAD]
        return (x * cos_ref[...] + half_turn(x) * sin_ref[...]).astype(BF)

    for g in range(KV_HEADS):
        kvbuf[z, :, g * HEAD:(g + 1) * HEAD] = rotated(QUERY_HEADS + g)
    kvbuf[z, :, KV_WIDTH:] = proj_ref[:, Q_WIDTH + KV_WIDTH:].astype(BF)
    spreads = []
    stages = 0
    if count:
        cube = Cube(owners)
        stages = len(cube.chip_bits)
        for i in range(count):
            at = 3 + SPREAD_SEMS * i
            spreads.append(Spread(cube, own[i], full[i], *sems[at:at + SPREAD_SEMS]))
        joint_barrier(line, cube)
    else:
        line.barrier()
    gather.start(kvbuf.at[z])
    for s in spreads:
        s.start()
    for h in range(QUERY_HEADS):
        q_ref[:, h * HEAD:(h + 1) * HEAD] = rotated(h)
    for i in range(1, n):
        gather.arrive(line.order(i))
    kvall_ref[...] = kvbuf[...]
    allowed = pk_ref[...] <= pq_ref[...]
    for g in range(KV_HEADS):
        v = kvbuf[:, :, KV_WIDTH + g * HEAD:KV_WIDTH + (g + 1) * HEAD].reshape(total, HEAD)
        vt[g] = v.T
    for g in range(KV_HEADS):
        for r in range(PER_GROUP):
            h = g * PER_GROUP + r
            k = kvbuf[:, :, g * HEAD:(g + 1) * HEAD].reshape(total, HEAD)
            s = dot_nt(k, q_ref[:, h * HEAD:(h + 1) * HEAD]) * SCALE
            s = jnp.where(allowed, s, -1e30)
            top = jnp.max(s, axis=0, keepdims=True)
            e = jnp.exp(s - top)
            den = jnp.sum(e, axis=0, keepdims=True)
            o = dot_nn(vt[g], e.astype(BF)) / den
            mixed_ref[:, h * HEAD:(h + 1) * HEAD] = o.T.astype(BF)
            lse_ref[h:h + 1, :] = top + jnp.log(den)
            if h == 5 and stages:
                for sp in spreads:
                    sp.phase(1)
    for k in range(2, stages + 1):
        for sp in spreads:
            sp.phase(k)
    gather.finish()
    for sp in spreads:
        sp.finish()


def attention_forward(projected, cosine, sine, pos_q, pos_k, n, owners, following=()):
    rows = projected.shape[0]
    count = len(following)
    return pl.pallas_call(
        functools.partial(attention_forward_kernel, n, owners, count),
        out_shape=(
            jax.ShapeDtypeStruct((rows, Q_WIDTH), BF),
            jax.ShapeDtypeStruct((16, rows), F32),
            jax.ShapeDtypeStruct((n, rows, 2 * KV_WIDTH), BF),
            jax.ShapeDtypeStruct((rows, Q_WIDTH), BF),
        ) + spread_shapes(owners, following),
        in_specs=[VM] * (5 + count),
        out_specs=[VM] * 4 + [ANY] * count,
        scratch_shapes=[
            pltpu.VMEM((n, rows, 2 * KV_WIDTH), BF),
            pltpu.VMEM((KV_HEADS, HEAD, n * rows), BF),
        ] + gather_sems(n) + spread_sems(owners) * count,
        compiler_params=params(9 if count else 3),
        cost_estimate=pl.CostEstimate(
            flops=4 * n * rows * rows * Q_WIDTH, transcendentals=n * rows * rows * QUERY_HEADS,
            bytes_accessed=16 << 20),
        name="attention_forward",
    )(projected, cosine, sine, pos_q, pos_k, *following)


def attention_backward_kernel(n, q_ref, kvall_ref, lse_ref, dm_ref, cos_ref, sin_ref, pq_ref,
                              pk_ref, dproj_ref, dkv_ref, kt, dk_acc, dv_acc, part,
                              from_l, from_r, *sems):
    line = Line(n)
    z = line.z
    rows = q_ref.shape[0]
    total = n * rows
    pieces = KV_HEADS
    scatter = Scatter(line, pieces, part, from_l, from_r, *sems)
    line.barrier()

    def rotated_back(x):
        return (x * cos_ref[...] - half_turn(x) * sin_ref[...]).astype(BF)

    allowed = pk_ref[...] <= pq_ref[...]
    for g in range(KV_HEADS):
        k = kvall_ref[:, :, g * HEAD:(g + 1) * HEAD].reshape(total, HEAD)
        kt[g] = k.T
    for g in range(KV_HEADS):
        for r in range(PER_GROUP):
            h = g * PER_GROUP + r
            cols = slice(h * HEAD, (h + 1) * HEAD)
            k = kvall_ref[:, :, g * HEAD:(g + 1) * HEAD].reshape(total, HEAD)
            v = kvall_ref[:, :, KV_WIDTH + g * HEAD:KV_WIDTH + (g + 1) * HEAD].reshape(total, HEAD)
            q = q_ref[:, cols]
            dm = dm_ref[:, cols]
            s = dot_nt(k, q) * SCALE
            pr = jnp.where(allowed, jnp.exp(s - lse_ref[h:h + 1, :]), 0.0)
            dp = dot_nt(v, dm)
            delta = jnp.sum(pr * dp, axis=0, keepdims=True)
            ds = (pr * (dp - delta) * SCALE).astype(BF)
            dv = dot_nn(pr.astype(BF), dm)
            dk = dot_nn(ds, q)
            if r == 0:
                dk_acc[...] = dk
                dv_acc[...] = dv
            else:
                dk_acc[...] += dk
                dv_acc[...] += dv
            dproj_ref[:, cols] = rotated_back(dot_nn(kt[g], ds).T)
        for b in range(n):
            sl = slice(b * rows, (b + 1) * rows)

            @pl.when(b == z)
            def _():
                dkv_ref[:, g * HEAD:(g + 1) * HEAD] = dk_acc[sl]
                dkv_ref[:, KV_WIDTH + g * HEAD:KV_WIDTH + (g + 1) * HEAD] = dv_acc[sl]

            @pl.when(b != z)
            def _():
                part[b, g, :, 0:HEAD] = dk_acc[sl].astype(BF)
                part[b, g, :, HEAD:2 * HEAD] = dv_acc[sl].astype(BF)

            scatter.computed(b, g)

    def add_own(p, value):
        a = slice(p * HEAD, (p + 1) * HEAD)
        c = slice(KV_WIDTH + p * HEAD, KV_WIDTH + (p + 1) * HEAD)
        dkv_ref[:, a] = dkv_ref[:, a] + value[:, :HEAD]
        dkv_ref[:, c] = dkv_ref[:, c] + value[:, HEAD:]

    for t in scatter.steps():
        scatter.step(t, add_own)
    for g in range(KV_HEADS):
        cols = slice(Q_WIDTH + g * HEAD, Q_WIDTH + (g + 1) * HEAD)
        dproj_ref[:, cols] = rotated_back(dkv_ref[:, g * HEAD:(g + 1) * HEAD])
    dproj_ref[:, Q_WIDTH + KV_WIDTH:] = dkv_ref[:, KV_WIDTH:].astype(BF)
    scatter.finish()


def attention_backward(q, kvall, lse, dm, cosine, sine, pos_q, pos_k, n):
    rows = q.shape[0]
    return pl.pallas_call(
        functools.partial(attention_backward_kernel, n),
        out_shape=jax.ShapeDtypeStruct((rows, Q_WIDTH + 2 * KV_WIDTH), BF),
        in_specs=[VM] * 8,
        out_specs=VM,
        scratch_shapes=[
            pltpu.VMEM((rows, 2 * KV_WIDTH), F32),
            pltpu.VMEM((KV_HEADS, HEAD, n * rows), BF),
            pltpu.VMEM((n * rows, HEAD), F32),
            pltpu.VMEM((n * rows, HEAD), F32),
        ] + [pltpu.VMEM((n, KV_HEADS, rows, 2 * HEAD), BF)] * 3 + scatter_sems(n, KV_HEADS),
        compiler_params=params(4),
        cost_estimate=pl.CostEstimate(
            flops=10 * n * rows * rows * Q_WIDTH, transcendentals=n * rows * rows * QUERY_HEADS,
            bytes_accessed=16 << 20),
        name="attention_backward",
    )(q, kvall, lse, dm, cosine, sine, pos_q, pos_k)


class Fold:
    def __init__(self, cube, src, mine, first, later, load_sem, send1, recv1, send2, recv2):
        self.cube, self.src = cube, src
        self.mine, self.first, self.later = mine, first, later
        self.load_sem, self.send1, self.recv1 = load_sem, send1, recv1
        self.send2, self.recv2 = send2, recv2
        self.rows = mine.shape[1]
        self.half = self.rows // 2
        self.steps = cube.plan()
        self.stages = len(cube.chip_bits)

    def _load(self, d):
        return pltpu.make_async_copy(
            self.src(self.cube.flip(2 * d)), self.mine.at[d], self.load_sem.at[d])

    def _core(self, d):
        return pltpu.make_async_remote_copy(
            src_ref=self.src(self.cube.flip(2 * d | 1)), dst_ref=self.first.at[d],
            send_sem=self.send1.at[d], recv_sem=self.recv1.at[d],
            device_id={"fsdp": self.cube.flip(1)}, device_id_type=MESH)

    def _hop(self, half, stage, index):
        bit, rest, slot = self.steps[half, stage]
        rows = pl.ds(half * self.half, self.half)
        return pltpu.make_async_remote_copy(
            src_ref=self.mine.at[bit | rest[index], rows],
            dst_ref=self.later.at[half, slot + index],
            send_sem=self.send2.at[half, slot + index],
            recv_sem=self.recv2.at[half, slot + index],
            device_id={"fsdp": self.cube.flip(2 * bit)}, device_id_type=MESH)

    def _hops(self, stage):
        return [self._hop(half, stage, i)
                for half in (0, 1) for i in range(len(self.steps[half, stage][1]))]

    def _add(self, d, base, size, other):
        dtype = self.mine.dtype
        strip = 48 if size % 48 == 0 else size

        @pl.loop(0, size // strip)
        def _(i):
            into = pl.ds(pl.multiple_of(base + i * strip, 8), strip)
            rows = pl.ds(pl.multiple_of(i * strip, 8), strip)
            self.mine[d, into] = (
                self.mine[d, into].astype(F32) + other(rows).astype(F32)).astype(dtype)

    def start(self):
        for d in range(self.cube.chips):
            self._core(d).start()
        for d in range(self.cube.chips):
            self._load(d).start()

    def phase(self, k):
        if k == 0:
            for d in range(self.cube.chips):
                self._load(d).wait()
                self._core(d).wait_recv()
                self._add(d, 0, self.rows, lambda rows, d=d: self.first[d, rows])
        else:
            for half in (0, 1):
                _, rest, slot = self.steps[half, k - 1]
                for i, e in enumerate(rest):
                    self._hop(half, k - 1, i).wait_recv()
                    self._add(e, half * self.half, self.half,
                              lambda rows, h=half, j=slot + i: self.later[h, j, rows])
        if k < self.stages:
            for c in self._hops(k):
                c.start()

    def finish(self):
        for d in range(self.cube.chips):
            self._core(d).wait_send()
        for stage in range(self.stages):
            for c in self._hops(stage):
                c.wait_send()


def fold_scratch(owners, rows, width, dtype):
    chips = owners // 2
    return [
        pltpu.VMEM((chips, rows, width), dtype),
        pltpu.VMEM((chips, rows, width), dtype),
        pltpu.VMEM((2, chips - 1, rows // 2, width), dtype),
        pltpu.SemaphoreType.DMA((chips,)),
        pltpu.SemaphoreType.DMA((chips,)),
        pltpu.SemaphoreType.DMA((chips,)),
        pltpu.SemaphoreType.DMA((2, chips - 1)),
        pltpu.SemaphoreType.DMA((2, chips - 1)),
    ]


FOLD_REFS = 8


def reduce_kernel(n, owners, small_ref, out_ref, qkv_ref, dw_ref, early_out, early_qkv,
                  small_o, out_o, qkv_o, dw_o, early_out_o, early_qkv_o, *refs):
    line = Line(n)
    cube = Cube(owners)
    refs = list(refs)

    def take(count):
        taken = refs[:count]
        del refs[:count]
        return taken

    sources = [
        lambda q: small_ref.at[q],
        lambda q: out_ref.at[q],
        lambda q: qkv_ref.at[q],
        lambda q: dw_ref.at[q, 0],
        lambda q: dw_ref.at[q, 1],
        lambda q: dw_ref.at[q, 2],
    ]
    folds = [Fold(cube, src, *take(FOLD_REFS)) for src in sources]
    small_all, = take(1)
    gather_small = Gather(line, small_all, *take(3))
    shared = []
    for _ in range(4):
        part, from_l, from_r, total, own = take(5)
        shared.append((Scatter(line, 1, part, from_l, from_r, *take(4)), part,
                       Gather(line, total, *take(3)), total, own))
    write_sem, = take(1)
    targets = (out_o, qkv_o, early_out_o, early_qkv_o)

    def share(index, value):
        scatter, part, _, _, own = shared[index]
        rows = part.shape[2]
        for b in range(n):
            @pl.when(b == line.z)
            def _():
                own[...] = value(slice(b * rows, (b + 1) * rows)).astype(F32)

            @pl.when(b != line.z)
            def _():
                part[b, 0] = value(slice(b * rows, (b + 1) * rows))

            scatter.computed(b, 0)

    def scatter_step(indices, t):
        for index in indices:
            scatter, _, _, _, own = shared[index]

            def add_own(p, value):
                own[...] = own[...] + value

            scatter.step(t, add_own)

    def gather_start(indices):
        for index in indices:
            _, _, gather, total, own = shared[index]
            total[line.z] = own[...].astype(BF)
            gather.start(total.at[line.z])

    def gather_step(indices, i):
        for index in indices:
            shared[index][2].arrive(line.order(i))

    def collect(indices):
        for index in indices:
            targets[index][...] = shared[index][3][...].reshape(targets[index].shape)

    def line_jobs(indices):
        jobs = [functools.partial(scatter_step, indices, t)
                for t in range(1, 2 * (n - 1) + 1)]
        jobs.append(functools.partial(gather_start, indices))
        jobs += [functools.partial(gather_step, indices, i) for i in range(1, n)]
        jobs.append(functools.partial(collect, indices))
        return jobs

    def small_job():
        for i in range(1, n):
            gather_small.arrive(line.order(i))
        small_o[...] = jnp.sum(small_all[...], axis=0)

    joint_barrier(line, cube)
    for f in folds:
        f.start()
    share(2, lambda rows: early_out[rows])
    share(3, lambda rows: early_qkv[rows])
    last = folds[0].stages
    jobs = line_jobs((2, 3))

    def after(index):
        fold = folds[index]
        if index == 0:
            small_all[line.z] = fold.mine[0]
            gather_small.start(small_all.at[line.z])
            jobs.append(small_job)
        elif index <= 2:
            share(index - 1, lambda rows: fold.mine[0, rows])
            if index == 2:
                jobs.extend(line_jobs((0, 1)))
        else:
            pltpu.make_async_copy(fold.mine.at[0], dw_o.at[index - 3], write_sem.at[index - 3]).start()

    count = len(folds)
    for t in range(count + last):
        for k in range(last + 1):
            if 0 <= t - k < count:
                folds[t - k].phase(k)
                if k == last:
                    after(t - k)
                for _ in range(2):
                    if jobs and t >= 1:
                        jobs.pop(0)()
    for job in jobs:
        job()
    for k in range(3):
        pltpu.make_async_copy(folds[3 + k].mine.at[0], dw_o.at[k], write_sem.at[k]).wait()
    for f in folds:
        f.finish()
    gather_small.finish()
    for scatter, _, gather, _, _ in shared:
        scatter.finish()
        gather.finish()


def reduce_all(small, out_g, qkv_g, dw, early_out, early_qkv, n):
    owners, shard, d_model = out_g.shape
    width = dw.shape[3]
    qkv_width = qkv_g.shape[2]
    scratch = fold_scratch(owners, small.shape[1], 128, F32)
    scratch += fold_scratch(owners, shard, d_model, BF)
    scratch += fold_scratch(owners, shard, qkv_width, BF)
    for _ in range(3):
        scratch += fold_scratch(owners, shard, width, BF)
    scratch += [pltpu.VMEM((n, small.shape[1], 128), F32)] + gather_sems(n)
    for w in (d_model, qkv_width, d_model, qkv_width):
        scratch += [pltpu.VMEM((n, 1, shard // n, w), BF)] * 3
        scratch += [pltpu.VMEM((n, shard // n, w), BF), pltpu.VMEM((shard // n, w), F32)]
        scratch += scatter_sems(n, 1) + gather_sems(n)
    scratch += [pltpu.SemaphoreType.DMA((3,))]
    return pl.pallas_call(
        functools.partial(reduce_kernel, n, owners),
        out_shape=(
            jax.ShapeDtypeStruct(small.shape[1:], F32),
            jax.ShapeDtypeStruct((shard, d_model), BF),
            jax.ShapeDtypeStruct((shard, qkv_width), BF),
            jax.ShapeDtypeStruct((3, shard, width), BF),
            jax.ShapeDtypeStruct((shard, d_model), BF),
            jax.ShapeDtypeStruct((shard, qkv_width), BF),
        ),
        in_specs=[ANY] * 4 + [VM] * 2,
        out_specs=[VM, VM, VM, ANY, VM, VM],
        scratch_shapes=scratch,
        compiler_params=params(5),
        cost_estimate=pl.CostEstimate(
            flops=1 << 20, transcendentals=0, bytes_accessed=300 << 20),
        name="reduce_all",
    )(small, out_g, qkv_g, dw, early_out, early_qkv)


def normalize(stream, gain):
    return stream * lax.rsqrt(jnp.mean(stream * stream, axis=-1, keepdims=True) + EPSILON) * gain


def normalize_back(grad, stream, gain):
    r = lax.rsqrt(jnp.mean(stream * stream, axis=-1, keepdims=True) + EPSILON)
    u = grad * gain
    back = r * (u - stream * (r * r) * jnp.mean(u * stream, axis=-1, keepdims=True))
    return back, jnp.sum(grad * stream * r, axis=0)


def frequencies():
    return jnp.power(ROPE_BASE, -(jnp.arange(HEAD // 2, dtype=F32) * 2.0 / HEAD))


def shards(hidden_in, cotangent, seq_lengths, tile_place, norm_attn, w_qkv, b_qkv, w_out,
           norm_mlp, w_gate, w_up, w_down):
    n = lax.axis_size("context")
    owners = lax.axis_size("fsdp")
    rows, d_model = hidden_in.shape[1:]
    hidden_units = w_gate.shape[2]
    width = -(-hidden_units // 128) * 128
    pad = width - hidden_units
    total = n * rows

    row_index = jnp.arange(total, dtype=jnp.int32)
    tile_order = tile_place[0]
    selector = (
        row_index[:, None] // TILE == jnp.arange(tile_order.shape[0], dtype=jnp.int32)[None, :]
    ).astype(jnp.int32)
    position = jnp.sum(selector * tile_order[None, :], axis=1) * TILE + row_index % TILE
    valid = position < seq_lengths[0]
    offset = lax.axis_index("context") * rows
    my_position = lax.dynamic_slice_in_dim(position, offset, rows)
    my_valid = lax.dynamic_slice_in_dim(valid, offset, rows)
    pos_q = my_position[None, :]
    pos_k = jnp.where(valid, position, 1 << 30)[:, None]
    angles = my_position.astype(F32)[:, None] * frequencies()
    cosine, sine = jnp.cos(angles), jnp.sin(angles)
    cosine = jnp.concatenate([cosine, cosine], axis=1)
    sine = jnp.concatenate([-sine, sine], axis=1)

    shard = norm_attn.shape[1]
    bias_shard = b_qkv.shape[1]

    def ffn_shard(l):
        return jnp.stack([
            jnp.pad(m, ((0, 0), (0, pad))) for m in (w_gate[l], w_up[l], w_down[l].T)])

    def packed(parts, lead):
        flat = jnp.concatenate(parts, axis=-1)
        used = flat.shape[-1]
        lines = -(-used // (16 * 128)) * 16
        flat = jnp.pad(flat, ((0, 0),) * (flat.ndim - 1) + ((0, lines * 128 - used),))
        return flat.reshape(lead + (lines, 128))

    small = packed(
        [m.reshape(-1).astype(F32) for m in (norm_attn, norm_mlp, b_qkv)], ())
    first_ffn = ffn_shard(0)
    first_ffn, small = lax.optimization_barrier((first_ffn, small))
    ffn_weights = [lax.all_gather(first_ffn, "fsdp", axis=0, tiled=False)]
    small, qkv_w = spread_all(owners, small, w_qkv[0])
    qkv_weights = [qkv_w.reshape(d_model, -1)]
    out_weights = []
    small = small.reshape(owners, -1)
    gains_attn, gains_mlp, biases = [], [], []
    for l in range(LAYERS):
        gains_attn.append(small[:, l * shard:(l + 1) * shard].reshape(-1))
        gains_mlp.append(small[:, (LAYERS + l) * shard:(LAYERS + l + 1) * shard].reshape(-1))
        start = 2 * LAYERS * shard + l * bias_shard
        biases.append(small[:, start:start + bias_shard].reshape(-1))

    stream = hidden_in[0].astype(F32)
    kept = []
    for l in range(LAYERS):
        qkv_w, ffn_w = qkv_weights[l], ffn_weights[l]
        if l + 1 < LAYERS:
            ffn_weights.append(lax.all_gather(ffn_shard(l + 1), "fsdp", axis=0, tiled=False))
        normed = normalize(stream, gains_attn[l]).astype(BF)
        projected = jnp.dot(normed, qkv_w, preferred_element_type=F32) + biases[l]
        following = (w_out[l],) if l == 0 else ()
        mixed, lse, kvall, q, *out_w = attention_forward(
            projected, cosine, sine, pos_q, pos_k, n, owners, following)
        out_weights += [m.reshape(Q_WIDTH, d_model) for m in out_w]
        out_w = out_weights[l]
        middle = stream + jnp.dot(mixed, out_w, preferred_element_type=F32)
        normed_two = normalize(middle, gains_mlp[l]).astype(BF)
        if l + 1 < LAYERS:
            xall, gate, up, y, next_qkv, next_out = ffn_forward(
                normed_two, ffn_w, n, (w_qkv[l + 1], w_out[l + 1]))
            qkv_weights.append(next_qkv.reshape(d_model, -1))
            out_weights.append(next_out.reshape(Q_WIDTH, d_model))
        else:
            xall, gate, up, y = ffn_forward(normed_two, ffn_w, n)
        kept.append((stream, normed, q, kvall, lse, mixed, middle, xall, gate, up,
                     qkv_w, out_w, ffn_w))
        stream = middle + y
    layer_out = stream.astype(BF)[None]

    gradient = cotangent[0].astype(F32) * my_valid[:, None].astype(F32)
    small_grads = [None] * LAYERS
    big_grads = [None] * LAYERS
    for l in reversed(range(LAYERS)):
        (stream, normed, q, kvall, lse, mixed, middle, xall, gate, up,
         qkv_w, out_w, ffn_w) = kept[l]
        dw, dx = ffn_backward(gradient.astype(BF), ffn_w, xall, gate, up, n)
        if l < LAYERS - 1:
            out_sum, qkv_sum, dw_sum = big_grads[l + 1]
            dx, dw_sum = lax.optimization_barrier((dx, dw_sum))
        back, gain_two = normalize_back(dx, middle, gains_mlp[l])
        d_middle = gradient + back
        d_low = d_middle.astype(BF)
        d_mixed = jnp.einsum("td,cd->tc", d_low, out_w, preferred_element_type=F32).astype(BF)
        out_grad = jnp.einsum("tc,td->cd", mixed, d_low, preferred_element_type=F32).astype(BF)
        d_projected = attention_backward(
            q, kvall, lse, d_mixed, cosine, sine, pos_q, pos_k, n)
        if l < LAYERS - 1:
            d_projected, out_sum = lax.optimization_barrier((d_projected, out_sum))
            big_grads[l + 1] = (out_sum, qkv_sum, dw_sum)
        bias_grad = jnp.sum(d_projected.astype(F32), axis=0)
        d_normed = jnp.einsum("tc,dc->td", d_projected, qkv_w, preferred_element_type=F32)
        qkv_grad = jnp.einsum(
            "td,tc->dc", normed, d_projected, preferred_element_type=F32).astype(BF)
        back, gain_one = normalize_back(d_normed, stream, gains_attn[l])
        gradient = d_middle + back
        small_grads[l] = (gain_one, gain_two, bias_grad)
        if l > 0:
            big_grads[l] = (
                lax.psum_scatter(out_grad, "fsdp", scatter_dimension=0, tiled=True),
                lax.psum_scatter(qkv_grad, "fsdp", scatter_dimension=0, tiled=True),
                lax.psum_scatter(dw, "fsdp", scatter_dimension=0, tiled=False))
        else:
            small = packed([
                m.reshape(owners, -1)
                for k in range(3) for m in (small_grads[i][k] for i in range(LAYERS))], (owners,))
            out_early, qkv_early, dw_sum = big_grads[l + 1]
            small, out_sum, qkv_sum, dw_last, out_early, qkv_early = reduce_all(
                small, out_grad.reshape(owners, shard, d_model),
                qkv_grad.reshape(owners, shard, qkv_grad.shape[1]), dw, out_early, qkv_early, n)
            big_grads[l + 1] = (out_early, qkv_early, dw_sum)
            small = small.reshape(-1)
            big_grads[l] = (out_sum, qkv_sum, dw_last)

    grad_norm_attn = small[:LAYERS * shard].reshape(LAYERS, shard)
    grad_norm_mlp = small[LAYERS * shard:2 * LAYERS * shard].reshape(LAYERS, shard)
    start = 2 * LAYERS * shard
    grad_b_qkv = small[start:start + LAYERS * bias_shard].reshape(LAYERS, bias_shard)

    def stacked(pick):
        return jnp.stack([pick(big_grads[l]).astype(F32) for l in range(LAYERS)])

    return (
        layer_out,
        gradient[None],
        grad_norm_attn,
        stacked(lambda m: m[1]),
        grad_b_qkv,
        stacked(lambda m: m[0]),
        grad_norm_mlp,
        stacked(lambda m: m[2][0, :, :hidden_units]),
        stacked(lambda m: m[2][1, :, :hidden_units]),
        stacked(lambda m: m[2][2, :, :hidden_units].T),
    )


def solution(mesh):
    return jax.shard_map(
        shards,
        mesh=mesh,
        in_specs=(
            P("fsdp", "context", None),
            P("fsdp", "context", None),
            P("fsdp"),
            P("fsdp", None),
            P(None, "fsdp"),
            P(None, "fsdp", None),
            P(None, "fsdp"),
            P(None, "fsdp", None),
            P(None, "fsdp"),
            P(None, "fsdp", "context"),
            P(None, "fsdp", "context"),
            P(None, "context", "fsdp"),
        ),
        out_specs=(
            P("fsdp", "context", None),
            P("fsdp", "context", None),
            P(None, "fsdp"),
            P(None, "fsdp", None),
            P(None, "fsdp"),
            P(None, "fsdp", None),
            P(None, "fsdp"),
            P(None, "fsdp", "context"),
            P(None, "fsdp", "context"),
            P(None, "context", "fsdp"),
        ),
        check_vma=False,
    )
```

```python
import functools
import math

import jax
import jax.numpy as jnp
from jax import lax
from jax.experimental import pallas as pl
from jax.experimental.pallas import tpu as pltpu
from jax.sharding import PartitionSpec as P

QUERY_HEADS = 12
KV_HEADS = 2
HEAD = 128
LAYERS = 2
TILE = 128
Q_WIDTH = QUERY_HEADS * HEAD
KV_WIDTH = KV_HEADS * HEAD
PER_GROUP = QUERY_HEADS // KV_HEADS
SCALE = 1.0 / math.sqrt(HEAD)
EPSILON = 1e-06
ROPE_BASE = 1000000.0
BF = jnp.bfloat16
F32 = jnp.float32
MESH = pl.DeviceIdType.MESH
VMEM_LIMIT = 66 * 1024 * 1024
ANY = pl.BlockSpec(memory_space=pl.ANY)
VM = pl.BlockSpec(memory_space=pltpu.VMEM)


def dot_nn(a, b):
    return lax.dot_general(a, b, (((1,), (0,)), ((), ())), preferred_element_type=F32)


def dot_nt(a, b):
    return lax.dot_general(a, b, (((1,), (1,)), ((), ())), preferred_element_type=F32)


def dot_tn(a, b):
    return lax.dot_general(a, b, (((0,), (0,)), ((), ())), preferred_element_type=F32)


def lane_tile(width, most):
    best = 128
    for k in range(1, most // 128 + 1):
        if width % (128 * k) == 0:
            best = 128 * k
    return best


class Line:
    def __init__(self, n):
        self.n = n
        self.z = lax.axis_index("context")
        self.right = lax.rem(self.z + 1, n)
        self.left = lax.rem(self.z + n - 1, n)
        self.has_right = self.z < n - 1
        self.has_left = self.z > 0

    def barrier(self):
        bar = pltpu.get_barrier_semaphore()

        @pl.when(self.has_right)
        def _():
            pl.semaphore_signal(bar, inc=1, device_id={"context": self.right}, device_id_type=MESH)

        @pl.when(self.has_left)
        def _():
            pl.semaphore_signal(bar, inc=1, device_id={"context": self.left}, device_id_type=MESH)

        both = self.has_right & self.has_left

        @pl.when(both)
        def _():
            pl.semaphore_wait(bar, 2)

        @pl.when(jnp.logical_not(both))
        def _():
            pl.semaphore_wait(bar, 1)

    def order(self, i):
        z, n = self.z, self.n
        short = jnp.minimum(z, n - 1 - z)
        j = i - 1
        paired = j < 2 * short
        k = jnp.where(paired, j // 2 + 1, j - short + 1)
        goes_left = jnp.where(paired, lax.rem(j, 2) == 0, z > n - 1 - z)
        return jnp.where(i == 0, z, jnp.where(goes_left, z - k, z + k))


def remote(src, dst, send, recv, target):
    return pltpu.make_async_remote_copy(
        src_ref=src, dst_ref=dst, send_sem=send, recv_sem=recv,
        device_id={"context": target}, device_id_type=MESH,
    )


class Gather:
    def __init__(self, line, slots, send_r, send_l, recv):
        self.line, self.slots = line, slots
        self.send_r, self.send_l, self.recv = send_r, send_l, recv

    def _right(self, b, src):
        return remote(src, self.slots.at[b], self.send_r.at[b], self.recv.at[b], self.line.right)

    def _left(self, b, src):
        return remote(src, self.slots.at[b], self.send_l.at[b], self.recv.at[b], self.line.left)

    def start(self, own):
        line = self.line

        @pl.when(line.has_right)
        def _():
            self._right(line.z, own).start()

        @pl.when(line.has_left)
        def _():
            self._left(line.z, own).start()

    def arrive(self, b):
        line = self.line
        self._right(b, self.slots.at[b]).wait_recv()

        @pl.when((b < line.z) & line.has_right)
        def _():
            self._right(b, self.slots.at[b]).start()

        @pl.when((b > line.z) & line.has_left)
        def _():
            self._left(b, self.slots.at[b]).start()

    def finish(self):
        line = self.line
        for b in range(line.n):
            @pl.when((b <= line.z) & line.has_right)
            def _():
                self._right(b, self.slots.at[b]).wait_send()

            @pl.when((b >= line.z) & line.has_left)
            def _():
                self._left(b, self.slots.at[b]).wait_send()


class Scatter:
    def __init__(self, line, pieces, part, from_left, from_right, send_r, send_l, recv_l, recv_r,
                 trim=0):
        self.line, self.pieces, self.part, self.trim = line, pieces, part, trim
        self.from_left, self.from_right = from_left, from_right
        self.send_r, self.send_l, self.recv_l, self.recv_r = send_r, send_l, recv_l, recv_r

    def left_slot(self, b):
        return max(b - self.trim, 0) if isinstance(b, int) else b - self.trim

    def right_slot(self, b):
        return min(b, self.line.n - 1 - self.trim) if isinstance(b, int) else b

    def _right(self, b, p):
        return remote(self.part.at[b, p], self.from_left.at[self.left_slot(b), p], self.send_r.at[b, p],
                      self.recv_l.at[b, p], self.line.right)

    def _left(self, b, p):
        return remote(self.part.at[b, p], self.from_right.at[self.right_slot(b), p], self.send_l.at[b, p],
                      self.recv_r.at[b, p], self.line.left)

    def computed(self, b, p):
        line = self.line

        @pl.when((line.z == 0) & (b > 0))
        def _():
            self._right(b, p).start()

        @pl.when((line.z == line.n - 1) & (b < line.n - 1))
        def _():
            self._left(b, p).start()

    def steps(self):
        return range(1, 2 * (self.line.n - 1) + 1)

    def step(self, t, add_own):
        line = self.line
        n, z = line.n, line.z
        b_left = t - z

        @pl.when(line.has_left & (b_left >= z) & (b_left < n))
        def _():
            for p in range(self.pieces):
                self._right(b_left, p).wait_recv()

                @pl.when(b_left == z)
                def _():
                    add_own(p, self.from_left[self.left_slot(b_left), p].astype(F32))

                @pl.when(b_left != z)
                def _():
                    self.part[b_left, p] = (
                        self.part[b_left, p].astype(F32) + self.from_left[self.left_slot(b_left), p].astype(F32)
                    ).astype(BF)
                    self._right(b_left, p).start()

        b_right = 2 * (n - 1) - t - z

        @pl.when(line.has_right & (b_right >= 0) & (b_right <= z))
        def _():
            for p in range(self.pieces):
                self._left(b_right, p).wait_recv()

                @pl.when(b_right == z)
                def _():
                    add_own(p, self.from_right[self.right_slot(b_right), p].astype(F32))

                @pl.when(b_right != z)
                def _():
                    self.part[b_right, p] = (
                        self.part[b_right, p].astype(F32) + self.from_right[self.right_slot(b_right), p].astype(F32)
                    ).astype(BF)
                    self._left(b_right, p).start()

    def finish(self):
        line = self.line
        for b in range(line.n):
            @pl.when((b > line.z) & line.has_right)
            def _():
                for p in range(self.pieces):
                    self._right(b, p).wait_send()

            @pl.when((b < line.z) & line.has_left)
            def _():
                for p in range(self.pieces):
                    self._left(b, p).wait_send()


def gather_sems(n):
    return [pltpu.SemaphoreType.DMA((n,))] * 3


def scatter_sems(n, pieces):
    return [pltpu.SemaphoreType.DMA((n, pieces))] * 4


def params(cid):
    return pltpu.CompilerParams(
        collective_id=cid, has_side_effects=True, vmem_limit_bytes=VMEM_LIMIT
    )


def bits_of(owners):
    return [1 << i for i in range(owners.bit_length() - 1)]


class Cube:
    def __init__(self, owners):
        self.owners = owners
        self.me = lax.axis_index("fsdp")
        self.bits = bits_of(owners)
        self.chip_bits = [b // 2 for b in self.bits[1:]]
        self.chips = owners // 2

    def flip(self, mask):
        index = self.me
        for b in self.bits:
            if mask & b:
                index = index + b - 2 * b * lax.rem(self.me // b, 2)
        return index

    def signal(self, bar):
        for b in self.bits:
            pl.semaphore_signal(bar, inc=1, device_id={"fsdp": self.flip(b)}, device_id_type=MESH)

    def order(self, half):
        return self.chip_bits[::-1] if half == 0 else self.chip_bits

    def plan(self):
        steps = {}
        for half in (0, 1):
            order, slot = self.order(half), 0
            for stage, bit in enumerate(order):
                rest = [0]
                for other in order[stage + 1:]:
                    rest = rest + [m | other for m in rest]
                steps[half, stage] = (bit, rest, slot)
                slot += len(rest)
        return steps


def joint_barrier(line, cube):
    bar = pltpu.get_barrier_semaphore()
    cube.signal(bar)
    peers = len(cube.bits)

    @pl.when(line.has_right)
    def _():
        pl.semaphore_signal(bar, inc=1, device_id={"context": line.right}, device_id_type=MESH)

    @pl.when(line.has_left)
    def _():
        pl.semaphore_signal(bar, inc=1, device_id={"context": line.left}, device_id_type=MESH)

    both = line.has_right & line.has_left

    @pl.when(both)
    def _():
        pl.semaphore_wait(bar, peers + 2)

    @pl.when(jnp.logical_not(both))
    def _():
        pl.semaphore_wait(bar, peers + 1)


class Spread:
    def __init__(self, cube, own, full, own_sem, send, recv, core_send, core_recv):
        self.cube, self.own, self.full = cube, own, full
        self.own_sem, self.send, self.recv = own_sem, send, recv
        self.core_send, self.core_recv = core_send, core_recv
        self.half = own.shape[0] // 2
        self.stages = len(cube.chip_bits)

    def _rows(self, half):
        return pl.ds(half * self.half, self.half)

    def _block(self, half, mask):
        return self.full.at[self.cube.flip(mask), self._rows(half)]

    def _source(self, half, mask):
        return self._block(half, 2 * mask) if mask else self.own.at[self._rows(half)]

    def _masks(self, half, stage):
        masks = [0]
        for bit in self.cube.order(half)[:stage]:
            masks = masks + [m | bit for m in masks]
        return masks

    def _hop(self, half, stage, mask):
        bit = self.cube.order(half)[stage]
        return pltpu.make_async_remote_copy(
            src_ref=self._source(half, mask), dst_ref=self._block(half, 2 * mask),
            send_sem=self.send.at[half, mask | bit], recv_sem=self.recv.at[half, mask | bit],
            device_id={"fsdp": self.cube.flip(2 * bit)}, device_id_type=MESH)

    def _arrival(self, half, mask):
        block = self._block(half, 2 * mask)
        return pltpu.make_async_remote_copy(
            src_ref=block, dst_ref=block,
            send_sem=self.send.at[half, mask], recv_sem=self.recv.at[half, mask],
            device_id={"fsdp": self.cube.flip(1)}, device_id_type=MESH)

    def _core(self, half, mask):
        return pltpu.make_async_remote_copy(
            src_ref=self._source(half, mask), dst_ref=self._block(half, 2 * mask),
            send_sem=self.core_send.at[half, mask], recv_sem=self.core_recv.at[half, mask],
            device_id={"fsdp": self.cube.flip(1)}, device_id_type=MESH)

    def _core_arrival(self, half, mask):
        block = self._block(half, 2 * mask | 1)
        return pltpu.make_async_remote_copy(
            src_ref=block, dst_ref=block,
            send_sem=self.core_send.at[half, mask], recv_sem=self.core_recv.at[half, mask],
            device_id={"fsdp": self.cube.flip(1)}, device_id_type=MESH)

    def _own_copy(self):
        return pltpu.make_async_copy(self.own, self.full.at[self.cube.me], self.own_sem)

    def start(self):
        for stage in range(self.stages):
            for half in (0, 1):
                self._hop(half, stage, 0).start()
        for half in (0, 1):
            self._core(half, 0).start()
        self._own_copy().start()

    def phase(self, k):
        for half in (0, 1):
            bit = self.cube.order(half)[k - 1]
            for m in self._masks(half, k - 1):
                self._arrival(half, m | bit).wait_recv()
                for stage in range(k, self.stages):
                    self._hop(half, stage, m | bit).start()
                self._core(half, m | bit).start()

    def finish(self):
        self._own_copy().wait()
        for half in (0, 1):
            for m in range(self.cube.chips):
                self._core_arrival(half, m).wait_recv()
                self._core(half, m).wait_send()
            for stage in range(self.stages):
                for m in self._masks(half, stage):
                    self._hop(half, stage, m).wait_send()


SPREAD_SEMS = 5


def spread_sems(owners):
    chips = owners // 2
    return [pltpu.SemaphoreType.DMA] + [pltpu.SemaphoreType.DMA((2, chips))] * 4


def spread_shapes(owners, shards):
    return tuple(jax.ShapeDtypeStruct((owners,) + m.shape, m.dtype) for m in shards)


def spread_kernel(owners, count, *refs):
    cube = Cube(owners)
    spreads = [
        Spread(cube, refs[i], refs[count + i],
               *refs[2 * count + SPREAD_SEMS * i:2 * count + SPREAD_SEMS * (i + 1)])
        for i in range(count)]
    bar = pltpu.get_barrier_semaphore()
    cube.signal(bar)
    pl.semaphore_wait(bar, len(cube.bits))
    for s in spreads:
        s.start()
    for k in range(1, len(cube.chip_bits) + 1):
        for s in spreads:
            s.phase(k)
    for s in spreads:
        s.finish()


def spread_all(owners, *shards):
    count = len(shards)
    return pl.pallas_call(
        functools.partial(spread_kernel, owners, count),
        out_shape=spread_shapes(owners, shards),
        in_specs=[VM] * count,
        out_specs=[ANY] * count,
        scratch_shapes=spread_sems(owners) * count,
        compiler_params=params(6),
        cost_estimate=pl.CostEstimate(
            flops=1 << 20, transcendentals=0, bytes_accessed=150 << 20),
        name="spread_all",
    )(*shards)


def ffn_forward_kernel(n, pieces, count, *refs):
    x_ref, w_ref = refs[:2]
    next_own = refs[2:2 + count]
    xall_ref, gate_ref, up_ref, y_ref = refs[2 + count:6 + count]
    next_full = refs[6 + count:6 + 2 * count]
    (w_v, xbuf, gbuf, ubuf, hbuf, part, from_l, from_r,
     w_sem, x_sem, out_sem, *sems) = refs[6 + 2 * count:]
    line = Line(n)
    z = line.z
    owners, _, rows, width = w_ref.shape
    d_model = x_ref.shape[1]
    tile = lane_tile(width, 256)
    piece = d_model // pieces
    gather = Gather(line, xbuf, *sems[:3])
    scatter = Scatter(line, pieces, part, from_l, from_r, *sems[3:7])
    spreads = []
    stages = 0
    if count:
        cube = Cube(owners)
        stages = len(cube.chip_bits)
        for i in range(count):
            at = 7 + SPREAD_SEMS * i
            spreads.append(Spread(cube, next_own[i], next_full[i], *sems[at:at + SPREAD_SEMS]))

    def w_copy(k, f):
        return pltpu.make_async_copy(
            w_ref.at[f, k], w_v.at[k, pl.ds(f * rows, rows)], w_sem.at[k, f]
        )

    def x_out(b):
        return pltpu.make_async_copy(xbuf.at[b], xall_ref.at[b], x_sem.at[b])

    if count:
        joint_barrier(line, cube)
    else:
        line.barrier()
    gather.start(x_ref)
    for s in spreads:
        s.start()
    for k in range(3):
        for f in range(owners):
            w_copy(k, f).start()
    xbuf[z] = x_ref[...]
    for k in range(3):
        for f in range(owners):
            w_copy(k, f).wait()

    @pl.loop(0, n)
    def _(i):
        b = line.order(i)

        @pl.when(i > 0)
        def _():
            gather.arrive(b)

        x_out(b).start()
        slot = lax.rem(i, 2)
        g_copy = pltpu.make_async_copy(gbuf.at[slot], gate_ref.at[b], out_sem.at[0, slot])
        u_copy = pltpu.make_async_copy(ubuf.at[slot], up_ref.at[b], out_sem.at[1, slot])

        @pl.when(i > 1)
        def _():
            g_copy.wait()
            u_copy.wait()

        @pl.loop(0, width // tile)
        def _(j):
            cols = pl.ds(pl.multiple_of(j * tile, tile), tile)
            xb = xbuf[b]
            gate = dot_nn(xb, w_v[0, :, cols])
            up = dot_nn(xb, w_v[1, :, cols])
            gbuf[slot, :, cols] = gate.astype(BF)
            ubuf[slot, :, cols] = up.astype(BF)
            hbuf[:, cols] = (gate * jax.nn.sigmoid(gate) * up).astype(BF)

        g_copy.start()
        u_copy.start()
        for p in range(pieces):
            out = dot_nt(hbuf[...], w_v[2, pl.ds(p * piece, piece)])

            @pl.when(b == z)
            def _():
                y_ref[:, p * piece:(p + 1) * piece] = out

            @pl.when(b != z)
            def _():
                part[b, p] = out.astype(BF)

            scatter.computed(b, p)

        if spreads:
            @pl.when(i == n // 2)
            def _():
                for s in spreads:
                    s.phase(1)

    def add_own(p, value):
        cols = slice(p * piece, (p + 1) * piece)
        y_ref[:, cols] = y_ref[:, cols] + value

    for t in scatter.steps():
        scatter.step(t, add_own)
    for k in range(2, stages + 1):
        for s in spreads:
            s.phase(k)
    for i in range(max(0, n - 2), n):
        slot = i % 2
        pltpu.make_async_copy(gbuf.at[slot], gate_ref.at[0], out_sem.at[0, slot]).wait()
        pltpu.make_async_copy(ubuf.at[slot], up_ref.at[0], out_sem.at[1, slot]).wait()
    for b in range(n):
        x_out(b).wait()
    gather.finish()
    scatter.finish()
    for s in spreads:
        s.finish()


def ffn_forward(x, w, n, following=()):
    rows, d_model = x.shape
    owners, _, shard, width = w.shape
    pieces = 3
    piece = d_model // pieces
    count = len(following)
    return pl.pallas_call(
        functools.partial(ffn_forward_kernel, n, pieces, count),
        out_shape=(
            jax.ShapeDtypeStruct((n, rows, d_model), BF),
            jax.ShapeDtypeStruct((n, rows, width), BF),
            jax.ShapeDtypeStruct((n, rows, width), BF),
            jax.ShapeDtypeStruct((rows, d_model), F32),
        ) + spread_shapes(owners, following),
        in_specs=[VM, ANY] + [VM] * count,
        out_specs=[ANY, ANY, ANY, VM] + [ANY] * count,
        scratch_shapes=[
            pltpu.VMEM((3, d_model, width), BF),
            pltpu.VMEM((n, rows, d_model), BF),
            pltpu.VMEM((2, rows, width), BF),
            pltpu.VMEM((2, rows, width), BF),
            pltpu.VMEM((rows, width), BF),
            pltpu.VMEM((n, pieces, rows, piece), BF),
            pltpu.VMEM((n, pieces, rows, piece), BF),
            pltpu.VMEM((n, pieces, rows, piece), BF),
            pltpu.SemaphoreType.DMA((3, owners)),
            pltpu.SemaphoreType.DMA((n,)),
            pltpu.SemaphoreType.DMA((2, 2)),
        ] + gather_sems(n) + scatter_sems(n, pieces) + spread_sems(owners) * count,
        compiler_params=params(7 if count else 1),
        cost_estimate=pl.CostEstimate(
            flops=6 * n * rows * d_model * width, transcendentals=n * rows * width,
            bytes_accessed=60 << 20),
        name="ffn_forward",
    )(x, w, *following)


def ffn_backward_kernel(n, pieces, groups, g_ref, w_ref, xall_ref, gate_ref, up_ref, dw_ref, dx_ref,
                        w_v, gbuf, xv, gate_v, up_v, hid_v, part, from_l, from_r, stage,
                        w_sem, in_sem, out_sem, *sems):
    line = Line(n)
    z = line.z
    owners, _, shard, width = w_ref.shape
    rows, d_model = g_ref.shape
    tile = lane_tile(width, 256)
    piece = d_model // pieces
    gather = Gather(line, gbuf, *sems[:3])
    scatter = Scatter(line, pieces, part, from_l, from_r, *sems[3:])

    def w_copy(k, f):
        return pltpu.make_async_copy(
            w_ref.at[f, k], w_v.at[k, pl.ds(f * shard, shard)], w_sem.at[k, f]
        )

    def loads(b):
        return (
            pltpu.make_async_copy(gate_ref.at[b], gate_v.at[b], in_sem.at[0, b]),
            pltpu.make_async_copy(up_ref.at[b], up_v.at[b], in_sem.at[1, b]),
        )

    def x_load(b):
        return pltpu.make_async_copy(xall_ref.at[b], xv.at[b], in_sem.at[2, b])

    line.barrier()
    gather.start(g_ref)
    for f in range(owners):
        w_copy(2, f).start()
    for c in loads(z):
        c.start()
    for k in range(2):
        for f in range(owners):
            w_copy(k, f).start()
    for b in range(n):
        @pl.when(b != z)
        def _():
            for c in loads(b):
                c.start()
    for b in range(n):
        x_load(b).start()
    gbuf[z] = g_ref[...]
    for k in (2, 0, 1):
        for f in range(owners):
            w_copy(k, f).wait()

    @pl.loop(0, n)
    def _(i):
        b = line.order(i)

        @pl.when(i > 0)
        def _():
            gather.arrive(b)

        for c in loads(b):
            c.wait()

        @pl.loop(0, width // tile)
        def _(j):
            cols = pl.ds(pl.multiple_of(j * tile, tile), tile)
            d_hidden = dot_nn(gbuf[b], w_v[2, :, cols])
            gate = gate_v[b, :, cols].astype(F32)
            up = up_v[b, :, cols].astype(F32)
            sig = jax.nn.sigmoid(gate)
            act = gate * sig
            hid_v[b, :, cols] = (act * up).astype(BF)
            gate_v[b, :, cols] = (d_hidden * up * (sig + act * (1.0 - sig))).astype(BF)
            up_v[b, :, cols] = (d_hidden * act).astype(BF)

        for p in range(pieces):
            sl = pl.ds(p * piece, piece)
            out = dot_nt(gate_v[b], w_v[0, sl]) + dot_nt(up_v[b], w_v[1, sl])

            @pl.when(b == z)
            def _():
                dx_ref[:, p * piece:(p + 1) * piece] = out

            @pl.when(b != z)
            def _():
                part[b, p] = out.astype(BF)

            scatter.computed(b, p)

    def add_own(p, value):
        cols = slice(p * piece, (p + 1) * piece)
        dx_ref[:, cols] = dx_ref[:, cols] + value

    for b in range(n):
        x_load(b).wait()

    group = d_model // groups
    per = group // shard

    def dw_copies(k, q, slot):
        return [
            pltpu.make_async_copy(
                stage.at[slot, pl.ds(s * shard, shard)], dw_ref.at[q * per + s, k],
                out_sem.at[slot, s])
            for s in range(per)
        ]

    def weight_unit(unit):
        k, q = unit // groups, unit % groups
        slot = unit % 2
        left = (xv, xv, gbuf)[k]
        right = (gate_v, up_v, hid_v)[k]
        if unit >= 2:
            for c in dw_copies((unit - 2) // groups, (unit - 2) % groups, slot):
                c.wait()
        lt = left[:, :, q * group:(q + 1) * group].reshape(n * rows, group)

        @pl.loop(0, width // tile)
        def _(j):
            cols = pl.ds(pl.multiple_of(j * tile, tile), tile)
            stage[slot, :, cols] = dot_tn(
                lt, right[:, :, cols].reshape(n * rows, tile)
            ).astype(BF)

        for c in dw_copies(k, q, slot):
            c.start()

    units = 3 * groups
    steps = list(scatter.steps())
    done = 0
    for index, t in enumerate(steps):
        scatter.step(t, add_own)
        until = units * (index + 1) // len(steps)
        while done < until:
            weight_unit(done)
            done += 1
    for unit in range(units - 2, units):
        for c in dw_copies(unit // groups, unit % groups, unit % 2):
            c.wait()
    gather.finish()
    scatter.finish()


def ffn_backward(g, w, xall, gate, up, n):
    rows, d_model = g.shape
    owners, _, shard, width = w.shape
    pieces, groups = 3, 4
    piece = d_model // pieces
    per = d_model // groups // shard
    return pl.pallas_call(
        functools.partial(ffn_backward_kernel, n, pieces, groups),
        out_shape=(
            jax.ShapeDtypeStruct((owners, 3, shard, width), BF),
            jax.ShapeDtypeStruct((rows, d_model), F32),
        ),
        in_specs=[VM, ANY, ANY, ANY, ANY],
        out_specs=[ANY, VM],
        scratch_shapes=[
            pltpu.VMEM((3, d_model, width), BF),
            pltpu.VMEM((n, rows, d_model), BF),
            pltpu.VMEM((n, rows, d_model), BF),
            pltpu.VMEM((n, rows, width), BF),
            pltpu.VMEM((n, rows, width), BF),
            pltpu.VMEM((n, rows, width), BF),
            pltpu.VMEM((n, pieces, rows, piece), BF),
            pltpu.VMEM((n, pieces, rows, piece), BF),
            pltpu.VMEM((n, pieces, rows, piece), BF),
            pltpu.VMEM((2, d_model // groups, width), BF),
            pltpu.SemaphoreType.DMA((3, owners)),
            pltpu.SemaphoreType.DMA((3, n)),
            pltpu.SemaphoreType.DMA((2, per)),
        ] + gather_sems(n) + scatter_sems(n, pieces),
        compiler_params=params(2),
        cost_estimate=pl.CostEstimate(
            flops=12 * n * rows * d_model * width, transcendentals=n * rows * width,
            bytes_accessed=100 << 20),
        name="ffn_backward",
    )(g, w, xall, gate, up)


def ffn_both_kernel(n, pieces, groups, x_ref, g_ref, w_ref, dw_ref, dx_ref, y_ref,
                    w_v, gbuf, xv, gate_v, up_v, hid_v, y_part, y_left, y_right,
                    x_part, x_left, x_right, stage, w_sem, own_sem, out_sem, *sems):
    line = Line(n)
    z = line.z
    owners, _, shard, width = w_ref.shape
    rows, d_model = y_ref.shape
    tile = lane_tile(width, 256)
    piece = d_model // pieces
    gather_x = Gather(line, xv, *sems[:3])
    gather_g = Gather(line, gbuf, *sems[3:6])
    scatter_y = Scatter(line, pieces, y_part, y_left, y_right, *sems[6:10], trim=1)
    scatter_x = Scatter(line, pieces, x_part, x_left, x_right, *sems[10:14], trim=1)

    def w_copy(k, f):
        return pltpu.make_async_copy(
            w_ref.at[f, k], w_v.at[k, pl.ds(f * shard, shard)], w_sem.at[k, f]
        )

    own = (pltpu.make_async_copy(x_ref, xv.at[z], own_sem.at[0]),
           pltpu.make_async_copy(g_ref, gbuf.at[z], own_sem.at[1]))
    line.barrier()
    gather_x.start(x_ref)
    gather_g.start(g_ref)
    for c in own:
        c.start()
    for k in range(3):
        for f in range(owners):
            w_copy(k, f).start()
    for c in own:
        c.wait()
    for k in range(3):
        for f in range(owners):
            w_copy(k, f).wait()

    def add_to(ref):
        def add_own(p, value):
            cols = slice(p * piece, (p + 1) * piece)
            ref[:, cols] = ref[:, cols] + value
        return add_own

    add_y, add_x = add_to(y_ref), add_to(dx_ref)

    def give(b, p, out, ref, part, scatter):
        @pl.when(b == z)
        def _():
            ref[:, p * piece:(p + 1) * piece] = out

        @pl.when(b != z)
        def _():
            part[b, p] = out.astype(BF)

        scatter.computed(b, p)

    @pl.loop(0, n)
    def _(i):
        b = line.order(i)

        @pl.when(i > 0)
        def _():
            gather_x.arrive(b)

        @pl.loop(0, width // tile)
        def _(j):
            cols = pl.ds(pl.multiple_of(j * tile, tile), tile)
            xb = xv[b]
            gate = dot_nn(xb, w_v[0, :, cols])
            up = dot_nn(xb, w_v[1, :, cols])
            gate_v[b, :, cols] = gate.astype(BF)
            up_v[b, :, cols] = up.astype(BF)
            hid_v[b, :, cols] = (gate * jax.nn.sigmoid(gate) * up).astype(BF)

        for p in range(pieces):
            out = dot_nt(hid_v[b], w_v[2, pl.ds(p * piece, piece)])
            give(b, p, out, y_ref, y_part, scatter_y)

        @pl.when(i > 0)
        def _():
            gather_g.arrive(b)

        @pl.when(i == n - 1)
        def _():
            for t in range(1, n):
                scatter_y.step(t, add_y)

        @pl.loop(0, width // tile)
        def _(j):
            cols = pl.ds(pl.multiple_of(j * tile, tile), tile)
            d_hidden = dot_nn(gbuf[b], w_v[2, :, cols])
            gate = gate_v[b, :, cols].astype(F32)
            up = up_v[b, :, cols].astype(F32)
            sig = jax.nn.sigmoid(gate)
            act = gate * sig
            gate_v[b, :, cols] = (d_hidden * up * (sig + act * (1.0 - sig))).astype(BF)
            up_v[b, :, cols] = (d_hidden * act).astype(BF)

        for p in range(pieces):
            sl = pl.ds(p * piece, piece)
            out = dot_nt(gate_v[b], w_v[0, sl]) + dot_nt(up_v[b], w_v[1, sl])
            give(b, p, out, dx_ref, x_part, scatter_x)

    group = d_model // groups
    per = group // shard

    def dw_copies(k, q, slot):
        return [
            pltpu.make_async_copy(
                stage.at[slot, pl.ds(s * shard, shard)], dw_ref.at[q * per + s, k],
                out_sem.at[slot, s])
            for s in range(per)
        ]

    def weight_unit(unit):
        k, q = unit // groups, unit % groups
        slot = unit % 2
        left = (xv, xv, gbuf)[k]
        right = (gate_v, up_v, hid_v)[k]
        if unit >= 2:
            for c in dw_copies((unit - 2) // groups, (unit - 2) % groups, slot):
                c.wait()
        lt = left[:, :, q * group:(q + 1) * group].reshape(n * rows, group)

        @pl.loop(0, width // tile)
        def _(j):
            cols = pl.ds(pl.multiple_of(j * tile, tile), tile)
            stage[slot, :, cols] = dot_tn(
                lt, right[:, :, cols].reshape(n * rows, tile)
            ).astype(BF)

        for c in dw_copies(k, q, slot):
            c.start()

    units = 3 * groups
    steps = list(scatter_x.steps())
    done = 0
    for index, t in enumerate(steps):
        if t >= n:
            scatter_y.step(t, add_y)
        scatter_x.step(t, add_x)
        until = units * (index + 1) // len(steps)
        while done < until:
            weight_unit(done)
            done += 1
    for unit in range(units - 2, units):
        for c in dw_copies(unit // groups, unit % groups, unit % 2):
            c.wait()
    gather_x.finish()
    gather_g.finish()
    scatter_y.finish()
    scatter_x.finish()


def ffn_both(x, g, w, n):
    rows, d_model = g.shape
    owners, _, shard, width = w.shape
    pieces, groups = 3, 4
    piece = d_model // pieces
    per = d_model // groups // shard
    part = [pltpu.VMEM((n, pieces, rows, piece), BF)]
    part += [pltpu.VMEM((n - 1, pieces, rows, piece), BF)] * 2
    return pl.pallas_call(
        functools.partial(ffn_both_kernel, n, pieces, groups),
        out_shape=(
            jax.ShapeDtypeStruct((owners, 3, shard, width), BF),
            jax.ShapeDtypeStruct((rows, d_model), F32),
            jax.ShapeDtypeStruct((rows, d_model), F32),
        ),
        in_specs=[ANY, ANY, ANY],
        out_specs=[ANY, VM, VM],
        scratch_shapes=[
            pltpu.VMEM((3, d_model, width), BF),
            pltpu.VMEM((n, rows, d_model), BF),
            pltpu.VMEM((n, rows, d_model), BF),
            pltpu.VMEM((n, rows, width), BF),
            pltpu.VMEM((n, rows, width), BF),
            pltpu.VMEM((n, rows, width), BF),
        ] + part + part + [
            pltpu.VMEM((2, d_model // groups, width), BF),
            pltpu.SemaphoreType.DMA((3, owners)),
            pltpu.SemaphoreType.DMA((2,)),
            pltpu.SemaphoreType.DMA((2, per)),
        ] + gather_sems(n) * 2 + scatter_sems(n, pieces) * 2,
        compiler_params=params(10),
        cost_estimate=pl.CostEstimate(
            flops=18 * n * rows * d_model * width, transcendentals=2 * n * rows * width,
            bytes_accessed=80 << 20),
        name="ffn_both",
    )(x, g, w)


def half_turn(x):
    return pltpu.roll(x, HEAD // 2, 1)


def attention_forward_kernel(n, owners, count, proj_ref, cos_ref, sin_ref, pq_ref, pk_ref, *refs):
    own = refs[:count]
    mixed_ref, lse_ref, kvall_ref, q_ref = refs[count:count + 4]
    full = refs[count + 4:2 * count + 4]
    kvbuf, vt, *sems = refs[2 * count + 4:]
    line = Line(n)
    z = line.z
    rows = q_ref.shape[0]
    total = n * rows
    gather = Gather(line, kvbuf, *sems[:3])

    def rotated(h):
        x = proj_ref[:, h * HEAD:(h + 1) * HEAD]
        return (x * cos_ref[...] + half_turn(x) * sin_ref[...]).astype(BF)

    for g in range(KV_HEADS):
        kvbuf[z, :, g * HEAD:(g + 1) * HEAD] = rotated(QUERY_HEADS + g)
    kvbuf[z, :, KV_WIDTH:] = proj_ref[:, Q_WIDTH + KV_WIDTH:].astype(BF)
    spreads = []
    stages = 0
    if count:
        cube = Cube(owners)
        stages = len(cube.chip_bits)
        for i in range(count):
            at = 3 + SPREAD_SEMS * i
            spreads.append(Spread(cube, own[i], full[i], *sems[at:at + SPREAD_SEMS]))
        joint_barrier(line, cube)
    else:
        line.barrier()
    gather.start(kvbuf.at[z])
    for s in spreads:
        s.start()
    for h in range(QUERY_HEADS):
        q_ref[:, h * HEAD:(h + 1) * HEAD] = rotated(h)
    for i in range(1, n):
        gather.arrive(line.order(i))
    kvall_ref[...] = kvbuf[...]
    allowed = pk_ref[...] <= pq_ref[...]
    for g in range(KV_HEADS):
        v = kvbuf[:, :, KV_WIDTH + g * HEAD:KV_WIDTH + (g + 1) * HEAD].reshape(total, HEAD)
        vt[g] = v.T
    for g in range(KV_HEADS):
        for r in range(PER_GROUP):
            h = g * PER_GROUP + r
            k = kvbuf[:, :, g * HEAD:(g + 1) * HEAD].reshape(total, HEAD)
            s = dot_nt(k, q_ref[:, h * HEAD:(h + 1) * HEAD]) * SCALE
            s = jnp.where(allowed, s, -1e30)
            top = jnp.max(s, axis=0, keepdims=True)
            e = jnp.exp(s - top)
            den = jnp.sum(e, axis=0, keepdims=True)
            o = dot_nn(vt[g], e.astype(BF)) / den
            mixed_ref[:, h * HEAD:(h + 1) * HEAD] = o.T.astype(BF)
            lse_ref[h:h + 1, :] = top + jnp.log(den)
            if h == 5 and stages:
                for sp in spreads:
                    sp.phase(1)
    for k in range(2, stages + 1):
        for sp in spreads:
            sp.phase(k)
    gather.finish()
    for sp in spreads:
        sp.finish()


def attention_forward(projected, cosine, sine, pos_q, pos_k, n, owners, following=()):
    rows = projected.shape[0]
    count = len(following)
    return pl.pallas_call(
        functools.partial(attention_forward_kernel, n, owners, count),
        out_shape=(
            jax.ShapeDtypeStruct((rows, Q_WIDTH), BF),
            jax.ShapeDtypeStruct((16, rows), F32),
            jax.ShapeDtypeStruct((n, rows, 2 * KV_WIDTH), BF),
            jax.ShapeDtypeStruct((rows, Q_WIDTH), BF),
        ) + spread_shapes(owners, following),
        in_specs=[VM] * (5 + count),
        out_specs=[VM] * 4 + [ANY] * count,
        scratch_shapes=[
            pltpu.VMEM((n, rows, 2 * KV_WIDTH), BF),
            pltpu.VMEM((KV_HEADS, HEAD, n * rows), BF),
        ] + gather_sems(n) + spread_sems(owners) * count,
        compiler_params=params(9 if count else 3),
        cost_estimate=pl.CostEstimate(
            flops=4 * n * rows * rows * Q_WIDTH, transcendentals=n * rows * rows * QUERY_HEADS,
            bytes_accessed=16 << 20),
        name="attention_forward",
    )(projected, cosine, sine, pos_q, pos_k, *following)


def attention_backward_kernel(n, q_ref, kvall_ref, lse_ref, dm_ref, cos_ref, sin_ref, pq_ref,
                              pk_ref, dproj_ref, dkv_ref, kt, dk_acc, dv_acc, part,
                              from_l, from_r, *sems):
    line = Line(n)
    z = line.z
    rows = q_ref.shape[0]
    total = n * rows
    pieces = KV_HEADS
    scatter = Scatter(line, pieces, part, from_l, from_r, *sems)
    line.barrier()

    def rotated_back(x):
        return (x * cos_ref[...] - half_turn(x) * sin_ref[...]).astype(BF)

    allowed = pk_ref[...] <= pq_ref[...]
    for g in range(KV_HEADS):
        k = kvall_ref[:, :, g * HEAD:(g + 1) * HEAD].reshape(total, HEAD)
        kt[g] = k.T
    for g in range(KV_HEADS):
        for r in range(PER_GROUP):
            h = g * PER_GROUP + r
            cols = slice(h * HEAD, (h + 1) * HEAD)
            k = kvall_ref[:, :, g * HEAD:(g + 1) * HEAD].reshape(total, HEAD)
            v = kvall_ref[:, :, KV_WIDTH + g * HEAD:KV_WIDTH + (g + 1) * HEAD].reshape(total, HEAD)
            q = q_ref[:, cols]
            dm = dm_ref[:, cols]
            s = dot_nt(k, q) * SCALE
            pr = jnp.where(allowed, jnp.exp(s - lse_ref[h:h + 1, :]), 0.0)
            dp = dot_nt(v, dm)
            delta = jnp.sum(pr * dp, axis=0, keepdims=True)
            ds = (pr * (dp - delta) * SCALE).astype(BF)
            dv = dot_nn(pr.astype(BF), dm)
            dk = dot_nn(ds, q)
            if r == 0:
                dk_acc[...] = dk
                dv_acc[...] = dv
            else:
                dk_acc[...] += dk
                dv_acc[...] += dv
            dproj_ref[:, cols] = rotated_back(dot_nn(kt[g], ds).T)
        for b in range(n):
            sl = slice(b * rows, (b + 1) * rows)

            @pl.when(b == z)
            def _():
                dkv_ref[:, g * HEAD:(g + 1) * HEAD] = dk_acc[sl]
                dkv_ref[:, KV_WIDTH + g * HEAD:KV_WIDTH + (g + 1) * HEAD] = dv_acc[sl]

            @pl.when(b != z)
            def _():
                part[b, g, :, 0:HEAD] = dk_acc[sl].astype(BF)
                part[b, g, :, HEAD:2 * HEAD] = dv_acc[sl].astype(BF)

            scatter.computed(b, g)

    def add_own(p, value):
        a = slice(p * HEAD, (p + 1) * HEAD)
        c = slice(KV_WIDTH + p * HEAD, KV_WIDTH + (p + 1) * HEAD)
        dkv_ref[:, a] = dkv_ref[:, a] + value[:, :HEAD]
        dkv_ref[:, c] = dkv_ref[:, c] + value[:, HEAD:]

    for t in scatter.steps():
        scatter.step(t, add_own)
    for g in range(KV_HEADS):
        cols = slice(Q_WIDTH + g * HEAD, Q_WIDTH + (g + 1) * HEAD)
        dproj_ref[:, cols] = rotated_back(dkv_ref[:, g * HEAD:(g + 1) * HEAD])
    dproj_ref[:, Q_WIDTH + KV_WIDTH:] = dkv_ref[:, KV_WIDTH:].astype(BF)
    scatter.finish()


def attention_backward(q, kvall, lse, dm, cosine, sine, pos_q, pos_k, n):
    rows = q.shape[0]
    return pl.pallas_call(
        functools.partial(attention_backward_kernel, n),
        out_shape=jax.ShapeDtypeStruct((rows, Q_WIDTH + 2 * KV_WIDTH), BF),
        in_specs=[VM] * 8,
        out_specs=VM,
        scratch_shapes=[
            pltpu.VMEM((rows, 2 * KV_WIDTH), F32),
            pltpu.VMEM((KV_HEADS, HEAD, n * rows), BF),
            pltpu.VMEM((n * rows, HEAD), F32),
            pltpu.VMEM((n * rows, HEAD), F32),
        ] + [pltpu.VMEM((n, KV_HEADS, rows, 2 * HEAD), BF)] * 3 + scatter_sems(n, KV_HEADS),
        compiler_params=params(4),
        cost_estimate=pl.CostEstimate(
            flops=10 * n * rows * rows * Q_WIDTH, transcendentals=n * rows * rows * QUERY_HEADS,
            bytes_accessed=16 << 20),
        name="attention_backward",
    )(q, kvall, lse, dm, cosine, sine, pos_q, pos_k)


class Fold:
    def __init__(self, cube, src, mine, first, later, load_sem, send1, recv1, send2, recv2):
        self.cube, self.src = cube, src
        self.mine, self.first, self.later = mine, first, later
        self.load_sem, self.send1, self.recv1 = load_sem, send1, recv1
        self.send2, self.recv2 = send2, recv2
        self.rows = mine.shape[1]
        self.half = self.rows // 2
        self.steps = cube.plan()
        self.stages = len(cube.chip_bits)

    def _load(self, d):
        return pltpu.make_async_copy(
            self.src(self.cube.flip(2 * d)), self.mine.at[d], self.load_sem.at[d])

    def _core(self, d):
        return pltpu.make_async_remote_copy(
            src_ref=self.src(self.cube.flip(2 * d | 1)), dst_ref=self.first.at[d],
            send_sem=self.send1.at[d], recv_sem=self.recv1.at[d],
            device_id={"fsdp": self.cube.flip(1)}, device_id_type=MESH)

    def _hop(self, half, stage, index):
        bit, rest, slot = self.steps[half, stage]
        rows = pl.ds(half * self.half, self.half)
        return pltpu.make_async_remote_copy(
            src_ref=self.mine.at[bit | rest[index], rows],
            dst_ref=self.later.at[half, slot + index],
            send_sem=self.send2.at[half, slot + index],
            recv_sem=self.recv2.at[half, slot + index],
            device_id={"fsdp": self.cube.flip(2 * bit)}, device_id_type=MESH)

    def _hops(self, stage):
        return [self._hop(half, stage, i)
                for half in (0, 1) for i in range(len(self.steps[half, stage][1]))]

    def _add(self, d, base, size, other):
        dtype = self.mine.dtype
        strip = 48 if size % 48 == 0 else size

        @pl.loop(0, size // strip)
        def _(i):
            into = pl.ds(pl.multiple_of(base + i * strip, 8), strip)
            rows = pl.ds(pl.multiple_of(i * strip, 8), strip)
            self.mine[d, into] = (
                self.mine[d, into].astype(F32) + other(rows).astype(F32)).astype(dtype)

    def start(self):
        for d in range(self.cube.chips):
            self._core(d).start()
        for d in range(self.cube.chips):
            self._load(d).start()

    def phase(self, k):
        if k == 0:
            for d in range(self.cube.chips):
                self._load(d).wait()
                self._core(d).wait_recv()
                self._add(d, 0, self.rows, lambda rows, d=d: self.first[d, rows])
        else:
            for half in (0, 1):
                _, rest, slot = self.steps[half, k - 1]
                for i, e in enumerate(rest):
                    self._hop(half, k - 1, i).wait_recv()
                    self._add(e, half * self.half, self.half,
                              lambda rows, h=half, j=slot + i: self.later[h, j, rows])
        if k < self.stages:
            for c in self._hops(k):
                c.start()

    def finish(self):
        for d in range(self.cube.chips):
            self._core(d).wait_send()
        for stage in range(self.stages):
            for c in self._hops(stage):
                c.wait_send()


def fold_scratch(owners, rows, width, dtype):
    chips = owners // 2
    return [
        pltpu.VMEM((chips, rows, width), dtype),
        pltpu.VMEM((chips, rows, width), dtype),
        pltpu.VMEM((2, chips - 1, rows // 2, width), dtype),
        pltpu.SemaphoreType.DMA((chips,)),
        pltpu.SemaphoreType.DMA((chips,)),
        pltpu.SemaphoreType.DMA((chips,)),
        pltpu.SemaphoreType.DMA((2, chips - 1)),
        pltpu.SemaphoreType.DMA((2, chips - 1)),
    ]


FOLD_REFS = 8


def reduce_kernel(n, owners, small_ref, out_ref, qkv_ref, dw_ref, early_out, early_qkv,
                  small_o, out_o, qkv_o, dw_o, early_out_o, early_qkv_o, *refs):
    line = Line(n)
    cube = Cube(owners)
    refs = list(refs)

    def take(count):
        taken = refs[:count]
        del refs[:count]
        return taken

    sources = [
        lambda q: small_ref.at[q],
        lambda q: out_ref.at[q],
        lambda q: qkv_ref.at[q],
        lambda q: dw_ref.at[q, 0],
        lambda q: dw_ref.at[q, 1],
        lambda q: dw_ref.at[q, 2],
    ]
    folds = [Fold(cube, src, *take(FOLD_REFS)) for src in sources]
    small_all, = take(1)
    gather_small = Gather(line, small_all, *take(3))
    shared = []
    for _ in range(4):
        part, from_l, from_r, total, own = take(5)
        shared.append((Scatter(line, 1, part, from_l, from_r, *take(4)), part,
                       Gather(line, total, *take(3)), total, own))
    write_sem, = take(1)
    targets = (out_o, qkv_o, early_out_o, early_qkv_o)

    def share(index, value):
        scatter, part, _, _, own = shared[index]
        rows = part.shape[2]
        for b in range(n):
            @pl.when(b == line.z)
            def _():
                own[...] = value(slice(b * rows, (b + 1) * rows)).astype(F32)

            @pl.when(b != line.z)
            def _():
                part[b, 0] = value(slice(b * rows, (b + 1) * rows))

            scatter.computed(b, 0)

    def scatter_step(indices, t):
        for index in indices:
            scatter, _, _, _, own = shared[index]

            def add_own(p, value):
                own[...] = own[...] + value

            scatter.step(t, add_own)

    def gather_start(indices):
        for index in indices:
            _, _, gather, total, own = shared[index]
            total[line.z] = own[...].astype(BF)
            gather.start(total.at[line.z])

    def gather_step(indices, i):
        for index in indices:
            shared[index][2].arrive(line.order(i))

    def collect(indices):
        for index in indices:
            targets[index][...] = shared[index][3][...].reshape(targets[index].shape)

    def line_jobs(indices):
        jobs = [functools.partial(scatter_step, indices, t)
                for t in range(1, 2 * (n - 1) + 1)]
        jobs.append(functools.partial(gather_start, indices))
        jobs += [functools.partial(gather_step, indices, i) for i in range(1, n)]
        jobs.append(functools.partial(collect, indices))
        return jobs

    def small_job():
        for i in range(1, n):
            gather_small.arrive(line.order(i))
        small_o[...] = jnp.sum(small_all[...], axis=0)

    joint_barrier(line, cube)
    for f in folds:
        f.start()
    share(2, lambda rows: early_out[rows])
    share(3, lambda rows: early_qkv[rows])
    last = folds[0].stages
    jobs = line_jobs((2, 3))

    def after(index):
        fold = folds[index]
        if index == 0:
            small_all[line.z] = fold.mine[0]
            gather_small.start(small_all.at[line.z])
            jobs.append(small_job)
        elif index <= 2:
            share(index - 1, lambda rows: fold.mine[0, rows])
            if index == 2:
                jobs.extend(line_jobs((0, 1)))
        else:
            pltpu.make_async_copy(fold.mine.at[0], dw_o.at[index - 3], write_sem.at[index - 3]).start()

    count = len(folds)
    for t in range(count + last):
        for k in range(last + 1):
            if 0 <= t - k < count:
                folds[t - k].phase(k)
                if k == last:
                    after(t - k)
                for _ in range(2):
                    if jobs and t >= 1:
                        jobs.pop(0)()
    for job in jobs:
        job()
    for k in range(3):
        pltpu.make_async_copy(folds[3 + k].mine.at[0], dw_o.at[k], write_sem.at[k]).wait()
    for f in folds:
        f.finish()
    gather_small.finish()
    for scatter, _, gather, _, _ in shared:
        scatter.finish()
        gather.finish()


def reduce_all(small, out_g, qkv_g, dw, early_out, early_qkv, n):
    owners, shard, d_model = out_g.shape
    width = dw.shape[3]
    qkv_width = qkv_g.shape[2]
    scratch = fold_scratch(owners, small.shape[1], 128, F32)
    scratch += fold_scratch(owners, shard, d_model, BF)
    scratch += fold_scratch(owners, shard, qkv_width, BF)
    for _ in range(3):
        scratch += fold_scratch(owners, shard, width, BF)
    scratch += [pltpu.VMEM((n, small.shape[1], 128), F32)] + gather_sems(n)
    for w in (d_model, qkv_width, d_model, qkv_width):
        scratch += [pltpu.VMEM((n, 1, shard // n, w), BF)] * 3
        scratch += [pltpu.VMEM((n, shard // n, w), BF), pltpu.VMEM((shard // n, w), F32)]
        scratch += scatter_sems(n, 1) + gather_sems(n)
    scratch += [pltpu.SemaphoreType.DMA((3,))]
    return pl.pallas_call(
        functools.partial(reduce_kernel, n, owners),
        out_shape=(
            jax.ShapeDtypeStruct(small.shape[1:], F32),
            jax.ShapeDtypeStruct((shard, d_model), BF),
            jax.ShapeDtypeStruct((shard, qkv_width), BF),
            jax.ShapeDtypeStruct((3, shard, width), BF),
            jax.ShapeDtypeStruct((shard, d_model), BF),
            jax.ShapeDtypeStruct((shard, qkv_width), BF),
        ),
        in_specs=[ANY] * 4 + [VM] * 2,
        out_specs=[VM, VM, VM, ANY, VM, VM],
        scratch_shapes=scratch,
        compiler_params=params(5),
        cost_estimate=pl.CostEstimate(
            flops=1 << 20, transcendentals=0, bytes_accessed=300 << 20),
        name="reduce_all",
    )(small, out_g, qkv_g, dw, early_out, early_qkv)


def normalize(stream, gain):
    return stream * lax.rsqrt(jnp.mean(stream * stream, axis=-1, keepdims=True) + EPSILON) * gain


def normalize_back(grad, stream, gain):
    r = lax.rsqrt(jnp.mean(stream * stream, axis=-1, keepdims=True) + EPSILON)
    u = grad * gain
    back = r * (u - stream * (r * r) * jnp.mean(u * stream, axis=-1, keepdims=True))
    return back, jnp.sum(grad * stream * r, axis=0)


def frequencies():
    return jnp.power(ROPE_BASE, -(jnp.arange(HEAD // 2, dtype=F32) * 2.0 / HEAD))


def shards(hidden_in, cotangent, seq_lengths, tile_place, norm_attn, w_qkv, b_qkv, w_out,
           norm_mlp, w_gate, w_up, w_down):
    n = lax.axis_size("context")
    owners = lax.axis_size("fsdp")
    rows, d_model = hidden_in.shape[1:]
    hidden_units = w_gate.shape[2]
    width = -(-hidden_units // 128) * 128
    pad = width - hidden_units
    total = n * rows

    row_index = jnp.arange(total, dtype=jnp.int32)
    tile_order = tile_place[0]
    selector = (
        row_index[:, None] // TILE == jnp.arange(tile_order.shape[0], dtype=jnp.int32)[None, :]
    ).astype(jnp.int32)
    position = jnp.sum(selector * tile_order[None, :], axis=1) * TILE + row_index % TILE
    valid = position < seq_lengths[0]
    offset = lax.axis_index("context") * rows
    my_position = lax.dynamic_slice_in_dim(position, offset, rows)
    my_valid = lax.dynamic_slice_in_dim(valid, offset, rows)
    pos_q = my_position[None, :]
    pos_k = jnp.where(valid, position, 1 << 30)[:, None]
    angles = my_position.astype(F32)[:, None] * frequencies()
    cosine, sine = jnp.cos(angles), jnp.sin(angles)
    cosine = jnp.concatenate([cosine, cosine], axis=1)
    sine = jnp.concatenate([-sine, sine], axis=1)

    shard = norm_attn.shape[1]
    bias_shard = b_qkv.shape[1]

    def ffn_shard(l):
        return jnp.stack([
            jnp.pad(m, ((0, 0), (0, pad))) for m in (w_gate[l], w_up[l], w_down[l].T)])

    def packed(parts, lead):
        flat = jnp.concatenate(parts, axis=-1)
        used = flat.shape[-1]
        lines = -(-used // (16 * 128)) * 16
        flat = jnp.pad(flat, ((0, 0),) * (flat.ndim - 1) + ((0, lines * 128 - used),))
        return flat.reshape(lead + (lines, 128))

    small = packed(
        [m.reshape(-1).astype(F32) for m in (norm_attn, norm_mlp, b_qkv)], ())
    first_ffn = ffn_shard(0)
    first_ffn, small = lax.optimization_barrier((first_ffn, small))
    ffn_weights = [lax.all_gather(first_ffn, "fsdp", axis=0, tiled=False)]
    small, qkv_w = spread_all(owners, small, w_qkv[0])
    qkv_weights = [qkv_w.reshape(d_model, -1)]
    out_weights = []
    small = small.reshape(owners, -1)
    gains_attn, gains_mlp, biases = [], [], []
    for l in range(LAYERS):
        gains_attn.append(small[:, l * shard:(l + 1) * shard].reshape(-1))
        gains_mlp.append(small[:, (LAYERS + l) * shard:(LAYERS + l + 1) * shard].reshape(-1))
        start = 2 * LAYERS * shard + l * bias_shard
        biases.append(small[:, start:start + bias_shard].reshape(-1))

    stream = hidden_in[0].astype(F32)
    gradient = cotangent[0].astype(F32) * my_valid[:, None].astype(F32)
    kept = []
    for l in range(LAYERS):
        qkv_w, ffn_w = qkv_weights[l], ffn_weights[l]
        if l + 1 < LAYERS:
            ffn_weights.append(lax.all_gather(ffn_shard(l + 1), "fsdp", axis=0, tiled=False))
        normed = normalize(stream, gains_attn[l]).astype(BF)
        projected = jnp.dot(normed, qkv_w, preferred_element_type=F32) + biases[l]
        following = (w_out[l],) if l == 0 else ()
        mixed, lse, kvall, q, *out_w = attention_forward(
            projected, cosine, sine, pos_q, pos_k, n, owners, following)
        out_weights += [m.reshape(Q_WIDTH, d_model) for m in out_w]
        out_w = out_weights[l]
        middle = stream + jnp.dot(mixed, out_w, preferred_element_type=F32)
        normed_two = normalize(middle, gains_mlp[l]).astype(BF)
        if l + 1 < LAYERS:
            xall, gate, up, y, next_qkv, next_out = ffn_forward(
                normed_two, ffn_w, n, (w_qkv[l + 1], w_out[l + 1]))
            qkv_weights.append(next_qkv.reshape(d_model, -1))
            out_weights.append(next_out.reshape(Q_WIDTH, d_model))
        else:
            dw, dx, y = ffn_both(normed_two, gradient.astype(BF), ffn_w, n)
            xall, gate, up = None, None, None
        kept.append((stream, normed, q, kvall, lse, mixed, middle, xall, gate, up,
                     qkv_w, out_w, ffn_w))
        stream = middle + y
    layer_out = stream.astype(BF)[None]

    small_grads = [None] * LAYERS
    big_grads = [None] * LAYERS
    for l in reversed(range(LAYERS)):
        (stream, normed, q, kvall, lse, mixed, middle, xall, gate, up,
         qkv_w, out_w, ffn_w) = kept[l]
        if l < LAYERS - 1:
            dw, dx = ffn_backward(gradient.astype(BF), ffn_w, xall, gate, up, n)
            out_sum, qkv_sum, dw_sum = big_grads[l + 1]
            dx, dw_sum = lax.optimization_barrier((dx, dw_sum))
        back, gain_two = normalize_back(dx, middle, gains_mlp[l])
        d_middle = gradient + back
        d_low = d_middle.astype(BF)
        d_mixed = jnp.einsum("td,cd->tc", d_low, out_w, preferred_element_type=F32).astype(BF)
        out_grad = jnp.einsum("tc,td->cd", mixed, d_low, preferred_element_type=F32).astype(BF)
        d_projected = attention_backward(
            q, kvall, lse, d_mixed, cosine, sine, pos_q, pos_k, n)
        if l < LAYERS - 1:
            d_projected, out_sum = lax.optimization_barrier((d_projected, out_sum))
            big_grads[l + 1] = (out_sum, qkv_sum, dw_sum)
        bias_grad = jnp.sum(d_projected.astype(F32), axis=0)
        d_normed = jnp.einsum("tc,dc->td", d_projected, qkv_w, preferred_element_type=F32)
        qkv_grad = jnp.einsum(
            "td,tc->dc", normed, d_projected, preferred_element_type=F32).astype(BF)
        back, gain_one = normalize_back(d_normed, stream, gains_attn[l])
        gradient = d_middle + back
        small_grads[l] = (gain_one, gain_two, bias_grad)
        if l > 0:
            big_grads[l] = (
                lax.psum_scatter(out_grad, "fsdp", scatter_dimension=0, tiled=True),
                lax.psum_scatter(qkv_grad, "fsdp", scatter_dimension=0, tiled=True),
                lax.psum_scatter(dw, "fsdp", scatter_dimension=0, tiled=False))
        else:
            small = packed([
                m.reshape(owners, -1)
                for k in range(3) for m in (small_grads[i][k] for i in range(LAYERS))], (owners,))
            out_early, qkv_early, dw_sum = big_grads[l + 1]
            small, out_sum, qkv_sum, dw_last, out_early, qkv_early = reduce_all(
                small, out_grad.reshape(owners, shard, d_model),
                qkv_grad.reshape(owners, shard, qkv_grad.shape[1]), dw, out_early, qkv_early, n)
            big_grads[l + 1] = (out_early, qkv_early, dw_sum)
            small = small.reshape(-1)
            big_grads[l] = (out_sum, qkv_sum, dw_last)

    grad_norm_attn = small[:LAYERS * shard].reshape(LAYERS, shard)
    grad_norm_mlp = small[LAYERS * shard:2 * LAYERS * shard].reshape(LAYERS, shard)
    start = 2 * LAYERS * shard
    grad_b_qkv = small[start:start + LAYERS * bias_shard].reshape(LAYERS, bias_shard)

    def stacked(pick):
        return jnp.stack([pick(big_grads[l]).astype(F32) for l in range(LAYERS)])

    return (
        layer_out,
        gradient[None],
        grad_norm_attn,
        stacked(lambda m: m[1]),
        grad_b_qkv,
        stacked(lambda m: m[0]),
        grad_norm_mlp,
        stacked(lambda m: m[2][0, :, :hidden_units]),
        stacked(lambda m: m[2][1, :, :hidden_units]),
        stacked(lambda m: m[2][2, :, :hidden_units].T),
    )


def solution(mesh):
    return jax.shard_map(
        shards,
        mesh=mesh,
        in_specs=(
            P("fsdp", "context", None),
            P("fsdp", "context", None),
            P("fsdp"),
            P("fsdp", None),
            P(None, "fsdp"),
            P(None, "fsdp", None),
            P(None, "fsdp"),
            P(None, "fsdp", None),
            P(None, "fsdp"),
            P(None, "fsdp", "context"),
            P(None, "fsdp", "context"),
            P(None, "context", "fsdp"),
        ),
        out_specs=(
            P("fsdp", "context", None),
            P("fsdp", "context", None),
            P(None, "fsdp"),
            P(None, "fsdp", None),
            P(None, "fsdp"),
            P(None, "fsdp", None),
            P(None, "fsdp"),
            P(None, "fsdp", "context"),
            P(None, "fsdp", "context"),
            P(None, "context", "fsdp"),
        ),
        check_vma=False,
    )
```
